32 devices in a mesh: dp: 16 (over z, y, x), tensor: 2 (over core).
Axes of the slice: x: 2, y: 2, z: 4, core: 2. Of those that a mesh axis runs over, the one named last changes fastest.
Arguments:
- inputs: bfloat16 [12288, 1536], P(('dp', 'tensor')), may hold values from -6 to 6
- cotangent: bfloat16 [12288, 1536], P(('dp', 'tensor')), may hold values from -12 to 12
- context: bfloat16 [16, 130, 768], P('dp'), may hold values from -6 to 6
- context_live: int32 [16, 130], P('dp'), may hold values from 0 to 1, as said below
- lengths: int32 [16], P('dp'), may hold values from 384 to 768, as said below
- threshold: float32 [1], replicated, may hold values from 5 to 8
- self_gain: bfloat16 [1536], P('dp'), may hold values from 0.5 to 1.5
- self_bias: bfloat16 [1536], P('dp'), may hold values from -1.75 to 1.75
- self_query: bfloat16 [1536, 1536], P('dp', 'tensor')
- self_key: bfloat16 [1536, 1536], P('dp', 'tensor'), may hold values from -0.15625 to 0.15625
- self_value: bfloat16 [1536, 1536], P('dp', 'tensor'), may hold values from -0.15625 to 0.15625
- self_output: bfloat16 [1536, 1536], P('tensor', 'dp'), may hold values from -0.875 to 0.875
- cross_gain: bfloat16 [1536], P('dp'), may hold values from 0.5 to 1.5
- cross_bias: bfloat16 [1536], P('dp'), may hold values from -1.75 to 1.75
- cross_query: bfloat16 [1536, 1536], P('dp', 'tensor')
- cross_key: bfloat16 [768, 1536], P('dp', 'tensor'), may hold values from -0.21875 to 0.21875
- cross_value: bfloat16 [768, 1536], P('dp', 'tensor'), may hold values from -0.21875 to 0.21875
- cross_output: bfloat16 [1536, 1536], P('tensor', 'dp'), may hold values from -0.4375 to 0.4375
- feed_gain: bfloat16 [1536], P('dp'), may hold values from 0.5 to 1.5
- feed_bias: bfloat16 [1536], P('dp'), may hold values from -1.75 to 1.75
- gate_weight: bfloat16 [1536, 6144], P('dp', 'tensor'), may hold values from -0.15625 to 0.15625
- up_weight: bfloat16 [1536, 6144], P('dp', 'tensor'), may hold values from -0.15625 to 0.15625
- down_weight: bfloat16 [6144, 1536], P('tensor', 'dp'), may hold values from -0.078125 to 0.078125
Outputs:
- result: bfloat16 [12288, 1536], P(('dp', 'tensor'))
- input_grad: float32 [12288, 1536], P(('dp', 'tensor'))
- grad_self_gain: float32 [1536], P('dp')
- grad_self_bias: float32 [1536], P('dp')
- grad_self_query: float32 [1536, 1536], P('dp', 'tensor')
- grad_self_key: float32 [1536, 1536], P('dp', 'tensor')
- grad_self_value: float32 [1536, 1536], P('dp', 'tensor')
- grad_self_output: float32 [1536, 1536], P('tensor', 'dp')
- grad_cross_gain: float32 [1536], P('dp')
- grad_cross_bias: float32 [1536], P('dp')
- grad_cross_query: float32 [1536, 1536], P('dp', 'tensor')
- grad_cross_key: float32 [768, 1536], P('dp', 'tensor')
- grad_cross_value: float32 [768, 1536], P('dp', 'tensor')
- grad_cross_output: float32 [1536, 1536], P('tensor', 'dp')
- grad_feed_gain: float32 [1536], P('dp')
- grad_feed_bias: float32 [1536], P('dp')
- grad_gate_weight: float32 [1536, 6144], P('dp', 'tensor')
- grad_up_weight: float32 [1536, 6144], P('dp', 'tensor')
- grad_down_weight: float32 [6144, 1536], P('tensor', 'dp')
- peaks: float32 [24], P('tensor')
- scaled_self_query: float32 [1536, 1536], P('dp', 'tensor')
- scaled_self_key: float32 [1536, 1536], P('dp', 'tensor')
- scaled_cross_query: float32 [1536, 1536], P('dp', 'tensor')
- scaled_cross_key: float32 [768, 1536], P('dp', 'tensor')
The draws below stay inside these ranges and needn't reach their ends.
Inputs may be any that keep to these rules, and one draw needn't show every extreme that they name: lengths counts the valid latent tokens of a sequence; the first sequence is full. `context_live`: the first conditioning token of every sequence is live.
All inputs are finite; a program needn't handle non-finite values.
Results may differ from the reference program's by a relative error of at most 0.025.
The reference program's roundings to bfloat16 on the way count: a program that leaves them out, or rounds other values in their place, can miss the bound.
Values may be sent and summed in bfloat16 or wider, within the bound.
A program may use at most 256 MiB of HBM per device.

```python
import math
import jax
import jax.numpy as jnp
from jax import lax

D = 1536
HEADS = 24
HEAD_DIM = 64
FF = 6144
COND_DIM = 768
COND_TOK = 130
ROT_DIM = 32
SEQ_LEN = 768
SEQS = 16
TOKENS = 12288


def query_draw(key, salt):
    base_key = jax.random.fold_in(key, salt)
    entry_key, factor_key = jax.random.split(base_key)
    entries = jax.random.normal(entry_key, (D, D), jnp.float32)
    factors = jnp.exp(jax.random.uniform(factor_key, (HEADS,), jnp.float32, 0.0, math.log(3.0)))
    columns = jnp.repeat(factors, HEAD_DIM)
    return (entries * columns[None, :] / math.sqrt(D)).astype(jnp.bfloat16)


def draw_self_query(key, part):
    return query_draw(key, 101)


def draw_cross_query(key, part):
    return query_draw(key, 202)


def draw_lengths(key, part):
    drawn = jax.random.randint(jax.random.fold_in(key, 303), (SEQS,), SEQ_LEN // 2, SEQ_LEN + 1)
    return drawn.at[0].set(SEQ_LEN).astype(jnp.int32)


def draw_context_live(key, part):
    drawn = jax.random.randint(jax.random.fold_in(key, 404), (SEQS, COND_TOK), 0, 10)
    live = (drawn < 7).astype(jnp.int32)
    return live.at[:, 0].set(1)


def strengthened(values, rng, source, target, parts, factor):
    owner, partner = [(jnp.arange(values.shape[dim]) // (values.shape[dim] // parts)).reshape([-1 if axis == dim else 1 for axis in range(values.ndim)]) for dim in (source, target)]
    chosen = jax.random.permutation(rng, parts)[partner]
    strong = (owner == chosen) | (owner == (partner + parts // 2) % parts)
    return jnp.where(strong, factor * values, values)


def shard_levels(stream_key, shape, shards, smallest, largest):
    def one(axis_at, blocks):
        heights = jax.random.uniform(jax.random.fold_in(jax.random.fold_in(stream_key, 6), axis_at), (blocks,), jnp.float32, smallest / len(shards), largest / len(shards))
        return jnp.repeat(jnp.exp(heights), shape[axis_at] // blocks).reshape((-1,) + (1,) * (len(shape) - axis_at - 1))

    factor_of = one(*shards[0])
    for cut in shards[1:]:
        factor_of = factor_of * one(*cut)
    return factor_of


def gaussian(rng, extent, spread, bound, shards=(), held_as=jnp.bfloat16):
    gain = shard_levels(rng, extent, shards, -0.22, 0.18) if shards else 1.0
    values = jax.random.normal(rng, extent, jnp.float32) * spread * gain
    return jnp.minimum(jnp.maximum(values, -bound), bound).astype(held_as)


def bell_draw_with(stream_key, shape, spread, bound, cuts, heavy, dtype=jnp.bfloat16):
    values = spread * jax.random.normal(stream_key, shape, jnp.float32)
    if cuts:
        values = values * shard_levels(stream_key, shape, cuts, -0.22, 0.18)
    return jnp.clip(strengthened(values, jax.random.fold_in(stream_key, 3), *heavy), -bound, bound).astype(dtype)


def setup_inputs(seed: int = 0) -> dict:
    arg_keys = jax.random.split(jax.random.key(seed), 24)
    inputs = gaussian(arg_keys[0], (TOKENS, D), 1.0, 6.0, ((0, 32),))
    cotangent = bell_draw_with(arg_keys[1], (TOKENS, D), 1.0, 12.0, ((0, 32),), (0, 1, 32, 2.75))
    context = gaussian(arg_keys[2], (SEQS, COND_TOK, COND_DIM), 1.0, 6.0, ((0, 16),))
    context_live = draw_context_live(jax.random.fold_in(arg_keys[23], 71), 0)
    lengths = draw_lengths(jax.random.fold_in(arg_keys[23], 71), 0)
    threshold = jnp.clip(jax.random.uniform(arg_keys[5], (1,), jnp.float32, 5.0, 8.0), 5.0, 8.0)
    self_gain = jnp.clip(1.0 + 0.1 * jax.random.normal(arg_keys[6], (D,), jnp.float32), 0.5, 1.5).astype(jnp.bfloat16)
    self_bias = gaussian(arg_keys[7], (D,), 0.3, 1.75, ((0, 16),))
    self_query = draw_self_query(jax.random.fold_in(arg_keys[23], 71), 0)
    self_key = gaussian(arg_keys[9], (D, D), D ** -0.5, 0.15625, ((0, 16), (1, 2)))
    self_value = gaussian(arg_keys[10], (D, D), D ** -0.5, 0.15625, ((0, 16), (1, 2)))
    self_output = gaussian(arg_keys[11], (D, D), (D // 32) ** -0.5, 0.875, ((0, 2), (1, 16)))
    cross_gain = jnp.clip(1.0 + 0.1 * jax.random.normal(arg_keys[12], (D,), jnp.float32), 0.5, 1.5).astype(jnp.bfloat16)
    cross_bias = gaussian(arg_keys[13], (D,), 0.3, 1.75, ((0, 16),))
    cross_query = draw_cross_query(jax.random.fold_in(arg_keys[23], 71), 0)
    cross_key = gaussian(arg_keys[15], (COND_DIM, D), COND_DIM ** -0.5, 0.21875, ((0, 16), (1, 2)))
    cross_value = gaussian(arg_keys[16], (COND_DIM, D), COND_DIM ** -0.5, 0.21875, ((0, 16), (1, 2)))
    cross_output = gaussian(arg_keys[17], (D, D), (D // 8) ** -0.5, 0.4375, ((0, 2), (1, 16)))
    feed_gain = jnp.clip(1.0 + 0.1 * jax.random.normal(arg_keys[18], (D,), jnp.float32), 0.5, 1.5).astype(jnp.bfloat16)
    feed_bias = gaussian(arg_keys[19], (D,), 0.3, 1.75, ((0, 16),))
    gate_weight = gaussian(arg_keys[20], (D, FF), D ** -0.5, 0.15625, ((0, 16), (1, 2)))
    up_weight = gaussian(arg_keys[21], (D, FF), D ** -0.5, 0.15625, ((0, 16), (1, 2)))
    down_weight = gaussian(arg_keys[22], (FF, D), FF ** -0.5, 0.078125, ((0, 2), (1, 16)))
    return dict(inputs=inputs, cotangent=cotangent, context=context, context_live=context_live, lengths=lengths, threshold=threshold, self_gain=self_gain, self_bias=self_bias, self_query=self_query, self_key=self_key, self_value=self_value, self_output=self_output, cross_gain=cross_gain, cross_bias=cross_bias, cross_query=cross_query, cross_key=cross_key, cross_value=cross_value, cross_output=cross_output, feed_gain=feed_gain, feed_bias=feed_bias, gate_weight=gate_weight, up_weight=up_weight, down_weight=down_weight)


@jax.custom_vjp
def low(v):
    return lax.optimization_barrier(v.astype(jnp.bfloat16)).astype(jnp.float32)

@jax.custom_vjp
def low_back(v):
    return v

def low_keep(v):
    return (low(v), None)

def low_pass(kept, grad):
    return (grad,)

def back_keep(v):
    return (v, None)

def back_low(kept, grad):
    return (low(grad),)
low.defvjp(low_keep, low_pass)
low_back.defvjp(back_keep, back_low)
EPSILON = 1e-05
HIGHEST = lax.Precision.HIGHEST
NEGATIVE = -1e+30

def product(left, right):
    return jnp.dot(left, right, precision=HIGHEST)

def norm_apply(stream, gain_vec, bias_vec):
    average = lax.optimization_barrier(jnp.mean(stream, axis=-1, keepdims=True))
    centred = stream - average
    inverse = lax.rsqrt(lax.optimization_barrier(jnp.mean(centred * centred, axis=-1, keepdims=True)) + EPSILON)
    return centred * inverse * gain_vec + bias_vec

def rotate(field, positions):
    half_count = ROT_DIM // 2
    rates = 10000.0 ** (-jnp.arange(0, ROT_DIM, 2).astype(jnp.float32) / ROT_DIM)
    angles = positions[:, None] * rates[None, :]
    cosine = jnp.cos(angles)[:, None, :]
    sine = jnp.sin(angles)[:, None, :]
    first = field[..., :half_count]
    second = field[..., half_count:ROT_DIM]
    return jnp.concatenate([first * cosine - second * sine, second * cosine + first * sine, field[..., ROT_DIM:]], axis=-1)

def attend(query, keys, values, allowed):
    raw_scores = low_back(jnp.einsum('qhe,khe->hqk', query, keys, precision=HIGHEST))
    scores = jnp.where(allowed[None, None, :], raw_scores * HEAD_DIM ** (-0.5), NEGATIVE)
    head_peak = lax.optimization_barrier(jnp.max(scores, axis=(1, 2)))
    weighting = jax.nn.softmax(scores, axis=-1)
    mixed = jnp.einsum('hqk,khe->qhe', low(weighting), values, precision=HIGHEST)
    return (mixed, head_peak)

def block(rows, params, memory, live_row, length):
    self_gain, self_bias, self_query, self_key, self_value, self_output, cross_gain, cross_bias, cross_query, cross_key, cross_value, cross_output, feed_gain, feed_bias, gate_weight, up_weight, down_weight = params
    positions = jnp.arange(SEQ_LEN).astype(jnp.float32)
    head_shape = (SEQ_LEN, HEADS, HEAD_DIM)
    memory_shape = (COND_TOK, HEADS, HEAD_DIM)
    normed = low(norm_apply(rows, self_gain, self_bias))
    query = low(rotate(low_back(product(normed, self_query)).reshape(head_shape), positions))
    keys = low(rotate(low_back(product(normed, self_key)).reshape(head_shape), positions))
    values = low(low_back(product(normed, self_value))).reshape(head_shape)
    allowed = jnp.arange(SEQ_LEN) < length
    mixed, self_peak = attend(query, keys, values, allowed)
    mixed = low(low_back(mixed.reshape(SEQ_LEN, D)))
    stream_cross = rows + low_back(product(mixed, self_output))
    normed = low(norm_apply(stream_cross, cross_gain, cross_bias))
    query = low(low_back(product(normed, cross_query))).reshape(head_shape)
    keys = low(low_back(product(memory, cross_key))).reshape(memory_shape)
    values = low(low_back(product(memory, cross_value))).reshape(memory_shape)
    mixed, cross_peak = attend(query, keys, values, live_row > 0)
    mixed = low(low_back(mixed.reshape(SEQ_LEN, D)))
    stream_feed = stream_cross + low_back(product(mixed, cross_output))
    normed = low(norm_apply(stream_feed, feed_gain, feed_bias))
    gate_pre = low_back(product(normed, gate_weight))
    upward = low_back(product(normed, up_weight))
    hidden = low(jax.nn.silu(gate_pre) * upward)
    outcome = stream_feed + low_back(product(hidden, down_weight))
    return (outcome, jnp.maximum(self_peak, cross_peak))

def reference(inputs, cotangent, context, context_live, lengths, threshold, self_gain, self_bias, self_query, self_key, self_value, self_output, cross_gain, cross_bias, cross_query, cross_key, cross_value, cross_output, feed_gain, feed_bias, gate_weight, up_weight, down_weight):
    params = tuple((weight.astype(jnp.float32) for weight in (self_gain, self_bias, self_query, self_key, self_value, self_output, cross_gain, cross_bias, cross_query, cross_key, cross_value, cross_output, feed_gain, feed_bias, gate_weight, up_weight, down_weight)))
    row_blocks = inputs.astype(jnp.float32).reshape(SEQS, SEQ_LEN, D)
    cot_blocks = cotangent.astype(jnp.float32).reshape(SEQS, SEQ_LEN, D)
    memories = context.astype(jnp.float32)

    def one_sequence(carry, item):
        totals, peak_now = carry
        rows, cot_rows, memory, live_row, length = item

        def forward(rows_in, params_in):
            return block(rows_in, params_in, memory, live_row, length)
        outcome, pullback, head_peak = jax.vjp(forward, rows, params, has_aux=True)
        row_grad, param_grads = pullback(cot_rows)
        totals = jax.tree.map(jnp.add, totals, param_grads)
        return ((totals, jnp.maximum(peak_now, head_peak)), (outcome.astype(jnp.bfloat16), row_grad))
    start = (jax.tree.map(jnp.zeros_like, params), jnp.full((HEADS,), NEGATIVE, jnp.float32))
    (totals, peaks), (outcomes, row_grads) = lax.scan(one_sequence, start, (row_blocks, cot_blocks, memories, context_live, lengths))
    factor = jnp.sqrt(threshold[0] / jnp.maximum(peaks, threshold[0]))
    columns = jnp.repeat(factor, HEAD_DIM)[None, :]
    return (outcomes.reshape(TOKENS, D), row_grads.reshape(TOKENS, D), totals[0], totals[1], totals[2], totals[3], totals[4], totals[5], totals[6], totals[7], totals[8], totals[9], totals[10], totals[11], totals[12], totals[13], totals[14], totals[15], totals[16], peaks, self_query.astype(jnp.float32) * columns, self_key.astype(jnp.float32) * columns, cross_query.astype(jnp.float32) * columns, cross_key.astype(jnp.float32) * columns)
```

```python
import jax
import jax.numpy as jnp
from jax import lax
from jax.sharding import Mesh
from jax.sharding import PartitionSpec as P

HEAD_DIM = 64
ROT_DIM = 32
EPSILON = 1e-05
NEGATIVE = -1e30
BF = jnp.bfloat16
F32 = jnp.float32


def swap(value, axis):
    return lax.ppermute(value, axis, [(0, 1), (1, 0)])


def join(own, other, axis_name, dim):
    size = own.shape[dim]
    whole = own.shape[:dim] + (2 * size,) + own.shape[dim + 1 :]
    at = lax.axis_index(axis_name)
    out = jnp.zeros(whole, own.dtype)
    out = lax.dynamic_update_slice_in_dim(out, own, at * size, dim)
    return lax.dynamic_update_slice_in_dim(out, other, (1 - at) * size, dim)


def pick(value, index, dim):
    return lax.dynamic_index_in_dim(value, index, dim, keepdims=False)


def gather_weights(shard):
    held = lax.all_gather(shard, "z", axis=0, tiled=False)
    held = held[:, None]
    held = join(held, swap(held, "y"), "y", 1)
    held = held[:, :, None]
    held = join(held, swap(held, "x"), "x", 2)
    return held.reshape(-1, shard.shape[1])


def gather_pair_weights(held):
    held = lax.all_gather(held, "z", axis=0, tiled=False)
    held = held[:, None]
    held = join(held, swap(held, "y"), "y", 1)
    return held.reshape(-1, held.shape[-1])


def nn(left, right):
    return lax.dot_general(left, right, (((1,), (0,)), ((), ())), preferred_element_type=F32)


def nt(left, right):
    return lax.dot_general(left, right, (((1,), (1,)), ((), ())), preferred_element_type=F32)


def tn(left, right):
    return lax.dot_general(left, right, (((0,), (0,)), ((), ())), preferred_element_type=F32)


def columns_by(value, axis_name, zs):
    rows = value.shape[0]
    at = lax.axis_index(axis_name)
    if axis_name == "y":
        split = value.reshape(rows, zs, 2, -1)
        dim = 2
    else:
        split = value.reshape(rows, 2 * zs, 2, -1)
        dim = 2
    return (
        pick(split, at, dim).reshape(rows, -1),
        pick(split, 1 - at, dim).reshape(rows, -1),
    )


def reduce_full(left_keep, left_send, right, zs):
    got = swap(tn(left_send, right).astype(BF), "x")
    held = (tn(left_keep, right) + got.astype(F32)).astype(BF)
    held = held.reshape(zs, 2, -1, right.shape[1])
    at = lax.axis_index("y")
    got = swap(pick(held, 1 - at, 1), "y")
    held = (pick(held, at, 1).astype(F32) + got.astype(F32)).astype(BF)
    return lax.psum_scatter(held, "z", scatter_dimension=0, tiled=False)


def reduce_pair(left_keep, left_send, right, zs):
    got = swap(tn(left_send, right).astype(BF), "y")
    held = (tn(left_keep, right) + got.astype(F32)).astype(BF)
    held = held.reshape(zs, -1, right.shape[1])
    held = lax.psum_scatter(held, "z", scatter_dimension=0, tiled=False)
    held = held.reshape(2, -1, right.shape[1])
    at = lax.axis_index("x")
    got = swap(pick(held, 1 - at, 0), "x")
    return pick(held, at, 0), got


def norm_forward(stream, gain_vec, bias_vec):
    average = jnp.mean(stream, axis=-1, keepdims=True)
    centred = stream - average
    inverse = lax.rsqrt(jnp.mean(centred * centred, axis=-1, keepdims=True) + EPSILON)
    unit_rows = centred * inverse
    return (unit_rows * gain_vec + bias_vec, unit_rows, inverse)


def norm_backward(incoming, unit_rows, inverse, gain_vec):
    gain_grad = jnp.sum(incoming * unit_rows, axis=0)
    bias_grad = jnp.sum(incoming, axis=0)
    scaled = incoming * gain_vec
    stream_grad = inverse * (
        scaled
        - jnp.mean(scaled, axis=-1, keepdims=True)
        - unit_rows * jnp.mean(scaled * unit_rows, axis=-1, keepdims=True)
    )
    return (stream_grad, gain_grad, bias_grad)


def rotate(field, positions, direction):
    half_count = ROT_DIM // 2
    rates = 10000.0 ** (-jnp.arange(0, ROT_DIM, 2).astype(F32) / ROT_DIM)
    angles = positions[:, None] * rates[None, :]
    cosine = jnp.cos(angles)[:, None, :]
    sine = direction * jnp.sin(angles)[:, None, :]
    first = field[..., :half_count]
    second = field[..., half_count:ROT_DIM]
    return jnp.concatenate(
        [first * cosine - second * sine, second * cosine + first * sine, field[..., ROT_DIM:]],
        axis=-1,
    )


def attend_forward(query, keys, values, allowed):
    raw_scores = jnp.einsum("qhe,khe->hqk", query, keys, preferred_element_type=F32)
    scores = jnp.where(allowed[None, None, :], raw_scores * HEAD_DIM ** (-0.5), NEGATIVE)
    head_peak = jnp.max(scores, axis=(1, 2))
    row_top = jnp.max(scores, axis=-1, keepdims=True)
    log_total = jnp.log(jnp.sum(jnp.exp(scores - row_top), axis=-1, keepdims=True)) + row_top
    weighting = jnp.exp(scores - log_total).astype(BF)
    mixed = jnp.einsum("hqk,khe->qhe", weighting, values, preferred_element_type=F32)
    return (mixed, log_total, head_peak)


def attend_backward(query, keys, values, allowed, log_total, grad_mixed):
    raw_scores = jnp.einsum("qhe,khe->hqk", query, keys, preferred_element_type=F32)
    scores = jnp.where(allowed[None, None, :], raw_scores * HEAD_DIM ** (-0.5), NEGATIVE)
    weighting = jnp.exp(scores - log_total)
    grad_weights = jnp.einsum("qhe,khe->hqk", grad_mixed, values, preferred_element_type=F32)
    grad_values = jnp.einsum(
        "hqk,qhe->khe", weighting.astype(BF), grad_mixed, preferred_element_type=F32
    )
    grad_scores = weighting * (
        grad_weights - jnp.sum(grad_weights * weighting, axis=-1, keepdims=True)
    )
    grad_raw = (grad_scores * HEAD_DIM ** (-0.5)).astype(BF)
    grad_query = jnp.einsum("hqk,khe->qhe", grad_raw, keys, preferred_element_type=F32)
    grad_keys = jnp.einsum("hqk,qhe->khe", grad_raw, query, preferred_element_type=F32)
    return (grad_query, grad_keys, grad_values)


def pair_rows(own):
    return jnp.concatenate([own, swap(own, "tensor")], axis=0)


def group_rows(own):
    both = jnp.stack([own, swap(own, "x")])
    other = swap(both, "tensor")
    return jnp.concatenate([both[0], other[0], both[1], other[1]], axis=0)


def spread_pair(left, right_t):
    rows = left.shape[0] // 2
    got = swap(nt(left[rows:], right_t), "tensor")
    return nt(left[:rows], right_t) + got


def spread_group(product):
    quarter = product.rows // 4
    far_send = product(3 * quarter, quarter)
    far = product(2 * quarter, quarter) + swap(far_send, "tensor")
    got_far = swap(far.astype(BF), "x")
    near = product(0, quarter) + swap(product(quarter, quarter), "tensor")
    return near + got_far.astype(F32)


class Product:
    def __init__(self, terms, transposed):
        self.terms = terms
        self.transposed = transposed
        self.rows = terms[0][0].shape[0]

    def __call__(self, first, count):
        total = None
        for left, right in self.terms:
            part = (nt if self.transposed else nn)(left[first : first + count], right)
            total = part if total is None else total + part
        return total


def per_device(
    inputs,
    cotangent,
    context,
    context_live,
    lengths,
    threshold,
    self_gain,
    self_bias,
    self_query,
    self_key,
    self_value,
    self_output,
    cross_gain,
    cross_bias,
    cross_query,
    cross_key,
    cross_value,
    cross_output,
    feed_gain,
    feed_bias,
    gate_weight,
    up_weight,
    down_weight,
):
    zs = lax.axis_size("z")
    x_at = lax.axis_index("x")
    t_at = lax.axis_index("tensor")
    width = inputs.shape[1]
    rows = inputs.shape[0]
    seq_len = 2 * rows
    inner = self_query.shape[1]
    heads_here = inner // HEAD_DIM
    ff_half = gate_weight.shape[1]
    ff = ff_half // 2
    shard_rows = self_query.shape[0]
    context_rows = cross_key.shape[0]

    vectors = jnp.stack(
        [self_gain, self_bias, cross_gain, cross_bias, feed_gain, feed_bias], axis=1
    )
    vectors = jnp.pad(vectors, ((0, 0), (0, 122)))
    first = gather_weights(
        jnp.concatenate([self_query, self_key, self_value, vectors], axis=1)
    )
    in_weight = first[:, : 3 * inner]
    norms = first[:, 3 * inner :].astype(F32).T
    second = gather_weights(
        jnp.concatenate(
            [
                self_output.T,
                cross_query,
                cross_output.T,
                jnp.concatenate([cross_key, cross_value], axis=0),
            ],
            axis=1,
        )
    )
    self_out_t = second[:, :inner]
    cross_in = second[:, inner : 2 * inner]
    cross_out_t = second[:, 2 * inner : 3 * inner]
    memory_weights = second[:, 3 * inner :].reshape(-1, 2, context_rows, inner)
    cross_keys_w = memory_weights[:, 0].reshape(-1, inner)
    cross_values_w = memory_weights[:, 1].reshape(-1, inner)

    feed = jnp.stack([gate_weight, up_weight, down_weight.T], axis=1)
    feed = feed.reshape(shard_rows, 3, 2, ff)
    kept = pick(feed, x_at, 2).reshape(shard_rows, 3 * ff)
    sent = pick(feed, 1 - x_at, 2).reshape(shard_rows, 3 * ff)
    feed = join(kept[None], swap(sent, "x")[None], "x", 0)
    gate_up = gather_pair_weights(feed[:, :, : 2 * ff])
    down_t = gather_pair_weights(feed[:, :, 2 * ff :])

    local = jnp.arange(rows)
    places = jnp.concatenate([t_at * rows + local, (1 - t_at) * rows + local])
    positions = places.astype(F32)
    self_allowed = places < lengths[0]
    cross_allowed = context_live[0] > 0
    memory = context[0]
    head_shape = (seq_len, heads_here, HEAD_DIM)
    memory_shape = (memory.shape[0], heads_here, HEAD_DIM)

    cot_group = group_rows(cotangent)
    all_inputs = pair_rows(inputs)
    stream = inputs.astype(F32)
    normed, _, _ = norm_forward(all_inputs.astype(F32), norms[0], norms[1])
    normed_self = normed.astype(BF)
    projected = nn(normed_self, in_weight)
    query_self = rotate(projected[:, :inner].reshape(head_shape), positions, 1.0).astype(BF)
    key_self = rotate(
        projected[:, inner : 2 * inner].reshape(head_shape), positions, 1.0
    ).astype(BF)
    value_self = projected[:, 2 * inner :].astype(BF).reshape(head_shape)
    mixed, total_self, peak_self = attend_forward(query_self, key_self, value_self, self_allowed)
    mixed_self = mixed.reshape(seq_len, -1).astype(BF)
    stream_cross = stream + spread_pair(mixed_self, self_out_t)
    normed, unit_cross, inverse_cross = norm_forward(stream_cross, norms[2], norms[3])
    normed_cross = pair_rows(normed.astype(BF))
    query_cross = nn(normed_cross, cross_in).astype(BF).reshape(head_shape)
    key_cross = nn(memory, cross_keys_w).astype(BF).reshape(memory_shape)
    value_cross = nn(memory, cross_values_w).astype(BF).reshape(memory_shape)
    mixed, total_cross, peak_cross = attend_forward(
        query_cross, key_cross, value_cross, cross_allowed
    )
    mixed_cross = mixed.reshape(seq_len, -1).astype(BF)
    stream_feed = stream_cross + spread_pair(mixed_cross, cross_out_t)
    normed, unit_feed, inverse_feed = norm_forward(stream_feed, norms[4], norms[5])
    normed_feed = group_rows(normed.astype(BF))
    gates = nn(normed_feed, gate_up)
    gate_pre = gates[:, :ff]
    upward = gates[:, ff:]
    sigmoid_gate = jax.nn.sigmoid(gate_pre)
    hidden = (gate_pre * sigmoid_gate * upward).astype(BF)
    result = (stream_feed + spread_group(Product([(hidden, down_t)], True))).astype(BF)
    peaks = lax.pmax(jnp.maximum(peak_self, peak_cross), ("z", "y", "x"))

    cot_keep, cot_send = columns_by(cot_group, "y", zs)
    down_keep, down_got = reduce_pair(cot_keep, cot_send, hidden, zs)
    grad_hidden = nn(cot_group, down_t)
    grad_gate = grad_hidden * upward * sigmoid_gate * (1.0 + gate_pre * (1.0 - sigmoid_gate))
    grad_upward = grad_hidden * gate_pre * sigmoid_gate
    grad_gates = jnp.concatenate([grad_gate.astype(BF), grad_upward.astype(BF)], axis=1)
    grad_normed = spread_group(Product([(grad_gates, gate_up)], True))
    feed_keep, feed_send = columns_by(normed_feed, "y", zs)
    gates_keep, gates_got = reduce_pair(feed_keep, feed_send, grad_gates, zs)
    stream_part, grad_feed_gain, grad_feed_bias = norm_backward(
        grad_normed, unit_feed, inverse_feed, norms[4]
    )
    grad_stream = cotangent.astype(F32) + stream_part
    grad_full = pair_rows(grad_stream.astype(BF))
    keep, send = columns_by(grad_full, "x", zs)
    sum_cross_output = reduce_full(keep, send, mixed_cross, zs)
    grad_mixed = nn(grad_full, cross_out_t).astype(BF).reshape(head_shape)
    grad_query, grad_keys, grad_values = attend_backward(
        query_cross, key_cross, value_cross, cross_allowed, total_cross, grad_mixed
    )
    grad_query = grad_query.astype(BF).reshape(seq_len, -1)
    grad_keys = grad_keys.astype(BF).reshape(memory.shape[0], -1)
    grad_values = grad_values.astype(BF).reshape(memory.shape[0], -1)
    grad_normed = spread_pair(grad_query, cross_in)
    keep, send = columns_by(normed_cross, "x", zs)
    sum_cross_query = reduce_full(keep, send, grad_query, zs)
    keep, send = columns_by(memory, "x", zs)
    sum_cross_memory = reduce_full(
        keep, send, jnp.concatenate([grad_keys, grad_values], axis=1), zs
    )
    stream_part, grad_cross_gain, grad_cross_bias = norm_backward(
        grad_normed, unit_cross, inverse_cross, norms[2]
    )
    grad_stream = grad_stream + stream_part
    grad_full = pair_rows(grad_stream.astype(BF))
    keep, send = columns_by(grad_full, "x", zs)
    sum_self_output = reduce_full(keep, send, mixed_self, zs)
    grad_mixed = nn(grad_full, self_out_t).astype(BF).reshape(head_shape)
    grad_query, grad_keys, grad_values = attend_backward(
        query_self, key_self, value_self, self_allowed, total_self, grad_mixed
    )
    grad_query = rotate(grad_query, positions, -1.0).astype(BF).reshape(seq_len, -1)
    grad_keys = rotate(grad_keys, positions, -1.0).astype(BF).reshape(seq_len, -1)
    grad_values = grad_values.astype(BF).reshape(seq_len, -1)
    grad_in = jnp.concatenate([grad_query, grad_keys, grad_values], axis=1)
    keep, send = columns_by(normed_self, "x", zs)
    sum_self_in = reduce_full(keep, send, grad_in, zs).astype(F32)
    grad_normed = spread_pair(grad_in, in_weight)
    _, unit_self, inverse_self = norm_forward(stream, norms[0], norms[1])
    stream_part, grad_self_gain, grad_self_bias = norm_backward(
        grad_normed, unit_self, inverse_self, norms[0]
    )
    grad_stream = grad_stream + stream_part

    vector_sums = jnp.stack(
        [
            grad_self_gain,
            grad_self_bias,
            grad_cross_gain,
            grad_cross_bias,
            grad_feed_gain,
            grad_feed_bias,
        ]
    ).reshape(6, zs, 2, 2, shard_rows)
    y_at = lax.axis_index("y")
    vector_sums = vector_sums + swap(vector_sums, "tensor")
    vector_sums = pick(vector_sums, x_at, 3) + swap(pick(vector_sums, 1 - x_at, 3), "x")
    vector_sums = pick(vector_sums, y_at, 2) + swap(pick(vector_sums, 1 - y_at, 2), "y")
    vector_sums = pick(lax.psum(vector_sums, "z"), lax.axis_index("z"), 1)

    factor = jnp.sqrt(threshold[0] / jnp.maximum(peaks, threshold[0]))
    columns = jnp.repeat(factor, HEAD_DIM)[None, :]
    down_sum = join(down_keep, down_got, "x", 1).T.astype(F32)
    gates_sum = join(
        gates_keep.reshape(-1, 2, 1, ff), gates_got.reshape(-1, 2, 1, ff), "x", 2
    ).astype(F32)
    return (
        result,
        grad_stream,
        vector_sums[0],
        vector_sums[1],
        sum_self_in[:, :inner],
        sum_self_in[:, inner : 2 * inner],
        sum_self_in[:, 2 * inner :],
        sum_self_output.T.astype(F32),
        vector_sums[2],
        vector_sums[3],
        sum_cross_query.astype(F32),
        sum_cross_memory[:, :inner].astype(F32),
        sum_cross_memory[:, inner:].astype(F32),
        sum_cross_output.T.astype(F32),
        vector_sums[4],
        vector_sums[5],
        gates_sum[:, 0].reshape(-1, ff_half),
        gates_sum[:, 1].reshape(-1, ff_half),
        down_sum,
        peaks,
        self_query.astype(F32) * columns,
        self_key.astype(F32) * columns,
        cross_query.astype(F32) * columns,
        cross_key.astype(F32) * columns,
    )


def solution(mesh):
    count = mesh.shape["dp"]
    mesh = Mesh(
        mesh.devices.reshape(count // 4, 2, 2, mesh.shape["tensor"]), ("z", "y", "x", "tensor")
    )
    dp = ("z", "y", "x")
    both = P(dp + ("tensor",), None)
    split = P(dp)
    row_major = P(dp, "tensor")
    column_major = P("tensor", dp)
    in_specs = (
        both,
        both,
        P(dp, None, None),
        P(dp, None),
        split,
        P(),
        split,
        split,
        row_major,
        row_major,
        row_major,
        column_major,
        split,
        split,
        row_major,
        row_major,
        row_major,
        column_major,
        split,
        split,
        row_major,
        row_major,
        column_major,
    )
    out_specs = (
        both,
        both,
        split,
        split,
        row_major,
        row_major,
        row_major,
        column_major,
        split,
        split,
        row_major,
        row_major,
        row_major,
        column_major,
        split,
        split,
        row_major,
        row_major,
        column_major,
        P("tensor"),
        row_major,
        row_major,
        row_major,
        row_major,
    )
    return jax.shard_map(
        per_device, mesh=mesh, in_specs=in_specs, out_specs=out_specs, check_vma=False
    )
```

```python
import functools

import jax
import jax.numpy as jnp
from jax import lax
from jax.experimental import pallas as pl
from jax.experimental.pallas import tpu as pltpu
from jax.sharding import Mesh
from jax.sharding import PartitionSpec as P

HEAD_DIM = 64
ROT_DIM = 32
EPSILON = 1e-05
NEGATIVE = -1e30
BF = jnp.bfloat16
F32 = jnp.float32


def swap(value, axis):
    return lax.ppermute(value, axis, [(0, 1), (1, 0)])


def join(own, other, axis_name, dim):
    size = own.shape[dim]
    whole = own.shape[:dim] + (2 * size,) + own.shape[dim + 1 :]
    at = lax.axis_index(axis_name)
    out = jnp.zeros(whole, own.dtype)
    out = lax.dynamic_update_slice_in_dim(out, own, at * size, dim)
    return lax.dynamic_update_slice_in_dim(out, other, (1 - at) * size, dim)


def pick(value, index, dim):
    return lax.dynamic_index_in_dim(value, index, dim, keepdims=False)


class Lanes:
    def __init__(self, send_sems, recv_sems, local_sems, zs):
        self.send_sems, self.recv_sems, self.local_sems = send_sems, recv_sems, local_sems
        self.used = self.used_local = 0
        self.z = lax.axis_index("z")
        self.y = lax.axis_index("y")
        self.x = lax.axis_index("x")
        self.zs = zs

    def local(self):
        self.used_local += 1
        return self.local_sems.at[self.used_local - 1]

    def copy(self, source, target, device):
        return self.copies([source], target, device)[0]

    def copies(self, sources, target, device):
        slot = self.used
        self.used += 1
        return [
            pltpu.make_async_remote_copy(
                src_ref=source,
                dst_ref=target,
                send_sem=self.send_sems.at[slot],
                recv_sem=self.recv_sems.at[slot],
                device_id=device,
                device_id_type=pl.DeviceIdType.MESH,
            )
            for source in sources
        ]


def guarded(condition, action):
    if condition is None:
        action()
    else:
        pl.when(condition)(action)


class Move:
    def __init__(self, copy, sends, receives):
        self.copy_, self.sends, self.receives = copy, sends, receives

    def start(self):
        guarded(self.sends, self.copy_.start)

    def arrived(self):
        guarded(self.receives, self.copy_.wait_recv)

    def sent(self):
        guarded(self.sends, self.copy_.wait_send)


class Gather:
    def __init__(self, lanes, own, whole):
        zs, z, y, x = lanes.zs, lanes.z, lanes.y, lanes.x
        self.lanes, self.own, self.whole = lanes, own, whole

        def block(zz, yy):
            return whole.at[zz, yy, x]

        def along(source, target, axis, to, sends=None, receives=None):
            return Move(lanes.copy(source, target, {axis: to}), sends, receives)

        self.first = [
            along(own, block(z, y), "y", 1 - y),
            along(own, block(z, y), "x", 1 - x),
        ]
        self.far = [[along(block(z, 1 - y), block(z, 1 - y), "x", 1 - x)]]
        self.steps = []
        for k in range(zs - 1):
            right, left = jnp.maximum(z - k, 0), jnp.minimum(z + k, zs - 1)
            step = []
            for zz, to, sends, receives, got in (
                (right, z + 1, (z >= k) & (z < zs - 1), z >= k + 1, jnp.maximum(z - 1 - k, 0)),
                (left, z - 1, (z + k < zs) & (z > 0), z + k + 1 < zs, jnp.minimum(z + 1 + k, zs - 1)),
            ):
                source = own if k == 0 else block(zz, y)
                move = along(source, block(zz, y), "z", to, sends, receives)
                follow = [
                    along(block(got, y), block(got, y), "y", 1 - y, receives, receives),
                    along(block(got, y), block(got, y), "x", 1 - x, receives, receives),
                    along(block(got, 1 - y), block(got, 1 - y), "x", 1 - x, receives, receives),
                ]
                step.append((move, follow))
            self.steps.append(step)

    def begin(self):
        for move, _ in self.steps[0]:
            move.start()
        for move in self.first:
            move.start()

    def step(self, k):
        for side in range(2):
            move, follow = self.steps[k][side]
            move.arrived()
            if k + 1 < len(self.steps):
                self.steps[k + 1][side][0].start()
            follow[0].start()
            follow[1].start()

    def far_first(self):
        self.first[0].arrived()
        self.far[0][0].start()

    def far_step(self, k):
        for side in range(2):
            _, follow = self.steps[k][side]
            follow[0].arrived()
            follow[2].start()

    def finish(self):
        self.first[1].arrived()
        self.far[0][0].arrived()
        for step in self.steps:
            for _, follow in step:
                follow[1].arrived()
                follow[2].arrived()
        for move in self.first + self.far[0]:
            move.sent()
        for step in self.steps:
            for move, follow in step:
                move.sent()
                for other in follow:
                    other.sent()


class PairGather:
    def __init__(self, lanes, kept, sent, whole, y_first):
        zs, z, y, x = lanes.zs, lanes.z, lanes.y, lanes.x
        self.y_first = y_first

        def along(piece, axis, to, sends=None, receives=None):
            return Move(lanes.copy(piece, piece, {axis: to}), sends, receives)

        self.swap = Move(lanes.copy(sent, whole.at[z, y, x], {"x": 1 - x}), None, None)
        self.local = pltpu.make_async_copy(kept, whole.at[z, y, x], lanes.local())
        self.own_y = along(whole.at[z, y], "y", 1 - y)
        self.steps = []
        for k in range(zs - 1):
            step = []
            for zz, to, sends, receives, got in (
                (jnp.maximum(z - k, 0), z + 1, (z >= k) & (z < zs - 1), z >= k + 1, jnp.maximum(z - 1 - k, 0)),
                (jnp.minimum(z + k, zs - 1), z - 1, (z + k < zs) & (z > 0), z + k + 1 < zs, jnp.minimum(z + 1 + k, zs - 1)),
            ):
                piece = whole.at[zz] if y_first else whole.at[zz, y]
                move = along(piece, "z", to, sends, receives)
                follow = [] if y_first else [along(whole.at[got, y], "y", 1 - y, receives, receives)]
                step.append((move, follow))
            self.steps.append(step)

    def begin(self):
        self.swap.start()
        self.local.start()

    def swapped(self):
        self.swap.arrived()
        self.local.wait()
        self.own_y.start()
        if not self.y_first:
            for move, _ in self.steps[0]:
                move.start()

    def own_y_arrived(self):
        self.own_y.arrived()
        if self.y_first:
            for move, _ in self.steps[0]:
                move.start()

    def step(self, k):
        for side in range(2):
            move, follow = self.steps[k][side]
            move.arrived()
            if k + 1 < len(self.steps):
                self.steps[k + 1][side][0].start()
            for other in follow:
                other.start()

    def finish(self):
        if not self.y_first:
            self.own_y.arrived()
        for step in self.steps:
            for move, follow in step:
                for other in follow:
                    other.arrived()
        self.swap.sent()
        self.own_y.sent()
        for step in self.steps:
            for move, follow in step:
                move.sent()
                for other in follow:
                    other.sent()


def greet(zs):
    z, y, x = lax.axis_index("z"), lax.axis_index("y"), lax.axis_index("x")
    barrier = pltpu.get_barrier_semaphore()

    def signal(device):
        pl.semaphore_signal(barrier, inc=1, device_id=device, device_id_type=pl.DeviceIdType.MESH)

    signal({"x": 1 - x})
    signal({"y": 1 - y})
    pl.when(z > 0)(lambda: signal({"z": z - 1}))
    pl.when(z < zs - 1)(lambda: signal({"z": z + 1}))
    peers = 2 + (z > 0).astype(jnp.int32) + (z < zs - 1).astype(jnp.int32)
    pl.semaphore_wait(barrier, peers)


def gather_kernel(zs, groups, pairs, *refs):
    owns = refs[:groups]
    pair_in = refs[groups : groups + 2 * pairs]
    outs = refs[groups + 2 * pairs : 2 * groups + 3 * pairs]
    send_sems, recv_sems, local_sems = refs[2 * groups + 3 * pairs :]
    lanes = Lanes(send_sems, recv_sems, local_sems, zs)
    greet(zs)
    gathers = [Gather(lanes, own, whole) for own, whole in zip(owns, outs)]
    quarters = [
        PairGather(lanes, pair_in[2 * i], pair_in[2 * i + 1], outs[groups + i], i == 0)
        for i in range(pairs)
    ]
    locals_ = [
        pltpu.make_async_copy(own, whole.at[lanes.z, lanes.y, lanes.x], lanes.local())
        for own, whole in zip(owns, outs)
    ]
    for quarter in quarters:
        quarter.begin()
    for copy, gather in zip(locals_, gathers):
        copy.start()
        gather.begin()
    for quarter in quarters:
        quarter.swapped()
    for gather in gathers:
        gather.far_first()
    for k in range(zs - 1):
        for gather in gathers:
            gather.step(k)
        for quarter in quarters:
            if quarter.y_first:
                if k == 0:
                    quarter.own_y_arrived()
            else:
                quarter.step(k)
        for gather in gathers:
            gather.far_step(k)
        for quarter in quarters:
            if quarter.y_first:
                quarter.step(k)
    for copy in locals_:
        copy.wait()
    for gather in gathers:
        gather.finish()
    for quarter in quarters:
        quarter.finish()


def gather_all(shards, quarters, zs):
    groups, pairs = len(shards), len(quarters)
    flat = list(shards) + [array for pair in quarters for array in pair]
    outs = [
        jax.ShapeDtypeStruct((zs, 2, 2) + array.shape, array.dtype)
        for array in list(shards) + [kept for kept, _ in quarters]
    ]
    moves = groups * (3 + 8 * (zs - 1)) + pairs * (2 + 4 * (zs - 1))
    hbm = pl.BlockSpec(memory_space=pltpu.HBM)
    return pl.pallas_call(
        functools.partial(gather_kernel, zs, groups, pairs),
        out_shape=outs,
        in_specs=[hbm] * len(flat),
        out_specs=[hbm] * len(outs),
        scratch_shapes=[
            pltpu.SemaphoreType.DMA((moves,)),
            pltpu.SemaphoreType.DMA((moves,)),
            pltpu.SemaphoreType.DMA((groups + pairs,)),
        ],
        compiler_params=pltpu.CompilerParams(collective_id=1, has_side_effects=True),
    )(*flat)


def plus(*terms):
    total = terms[0].astype(F32)
    for term in terms[1:]:
        total = total + term.astype(F32)
    return total


def ends_first(zs):
    order = []
    for i in range(zs // 2):
        order += [zs - 1 - i, i]
    return order


class Line:
    def __init__(self, lanes, part, from_left, from_right):
        zs, z = lanes.zs, lanes.z
        self.zs, self.z, self.part = zs, z, part
        self.from_left, self.from_right = from_left, from_right
        self.right, self.left = {}, {}
        for d in ends_first(zs):
            after, before = jnp.minimum(z + 1, zs - 1), jnp.maximum(z - 1, 0)
            self.right[d] = lanes.copies(
                (part.at[d], from_left.at[d]), from_left.at[d], {"z": after}
            )
            self.left[d] = lanes.copies(
                (part.at[d], from_right.at[d]), from_right.at[d], {"z": before}
            )

    def pass_on(self, d):
        for moves, inbox, sends, edge in (
            (self.right[d], self.from_left, self.z < d, self.z == 0),
            (self.left[d], self.from_right, self.z > d, self.z == self.zs - 1),
        ):

            @pl.when(sends & edge)
            def _():
                moves[0].start()

            @pl.when(sends & jnp.logical_not(edge))
            def _():
                moves[1].wait_recv()
                inbox[d] = plus(self.part[d], inbox[d]).astype(inbox.dtype)
                moves[1].start()

    def total(self, sink):
        for d in range(self.zs):

            @pl.when(self.z == d)
            def _():
                terms = [self.part[d]]
                if d > 0:
                    self.right[d][0].wait_recv()
                    terms.append(self.from_left[d])
                if d < self.zs - 1:
                    self.left[d][0].wait_recv()
                    terms.append(self.from_right[d])
                sink[...] = plus(*terms).astype(sink.dtype)

    def finish(self):
        for d in ends_first(self.zs):
            pl.when(self.z < d)(self.right[d][0].wait_send)
            pl.when(self.z > d)(self.left[d][0].wait_send)


class Scatter:
    def __init__(self, lanes, part, held, out, first):
        zs, z, y, x = lanes.zs, lanes.z, lanes.y, lanes.x
        got, near, from_left, from_right, ready = held
        second = "y" if first == "x" else "x"
        self.lanes, self.part, self.got, self.near, self.ready, self.out = (
            lanes, part, got, near, ready, out,
        )
        f, s = (x, y) if first == "x" else (y, x)
        self.f, self.s = f, s

        def block(zz, a, b):
            return part.at[zz, b, a] if first == "x" else part.at[zz, a, b]

        self.block = block
        self.one, self.two = {}, {}
        for zz in ends_first(zs):
            for j, b in enumerate((1 - s, s)):
                self.one[zz, j] = Move(
                    lanes.copy(block(zz, 1 - f, b), got.at[zz, j], {first: 1 - f}), None, None
                )
        for zz in ends_first(zs):
            self.two[zz] = Move(
                lanes.copy(got.at[zz, 0], near.at[zz], {second: 1 - s}), None, None
            )
        self.line = Line(lanes, ready, from_left, from_right)

    def begin(self):
        for zz in ends_first(self.lanes.zs):
            for j in range(2):
                self.one[zz, j].start()

    def second(self, zz):
        self.one[zz, 0].arrived()
        mine, got = self.block(zz, self.f, 1 - self.s), self.got
        got[zz, 0] = plus(mine[...], got[zz, 0]).astype(got.dtype)
        self.two[zz].start()

    def third(self, zz):
        self.one[zz, 1].arrived()
        self.two[zz].arrived()
        mine = self.block(zz, self.f, self.s)
        self.ready[zz] = plus(mine[...], self.got[zz, 1], self.near[zz]).astype(self.ready.dtype)
        self.line.pass_on(zz)

    def finish(self):
        self.line.total(self.out)
        self.line.finish()
        for move in list(self.one.values()) + list(self.two.values()):
            move.sent()


class ScatterZ:
    def __init__(self, lanes, part, held, out):
        y, x = lanes.y, lanes.x
        from_left, from_right, held_z, near, last = held
        self.lanes, self.sum_z, self.near, self.last, self.out = lanes, held_z, near, last, out
        self.line = Line(lanes, part, from_left, from_right)
        self.two = Move(lanes.copy(held_z.at[1 - y], near, {"y": 1 - y}), None, None)
        self.three = Move(lanes.copy(near.at[1 - x], last, {"x": 1 - x}), None, None)

    def pass_on(self, d):
        self.line.pass_on(d)

    def total(self):
        self.line.total(self.sum_z)
        self.two.start()

    def after(self):
        self.two.arrived()
        self.near[...] = plus(self.sum_z[self.lanes.y], self.near[...]).astype(self.near.dtype)
        self.three.start()

    def finish(self):
        self.three.arrived()
        self.out[...] = plus(self.near[self.lanes.x], self.last[...]).astype(self.out.dtype)
        self.line.finish()
        self.two.sent()
        self.three.sent()


def scatter_kernel(zs, orders, *refs):
    count = len(orders)
    parts, outs, rest = refs[:count], refs[count : 2 * count], list(refs[2 * count :])
    send_sems, recv_sems = rest[:2]
    rest = rest[2:]
    lanes = Lanes(send_sems, recv_sems, None, zs)
    greet(zs)
    full, zfirst = [], []
    for i, order in enumerate(orders):
        held, rest = rest[:5], rest[5:]
        if order == "z":
            zfirst.append(ScatterZ(lanes, parts[i], held, outs[i]))
        else:
            full.append(Scatter(lanes, parts[i], held, outs[i], order))
    for item in full:
        item.begin()
    for d in ends_first(zs):
        for item in zfirst:
            item.pass_on(d)
        for item in full:
            item.second(d)
    for item in zfirst:
        item.total()
    for d in ends_first(zs):
        for item in full:
            item.third(d)
    for item in zfirst:
        item.after()
    for item in full:
        item.finish()
    for item in zfirst:
        item.finish()


def scatter_all(parts, orders, zs):
    scratch, moves = [], 0
    for part, order in zip(parts, orders):
        block = part.shape[3:]
        if order == "z":
            shapes = [(zs, 2, 2) + block] * 2 + [(2, 2) + block, (2,) + block, block]
            moves += 2 * zs + 2
        else:
            shapes = [(zs, 2) + block] + [(zs,) + block] * 4
            moves += 5 * zs
        scratch += [pltpu.VMEM(shape, part.dtype) for shape in shapes]
    vmem = pl.BlockSpec(memory_space=pltpu.VMEM)
    return pl.pallas_call(
        functools.partial(scatter_kernel, zs, orders),
        out_shape=[jax.ShapeDtypeStruct(part.shape[3:], F32) for part in parts],
        in_specs=[vmem] * len(parts),
        out_specs=[vmem] * len(parts),
        scratch_shapes=[pltpu.SemaphoreType.DMA((moves,)), pltpu.SemaphoreType.DMA((moves,))]
        + scratch,
        compiler_params=pltpu.CompilerParams(
            collective_id=2, has_side_effects=True, vmem_limit_bytes=56 * 2**20
        ),
    )(*parts)


def nn(left, right):
    return lax.dot_general(left, right, (((1,), (0,)), ((), ())), preferred_element_type=F32)


def nt(left, right):
    return lax.dot_general(left, right, (((1,), (1,)), ((), ())), preferred_element_type=F32)


def tn(left, right):
    return lax.dot_general(left, right, (((0,), (0,)), ((), ())), preferred_element_type=F32)


def columns_by(value, axis_name, zs):
    rows = value.shape[0]
    at = lax.axis_index(axis_name)
    if axis_name == "y":
        split = value.reshape(rows, zs, 2, -1)
        dim = 2
    else:
        split = value.reshape(rows, 2 * zs, 2, -1)
        dim = 2
    return (
        pick(split, at, dim).reshape(rows, -1),
        pick(split, 1 - at, dim).reshape(rows, -1),
    )


def reduce_pair(left_keep, left_send, right, zs):
    got = swap(tn(left_send, right).astype(BF), "y")
    held = (tn(left_keep, right) + got.astype(F32)).astype(BF)
    held = held.reshape(zs, -1, right.shape[1])
    held = lax.psum_scatter(held, "z", scatter_dimension=0, tiled=False)
    held = held.reshape(2, -1, right.shape[1])
    at = lax.axis_index("x")
    got = swap(pick(held, 1 - at, 0), "x")
    return pick(held, at, 0), got


def norm_forward(stream, gain_vec, bias_vec):
    average = jnp.mean(stream, axis=-1, keepdims=True)
    centred = stream - average
    inverse = lax.rsqrt(jnp.mean(centred * centred, axis=-1, keepdims=True) + EPSILON)
    unit_rows = centred * inverse
    return (unit_rows * gain_vec + bias_vec, unit_rows, inverse)


def norm_backward(incoming, unit_rows, inverse, gain_vec):
    gain_grad = jnp.sum(incoming * unit_rows, axis=0)
    bias_grad = jnp.sum(incoming, axis=0)
    scaled = incoming * gain_vec
    stream_grad = inverse * (
        scaled
        - jnp.mean(scaled, axis=-1, keepdims=True)
        - unit_rows * jnp.mean(scaled * unit_rows, axis=-1, keepdims=True)
    )
    return (stream_grad, gain_grad, bias_grad)


def rotate(field, positions, direction):
    half_count = ROT_DIM // 2
    rates = 10000.0 ** (-jnp.arange(0, ROT_DIM, 2).astype(F32) / ROT_DIM)
    angles = positions[:, None] * rates[None, :]
    cosine = jnp.cos(angles)[:, None, :]
    sine = direction * jnp.sin(angles)[:, None, :]
    first = field[..., :half_count]
    second = field[..., half_count:ROT_DIM]
    return jnp.concatenate(
        [first * cosine - second * sine, second * cosine + first * sine, field[..., ROT_DIM:]],
        axis=-1,
    )


def attend_forward(query, keys, values, allowed):
    raw_scores = jnp.einsum("qhe,khe->hqk", query, keys, preferred_element_type=F32)
    scores = jnp.where(allowed[None, None, :], raw_scores * HEAD_DIM ** (-0.5), NEGATIVE)
    head_peak = jnp.max(scores, axis=(1, 2))
    row_top = jnp.max(scores, axis=-1, keepdims=True)
    log_total = jnp.log(jnp.sum(jnp.exp(scores - row_top), axis=-1, keepdims=True)) + row_top
    weighting = jnp.exp(scores - log_total).astype(BF)
    mixed = jnp.einsum("hqk,khe->qhe", weighting, values, preferred_element_type=F32)
    return (mixed, log_total, head_peak)


def attend_backward(query, keys, values, allowed, log_total, grad_mixed):
    raw_scores = jnp.einsum("qhe,khe->hqk", query, keys, preferred_element_type=F32)
    scores = jnp.where(allowed[None, None, :], raw_scores * HEAD_DIM ** (-0.5), NEGATIVE)
    weighting = jnp.exp(scores - log_total)
    grad_weights = jnp.einsum("qhe,khe->hqk", grad_mixed, values, preferred_element_type=F32)
    grad_values = jnp.einsum(
        "hqk,qhe->khe", weighting.astype(BF), grad_mixed, preferred_element_type=F32
    )
    grad_scores = weighting * (
        grad_weights - jnp.sum(grad_weights * weighting, axis=-1, keepdims=True)
    )
    grad_raw = (grad_scores * HEAD_DIM ** (-0.5)).astype(BF)
    grad_query = jnp.einsum("hqk,khe->qhe", grad_raw, keys, preferred_element_type=F32)
    grad_keys = jnp.einsum("hqk,qhe->khe", grad_raw, query, preferred_element_type=F32)
    return (grad_query, grad_keys, grad_values)


def pair_rows(own):
    return jnp.concatenate([own, swap(own, "tensor")], axis=0)


def group_rows(own):
    both = jnp.stack([own, swap(own, "x")])
    other = swap(both, "tensor")
    return jnp.concatenate([both[0], other[0], both[1], other[1]], axis=0)


def spread_pair(left, right_t):
    rows = left.shape[0] // 2
    got = swap(nt(left[rows:], right_t), "tensor")
    return nt(left[:rows], right_t) + got


def spread_group(product):
    quarter = product.rows // 4
    far_send = product(3 * quarter, quarter)
    far = product(2 * quarter, quarter) + swap(far_send, "tensor")
    got_far = swap(far.astype(BF), "x")
    near = product(0, quarter) + swap(product(quarter, quarter), "tensor")
    return near + got_far.astype(F32)


class Product:
    def __init__(self, terms, transposed):
        self.terms = terms
        self.transposed = transposed
        self.rows = terms[0][0].shape[0]

    def __call__(self, first, count):
        total = None
        for left, right in self.terms:
            part = (nt if self.transposed else nn)(left[first : first + count], right)
            total = part if total is None else total + part
        return total


def per_device(
    inputs,
    cotangent,
    context,
    context_live,
    lengths,
    threshold,
    self_gain,
    self_bias,
    self_query,
    self_key,
    self_value,
    self_output,
    cross_gain,
    cross_bias,
    cross_query,
    cross_key,
    cross_value,
    cross_output,
    feed_gain,
    feed_bias,
    gate_weight,
    up_weight,
    down_weight,
):
    zs = lax.axis_size("z")
    x_at = lax.axis_index("x")
    t_at = lax.axis_index("tensor")
    width = inputs.shape[1]
    rows = inputs.shape[0]
    seq_len = 2 * rows
    inner = self_query.shape[1]
    heads_here = inner // HEAD_DIM
    ff_half = gate_weight.shape[1]
    ff = ff_half // 2
    shard_rows = self_query.shape[0]
    context_rows = cross_key.shape[0]

    vectors = jnp.stack(
        [self_gain, self_bias, cross_gain, cross_bias, feed_gain, feed_bias]
    ).astype(F32)
    vectors = jnp.pad(vectors, ((0, 2), (0, 128 - shard_rows)))
    feed = jnp.stack([gate_weight, up_weight, down_weight.T]).reshape(3, shard_rows, 2, ff)
    kept = pick(feed, x_at, 2)
    sent = pick(feed, 1 - x_at, 2)
    norms, in_weight, second, gate_full, up_full, down_t = gather_all(
        [
            vectors,
            jnp.concatenate([self_query, self_key, self_value], axis=1),
            jnp.concatenate(
                [
                    self_output.T,
                    cross_query,
                    cross_output.T,
                    jnp.concatenate([cross_key, cross_value], axis=0),
                ],
                axis=1,
            ),
        ],
        [(kept[i], sent[i]) for i in range(3)],
        zs,
    )
    norms = norms.reshape(-1, 8, 128)[:, :6, :shard_rows].transpose(1, 0, 2).reshape(6, width)
    in_weight = in_weight.reshape(width, -1)
    second = second.reshape(width, -1)
    gate_full, up_full, down_t = (w.reshape(width, ff) for w in (gate_full, up_full, down_t))
    self_out_t = second[:, :inner]
    cross_in = second[:, inner : 2 * inner]
    cross_out_t = second[:, 2 * inner : 3 * inner]
    memory_weights = second[:, 3 * inner :].reshape(-1, 2, context_rows, inner)
    cross_keys_w = memory_weights[:, 0].reshape(-1, inner)
    cross_values_w = memory_weights[:, 1].reshape(-1, inner)

    local = jnp.arange(rows)
    places = jnp.concatenate([t_at * rows + local, (1 - t_at) * rows + local])
    positions = places.astype(F32)
    self_allowed = places < lengths[0]
    cross_allowed = context_live[0] > 0
    memory = context[0]
    head_shape = (seq_len, heads_here, HEAD_DIM)
    memory_shape = (memory.shape[0], heads_here, HEAD_DIM)

    cot_group = group_rows(cotangent)
    all_inputs = pair_rows(inputs)
    stream = inputs.astype(F32)
    normed, _, _ = norm_forward(all_inputs.astype(F32), norms[0], norms[1])
    normed_self = normed.astype(BF)
    projected = nn(normed_self, in_weight)
    query_self = rotate(projected[:, :inner].reshape(head_shape), positions, 1.0).astype(BF)
    key_self = rotate(
        projected[:, inner : 2 * inner].reshape(head_shape), positions, 1.0
    ).astype(BF)
    value_self = projected[:, 2 * inner :].astype(BF).reshape(head_shape)
    mixed, total_self, peak_self = attend_forward(query_self, key_self, value_self, self_allowed)
    mixed_self = mixed.reshape(seq_len, -1).astype(BF)
    stream_cross = stream + spread_pair(mixed_self, self_out_t)
    normed, unit_cross, inverse_cross = norm_forward(stream_cross, norms[2], norms[3])
    normed_cross = pair_rows(normed.astype(BF))
    query_cross = nn(normed_cross, cross_in).astype(BF).reshape(head_shape)
    key_cross = nn(memory, cross_keys_w).astype(BF).reshape(memory_shape)
    value_cross = nn(memory, cross_values_w).astype(BF).reshape(memory_shape)
    mixed, total_cross, peak_cross = attend_forward(
        query_cross, key_cross, value_cross, cross_allowed
    )
    mixed_cross = mixed.reshape(seq_len, -1).astype(BF)
    stream_feed = stream_cross + spread_pair(mixed_cross, cross_out_t)
    normed, unit_feed, inverse_feed = norm_forward(stream_feed, norms[4], norms[5])
    normed_feed = group_rows(normed.astype(BF))
    gate_pre = nn(normed_feed, gate_full)
    upward = nn(normed_feed, up_full)
    sigmoid_gate = jax.nn.sigmoid(gate_pre)
    hidden = (gate_pre * sigmoid_gate * upward).astype(BF)
    result = (stream_feed + spread_group(Product([(hidden, down_t)], True))).astype(BF)
    peaks = lax.pmax(jnp.maximum(peak_self, peak_cross), ("z", "y", "x"))

    cot_keep, cot_send = columns_by(cot_group, "y", zs)
    down_keep, down_got = reduce_pair(cot_keep, cot_send, hidden, zs)
    grad_hidden = nn(cot_group, down_t)
    grad_gate = grad_hidden * upward * sigmoid_gate * (1.0 + gate_pre * (1.0 - sigmoid_gate))
    grad_upward = grad_hidden * gate_pre * sigmoid_gate
    grad_gate = grad_gate.astype(BF)
    grad_upward = grad_upward.astype(BF)
    grad_gates = jnp.concatenate([grad_gate, grad_upward], axis=1)
    grad_normed = spread_group(Product([(grad_gate, gate_full), (grad_upward, up_full)], True))
    feed_keep, feed_send = columns_by(normed_feed, "y", zs)
    gates_keep, gates_got = reduce_pair(feed_keep, feed_send, grad_gates, zs)
    stream_part, grad_feed_gain, grad_feed_bias = norm_backward(
        grad_normed, unit_feed, inverse_feed, norms[4]
    )
    grad_stream = cotangent.astype(F32) + stream_part
    grad_full = pair_rows(grad_stream.astype(BF))
    part_cross_output = tn(grad_full, mixed_cross)
    grad_mixed = nn(grad_full, cross_out_t).astype(BF).reshape(head_shape)
    grad_query, grad_keys, grad_values = attend_backward(
        query_cross, key_cross, value_cross, cross_allowed, total_cross, grad_mixed
    )
    grad_query = grad_query.astype(BF).reshape(seq_len, -1)
    grad_keys = grad_keys.astype(BF).reshape(memory.shape[0], -1)
    grad_values = grad_values.astype(BF).reshape(memory.shape[0], -1)
    grad_normed = spread_pair(grad_query, cross_in)
    part_cross_query = tn(normed_cross, grad_query)
    part_memory = tn(memory, jnp.concatenate([grad_keys, grad_values], axis=1))
    stream_part, grad_cross_gain, grad_cross_bias = norm_backward(
        grad_normed, unit_cross, inverse_cross, norms[2]
    )
    grad_stream = grad_stream + stream_part
    grad_full = pair_rows(grad_stream.astype(BF))
    part_self_output = tn(grad_full, mixed_self)
    grad_mixed = nn(grad_full, self_out_t).astype(BF).reshape(head_shape)
    grad_query, grad_keys, grad_values = attend_backward(
        query_self, key_self, value_self, self_allowed, total_self, grad_mixed
    )
    grad_query = rotate(grad_query, positions, -1.0).astype(BF).reshape(seq_len, -1)
    grad_keys = rotate(grad_keys, positions, -1.0).astype(BF).reshape(seq_len, -1)
    grad_values = grad_values.astype(BF).reshape(seq_len, -1)
    grad_in = jnp.concatenate([grad_query, grad_keys, grad_values], axis=1)
    part_self_in = tn(normed_self, grad_in)
    grad_normed = spread_pair(grad_in, in_weight)
    _, unit_self, inverse_self = norm_forward(stream, norms[0], norms[1])
    stream_part, grad_self_gain, grad_self_bias = norm_backward(
        grad_normed, unit_self, inverse_self, norms[0]
    )
    grad_stream = grad_stream + stream_part

    vector_sums = jnp.stack(
        [
            grad_self_gain,
            grad_self_bias,
            grad_cross_gain,
            grad_cross_bias,
            grad_feed_gain,
            grad_feed_bias,
        ]
    ).reshape(6, -1, shard_rows)
    vector_sums = vector_sums + swap(vector_sums, "tensor")
    vector_sums = jnp.pad(
        vector_sums.transpose(1, 0, 2), ((0, 0), (0, 2), (0, 128 - shard_rows))
    ).reshape(zs, 2, 2, 8, 128)

    def blocks(part):
        return part.astype(BF).reshape(zs, 2, 2, -1, part.shape[1])

    vector_sums, sum_self_in, sum_self_output, sum_cross_query, sum_cross_output, sum_memory = (
        scatter_all(
            [
                vector_sums,
                blocks(part_self_in),
                blocks(part_self_output),
                blocks(part_cross_query),
                blocks(part_cross_output),
                blocks(part_memory),
            ],
            ["x", "x", "y", "y", "y", "z"],
            zs,
        )
    )
    vector_sums = vector_sums[:, :shard_rows]
    factor = jnp.sqrt(threshold[0] / jnp.maximum(peaks, threshold[0]))
    columns = jnp.repeat(factor, HEAD_DIM)[None, :]
    down_sum = join(down_keep, down_got, "x", 1).T.astype(F32)
    gates_sum = join(
        gates_keep.reshape(-1, 2, 1, ff), gates_got.reshape(-1, 2, 1, ff), "x", 2
    ).astype(F32)
    return (
        result,
        grad_stream,
        vector_sums[0],
        vector_sums[1],
        sum_self_in[:, :inner],
        sum_self_in[:, inner : 2 * inner],
        sum_self_in[:, 2 * inner :],
        sum_self_output.T,
        vector_sums[2],
        vector_sums[3],
        sum_cross_query,
        sum_memory[:, :inner],
        sum_memory[:, inner:],
        sum_cross_output.T,
        vector_sums[4],
        vector_sums[5],
        gates_sum[:, 0].reshape(-1, ff_half),
        gates_sum[:, 1].reshape(-1, ff_half),
        down_sum,
        peaks,
        self_query.astype(F32) * columns,
        self_key.astype(F32) * columns,
        cross_query.astype(F32) * columns,
        cross_key.astype(F32) * columns,
    )


def solution(mesh):
    count = mesh.shape["dp"]
    mesh = Mesh(
        mesh.devices.reshape(count // 4, 2, 2, mesh.shape["tensor"]), ("z", "y", "x", "tensor")
    )
    dp = ("z", "y", "x")
    both = P(dp + ("tensor",), None)
    split = P(dp)
    row_major = P(dp, "tensor")
    column_major = P("tensor", dp)
    in_specs = (
        both,
        both,
        P(dp, None, None),
        P(dp, None),
        split,
        P(),
        split,
        split,
        row_major,
        row_major,
        row_major,
        column_major,
        split,
        split,
        row_major,
        row_major,
        row_major,
        column_major,
        split,
        split,
        row_major,
        row_major,
        column_major,
    )
    out_specs = (
        both,
        both,
        split,
        split,
        row_major,
        row_major,
        row_major,
        column_major,
        split,
        split,
        row_major,
        row_major,
        row_major,
        column_major,
        split,
        split,
        row_major,
        row_major,
        column_major,
        P("tensor"),
        row_major,
        row_major,
        row_major,
        row_major,
    )
    return jax.shard_map(
        per_device, mesh=mesh, in_specs=in_specs, out_specs=out_specs, check_vma=False
    )
```

```python
import functools

import jax
import jax.numpy as jnp
from jax import lax
from jax.experimental import pallas as pl
from jax.experimental.pallas import tpu as pltpu
from jax.sharding import Mesh
from jax.sharding import PartitionSpec as P

HEAD_DIM = 64
ROT_DIM = 32
EPSILON = 1e-05
NEGATIVE = -1e30
BF = jnp.bfloat16
F32 = jnp.float32


def swap(value, axis):
    return lax.ppermute(value, axis, [(0, 1), (1, 0)])


def pick(value, index, dim):
    return lax.dynamic_index_in_dim(value, index, dim, keepdims=False)


class Lanes:
    def __init__(self, send_sems, recv_sems, local_sems, zs):
        self.send_sems, self.recv_sems, self.local_sems = send_sems, recv_sems, local_sems
        self.used = self.used_local = 0
        self.z = lax.axis_index("z")
        self.y = lax.axis_index("y")
        self.x = lax.axis_index("x")
        self.zs = zs

    def local(self):
        self.used_local += 1
        return self.local_sems.at[self.used_local - 1]

    def copy(self, source, target, device):
        return self.copies([source], target, device)[0]

    def copies(self, sources, target, device):
        slot = self.used
        self.used += 1
        return [
            pltpu.make_async_remote_copy(
                src_ref=source,
                dst_ref=target,
                send_sem=self.send_sems.at[slot],
                recv_sem=self.recv_sems.at[slot],
                device_id=device,
                device_id_type=pl.DeviceIdType.MESH,
            )
            for source in sources
        ]


def guarded(condition, action):
    if condition is None:
        action()
    else:
        pl.when(condition)(action)


class Move:
    def __init__(self, copy, sends, receives):
        self.copy_, self.sends, self.receives = copy, sends, receives

    def start(self):
        guarded(self.sends, self.copy_.start)

    def arrived(self):
        guarded(self.receives, self.copy_.wait_recv)

    def sent(self):
        guarded(self.sends, self.copy_.wait_send)


class Gather:
    def __init__(self, lanes, whole):
        zs, z, y, x = lanes.zs, lanes.z, lanes.y, lanes.x
        own = whole.at[z, y, x]

        def block(zz, yy):
            return whole.at[zz, yy, x]

        def along(source, target, axis, to, sends=None, receives=None):
            return Move(lanes.copy(source, target, {axis: to}), sends, receives)

        self.first = [
            along(own, block(z, y), "y", 1 - y),
            along(own, block(z, y), "x", 1 - x),
        ]
        self.far = [[along(block(z, 1 - y), block(z, 1 - y), "x", 1 - x)]]
        self.steps = []
        for k in range(zs - 1):
            right, left = jnp.maximum(z - k, 0), jnp.minimum(z + k, zs - 1)
            step = []
            for zz, to, sends, receives, got in (
                (right, z + 1, (z >= k) & (z < zs - 1), z >= k + 1, jnp.maximum(z - 1 - k, 0)),
                (left, z - 1, (z + k < zs) & (z > 0), z + k + 1 < zs, jnp.minimum(z + 1 + k, zs - 1)),
            ):
                source = own if k == 0 else block(zz, y)
                move = along(source, block(zz, y), "z", to, sends, receives)
                follow = [
                    along(block(got, y), block(got, y), "y", 1 - y, receives, receives),
                    along(block(got, y), block(got, y), "x", 1 - x, receives, receives),
                    along(block(got, 1 - y), block(got, 1 - y), "x", 1 - x, receives, receives),
                ]
                step.append((move, follow))
            self.steps.append(step)

    def begin(self):
        for move, _ in self.steps[0]:
            move.start()
        for move in self.first:
            move.start()

    def step(self, k):
        for side in range(2):
            move, follow = self.steps[k][side]
            move.arrived()
            if k + 1 < len(self.steps):
                self.steps[k + 1][side][0].start()
            follow[0].start()
            follow[1].start()

    def far_first(self):
        self.first[0].arrived()
        self.far[0][0].start()

    def far_step(self, k):
        for side in range(2):
            _, follow = self.steps[k][side]
            follow[0].arrived()
            follow[2].start()

    def finish(self):
        self.first[1].arrived()
        self.far[0][0].arrived()
        for step in self.steps:
            for _, follow in step:
                follow[1].arrived()
                follow[2].arrived()
        for move in self.first + self.far[0]:
            move.sent()
        for step in self.steps:
            for move, follow in step:
                move.sent()
                for other in follow:
                    other.sent()


class PairGather:
    def __init__(self, lanes, shard, whole, y_first):
        zs, z, y, x = lanes.zs, lanes.z, lanes.y, lanes.x
        ff = whole.shape[-1]
        kept = shard.at[:, pl.ds(pl.multiple_of(x * ff, ff), ff)]
        sent = shard.at[:, pl.ds(pl.multiple_of((1 - x) * ff, ff), ff)]
        self.y_first = y_first

        def along(piece, axis, to, sends=None, receives=None):
            return Move(lanes.copy(piece, piece, {axis: to}), sends, receives)

        self.swap = Move(lanes.copy(sent, whole.at[z, y, x], {"x": 1 - x}), None, None)
        self.local = pltpu.make_async_copy(kept, whole.at[z, y, x], lanes.local())
        self.own_y = along(whole.at[z, y], "y", 1 - y)
        self.steps = []
        for k in range(zs - 1):
            step = []
            for zz, to, sends, receives, got in (
                (jnp.maximum(z - k, 0), z + 1, (z >= k) & (z < zs - 1), z >= k + 1, jnp.maximum(z - 1 - k, 0)),
                (jnp.minimum(z + k, zs - 1), z - 1, (z + k < zs) & (z > 0), z + k + 1 < zs, jnp.minimum(z + 1 + k, zs - 1)),
            ):
                piece = whole.at[zz] if y_first else whole.at[zz, y]
                move = along(piece, "z", to, sends, receives)
                follow = [] if y_first else [along(whole.at[got, y], "y", 1 - y, receives, receives)]
                step.append((move, follow))
            self.steps.append(step)

    def begin(self):
        self.swap.start()
        self.local.start()

    def swapped(self):
        self.swap.arrived()
        self.local.wait()
        self.own_y.start()
        if not self.y_first:
            for move, _ in self.steps[0]:
                move.start()

    def own_y_arrived(self):
        self.own_y.arrived()
        if self.y_first:
            for move, _ in self.steps[0]:
                move.start()

    def step(self, k):
        for side in range(2):
            move, follow = self.steps[k][side]
            move.arrived()
            if k + 1 < len(self.steps):
                self.steps[k + 1][side][0].start()
            for other in follow:
                other.start()

    def finish(self):
        if not self.y_first:
            self.own_y.arrived()
        for step in self.steps:
            for move, follow in step:
                for other in follow:
                    other.arrived()
        self.swap.sent()
        self.own_y.sent()
        for step in self.steps:
            for move, follow in step:
                move.sent()
                for other in follow:
                    other.sent()


def greet(zs):
    z, y, x = lax.axis_index("z"), lax.axis_index("y"), lax.axis_index("x")
    barrier = pltpu.get_barrier_semaphore()

    def signal(device):
        pl.semaphore_signal(barrier, inc=1, device_id=device, device_id_type=pl.DeviceIdType.MESH)

    signal({"x": 1 - x})
    signal({"y": 1 - y})
    pl.when(z > 0)(lambda: signal({"z": z - 1}))
    pl.when(z < zs - 1)(lambda: signal({"z": z + 1}))
    peers = 2 + (z > 0).astype(jnp.int32) + (z < zs - 1).astype(jnp.int32)
    pl.semaphore_wait(barrier, peers)


def gather_kernel(zs, groups, pairs, *refs):
    shards = sum(groups)
    owns, pair_in = refs[:shards], refs[shards : shards + pairs]
    refs = refs[shards + pairs :]
    outs = refs[: len(groups) + pairs]
    lanes = Lanes(*refs[len(groups) + pairs :], zs)
    z, y, x = lanes.z, lanes.y, lanes.x
    pieces, at = [], 0
    for count, whole in zip(groups, outs):
        width = whole.shape[-1] // count
        for i in range(count):
            target = whole.at[z, y, x, :, pl.ds(i * width, width)]
            pieces.append(pltpu.make_async_copy(owns[at], target, lanes.local()))
            at += 1
    for piece in pieces:
        piece.start()
    greet(zs)
    gathers = [Gather(lanes, whole) for whole in outs[: len(groups)]]
    quarters = [
        PairGather(lanes, pair_in[i], outs[len(groups) + i], i == 0) for i in range(pairs)
    ]
    for quarter in quarters:
        quarter.begin()
    for piece in pieces:
        piece.wait()
    for gather in gathers:
        gather.begin()
    for quarter in quarters:
        quarter.swapped()
    for gather in gathers:
        gather.far_first()
    for k in range(zs - 1):
        for gather in gathers:
            gather.step(k)
        for quarter in quarters:
            if quarter.y_first:
                if k == 0:
                    quarter.own_y_arrived()
            else:
                quarter.step(k)
        for gather in gathers:
            gather.far_step(k)
        for quarter in quarters:
            if quarter.y_first:
                quarter.step(k)
    for gather in gathers:
        gather.finish()
    for quarter in quarters:
        quarter.finish()


def gather_all(groups, quarters, zs):
    flat = [shard for group in groups for shard in group] + list(quarters)
    outs = []
    for group in groups:
        columns = sum(shard.shape[1] for shard in group)
        outs.append(
            jax.ShapeDtypeStruct((zs, 2, 2, group[0].shape[0], columns), group[0].dtype)
        )
    for shard in quarters:
        outs.append(
            jax.ShapeDtypeStruct((zs, 2, 2, shard.shape[0], shard.shape[1] // 2), shard.dtype)
        )
    count, pairs = len(groups), len(quarters)
    moves = count * (3 + 8 * (zs - 1)) + pairs * (2 + 4 * (zs - 1))
    hbm = pl.BlockSpec(memory_space=pltpu.HBM)
    return pl.pallas_call(
        functools.partial(gather_kernel, zs, tuple(len(group) for group in groups), pairs),
        out_shape=outs,
        in_specs=[hbm] * len(flat),
        out_specs=[hbm] * len(outs),
        scratch_shapes=[
            pltpu.SemaphoreType.DMA((moves,)),
            pltpu.SemaphoreType.DMA((moves,)),
            pltpu.SemaphoreType.DMA((len(flat),)),
        ],
        compiler_params=pltpu.CompilerParams(collective_id=1, has_side_effects=True),
    )(*flat)


def plus(*terms):
    total = terms[0].astype(F32)
    for term in terms[1:]:
        total = total + term.astype(F32)
    return total


def ends_first(zs):
    order = []
    for i in range(zs // 2):
        order += [zs - 1 - i, i]
    return order


class Line:
    def __init__(self, lanes, part, from_left, from_right):
        zs, z = lanes.zs, lanes.z
        self.zs, self.z, self.part = zs, z, part
        self.from_left, self.from_right = from_left, from_right
        self.right, self.left = {}, {}
        for d in ends_first(zs):
            after, before = jnp.minimum(z + 1, zs - 1), jnp.maximum(z - 1, 0)
            self.right[d] = lanes.copies(
                (part.at[d], from_left.at[d]), from_left.at[d], {"z": after}
            )
            self.left[d] = lanes.copies(
                (part.at[d], from_right.at[d]), from_right.at[d], {"z": before}
            )

    def pass_on(self, d):
        for moves, inbox, sends, edge in (
            (self.right[d], self.from_left, self.z < d, self.z == 0),
            (self.left[d], self.from_right, self.z > d, self.z == self.zs - 1),
        ):

            @pl.when(sends & edge)
            def _():
                moves[0].start()

            @pl.when(sends & jnp.logical_not(edge))
            def _():
                moves[1].wait_recv()
                inbox[d] = plus(self.part[d], inbox[d]).astype(inbox.dtype)
                moves[1].start()

    def total(self, sink):
        for d in range(self.zs):

            @pl.when(self.z == d)
            def _():
                terms = [self.part[d]]
                if d > 0:
                    self.right[d][0].wait_recv()
                    terms.append(self.from_left[d])
                if d < self.zs - 1:
                    self.left[d][0].wait_recv()
                    terms.append(self.from_right[d])
                sink[...] = plus(*terms).astype(sink.dtype)

    def finish(self):
        for d in ends_first(self.zs):
            pl.when(self.z < d)(self.right[d][0].wait_send)
            pl.when(self.z > d)(self.left[d][0].wait_send)


class Scatter:
    def __init__(self, lanes, part, held, out, first):
        zs, z, y, x = lanes.zs, lanes.z, lanes.y, lanes.x
        got, near, from_left, from_right, ready = held
        second = "y" if first == "x" else "x"
        self.lanes, self.part, self.got, self.near, self.ready, self.out = (
            lanes, part, got, near, ready, out,
        )
        f, s = (x, y) if first == "x" else (y, x)
        self.f, self.s = f, s

        def block(zz, a, b):
            return part.at[zz, b, a] if first == "x" else part.at[zz, a, b]

        self.block = block
        self.one, self.two = {}, {}
        for zz in ends_first(zs):
            for j, b in enumerate((1 - s, s)):
                self.one[zz, j] = Move(
                    lanes.copy(block(zz, 1 - f, b), got.at[zz, j], {first: 1 - f}), None, None
                )
        for zz in ends_first(zs):
            self.two[zz] = Move(
                lanes.copy(got.at[zz, 0], near.at[zz], {second: 1 - s}), None, None
            )
        self.line = Line(lanes, ready, from_left, from_right)

    def begin(self):
        for zz in ends_first(self.lanes.zs):
            for j in range(2):
                self.one[zz, j].start()

    def second(self, zz):
        self.one[zz, 0].arrived()
        mine, got = self.block(zz, self.f, 1 - self.s), self.got
        got[zz, 0] = plus(mine[...], got[zz, 0]).astype(got.dtype)
        self.two[zz].start()

    def third(self, zz):
        self.one[zz, 1].arrived()
        self.two[zz].arrived()
        mine = self.block(zz, self.f, self.s)
        self.ready[zz] = plus(mine[...], self.got[zz, 1], self.near[zz]).astype(self.ready.dtype)
        self.line.pass_on(zz)

    def finish(self):
        self.line.total(self.out)
        self.line.finish()
        for move in list(self.one.values()) + list(self.two.values()):
            move.sent()


class ScatterZ:
    def __init__(self, lanes, part, held, out):
        y, x = lanes.y, lanes.x
        from_left, from_right, held_z, near, last = held
        self.lanes, self.sum_z, self.near, self.last, self.out = lanes, held_z, near, last, out
        self.line = Line(lanes, part, from_left, from_right)
        self.two = Move(lanes.copy(held_z.at[1 - y], near, {"y": 1 - y}), None, None)
        self.three = Move(lanes.copy(near.at[1 - x], last, {"x": 1 - x}), None, None)

    def pass_on(self, d):
        self.line.pass_on(d)

    def total(self):
        self.line.total(self.sum_z)
        self.two.start()

    def after(self):
        self.two.arrived()
        self.near[...] = plus(self.sum_z[self.lanes.y], self.near[...]).astype(self.near.dtype)
        self.three.start()

    def finish(self):
        self.three.arrived()
        self.out[...] = plus(self.near[self.lanes.x], self.last[...]).astype(self.out.dtype)
        self.line.finish()
        self.two.sent()
        self.three.sent()


class Crest:
    def __init__(self, lanes, own, held, out):
        zs, z, y, x = lanes.zs, lanes.z, lanes.y, lanes.x
        near_x, near_y, mine_x, mine_y, right, left, inbox_r, inbox_l = (
            held.at[i] for i in range(8)
        )
        self.zs, self.z, self.own, self.out = zs, z, own, out
        self.near_x, self.near_y, self.mine_x, self.mine_y = near_x, near_y, mine_x, mine_y
        self.ways = (
            (right, inbox_r, z > 0, z < zs - 1),
            (left, inbox_l, z < zs - 1, z > 0),
        )
        self.one = Move(lanes.copy(own, near_x, {"x": 1 - x}), None, None)
        self.two = Move(lanes.copy(mine_x, near_y, {"y": 1 - y}), None, None)
        self.moves = [
            Move(lanes.copy(right, inbox_r, {"z": jnp.minimum(z + 1, zs - 1)}), z < zs - 1, z > 0),
            Move(lanes.copy(left, inbox_l, {"z": jnp.maximum(z - 1, 0)}), z > 0, z < zs - 1),
        ]

    def second(self):
        self.one.arrived()
        self.mine_x[...] = jnp.maximum(self.own[...], self.near_x[...])
        self.two.start()

    def finish(self):
        self.two.arrived()
        self.mine_y[...] = jnp.maximum(self.mine_x[...], self.near_y[...])
        self.out[...] = self.mine_y[...]
        for move, (held, inbox, has_before, has_after) in zip(self.moves, self.ways):

            @pl.when(has_before)
            def _():
                move.copy_.wait_recv()
                self.out[...] = jnp.maximum(self.out[...], inbox[...])
                held[...] = jnp.maximum(self.mine_y[...], inbox[...])

            @pl.when(jnp.logical_not(has_before))
            def _():
                held[...] = self.mine_y[...]

            move.start()
        for move in [self.one, self.two] + self.moves:
            move.sent()


def scatter_kernel(zs, orders, *refs):
    count = len(orders)
    parts, crest_in, refs = refs[:count], refs[count], refs[count + 1 :]
    outs, crest_out, rest = refs[:count], refs[count], list(refs[count + 1 :])
    send_sems, recv_sems = rest[:2]
    rest = rest[2:]
    lanes = Lanes(send_sems, recv_sems, None, zs)
    greet(zs)
    full, zfirst = [], []
    for i, order in enumerate(orders):
        held, rest = rest[:5], rest[5:]
        if order == "z":
            zfirst.append(ScatterZ(lanes, parts[i], held, outs[i]))
        else:
            full.append(Scatter(lanes, parts[i], held, outs[i], order))
    crest = Crest(lanes, crest_in, rest[0], crest_out)
    crest.one.start()
    for item in full:
        item.begin()
    crest.second()
    for d in ends_first(zs):
        for item in zfirst:
            item.pass_on(d)
        for item in full:
            item.second(d)
    for item in zfirst:
        item.total()
    crest.finish()
    for d in ends_first(zs):
        for item in full:
            item.third(d)
    for item in zfirst:
        item.after()
    for item in full:
        item.finish()
    for item in zfirst:
        item.finish()


def scatter_all(parts, orders, crest, zs):
    scratch, moves = [], 4
    for part, order in zip(parts, orders):
        block = part.shape[3:]
        if order == "z":
            shapes = [(zs, 2, 2) + block] * 2 + [(2, 2) + block, (2,) + block, block]
            moves += 2 * zs + 2
        else:
            shapes = [(zs, 2) + block] + [(zs,) + block] * 4
            moves += 5 * zs
        scratch += [pltpu.VMEM(shape, part.dtype) for shape in shapes]
    vmem = pl.BlockSpec(memory_space=pltpu.VMEM)
    return pl.pallas_call(
        functools.partial(scatter_kernel, zs, orders),
        out_shape=[jax.ShapeDtypeStruct(part.shape[3:], F32) for part in parts]
        + [jax.ShapeDtypeStruct(crest.shape, F32)],
        in_specs=[vmem] * (len(parts) + 1),
        out_specs=[vmem] * (len(parts) + 1),
        scratch_shapes=[pltpu.SemaphoreType.DMA((moves,)), pltpu.SemaphoreType.DMA((moves,))]
        + scratch
        + [pltpu.VMEM((8,) + crest.shape, F32)],
        compiler_params=pltpu.CompilerParams(
            collective_id=2, has_side_effects=True, vmem_limit_bytes=56 * 2**20
        ),
    )(*parts, crest)


def nn(left, right):
    return lax.dot_general(left, right, (((1,), (0,)), ((), ())), preferred_element_type=F32)


def nt(left, right):
    return lax.dot_general(left, right, (((1,), (1,)), ((), ())), preferred_element_type=F32)


def tn(left, right):
    return lax.dot_general(left, right, (((0,), (0,)), ((), ())), preferred_element_type=F32)


def columns_by(value, axis_name, zs):
    rows = value.shape[0]
    at = lax.axis_index(axis_name)
    if axis_name == "y":
        split = value.reshape(rows, zs, 2, -1)
        dim = 2
    else:
        split = value.reshape(rows, 2 * zs, 2, -1)
        dim = 2
    return (
        pick(split, at, dim).reshape(rows, -1),
        pick(split, 1 - at, dim).reshape(rows, -1),
    )


def reduce_pair(left_keep, left_send, right, zs):
    got = swap(tn(left_send, right).astype(BF), "y")
    held = (tn(left_keep, right) + got.astype(F32)).astype(BF)
    held = held.reshape(zs, -1, right.shape[1])
    held = lax.psum_scatter(held, "z", scatter_dimension=0, tiled=False)
    held = held.reshape(2, -1, right.shape[1])
    at = lax.axis_index("x")
    got = swap(pick(held, 1 - at, 0), "x")
    return pick(held, at, 0), got


def norm_forward(stream, gain_vec, bias_vec):
    average = jnp.mean(stream, axis=-1, keepdims=True)
    centred = stream - average
    inverse = lax.rsqrt(jnp.mean(centred * centred, axis=-1, keepdims=True) + EPSILON)
    unit_rows = centred * inverse
    return (unit_rows * gain_vec + bias_vec, unit_rows, inverse)


def norm_backward(incoming, unit_rows, inverse, gain_vec):
    gain_grad = jnp.sum(incoming * unit_rows, axis=0)
    bias_grad = jnp.sum(incoming, axis=0)
    scaled = incoming * gain_vec
    stream_grad = inverse * (
        scaled
        - jnp.mean(scaled, axis=-1, keepdims=True)
        - unit_rows * jnp.mean(scaled * unit_rows, axis=-1, keepdims=True)
    )
    return (stream_grad, gain_grad, bias_grad)


def turn_tables(positions):
    rates = 10000.0 ** (-jnp.arange(0, ROT_DIM, 2).astype(F32) / ROT_DIM)
    angles = positions[:, None] * rates[None, :]
    cosine, sine = jnp.cos(angles), jnp.sin(angles)
    rest = jnp.ones((positions.shape[0], HEAD_DIM - ROT_DIM), F32)
    zero, none = jnp.zeros_like(rest), jnp.zeros_like(sine)
    return (
        jnp.concatenate([cosine, cosine, rest] * 2, axis=1),
        jnp.concatenate([-sine, none, zero] * 2, axis=1),
        jnp.concatenate([none, sine, zero] * 2, axis=1),
    )


def turn(field, cosine, sine_a, sine_b, direction):
    half = ROT_DIM // 2
    width = field.shape[-1]
    ahead = pltpu.roll(field, width - half, 1)
    behind = pltpu.roll(field, half, 1)
    return field * cosine + direction * (ahead * sine_a + behind * sine_b)


def head_lanes(shape, which):
    lanes = lax.broadcasted_iota(jnp.int32, shape, 1)
    return (lanes >= which * HEAD_DIM) & (lanes < (which + 1) * HEAD_DIM)


def attend_tile(query, keys, values, bias):
    scores = nt(query, keys) + bias
    top = jnp.max(scores, axis=-1, keepdims=True)
    weights = jnp.exp(scores - top)
    total = jnp.sum(weights, axis=-1, keepdims=True)
    return nn(weights.astype(BF), values) / total, top


def attend_kernel(q_ref, k_ref, v_ref, bias_ref, mixed_ref, peak_ref):
    rows = q_ref.shape[0]
    tile = rows // 3 if rows % 3 == 0 and (rows // 3) % 16 == 0 else rows
    keys, values, bias = k_ref[...], v_ref[...], bias_ref[...]
    peaks = [None, None]
    for start in range(0, rows, tile):
        query = q_ref[start : start + tile, :] * BF(HEAD_DIM ** (-0.5))
        outs = []
        for which in range(2):
            one = jnp.where(head_lanes(query.shape, which), query, jnp.zeros_like(query))
            out, top = attend_tile(one, keys, values, bias)
            outs.append(out)
            top = jnp.max(top, axis=0, keepdims=True)
            peaks[which] = top if peaks[which] is None else jnp.maximum(peaks[which], top)
        mixed = jnp.where(head_lanes(outs[0].shape, 0), outs[0], outs[1])
        mixed_ref[start : start + tile, :] = mixed.astype(BF)
    spot = head_lanes((8, 2 * HEAD_DIM), 0)
    peak_ref[0] = jnp.where(
        spot, jnp.broadcast_to(peaks[0], spot.shape), jnp.broadcast_to(peaks[1], spot.shape)
    )


def attend(query, keys, values, bias, offsets):
    rows, tokens = query.shape[0], keys.shape[0]
    pairs = bias.shape[0]
    wide = 2 * HEAD_DIM
    mixed, peak = pl.pallas_call(
        attend_kernel,
        grid=(pairs,),
        out_shape=[
            jax.ShapeDtypeStruct((rows, pairs * wide), BF),
            jax.ShapeDtypeStruct((pairs, 8, wide), F32),
        ],
        in_specs=[
            pl.BlockSpec((rows, wide), lambda j: (0, offsets[0] + j)),
            pl.BlockSpec((tokens, wide), lambda j: (0, offsets[1] + j)),
            pl.BlockSpec((tokens, wide), lambda j: (0, offsets[2] + j)),
            pl.BlockSpec((1, tokens), lambda j: (0, 0)),
        ],
        out_specs=[
            pl.BlockSpec((rows, wide), lambda j: (0, j)),
            pl.BlockSpec((1, 8, wide), lambda j: (j, 0, 0)),
        ],
        compiler_params=pltpu.CompilerParams(vmem_limit_bytes=48 * 2**20),
        cost_estimate=pl.CostEstimate(
            flops=8 * rows * tokens * pairs * wide,
            bytes_accessed=4 * (rows + tokens) * pairs * wide,
            transcendentals=2 * pairs * rows * tokens,
        ),
    )(query, keys, values, bias[:1])
    return mixed, peak[:, 0, ::HEAD_DIM].reshape(-1)


def attend_back_kernel(turned, q_ref, k_ref, v_ref, g_ref, bias_ref, *refs):
    if turned:
        cos_ref, sa_ref, sb_ref = refs[:3]
        refs = refs[3:]
    dq_ref, dk_ref, dv_ref, dk_acc, dv_acc = refs
    rows = q_ref.shape[0]
    tile = rows // 3 if rows % 3 == 0 and (rows // 3) % 128 == 0 else rows
    scale = BF(HEAD_DIM ** (-0.5))
    keys, values, bias = k_ref[...], v_ref[...], bias_ref[...]
    for start in range(0, rows, tile):
        part = slice(start, start + tile)
        query, grad = q_ref[part, :] * scale, g_ref[part, :]
        dq = None
        for which in range(2):
            mine = head_lanes(query.shape, which)
            one = jnp.where(mine, query, jnp.zeros_like(query))
            out = jnp.where(mine, grad, jnp.zeros_like(grad))
            scores = nt(keys, one) + bias
            weights = jnp.exp(scores - jnp.max(scores, axis=0, keepdims=True))
            weights = weights * (1.0 / jnp.sum(weights, axis=0, keepdims=True))
            slope = nt(values, out)
            slope = weights * (slope - jnp.sum(weights * slope, axis=0, keepdims=True))
            slope = slope.astype(BF)
            dv = nn(weights.astype(BF), out)
            dk = nn(slope, one)
            other = jnp.where(head_lanes(keys.shape, which), keys, jnp.zeros_like(keys))
            piece = tn(slope, other * scale)
            dq = piece if dq is None else dq + piece
            if start == 0 and which == 0:
                dv_acc[...] = dv
                dk_acc[...] = dk
            else:
                dv_acc[...] += dv
                dk_acc[...] += dk
        if turned:
            dq = turn(dq, cos_ref[part, :], sa_ref[part, :], sb_ref[part, :], -1.0)
        dq_ref[part, :] = dq.astype(BF)
    dk = dk_acc[...]
    if turned:
        dk = turn(dk, cos_ref[...], sa_ref[...], sb_ref[...], -1.0)
    dk_ref[...] = dk.astype(BF)
    dv_ref[...] = dv_acc[...].astype(BF)


def attend_back(query, keys, values, grad, bias_column, offsets, turns):
    rows, tokens = query.shape[0], keys.shape[0]
    wide = 2 * HEAD_DIM
    pairs = grad.shape[1] // wide
    ins = [query, keys, values, grad, bias_column]
    specs = [
        pl.BlockSpec((rows, wide), lambda j: (0, offsets[0] + j)),
        pl.BlockSpec((tokens, wide), lambda j: (0, offsets[1] + j)),
        pl.BlockSpec((tokens, wide), lambda j: (0, offsets[2] + j)),
        pl.BlockSpec((rows, wide), lambda j: (0, j)),
        pl.BlockSpec((tokens, 1), lambda j: (0, 0)),
    ]
    if turns is not None:
        ins += list(turns)
        specs += [pl.BlockSpec((rows, wide), lambda j: (0, 0))] * 3
    return pl.pallas_call(
        functools.partial(attend_back_kernel, turns is not None),
        grid=(pairs,),
        out_shape=[
            jax.ShapeDtypeStruct((rows, pairs * wide), BF),
            jax.ShapeDtypeStruct((tokens, pairs * wide), BF),
            jax.ShapeDtypeStruct((tokens, pairs * wide), BF),
        ],
        in_specs=specs,
        out_specs=[
            pl.BlockSpec((rows, wide), lambda j: (0, j)),
            pl.BlockSpec((tokens, wide), lambda j: (0, j)),
            pl.BlockSpec((tokens, wide), lambda j: (0, j)),
        ],
        scratch_shapes=[pltpu.VMEM((tokens, wide), F32), pltpu.VMEM((tokens, wide), F32)],
        compiler_params=pltpu.CompilerParams(vmem_limit_bytes=48 * 2**20),
        cost_estimate=pl.CostEstimate(
            flops=20 * rows * tokens * pairs * wide,
            bytes_accessed=8 * (rows + tokens) * pairs * wide,
            transcendentals=2 * pairs * rows * tokens,
        ),
    )(*ins)


def project_kernel(turned, x_ref, w_ref, cos_ref, sa_ref, sb_ref, out_ref):
    wide = 2 * HEAD_DIM
    made = nn(x_ref[...], w_ref[...])

    @pl.when(pl.program_id(0) < turned)
    def _():
        for start in range(0, made.shape[1], wide):
            piece = turn(made[:, start : start + wide], cos_ref[...], sa_ref[...], sb_ref[...], 1.0)
            out_ref[:, start : start + wide] = piece.astype(BF)

    @pl.when(pl.program_id(0) >= turned)
    def _():
        out_ref[...] = made.astype(BF)


def project(rows, weight, turns, turned_columns):
    count, depth = rows.shape
    columns = weight.shape[1]
    block = 2 * HEAD_DIM * (2 if turned_columns % (4 * HEAD_DIM) == 0 else 1)
    table = pl.BlockSpec((count, 2 * HEAD_DIM), lambda j: (0, 0))
    return pl.pallas_call(
        functools.partial(project_kernel, turned_columns // block),
        grid=(columns // block,),
        out_shape=jax.ShapeDtypeStruct((count, columns), BF),
        in_specs=[
            pl.BlockSpec((count, depth), lambda j: (0, 0)),
            pl.BlockSpec((depth, block), lambda j: (0, j)),
            table,
            table,
            table,
        ],
        out_specs=pl.BlockSpec((count, block), lambda j: (0, j)),
        compiler_params=pltpu.CompilerParams(vmem_limit_bytes=48 * 2**20),
        cost_estimate=pl.CostEstimate(
            flops=2 * count * depth * columns,
            bytes_accessed=2 * (count * depth + depth * columns + count * columns),
            transcendentals=0,
        ),
    )(rows, weight, *turns)


def pair_rows(own):
    return jnp.concatenate([own, swap(own, "tensor")], axis=0)


def group_rows(own):
    both = jnp.stack([own, swap(own, "x")])
    other = swap(both, "tensor")
    return jnp.concatenate([both[0], other[0], both[1], other[1]], axis=0)


def spread_pair(left, right_t):
    rows = left.shape[0] // 2
    got = swap(nt(left[rows:], right_t), "tensor")
    return nt(left[:rows], right_t) + got


def spread_group(product):
    quarter = product.rows // 4
    far_send = product(3 * quarter, quarter)
    far = product(2 * quarter, quarter) + swap(far_send, "tensor")
    got_far = swap(far.astype(BF), "x")
    near = product(0, quarter) + swap(product(quarter, quarter), "tensor")
    return near + got_far.astype(F32)


class Product:
    def __init__(self, terms, transposed):
        self.terms = terms
        self.transposed = transposed
        self.rows = terms[0][0].shape[0]

    def __call__(self, first, count):
        total = None
        for left, right in self.terms:
            part = (nt if self.transposed else nn)(left[first : first + count], right)
            total = part if total is None else total + part
        return total


def per_device(
    inputs,
    cotangent,
    context,
    context_live,
    lengths,
    threshold,
    self_gain,
    self_bias,
    self_query,
    self_key,
    self_value,
    self_output,
    cross_gain,
    cross_bias,
    cross_query,
    cross_key,
    cross_value,
    cross_output,
    feed_gain,
    feed_bias,
    gate_weight,
    up_weight,
    down_weight,
):
    zs = lax.axis_size("z")
    x_at = lax.axis_index("x")
    t_at = lax.axis_index("tensor")
    width = inputs.shape[1]
    rows = inputs.shape[0]
    seq_len = 2 * rows
    inner = self_query.shape[1]
    heads_here = inner // HEAD_DIM
    ff = gate_weight.shape[1] // 2
    shard_rows = self_query.shape[0]

    vectors = jnp.stack(
        [self_gain, self_bias, cross_gain, cross_bias, feed_gain, feed_bias]
    ).astype(F32)
    vectors = jnp.pad(vectors, ((0, 2), (0, 128 - shard_rows)))
    (norms, in_weight, self_out_t, cross_in, memory_weight, cross_out_t, gate_full, up_full, down_t) = (
        gather_all(
            [
                [vectors],
                [self_query, self_key, self_value],
                [self_output.T],
                [cross_query],
                [cross_key, cross_value],
                [cross_output.T],
            ],
            [gate_weight, up_weight, down_weight.T],
            zs,
        )
    )
    norms = norms.reshape(-1, 8, 128)[:, :6, :shard_rows].transpose(1, 0, 2).reshape(6, width)
    in_weight, self_out_t, cross_in, cross_out_t, gate_full, up_full, down_t = (
        w.reshape(width, -1)
        for w in (in_weight, self_out_t, cross_in, cross_out_t, gate_full, up_full, down_t)
    )
    memory_weight = memory_weight.reshape(-1, 2 * inner)

    local = jnp.arange(rows)
    places = jnp.concatenate([t_at * rows + local, (1 - t_at) * rows + local])
    turns = turn_tables(places.astype(F32))
    self_bias_row = jnp.where(places < lengths[0], 0.0, NEGATIVE).astype(F32)
    tokens = context.shape[1]
    token_rows = -(-tokens // 128) * 128
    cross_bias_row = jnp.pad(
        jnp.where(context_live[0] > 0, 0.0, NEGATIVE).astype(F32),
        (0, token_rows - tokens),
        constant_values=NEGATIVE,
    )
    memory = jnp.pad(context[0], ((0, token_rows - tokens), (0, 0)))
    pairs = inner // (2 * HEAD_DIM)

    cot_group = group_rows(cotangent)
    all_inputs = pair_rows(inputs)
    stream = inputs.astype(F32)
    normed, _, _ = norm_forward(all_inputs.astype(F32), norms[0], norms[1])
    normed_self = normed.astype(BF)
    taken = project(normed_self, in_weight, turns, 2 * inner)
    self_bias_rows = jnp.broadcast_to(self_bias_row, (pairs, seq_len))
    mixed_self, peak_self = attend(taken, taken, taken, self_bias_rows, (0, pairs, 2 * pairs))
    stream_cross = stream + spread_pair(mixed_self, self_out_t)
    normed, unit_cross, inverse_cross = norm_forward(stream_cross, norms[2], norms[3])
    normed_cross = pair_rows(normed.astype(BF))
    query_cross = nn(normed_cross, cross_in).astype(BF)
    taken_cross = nn(memory, memory_weight).astype(BF)
    cross_bias_rows = jnp.broadcast_to(cross_bias_row, (pairs, token_rows))
    mixed_cross, peak_cross = attend(
        query_cross, taken_cross, taken_cross, cross_bias_rows, (0, 0, pairs)
    )
    stream_feed = stream_cross + spread_pair(mixed_cross, cross_out_t)
    normed, unit_feed, inverse_feed = norm_forward(stream_feed, norms[4], norms[5])
    normed_feed = group_rows(normed.astype(BF))
    gate_pre = nn(normed_feed, gate_full)
    upward = nn(normed_feed, up_full)
    sigmoid_gate = jax.nn.sigmoid(gate_pre)
    hidden = (gate_pre * sigmoid_gate * upward).astype(BF)
    result = (stream_feed + spread_group(Product([(hidden, down_t)], True))).astype(BF)
    crest = jnp.pad(
        jnp.maximum(peak_self, peak_cross)[None], ((0, 7), (0, 128 - heads_here))
    )

    cot_keep, cot_send = columns_by(cot_group, "y", zs)
    down_keep, down_got = reduce_pair(cot_keep, cot_send, hidden, zs)
    grad_hidden = nn(cot_group, down_t)
    grad_gate = grad_hidden * upward * sigmoid_gate * (1.0 + gate_pre * (1.0 - sigmoid_gate))
    grad_upward = grad_hidden * gate_pre * sigmoid_gate
    grad_gate = grad_gate.astype(BF)
    grad_upward = grad_upward.astype(BF)
    grad_gates = jnp.concatenate([grad_gate, grad_upward], axis=1)
    grad_normed = spread_group(Product([(grad_gate, gate_full), (grad_upward, up_full)], True))
    feed_keep, feed_send = columns_by(normed_feed, "y", zs)
    gates_keep, gates_got = reduce_pair(feed_keep, feed_send, grad_gates, zs)
    stream_part, grad_feed_gain, grad_feed_bias = norm_backward(
        grad_normed, unit_feed, inverse_feed, norms[4]
    )
    grad_stream = cotangent.astype(F32) + stream_part
    grad_full = pair_rows(grad_stream.astype(BF))
    part_cross_output = tn(grad_full, mixed_cross)
    grad_mixed = nn(grad_full, cross_out_t).astype(BF)
    grad_query, grad_keys, grad_values = attend_back(
        query_cross, taken_cross, taken_cross, grad_mixed, cross_bias_row[:, None], (0, 0, pairs), None
    )
    grad_normed = spread_pair(grad_query, cross_in)
    part_cross_query = tn(normed_cross, grad_query)
    part_memory = tn(memory, jnp.concatenate([grad_keys, grad_values], axis=1))
    stream_part, grad_cross_gain, grad_cross_bias = norm_backward(
        grad_normed, unit_cross, inverse_cross, norms[2]
    )
    grad_stream = grad_stream + stream_part
    grad_full = pair_rows(grad_stream.astype(BF))
    part_self_output = tn(grad_full, mixed_self)
    grad_mixed = nn(grad_full, self_out_t).astype(BF)
    grad_in = jnp.concatenate(
        attend_back(
            taken, taken, taken, grad_mixed, self_bias_row[:, None], (0, pairs, 2 * pairs), turns
        ),
        axis=1,
    )
    part_self_in = tn(normed_self, grad_in)
    grad_normed = spread_pair(grad_in, in_weight)
    _, unit_self, inverse_self = norm_forward(stream, norms[0], norms[1])
    stream_part, grad_self_gain, grad_self_bias = norm_backward(
        grad_normed, unit_self, inverse_self, norms[0]
    )
    grad_stream = grad_stream + stream_part

    vector_sums = jnp.stack(
        [
            grad_self_gain,
            grad_self_bias,
            grad_cross_gain,
            grad_cross_bias,
            grad_feed_gain,
            grad_feed_bias,
        ]
    ).reshape(6, -1, shard_rows)
    vector_sums = vector_sums + swap(vector_sums, "tensor")
    vector_sums = jnp.pad(
        vector_sums.transpose(1, 0, 2), ((0, 0), (0, 2), (0, 128 - shard_rows))
    ).reshape(zs, 2, 2, 8, 128)

    def blocks(part):
        return part.astype(BF).reshape(zs, 2, 2, -1, part.shape[1])

    (vector_sums, sum_self_in, sum_self_output, sum_cross_query, sum_cross_output, sum_memory, crest) = (
        scatter_all(
            [
                vector_sums,
                blocks(part_self_in),
                blocks(part_self_output),
                blocks(part_cross_query),
                blocks(part_cross_output),
                blocks(part_memory),
            ],
            ["x", "x", "y", "y", "y", "z"],
            crest,
            zs,
        )
    )
    vector_sums = vector_sums[:, :shard_rows]
    peaks = crest[0, :heads_here]
    factor = jnp.sqrt(threshold[0] / jnp.maximum(peaks, threshold[0]))
    columns = jnp.repeat(factor, HEAD_DIM)[None, :]

    def side_by_side(kept, got):
        low = jnp.where(x_at == 0, kept, got).astype(F32)
        high = jnp.where(x_at == 0, got, kept).astype(F32)
        return jnp.concatenate([low, high], axis=1)

    down_sum = side_by_side(down_keep, down_got).T
    gate_sum = side_by_side(gates_keep[:, :ff], gates_got[:, :ff])
    up_sum = side_by_side(gates_keep[:, ff:], gates_got[:, ff:])
    return (
        result,
        grad_stream,
        vector_sums[0],
        vector_sums[1],
        sum_self_in[:, :inner],
        sum_self_in[:, inner : 2 * inner],
        sum_self_in[:, 2 * inner :],
        sum_self_output.T,
        vector_sums[2],
        vector_sums[3],
        sum_cross_query,
        sum_memory[:, :inner],
        sum_memory[:, inner:],
        sum_cross_output.T,
        vector_sums[4],
        vector_sums[5],
        gate_sum,
        up_sum,
        down_sum,
        peaks,
        self_query.astype(F32) * columns,
        self_key.astype(F32) * columns,
        cross_query.astype(F32) * columns,
        cross_key.astype(F32) * columns,
    )


def solution(mesh):
    count = mesh.shape["dp"]
    mesh = Mesh(
        mesh.devices.reshape(count // 4, 2, 2, mesh.shape["tensor"]), ("z", "y", "x", "tensor")
    )
    dp = ("z", "y", "x")
    both = P(dp + ("tensor",), None)
    split = P(dp)
    row_major = P(dp, "tensor")
    column_major = P("tensor", dp)
    in_specs = (
        both,
        both,
        P(dp, None, None),
        P(dp, None),
        split,
        P(),
        split,
        split,
        row_major,
        row_major,
        row_major,
        column_major,
        split,
        split,
        row_major,
        row_major,
        row_major,
        column_major,
        split,
        split,
        row_major,
        row_major,
        column_major,
    )
    out_specs = (
        both,
        both,
        split,
        split,
        row_major,
        row_major,
        row_major,
        column_major,
        split,
        split,
        row_major,
        row_major,
        row_major,
        column_major,
        split,
        split,
        row_major,
        row_major,
        column_major,
        P("tensor"),
        row_major,
        row_major,
        row_major,
        row_major,
    )
    return jax.shard_map(
        per_device, mesh=mesh, in_specs=in_specs, out_specs=out_specs, check_vma=False
    )
```

```python
import functools

import jax
import jax.numpy as jnp
from jax import lax
from jax.experimental import pallas as pl
from jax.experimental.pallas import tpu as pltpu
from jax.sharding import Mesh
from jax.sharding import PartitionSpec as P

HEAD_DIM = 64
ROT_DIM = 32
EPSILON = 1e-05
NEGATIVE = -1e30
BF = jnp.bfloat16
F32 = jnp.float32


def swap(value, axis):
    return lax.ppermute(value, axis, [(0, 1), (1, 0)])


def pick(value, index, dim):
    return lax.dynamic_index_in_dim(value, index, dim, keepdims=False)


class Lanes:
    def __init__(self, send_sems, recv_sems, local_sems, zs):
        self.send_sems, self.recv_sems, self.local_sems = send_sems, recv_sems, local_sems
        self.used = self.used_local = 0
        self.z = lax.axis_index("z")
        self.y = lax.axis_index("y")
        self.x = lax.axis_index("x")
        self.zs = zs

    def local(self):
        self.used_local += 1
        return self.local_sems.at[self.used_local - 1]

    def copy(self, source, target, device):
        return self.copies([source], target, device)[0]

    def copies(self, sources, target, device):
        slot = self.used
        self.used += 1
        return [
            pltpu.make_async_remote_copy(
                src_ref=source,
                dst_ref=target,
                send_sem=self.send_sems.at[slot],
                recv_sem=self.recv_sems.at[slot],
                device_id=device,
                device_id_type=pl.DeviceIdType.MESH,
            )
            for source in sources
        ]


def guarded(condition, action):
    if condition is None:
        action()
    else:
        pl.when(condition)(action)


class Move:
    def __init__(self, copy, sends, receives):
        self.copy_, self.sends, self.receives = copy, sends, receives

    def start(self):
        guarded(self.sends, self.copy_.start)

    def arrived(self):
        guarded(self.receives, self.copy_.wait_recv)

    def sent(self):
        guarded(self.sends, self.copy_.wait_send)


class Gather:
    def __init__(self, lanes, whole):
        zs, z, y, x = lanes.zs, lanes.z, lanes.y, lanes.x
        own = whole.at[z, y, x]

        def block(zz, yy):
            return whole.at[zz, yy, x]

        def along(source, target, axis, to, sends=None, receives=None):
            return Move(lanes.copy(source, target, {axis: to}), sends, receives)

        self.first = [
            along(own, block(z, y), "y", 1 - y),
            along(own, block(z, y), "x", 1 - x),
        ]
        self.far = [[along(block(z, 1 - y), block(z, 1 - y), "x", 1 - x)]]
        self.steps = []
        for k in range(zs - 1):
            right, left = jnp.maximum(z - k, 0), jnp.minimum(z + k, zs - 1)
            step = []
            for zz, to, sends, receives, got in (
                (right, z + 1, (z >= k) & (z < zs - 1), z >= k + 1, jnp.maximum(z - 1 - k, 0)),
                (left, z - 1, (z + k < zs) & (z > 0), z + k + 1 < zs, jnp.minimum(z + 1 + k, zs - 1)),
            ):
                source = own if k == 0 else block(zz, y)
                move = along(source, block(zz, y), "z", to, sends, receives)
                follow = [
                    along(block(got, y), block(got, y), "y", 1 - y, receives, receives),
                    along(block(got, y), block(got, y), "x", 1 - x, receives, receives),
                    along(block(got, 1 - y), block(got, 1 - y), "x", 1 - x, receives, receives),
                ]
                step.append((move, follow))
            self.steps.append(step)

    def begin(self):
        for move, _ in self.steps[0]:
            move.start()
        for move in self.first:
            move.start()

    def step(self, k):
        for side in range(2):
            move, follow = self.steps[k][side]
            move.arrived()
            if k + 1 < len(self.steps):
                self.steps[k + 1][side][0].start()
            follow[0].start()
            follow[1].start()

    def far_first(self):
        self.first[0].arrived()
        self.far[0][0].start()

    def far_step(self, k):
        for side in range(2):
            _, follow = self.steps[k][side]
            follow[0].arrived()
            follow[2].start()

    def landed(self):
        self.first[1].arrived()
        self.far[0][0].arrived()
        for step in self.steps:
            for _, follow in step:
                follow[1].arrived()
                follow[2].arrived()

    def sent(self):
        for move in self.first + self.far[0]:
            move.sent()
        for step in self.steps:
            for move, follow in step:
                move.sent()
                for other in follow:
                    other.sent()


class PairGather:
    def __init__(self, lanes, shard, whole, y_first):
        zs, z, y, x = lanes.zs, lanes.z, lanes.y, lanes.x
        ff = whole.shape[-1]
        kept = shard.at[:, pl.ds(pl.multiple_of(x * ff, ff), ff)]
        sent = shard.at[:, pl.ds(pl.multiple_of((1 - x) * ff, ff), ff)]
        self.y_first = y_first

        def along(piece, axis, to, sends=None, receives=None):
            return Move(lanes.copy(piece, piece, {axis: to}), sends, receives)

        self.swap = Move(lanes.copy(sent, whole.at[z, y, x], {"x": 1 - x}), None, None)
        self.local = pltpu.make_async_copy(kept, whole.at[z, y, x], lanes.local())
        self.own_y = along(whole.at[z, y], "y", 1 - y)
        self.steps = []
        for k in range(zs - 1):
            step = []
            for zz, to, sends, receives, got in (
                (jnp.maximum(z - k, 0), z + 1, (z >= k) & (z < zs - 1), z >= k + 1, jnp.maximum(z - 1 - k, 0)),
                (jnp.minimum(z + k, zs - 1), z - 1, (z + k < zs) & (z > 0), z + k + 1 < zs, jnp.minimum(z + 1 + k, zs - 1)),
            ):
                piece = whole.at[zz] if y_first else whole.at[zz, y]
                move = along(piece, "z", to, sends, receives)
                follow = [] if y_first else [along(whole.at[got, y], "y", 1 - y, receives, receives)]
                step.append((move, follow))
            self.steps.append(step)

    def begin(self):
        self.swap.start()
        self.local.start()

    def swapped(self):
        self.swap.arrived()
        self.local.wait()
        self.own_y.start()
        if not self.y_first:
            for move, _ in self.steps[0]:
                move.start()

    def own_y_arrived(self):
        self.own_y.arrived()
        if self.y_first:
            for move, _ in self.steps[0]:
                move.start()

    def step(self, k):
        for side in range(2):
            move, follow = self.steps[k][side]
            move.arrived()
            if k + 1 < len(self.steps):
                self.steps[k + 1][side][0].start()
            for other in follow:
                other.start()

    def landed(self):
        if not self.y_first:
            self.own_y.arrived()
        for step in self.steps:
            for move, follow in step:
                for other in follow:
                    other.arrived()

    def sent(self):
        self.swap.sent()
        self.own_y.sent()
        for step in self.steps:
            for move, follow in step:
                move.sent()
                for other in follow:
                    other.sent()


def greet(zs, mates=False):
    z, y, x = lax.axis_index("z"), lax.axis_index("y"), lax.axis_index("x")
    barrier = pltpu.get_barrier_semaphore()

    def signal(device):
        pl.semaphore_signal(barrier, inc=1, device_id=device, device_id_type=pl.DeviceIdType.MESH)

    signal({"x": 1 - x})
    signal({"y": 1 - y})
    pl.when(z > 0)(lambda: signal({"z": z - 1}))
    pl.when(z < zs - 1)(lambda: signal({"z": z + 1}))
    if mates:
        signal({"tensor": 1 - lax.axis_index("tensor")})
    peers = (3 if mates else 2) + (z > 0).astype(jnp.int32) + (z < zs - 1).astype(jnp.int32)
    pl.semaphore_wait(barrier, peers)


def gather_kernel(zs, groups, pairs, *refs):
    shards = sum(groups)
    owns, pair_in = refs[:shards], refs[shards : shards + pairs]
    refs = refs[shards + pairs :]
    outs = refs[: len(groups) + pairs]
    lanes = Lanes(*refs[len(groups) + pairs :], zs)
    z, y, x = lanes.z, lanes.y, lanes.x
    pieces, at = [], 0
    for count, whole in zip(groups, outs):
        width = whole.shape[-1] // count
        for i in range(count):
            target = whole.at[z, y, x, :, pl.ds(i * width, width)]
            pieces.append(pltpu.make_async_copy(owns[at], target, lanes.local()))
            at += 1
    for piece in pieces:
        piece.start()
    greet(zs)
    gathers = [Gather(lanes, whole) for whole in outs[: len(groups)]]
    quarters = [
        PairGather(lanes, pair_in[i], outs[len(groups) + i], i == 0) for i in range(pairs)
    ]
    for quarter in quarters:
        quarter.begin()
    for piece in pieces:
        piece.wait()
    for gather in gathers:
        gather.begin()
    for quarter in quarters:
        quarter.swapped()
    for gather in gathers:
        gather.far_first()
    for k in range(zs - 1):
        for gather in gathers:
            gather.step(k)
        for quarter in quarters:
            if quarter.y_first:
                if k == 0:
                    quarter.own_y_arrived()
            else:
                quarter.step(k)
        for gather in gathers:
            gather.far_step(k)
        for quarter in quarters:
            if quarter.y_first:
                quarter.step(k)
    for item in gathers + quarters:
        item.landed()
        item.sent()


def gather_all(groups, quarters, zs):
    flat = [shard for group in groups for shard in group] + list(quarters)
    outs = []
    for group in groups:
        columns = sum(shard.shape[1] for shard in group)
        outs.append(
            jax.ShapeDtypeStruct((zs, 2, 2, group[0].shape[0], columns), group[0].dtype)
        )
    for shard in quarters:
        outs.append(
            jax.ShapeDtypeStruct((zs, 2, 2, shard.shape[0], shard.shape[1] // 2), shard.dtype)
        )
    count, pairs = len(groups), len(quarters)
    moves = count * (3 + 8 * (zs - 1)) + pairs * (2 + 4 * (zs - 1))
    hbm = pl.BlockSpec(memory_space=pltpu.HBM)
    return pl.pallas_call(
        functools.partial(gather_kernel, zs, tuple(len(group) for group in groups), pairs),
        out_shape=outs,
        in_specs=[hbm] * len(flat),
        out_specs=[hbm] * len(outs),
        scratch_shapes=[
            pltpu.SemaphoreType.DMA((moves,)),
            pltpu.SemaphoreType.DMA((moves,)),
            pltpu.SemaphoreType.DMA((len(flat),)),
        ],
        compiler_params=pltpu.CompilerParams(collective_id=1, has_side_effects=True),
    )(*flat)


def plus(*terms):
    total = terms[0].astype(F32)
    for term in terms[1:]:
        total = total + term.astype(F32)
    return total


def ends_first(zs):
    order = []
    for i in range(zs // 2):
        order += [zs - 1 - i, i]
    return order


class Line:
    def __init__(self, lanes, part, from_left, from_right):
        zs, z = lanes.zs, lanes.z
        self.zs, self.z, self.part = zs, z, part
        self.from_left, self.from_right = from_left, from_right
        self.right, self.left = {}, {}
        for d in ends_first(zs):
            after, before = jnp.minimum(z + 1, zs - 1), jnp.maximum(z - 1, 0)
            self.right[d] = lanes.copies(
                (part.at[d], from_left.at[d]), from_left.at[d], {"z": after}
            )
            self.left[d] = lanes.copies(
                (part.at[d], from_right.at[d]), from_right.at[d], {"z": before}
            )

    def pass_on(self, d):
        for moves, inbox, sends, edge in (
            (self.right[d], self.from_left, self.z < d, self.z == 0),
            (self.left[d], self.from_right, self.z > d, self.z == self.zs - 1),
        ):

            @pl.when(sends & edge)
            def _():
                moves[0].start()

            @pl.when(sends & jnp.logical_not(edge))
            def _():
                moves[1].wait_recv()
                inbox[d] = plus(self.part[d], inbox[d]).astype(inbox.dtype)
                moves[1].start()

    def total(self, sink):
        for d in range(self.zs):

            @pl.when(self.z == d)
            def _():
                terms = [self.part[d]]
                if d > 0:
                    self.right[d][0].wait_recv()
                    terms.append(self.from_left[d])
                if d < self.zs - 1:
                    self.left[d][0].wait_recv()
                    terms.append(self.from_right[d])
                sink[...] = plus(*terms).astype(sink.dtype)

    def finish(self):
        for d in ends_first(self.zs):
            pl.when(self.z < d)(self.right[d][0].wait_send)
            pl.when(self.z > d)(self.left[d][0].wait_send)


class Scatter:
    def __init__(self, lanes, part, held, out, first):
        zs, z, y, x = lanes.zs, lanes.z, lanes.y, lanes.x
        got, near, from_left, from_right, ready = held
        second = "y" if first == "x" else "x"
        self.lanes, self.part, self.got, self.near, self.ready, self.out = (
            lanes, part, got, near, ready, out,
        )
        f, s = (x, y) if first == "x" else (y, x)
        self.f, self.s = f, s

        def block(zz, a, b):
            return part.at[zz, b, a] if first == "x" else part.at[zz, a, b]

        self.block = block
        self.one, self.two = {}, {}
        for zz in ends_first(zs):
            for j, b in enumerate((1 - s, s)):
                self.one[zz, j] = Move(
                    lanes.copy(block(zz, 1 - f, b), got.at[zz, j], {first: 1 - f}), None, None
                )
        for zz in ends_first(zs):
            self.two[zz] = Move(
                lanes.copy(got.at[zz, 0], near.at[zz], {second: 1 - s}), None, None
            )
        self.line = Line(lanes, ready, from_left, from_right)

    def begin(self):
        for zz in ends_first(self.lanes.zs):
            for j in range(2):
                self.one[zz, j].start()

    def second(self, zz):
        self.one[zz, 0].arrived()
        mine, got = self.block(zz, self.f, 1 - self.s), self.got
        got[zz, 0] = plus(mine[...], got[zz, 0]).astype(got.dtype)
        self.two[zz].start()

    def third(self, zz):
        self.one[zz, 1].arrived()
        self.two[zz].arrived()
        mine = self.block(zz, self.f, self.s)
        self.ready[zz] = plus(mine[...], self.got[zz, 1], self.near[zz]).astype(self.ready.dtype)
        self.line.pass_on(zz)

    def finish(self):
        self.line.total(self.out)
        self.line.finish()
        for move in list(self.one.values()) + list(self.two.values()):
            move.sent()


class ScatterZ:
    def __init__(self, lanes, part, held, out):
        y, x = lanes.y, lanes.x
        from_left, from_right, held_z, near, last = held
        self.lanes, self.sum_z, self.near, self.last, self.out = lanes, held_z, near, last, out
        self.line = Line(lanes, part, from_left, from_right)
        self.two = Move(lanes.copy(held_z.at[1 - y], near, {"y": 1 - y}), None, None)
        self.three = Move(lanes.copy(near.at[1 - x], last, {"x": 1 - x}), None, None)

    def pass_on(self, d):
        self.line.pass_on(d)

    def total(self):
        self.line.total(self.sum_z)
        self.two.start()

    def after(self):
        self.two.arrived()
        self.near[...] = plus(self.sum_z[self.lanes.y], self.near[...]).astype(self.near.dtype)
        self.three.start()

    def finish(self):
        self.three.arrived()
        self.out[...] = plus(self.near[self.lanes.x], self.last[...]).astype(self.out.dtype)
        self.line.finish()
        self.two.sent()
        self.three.sent()


class Crest:
    def __init__(self, lanes, own, held, out):
        zs, z, y, x = lanes.zs, lanes.z, lanes.y, lanes.x
        near_x, near_y, mine_x, mine_y, right, left, inbox_r, inbox_l = (
            held.at[i] for i in range(8)
        )
        self.zs, self.z, self.own, self.out = zs, z, own, out
        self.near_x, self.near_y, self.mine_x, self.mine_y = near_x, near_y, mine_x, mine_y
        self.ways = (
            (right, inbox_r, z > 0, z < zs - 1),
            (left, inbox_l, z < zs - 1, z > 0),
        )
        self.one = Move(lanes.copy(own, near_x, {"x": 1 - x}), None, None)
        self.two = Move(lanes.copy(mine_x, near_y, {"y": 1 - y}), None, None)
        self.moves = [
            Move(lanes.copy(right, inbox_r, {"z": jnp.minimum(z + 1, zs - 1)}), z < zs - 1, z > 0),
            Move(lanes.copy(left, inbox_l, {"z": jnp.maximum(z - 1, 0)}), z > 0, z < zs - 1),
        ]

    def second(self):
        self.one.arrived()
        self.mine_x[...] = jnp.maximum(self.own[...], self.near_x[...])
        self.two.start()

    def finish(self):
        self.two.arrived()
        self.mine_y[...] = jnp.maximum(self.mine_x[...], self.near_y[...])
        self.out[...] = self.mine_y[...]
        for move, (held, inbox, has_before, has_after) in zip(self.moves, self.ways):

            @pl.when(has_before)
            def _():
                move.copy_.wait_recv()
                self.out[...] = jnp.maximum(self.out[...], inbox[...])
                held[...] = jnp.maximum(self.mine_y[...], inbox[...])

            @pl.when(jnp.logical_not(has_before))
            def _():
                held[...] = self.mine_y[...]

            move.start()
        for move in [self.one, self.two] + self.moves:
            move.sent()


def scatter_kernel(zs, orders, *refs):
    count = len(orders)
    parts, crest_in, refs = refs[:count], refs[count], refs[count + 1 :]
    outs, crest_out, rest = refs[:count], refs[count], list(refs[count + 1 :])
    send_sems, recv_sems = rest[:2]
    rest = rest[2:]
    lanes = Lanes(send_sems, recv_sems, None, zs)
    greet(zs)
    full, zfirst = [], []
    for i, order in enumerate(orders):
        held, rest = rest[:5], rest[5:]
        if order == "z":
            zfirst.append(ScatterZ(lanes, parts[i], held, outs[i]))
        else:
            full.append(Scatter(lanes, parts[i], held, outs[i], order))
    crest = Crest(lanes, crest_in, rest[0], crest_out)
    crest.one.start()
    for item in full:
        item.begin()
    crest.second()
    for d in ends_first(zs):
        for item in zfirst:
            item.pass_on(d)
        for item in full:
            item.second(d)
    for item in zfirst:
        item.total()
    for d in ends_first(zs):
        for item in full:
            item.third(d)
    crest.finish()
    for item in zfirst:
        item.after()
    for item in full:
        item.finish()
    for item in zfirst:
        item.finish()


def scatter_all(parts, orders, crest, zs):
    scratch, moves = [], 4
    for part, order in zip(parts, orders):
        block = part.shape[3:]
        if order == "z":
            shapes = [(zs, 2, 2) + block] * 2 + [(2, 2) + block, (2,) + block, block]
            moves += 2 * zs + 2
        else:
            shapes = [(zs, 2) + block] + [(zs,) + block] * 4
            moves += 5 * zs
        scratch += [pltpu.VMEM(shape, part.dtype) for shape in shapes]
    vmem = pl.BlockSpec(memory_space=pltpu.VMEM)
    return pl.pallas_call(
        functools.partial(scatter_kernel, zs, orders),
        out_shape=[jax.ShapeDtypeStruct(part.shape[3:], F32) for part in parts]
        + [jax.ShapeDtypeStruct(crest.shape, F32)],
        in_specs=[vmem] * (len(parts) + 1),
        out_specs=[vmem] * (len(parts) + 1),
        scratch_shapes=[pltpu.SemaphoreType.DMA((moves,)), pltpu.SemaphoreType.DMA((moves,))]
        + scratch
        + [pltpu.VMEM((8,) + crest.shape, F32)],
        compiler_params=pltpu.CompilerParams(
            collective_id=2, has_side_effects=True, vmem_limit_bytes=56 * 2**20
        ),
    )(*parts, crest)


def nn(left, right):
    return lax.dot_general(left, right, (((1,), (0,)), ((), ())), preferred_element_type=F32)


def nt(left, right):
    return lax.dot_general(left, right, (((1,), (1,)), ((), ())), preferred_element_type=F32)


def tn(left, right):
    return lax.dot_general(left, right, (((0,), (0,)), ((), ())), preferred_element_type=F32)


def columns_by(value, axis_name, zs):
    rows = value.shape[0]
    at = lax.axis_index(axis_name)
    if axis_name == "y":
        split = value.reshape(rows, zs, 2, -1)
        dim = 2
    else:
        split = value.reshape(rows, 2 * zs, 2, -1)
        dim = 2
    return (
        pick(split, at, dim).reshape(rows, -1),
        pick(split, 1 - at, dim).reshape(rows, -1),
    )


def reduce_full(left_keep, left_send, right, zs):
    got = swap(tn(left_send, right).astype(BF), "x")
    held = (tn(left_keep, right) + got.astype(F32)).astype(BF)
    held = held.reshape(zs, 2, -1, right.shape[1])
    at = lax.axis_index("y")
    got = swap(pick(held, 1 - at, 1), "y")
    held = (pick(held, at, 1).astype(F32) + got.astype(F32)).astype(BF)
    return lax.psum_scatter(held, "z", scatter_dimension=0, tiled=False)


def reduce_pair(left_keep, left_send, right, zs):
    got = swap(tn(left_send, right).astype(BF), "y")
    held = (tn(left_keep, right) + got.astype(F32)).astype(BF)
    held = held.reshape(zs, -1, right.shape[1])
    held = lax.psum_scatter(held, "z", scatter_dimension=0, tiled=False)
    held = held.reshape(2, -1, right.shape[1])
    at = lax.axis_index("x")
    got = swap(pick(held, 1 - at, 0), "x")
    return pick(held, at, 0), got


def norm_forward(stream, gain_vec, bias_vec):
    average = jnp.mean(stream, axis=-1, keepdims=True)
    centred = stream - average
    inverse = lax.rsqrt(jnp.mean(centred * centred, axis=-1, keepdims=True) + EPSILON)
    unit_rows = centred * inverse
    return (unit_rows * gain_vec + bias_vec, unit_rows, inverse)


def unit_rows_of(stream):
    _, unit_rows, inverse = norm_forward(stream, 1.0, 0.0)
    return unit_rows, inverse


def norm_backward(incoming, unit_rows, inverse, gain_vec):
    gain_grad = jnp.sum(incoming * unit_rows, axis=0)
    bias_grad = jnp.sum(incoming, axis=0)
    scaled = incoming * gain_vec
    stream_grad = inverse * (
        scaled
        - jnp.mean(scaled, axis=-1, keepdims=True)
        - unit_rows * jnp.mean(scaled * unit_rows, axis=-1, keepdims=True)
    )
    return (stream_grad, gain_grad, bias_grad)


def turn_tables(positions):
    rates = 10000.0 ** (-jnp.arange(0, ROT_DIM, 2).astype(F32) / ROT_DIM)
    angles = positions[:, None] * rates[None, :]
    cosine, sine = jnp.cos(angles), jnp.sin(angles)
    rest = jnp.ones((positions.shape[0], HEAD_DIM - ROT_DIM), F32)
    zero, none = jnp.zeros_like(rest), jnp.zeros_like(sine)
    return (
        jnp.concatenate([cosine, cosine, rest] * 2, axis=1),
        jnp.concatenate([-sine, none, zero] * 2, axis=1),
        jnp.concatenate([none, sine, zero] * 2, axis=1),
    )


def turn(field, cosine, sine_a, sine_b, direction):
    half = ROT_DIM // 2
    width = field.shape[-1]
    ahead = pltpu.roll(field, width - half, 1)
    behind = pltpu.roll(field, half, 1)
    return field * cosine + direction * (ahead * sine_a + behind * sine_b)


def head_lanes(shape, which):
    lanes = lax.broadcasted_iota(jnp.int32, shape, 1)
    return (lanes >= which * HEAD_DIM) & (lanes < (which + 1) * HEAD_DIM)


def attend_tile(query, keys, values, bias):
    scores = nt(query, keys) + bias
    top = jnp.max(scores, axis=-1, keepdims=True)
    weights = jnp.exp(scores - top)
    total = jnp.sum(weights, axis=-1, keepdims=True)
    return nn(weights.astype(BF), values) / total, top


def attend_kernel(q_ref, k_ref, v_ref, bias_ref, mixed_ref, peak_ref):
    rows = q_ref.shape[0]
    tile = rows // 3 if rows % 3 == 0 and (rows // 3) % 16 == 0 else rows
    keys, values, bias = k_ref[...], v_ref[...], bias_ref[...]
    peaks = [None, None]
    for start in range(0, rows, tile):
        query = q_ref[start : start + tile, :] * BF(HEAD_DIM ** (-0.5))
        outs = []
        for which in range(2):
            one = jnp.where(head_lanes(query.shape, which), query, jnp.zeros_like(query))
            out, top = attend_tile(one, keys, values, bias)
            outs.append(out)
            top = jnp.max(top, axis=0, keepdims=True)
            peaks[which] = top if peaks[which] is None else jnp.maximum(peaks[which], top)
        mixed = jnp.where(head_lanes(outs[0].shape, 0), outs[0], outs[1])
        mixed_ref[start : start + tile, :] = mixed.astype(BF)
    spot = head_lanes((8, 2 * HEAD_DIM), 0)
    peak_ref[0] = jnp.where(
        spot, jnp.broadcast_to(peaks[0], spot.shape), jnp.broadcast_to(peaks[1], spot.shape)
    )


def attend(query, keys, values, bias, offsets):
    rows, tokens = query.shape[0], keys.shape[0]
    pairs = bias.shape[0]
    wide = 2 * HEAD_DIM
    mixed, peak = pl.pallas_call(
        attend_kernel,
        grid=(pairs,),
        out_shape=[
            jax.ShapeDtypeStruct((rows, pairs * wide), BF),
            jax.ShapeDtypeStruct((pairs, 8, wide), F32),
        ],
        in_specs=[
            pl.BlockSpec((rows, wide), lambda j: (0, offsets[0] + j)),
            pl.BlockSpec((tokens, wide), lambda j: (0, offsets[1] + j)),
            pl.BlockSpec((tokens, wide), lambda j: (0, offsets[2] + j)),
            pl.BlockSpec((1, tokens), lambda j: (0, 0)),
        ],
        out_specs=[
            pl.BlockSpec((rows, wide), lambda j: (0, j)),
            pl.BlockSpec((1, 8, wide), lambda j: (j, 0, 0)),
        ],
        compiler_params=pltpu.CompilerParams(vmem_limit_bytes=48 * 2**20),
        cost_estimate=pl.CostEstimate(
            flops=8 * rows * tokens * pairs * wide,
            bytes_accessed=4 * (rows + tokens) * pairs * wide,
            transcendentals=2 * pairs * rows * tokens,
        ),
    )(query, keys, values, bias[:1])
    return mixed, peak[:, 0, ::HEAD_DIM].reshape(-1)


def attend_back_kernel(turned, q_ref, k_ref, v_ref, g_ref, bias_ref, *refs):
    if turned:
        cos_ref, sa_ref, sb_ref = refs[:3]
        refs = refs[3:]
    dq_ref, dk_ref, dv_ref, dk_acc, dv_acc = refs
    rows = q_ref.shape[0]
    tile = rows // 3 if rows % 3 == 0 and (rows // 3) % 128 == 0 else rows
    scale = BF(HEAD_DIM ** (-0.5))
    keys, values, bias = k_ref[...], v_ref[...], bias_ref[...]
    for start in range(0, rows, tile):
        part = slice(start, start + tile)
        query, grad = q_ref[part, :] * scale, g_ref[part, :]
        dq = None
        for which in range(2):
            mine = head_lanes(query.shape, which)
            one = jnp.where(mine, query, jnp.zeros_like(query))
            out = jnp.where(mine, grad, jnp.zeros_like(grad))
            scores = nt(keys, one) + bias
            weights = jnp.exp(scores - jnp.max(scores, axis=0, keepdims=True))
            weights = weights * (1.0 / jnp.sum(weights, axis=0, keepdims=True))
            slope = nt(values, out)
            slope = weights * (slope - jnp.sum(weights * slope, axis=0, keepdims=True))
            slope = slope.astype(BF)
            dv = nn(weights.astype(BF), out)
            dk = nn(slope, one)
            other = jnp.where(head_lanes(keys.shape, which), keys, jnp.zeros_like(keys))
            piece = tn(slope, other * scale)
            dq = piece if dq is None else dq + piece
            if start == 0 and which == 0:
                dv_acc[...] = dv
                dk_acc[...] = dk
            else:
                dv_acc[...] += dv
                dk_acc[...] += dk
        if turned:
            dq = turn(dq, cos_ref[part, :], sa_ref[part, :], sb_ref[part, :], -1.0)
        dq_ref[part, :] = dq.astype(BF)
    dk = dk_acc[...]
    if turned:
        dk = turn(dk, cos_ref[...], sa_ref[...], sb_ref[...], -1.0)
    dk_ref[...] = dk.astype(BF)
    dv_ref[...] = dv_acc[...].astype(BF)


def attend_back(query, keys, values, grad, bias_column, offsets, turns):
    rows, tokens = query.shape[0], keys.shape[0]
    wide = 2 * HEAD_DIM
    pairs = grad.shape[1] // wide
    ins = [query, keys, values, grad, bias_column]
    specs = [
        pl.BlockSpec((rows, wide), lambda j: (0, offsets[0] + j)),
        pl.BlockSpec((tokens, wide), lambda j: (0, offsets[1] + j)),
        pl.BlockSpec((tokens, wide), lambda j: (0, offsets[2] + j)),
        pl.BlockSpec((rows, wide), lambda j: (0, j)),
        pl.BlockSpec((tokens, 1), lambda j: (0, 0)),
    ]
    if turns is not None:
        ins += list(turns)
        specs += [pl.BlockSpec((rows, wide), lambda j: (0, 0))] * 3
    return pl.pallas_call(
        functools.partial(attend_back_kernel, turns is not None),
        grid=(pairs,),
        out_shape=[
            jax.ShapeDtypeStruct((rows, pairs * wide), BF),
            jax.ShapeDtypeStruct((tokens, pairs * wide), BF),
            jax.ShapeDtypeStruct((tokens, pairs * wide), BF),
        ],
        in_specs=specs,
        out_specs=[
            pl.BlockSpec((rows, wide), lambda j: (0, j)),
            pl.BlockSpec((tokens, wide), lambda j: (0, j)),
            pl.BlockSpec((tokens, wide), lambda j: (0, j)),
        ],
        scratch_shapes=[pltpu.VMEM((tokens, wide), F32), pltpu.VMEM((tokens, wide), F32)],
        compiler_params=pltpu.CompilerParams(vmem_limit_bytes=48 * 2**20),
        cost_estimate=pl.CostEstimate(
            flops=20 * rows * tokens * pairs * wide,
            bytes_accessed=8 * (rows + tokens) * pairs * wide,
            transcendentals=2 * pairs * rows * tokens,
        ),
    )(*ins)


def project_kernel(turned, x_ref, w_ref, cos_ref, sa_ref, sb_ref, out_ref):
    wide = 2 * HEAD_DIM
    made = nn(x_ref[...], w_ref[...])

    @pl.when(pl.program_id(0) < turned)
    def _():
        for start in range(0, made.shape[1], wide):
            piece = turn(made[:, start : start + wide], cos_ref[...], sa_ref[...], sb_ref[...], 1.0)
            out_ref[:, start : start + wide] = piece.astype(BF)

    @pl.when(pl.program_id(0) >= turned)
    def _():
        out_ref[...] = made.astype(BF)


def project(rows, weight, turns, turned_columns):
    count, depth = rows.shape
    columns = weight.shape[1]
    block = 2 * HEAD_DIM * (2 if turned_columns % (4 * HEAD_DIM) == 0 else 1)
    table = pl.BlockSpec((count, 2 * HEAD_DIM), lambda j: (0, 0))
    return pl.pallas_call(
        functools.partial(project_kernel, turned_columns // block),
        grid=(columns // block,),
        out_shape=jax.ShapeDtypeStruct((count, columns), BF),
        in_specs=[
            pl.BlockSpec((count, depth), lambda j: (0, 0)),
            pl.BlockSpec((depth, block), lambda j: (0, j)),
            table,
            table,
            table,
        ],
        out_specs=pl.BlockSpec((count, block), lambda j: (0, j)),
        compiler_params=pltpu.CompilerParams(vmem_limit_bytes=48 * 2**20),
        cost_estimate=pl.CostEstimate(
            flops=2 * count * depth * columns,
            bytes_accessed=2 * (count * depth + depth * columns + count * columns),
            transcendentals=0,
        ),
    )(rows, weight, *turns)


def normalise(stream, gain_vec, bias_vec):
    average = jnp.mean(stream, axis=-1, keepdims=True)
    centred = stream - average
    inverse = lax.rsqrt(jnp.mean(centred * centred, axis=-1, keepdims=True) + EPSILON)
    return centred * inverse * gain_vec + bias_vec


def attend_pair(query, keys, values, bias, tile):
    outs_all, peaks = [], [None, None]
    for start in range(0, tile[0], tile[1]):
        rows = query(start, tile[1]) * BF(HEAD_DIM ** (-0.5))
        outs = []
        for which in range(2):
            one = jnp.where(head_lanes(rows.shape, which), rows, jnp.zeros_like(rows))
            out, top = attend_tile(one, keys, values, bias)
            outs.append(out)
            top = jnp.max(top, axis=0, keepdims=True)
            peaks[which] = top if peaks[which] is None else jnp.maximum(peaks[which], top)
        outs_all.append((start, jnp.where(head_lanes(outs[0].shape, 0), outs[0], outs[1])))
    return outs_all, peaks


def forward_kernel(zs, *refs):
    refs = list(refs)

    def take(count):
        taken_refs = refs[:count]
        del refs[:count]
        return taken_refs

    shards = take(9)
    quarters_in = take(3)
    inputs_hbm, cot_hbm, cos_ref, sa_ref, sb_ref, self_bias, cross_bias, memory = take(8)
    wholes = take(6)
    quarter_outs = take(3)
    outs = take(10)
    cot_out = take(1)[0]
    peak_out = take(1)[0]
    send_sems, recv_sems, local_sems = take(3)
    w_vec, w_in, w_so, w_cq, w_kv, w_co = take(6)
    (
        x_all, normed_self, taken, mixed_self, stream_cross, normed_cross,
        query_cross, taken_cross, mixed_cross, stream_feed, normed_feed,
        part_send, part_got, part_send2, part_got2, vectors,
    ) = take(16)
    lanes = Lanes(send_sems, recv_sems, local_sems, zs)
    z, y, x = lanes.z, lanes.y, lanes.x
    t = lax.axis_index("tensor")
    rows, width = inputs_hbm.shape
    wide = 2 * HEAD_DIM

    def local(source, target):
        return pltpu.make_async_copy(source, target, lanes.local())

    pieces, at = [], 0
    for count, whole in zip((1, 3, 1, 1, 2, 1), wholes):
        columns = whole.shape[-1] // count
        for i in range(count):
            target = whole.at[z, y, x, :, pl.ds(i * columns, columns)]
            pieces.append(local(shards[at], target))
            at += 1
    own_inputs = local(inputs_hbm, x_all.at[0])
    own_cot = local(cot_hbm, cot_out.at[0])
    for piece in pieces + [own_inputs, own_cot]:
        piece.start()
    greet(zs, True)

    def mate(source, target):
        return Move(lanes.copy(source, target, {"tensor": 1 - t}), None, None)

    def across(source, target):
        return Move(lanes.copy(source, target, {"x": 1 - x}), None, None)

    mate_inputs = mate(inputs_hbm, x_all.at[1])
    cot_moves = [
        mate(cot_hbm, cot_out.at[1]),
        across(cot_hbm, cot_out.at[2]),
        mate(cot_out.at[2], cot_out.at[3]),
    ]
    feed_moves = [
        mate(normed_feed.at[0], normed_feed.at[1]),
        across(normed_feed.at[0], normed_feed.at[2]),
        mate(normed_feed.at[2], normed_feed.at[3]),
    ]
    mate_self = mate(part_send, part_got)
    mate_normed = mate(normed_cross.at[0], normed_cross.at[1])
    mate_cross = mate(part_send2, part_got2)
    gathers = [Gather(lanes, whole) for whole in wholes]
    quarters = [
        PairGather(lanes, quarters_in[i], quarter_outs[i], i == 0) for i in range(3)
    ]
    loads = [
        local(whole, held)
        for whole, held in zip(wholes, (w_vec, w_in, w_so, w_cq, w_kv, w_co))
    ]
    results = (
        normed_self, taken, mixed_self, stream_cross, normed_cross,
        query_cross, taken_cross, mixed_cross, stream_feed, normed_feed,
    )
    saves = [local(held, out) for held, out in zip(results, outs)]

    mate_inputs.start()
    cot_moves[0].start()
    for piece in pieces:
        piece.wait()
    early, late = gathers[:2], gathers[2:]
    for gather in early:
        gather.begin()
    for quarter in quarters:
        quarter.begin()

    news = []

    def every(items, name, *args):
        for item in items:
            news.append(functools.partial(getattr(item, name), *args))

    every(early, "far_first")
    every(early, "step", 0)
    every(quarters, "swapped")
    every(late, "begin")
    every(early, "far_step", 0)
    for k in range(1, zs - 1):
        every(early, "step", k)
        every(early, "far_step", k)
    news.append(cot_moves[1].start)
    every(early, "landed")
    until_in = len(news)
    every(late, "far_first")
    for k in range(zs - 1):
        every(late, "step", k)
        every(quarters[1:], "step", k)
        if k == 0:
            every(quarters[:1], "own_y_arrived")
        every(late, "far_step", k)
        every(quarters[:1], "step", k)
        if k == 0:
            news.append(cot_moves[1].arrived)
            news.append(cot_moves[2].start)
    until_late = {}
    for i, gather in enumerate(late):
        every([gather], "landed")
        news.append(loads[2 + i].start)
        until_late[i] = len(news)
    done = [0]

    def hear(upto):
        while done[0] < min(upto, len(news)):
            news[done[0]]()
            done[0] += 1

    def hear_some(count):
        hear(done[0] + count)

    hear(until_in)
    loads[0].start()
    loads[1].start()
    own_inputs.wait()
    mate_inputs.arrived()
    loads[0].wait()
    vectors[...] = jnp.transpose(w_vec[...].reshape(width, w_vec.shape[-1]))

    def vec(i):
        return vectors[i : i + 1, :]

    tile = 128 if rows % 128 == 0 else rows
    for side in range(2):
        for start in range(0, rows, tile):
            part = slice(start, start + tile)
            made = normalise(x_all[side, part, :].astype(F32), vec(0), vec(1))
            normed_self[side * rows + start : side * rows + start + tile, :] = made.astype(BF)
    saves[0].start()
    hear_some(2)
    loads[1].wait()
    columns = w_in.shape[-1]
    block = 2 * wide
    for start in range(0, columns, block):
        made = nn(normed_self[...], w_in[..., start : start + block].reshape(width, block))
        for at in range(0, block, wide):
            piece = made[:, at : at + wide]
            if start + at < columns * 2 // 3:
                piece = turn(piece, cos_ref[...], sa_ref[...], sb_ref[...], 1.0)
            taken[:, start + at : start + at + wide] = piece.astype(BF)
        hear_some(2)
    saves[1].start()
    inner = columns // 3
    pairs = inner // wide
    tops = []

    def attend_all(query_ref, keys_at, values_at, kv_ref, bias_ref, mixed_ref):
        total = 2 * rows
        step = total // 3 if total % 3 == 0 and (total // 3) % 16 == 0 else total
        for j in range(pairs):
            lanes_at = j * wide
            bits, peaks = attend_pair(
                lambda start, count: query_ref[start : start + count, lanes_at : lanes_at + wide],
                kv_ref[:, keys_at + lanes_at : keys_at + lanes_at + wide],
                kv_ref[:, values_at + lanes_at : values_at + lanes_at + wide],
                bias_ref[...],
                (total, step),
            )
            for start, bit in bits:
                mixed_ref[start : start + step, lanes_at : lanes_at + wide] = bit.astype(BF)
            tops.append(peaks)
            hear_some(2)

    def out_rows(mixed_ref, first, weight, zz):
        columns_here = weight[zz].reshape(-1, inner)
        return nt(mixed_ref[first : first + rows, :], columns_here)

    def out_project(mixed_ref, weight, move, send, got, base, target):
        chunk = width // zs
        for zz in range(zs):
            send[:, zz * chunk : (zz + 1) * chunk] = out_rows(mixed_ref, rows, weight, zz)
        move.start()
        for zz in range(zs):
            part = slice(zz * chunk, (zz + 1) * chunk)
            target[:, part] = out_rows(mixed_ref, 0, weight, zz) + base(part)
            hear_some(1)
        move.arrived()
        for start in range(0, rows, tile):
            part = slice(start, start + tile)
            target[part, :] = target[part, :] + got[part, :]

    attend_all(taken, inner, 2 * inner, taken, self_bias, mixed_self)
    saves[2].start()
    hear(until_late[0])
    loads[2].wait()
    out_project(
        mixed_self, w_so, mate_self, part_send, part_got,
        lambda part: x_all[0, :, part].astype(F32), stream_cross,
    )
    saves[3].start()
    for start in range(0, rows, tile):
        part = slice(start, start + tile)
        normed_cross[0, part, :] = normalise(stream_cross[part, :], vec(2), vec(3)).astype(BF)
    mate_normed.start()
    hear(until_late[2])
    loads[4].wait()
    depth = memory.shape[1]
    for start in range(0, 2 * inner, block):
        weight = w_kv[..., start : start + block].reshape(depth, block)
        taken_cross[:, start : start + block] = nn(memory[...], weight).astype(BF)
    saves[6].start()
    loads[3].wait()
    for side in range(2):
        if side == 1:
            mate_normed.arrived()
            saves[4].start()
        for start in range(0, inner, block):
            weight = w_cq[..., start : start + block].reshape(width, block)
            made = nn(normed_cross[side], weight).astype(BF)
            query_cross[side * rows : (side + 1) * rows, start : start + block] = made
        hear_some(1)
    saves[5].start()
    attend_all(query_cross, 0, inner, taken_cross, cross_bias, mixed_cross)
    saves[7].start()
    hear(until_late[3])
    loads[5].wait()
    out_project(
        mixed_cross, w_co, mate_cross, part_send2, part_got2,
        lambda part: stream_cross[:, part], stream_feed,
    )
    saves[8].start()
    for start in range(0, rows, tile):
        part = slice(start, start + tile)
        normed_feed[0, part, :] = normalise(stream_feed[part, :], vec(4), vec(5)).astype(BF)
    feed_moves[1].start()
    feed_moves[0].start()
    lane = lax.broadcasted_iota(jnp.int32, peak_out.shape, 1)
    crest = jnp.full(peak_out.shape, NEGATIVE, F32)
    for i, peaks in enumerate(tops):
        for which in range(2):
            head = (i % pairs) * 2 + which
            crest = jnp.where(lane == head, jnp.maximum(crest, peaks[which]), crest)
    peak_out[...] = crest
    hear(len(news))
    feed_moves[1].arrived()
    feed_moves[2].start()
    for quarter in quarters:
        quarter.landed()
    feed_moves[0].arrived()
    feed_moves[2].arrived()
    saves[9].start()
    cot_moves[0].arrived()
    cot_moves[2].arrived()
    own_cot.wait()
    for item in gathers + quarters:
        item.sent()
    for move in [mate_inputs, mate_self, mate_normed, mate_cross] + cot_moves + feed_moves:
        move.sent()
    for save in saves:
        save.wait()


def forward(shards, quarters, inputs, cotangent, turns, self_bias, cross_bias, memory, zs):
    rows, width = inputs.shape
    seq_len, inner = 2 * rows, shards[1].shape[1]
    tokens = memory.shape[0]
    spread = []
    groups = ([shards[0]], shards[1:4], [shards[4]], [shards[5]], shards[6:8], [shards[8]])
    for group in groups:
        columns = sum(shard.shape[1] for shard in group)
        spread.append(jax.ShapeDtypeStruct((zs, 2, 2, group[0].shape[0], columns), group[0].dtype))
    for shard in quarters:
        spread.append(
            jax.ShapeDtypeStruct((zs, 2, 2, shard.shape[0], shard.shape[1] // 2), shard.dtype)
        )
    results = [
        jax.ShapeDtypeStruct((seq_len, width), BF),
        jax.ShapeDtypeStruct((seq_len, 3 * inner), BF),
        jax.ShapeDtypeStruct((seq_len, inner), BF),
        jax.ShapeDtypeStruct((rows, width), F32),
        jax.ShapeDtypeStruct((2, rows, width), BF),
        jax.ShapeDtypeStruct((seq_len, inner), BF),
        jax.ShapeDtypeStruct((tokens, 2 * inner), BF),
        jax.ShapeDtypeStruct((seq_len, inner), BF),
        jax.ShapeDtypeStruct((rows, width), F32),
        jax.ShapeDtypeStruct((4, rows, width), BF),
    ]
    cot_out = jax.ShapeDtypeStruct((4, rows, width), BF)
    peak = jax.ShapeDtypeStruct((8, 2 * HEAD_DIM), F32)
    moves = 6 * (3 + 8 * (zs - 1)) + 3 * (2 + 4 * (zs - 1)) + 10
    hbm = pl.BlockSpec(memory_space=pltpu.HBM)
    vmem = pl.BlockSpec(memory_space=pltpu.VMEM)
    held = [pltpu.VMEM(shape.shape, shape.dtype) for shape in spread[:6]]
    held += [pltpu.VMEM((2, rows, width), BF)]
    held += [pltpu.VMEM(shape.shape, shape.dtype) for shape in results]
    held += [pltpu.VMEM((rows, width), F32)] * 4
    held += [pltpu.VMEM((shards[0].shape[1], width), F32)]
    flops = 2 * seq_len * inner * (7 * width + 4 * seq_len) // 1
    made = pl.pallas_call(
        functools.partial(forward_kernel, zs),
        out_shape=spread + results + [cot_out, peak],
        in_specs=[hbm] * 14 + [vmem] * 6,
        out_specs=[hbm] * 20 + [vmem],
        scratch_shapes=[
            pltpu.SemaphoreType.DMA((moves,)),
            pltpu.SemaphoreType.DMA((moves,)),
            pltpu.SemaphoreType.DMA((9 + 2 + 3 + 6 + 10,)),
        ]
        + held,
        compiler_params=pltpu.CompilerParams(
            collective_id=1, has_side_effects=True, vmem_limit_bytes=62 * 2**20
        ),
        cost_estimate=pl.CostEstimate(flops=flops, bytes_accessed=10**8, transcendentals=10**7),
    )(*shards, *quarters, inputs, cotangent, *turns, self_bias, cross_bias, memory)
    return made[:9], made[9:19], made[19], made[20]


def pair_rows(own):
    return jnp.concatenate([own, swap(own, "tensor")], axis=0)


def group_rows(own):
    both = jnp.stack([own, swap(own, "x")])
    other = swap(both, "tensor")
    return jnp.concatenate([both[0], other[0], both[1], other[1]], axis=0)


def spread_pair(left, right_t):
    rows = left.shape[0] // 2
    got = swap(nt(left[rows:], right_t), "tensor")
    return nt(left[:rows], right_t) + got


def spread_group(product):
    quarter = product.rows // 4
    far_send = product(3 * quarter, quarter)
    far = product(2 * quarter, quarter) + swap(far_send, "tensor")
    got_far = swap(far.astype(BF), "x")
    near = product(0, quarter) + swap(product(quarter, quarter), "tensor")
    return near + got_far.astype(F32)


class Product:
    def __init__(self, terms, transposed):
        self.terms = terms
        self.transposed = transposed
        self.rows = terms[0][0].shape[0]

    def __call__(self, first, count):
        total = None
        for left, right in self.terms:
            part = (nt if self.transposed else nn)(left[first : first + count], right)
            total = part if total is None else total + part
        return total


def per_device(
    inputs,
    cotangent,
    context,
    context_live,
    lengths,
    threshold,
    self_gain,
    self_bias,
    self_query,
    self_key,
    self_value,
    self_output,
    cross_gain,
    cross_bias,
    cross_query,
    cross_key,
    cross_value,
    cross_output,
    feed_gain,
    feed_bias,
    gate_weight,
    up_weight,
    down_weight,
):
    zs = lax.axis_size("z")
    x_at = lax.axis_index("x")
    t_at = lax.axis_index("tensor")
    width = inputs.shape[1]
    rows = inputs.shape[0]
    seq_len = 2 * rows
    inner = self_query.shape[1]
    heads_here = inner // HEAD_DIM
    ff = gate_weight.shape[1] // 2
    shard_rows = self_query.shape[0]

    quarters = [gate_weight, up_weight, down_weight.T]
    vector_list = [self_gain, self_bias, cross_gain, cross_bias, feed_gain, feed_bias]
    stream = inputs.astype(F32)
    local = jnp.arange(rows)
    places = jnp.concatenate([t_at * rows + local, (1 - t_at) * rows + local])
    turns = turn_tables(places.astype(F32))
    self_bias_row = jnp.where(places < lengths[0], 0.0, NEGATIVE).astype(F32)
    tokens = context.shape[1]
    token_rows = -(-tokens // 128) * 128
    cross_bias_row = jnp.pad(
        jnp.where(context_live[0] > 0, 0.0, NEGATIVE).astype(F32),
        (0, token_rows - tokens),
        constant_values=NEGATIVE,
    )
    memory = jnp.pad(context[0], ((0, token_rows - tokens), (0, 0)))
    pairs = inner // (2 * HEAD_DIM)

    if shard_rows % 32 == 0:
        vectors = jnp.pad(jnp.stack(vector_list, axis=1).astype(F32), ((0, 0), (0, 122)))
        spread, made, cot_group, crest = forward(
            [
                vectors,
                self_query,
                self_key,
                self_value,
                self_output.T,
                cross_query,
                cross_key,
                cross_value,
                cross_output.T,
            ],
            quarters,
            inputs,
            cotangent,
            turns,
            self_bias_row[None],
            cross_bias_row[None],
            memory,
            zs,
        )
        norms, in_weight, self_out_t, cross_in, memory_weight, cross_out_t = spread[:6]
        norms = norms.reshape(width, -1).T
        (
            normed_self,
            taken,
            mixed_self,
            stream_cross,
            normed_cross,
            query_cross,
            taken_cross,
            mixed_cross,
            stream_feed,
            normed_feed,
        ) = made
        gate_full, up_full, down_t = spread[6:]
        normed_cross = normed_cross.reshape(seq_len, width)
        normed_feed, cot_group = (v.reshape(-1, width) for v in (normed_feed, cot_group))
    else:
        vectors = jnp.stack(vector_list).astype(F32)
        vectors = jnp.pad(vectors, ((0, 2), (0, 128 - shard_rows)))
        (norms, in_weight, self_out_t, cross_in, memory_weight, cross_out_t, gate_full, up_full, down_t) = (
            gather_all(
                [
                    [vectors],
                    [self_query, self_key, self_value],
                    [self_output.T],
                    [cross_query],
                    [cross_key, cross_value],
                    [cross_output.T],
                ],
                quarters,
                zs,
            )
        )
        norms = norms.reshape(-1, 8, 128)[:, :6, :shard_rows].transpose(1, 0, 2).reshape(6, width)
        in_weight, memory_weight = in_weight.reshape(width, -1), memory_weight.reshape(-1, 2 * inner)
        self_out_t, cross_in, cross_out_t, gate_full, up_full, down_t = (
            w.reshape(width, -1)
            for w in (self_out_t, cross_in, cross_out_t, gate_full, up_full, down_t)
        )
        cot_group = group_rows(cotangent)
        all_inputs = pair_rows(inputs)
        normed, _, _ = norm_forward(all_inputs.astype(F32), norms[0], norms[1])
        normed_self = normed.astype(BF)
        taken = project(normed_self, in_weight, turns, 2 * inner)
        self_bias_rows = jnp.broadcast_to(self_bias_row, (pairs, seq_len))
        mixed_self, peak_self = attend(taken, taken, taken, self_bias_rows, (0, pairs, 2 * pairs))
        stream_cross = stream + spread_pair(mixed_self, self_out_t)
        normed, _, _ = norm_forward(stream_cross, norms[2], norms[3])
        normed_cross = pair_rows(normed.astype(BF))
        query_cross = nn(normed_cross, cross_in).astype(BF)
        taken_cross = nn(memory, memory_weight).astype(BF)
        cross_bias_rows = jnp.broadcast_to(cross_bias_row, (pairs, token_rows))
        mixed_cross, peak_cross = attend(
            query_cross, taken_cross, taken_cross, cross_bias_rows, (0, 0, pairs)
        )
        stream_feed = stream_cross + spread_pair(mixed_cross, cross_out_t)
        normed, _, _ = norm_forward(stream_feed, norms[4], norms[5])
        normed_feed = group_rows(normed.astype(BF))
        crest = jnp.pad(
            jnp.maximum(peak_self, peak_cross)[None], ((0, 7), (0, 128 - heads_here))
        )
    in_weight, self_out_t, cross_in, cross_out_t, gate_full, up_full, down_t = (
        w.reshape(width, -1)
        for w in (in_weight, self_out_t, cross_in, cross_out_t, gate_full, up_full, down_t)
    )
    unit_cross, inverse_cross = unit_rows_of(stream_cross)
    unit_feed, inverse_feed = unit_rows_of(stream_feed)
    gate_pre = nn(normed_feed, gate_full)
    upward = nn(normed_feed, up_full)
    sigmoid_gate = jax.nn.sigmoid(gate_pre)
    hidden = (gate_pre * sigmoid_gate * upward).astype(BF)
    result = (stream_feed + spread_group(Product([(hidden, down_t)], True))).astype(BF)

    cot_keep, cot_send = columns_by(cot_group, "y", zs)
    down_keep, down_got = reduce_pair(cot_keep, cot_send, hidden, zs)
    grad_hidden = nn(cot_group, down_t)
    grad_gate = grad_hidden * upward * sigmoid_gate * (1.0 + gate_pre * (1.0 - sigmoid_gate))
    grad_upward = grad_hidden * gate_pre * sigmoid_gate
    grad_gate = grad_gate.astype(BF)
    grad_upward = grad_upward.astype(BF)
    grad_gates = jnp.concatenate([grad_gate, grad_upward], axis=1)
    grad_normed = spread_group(Product([(grad_gate, gate_full), (grad_upward, up_full)], True))
    feed_keep, feed_send = columns_by(normed_feed, "y", zs)
    gates_keep, gates_got = reduce_pair(feed_keep, feed_send, grad_gates, zs)
    stream_part, grad_feed_gain, grad_feed_bias = norm_backward(
        grad_normed, unit_feed, inverse_feed, norms[4]
    )
    grad_stream = cotangent.astype(F32) + stream_part
    grad_full = pair_rows(grad_stream.astype(BF))
    keep, send = columns_by(grad_full, "x", zs)
    sum_cross_output = reduce_full(keep, send, mixed_cross, zs).astype(F32)
    grad_mixed = nn(grad_full, cross_out_t).astype(BF)
    grad_query, grad_keys, grad_values = attend_back(
        query_cross, taken_cross, taken_cross, grad_mixed, cross_bias_row[:, None], (0, 0, pairs), None
    )
    grad_normed = spread_pair(grad_query, cross_in)
    keep, send = columns_by(normed_cross, "x", zs)
    sum_cross_query = reduce_full(keep, send, grad_query, zs).astype(F32)
    part_memory = tn(memory, jnp.concatenate([grad_keys, grad_values], axis=1))
    stream_part, grad_cross_gain, grad_cross_bias = norm_backward(
        grad_normed, unit_cross, inverse_cross, norms[2]
    )
    grad_stream = grad_stream + stream_part
    grad_full = pair_rows(grad_stream.astype(BF))
    part_self_output = tn(grad_full, mixed_self)
    grad_mixed = nn(grad_full, self_out_t).astype(BF)
    grad_parts = attend_back(
        taken, taken, taken, grad_mixed, self_bias_row[:, None], (0, pairs, 2 * pairs), turns
    )
    grad_in = jnp.concatenate(grad_parts, axis=1)
    part_query, part_key, part_value = (tn(normed_self, part) for part in grad_parts)
    grad_normed = spread_pair(grad_in, in_weight)
    unit_self, inverse_self = unit_rows_of(stream)
    stream_part, grad_self_gain, grad_self_bias = norm_backward(
        grad_normed, unit_self, inverse_self, norms[0]
    )
    grad_stream = grad_stream + stream_part

    vector_sums = jnp.stack(
        [
            grad_self_gain,
            grad_self_bias,
            grad_cross_gain,
            grad_cross_bias,
            grad_feed_gain,
            grad_feed_bias,
        ]
    ).reshape(6, -1, shard_rows)
    vector_sums = vector_sums + swap(vector_sums, "tensor")
    vector_sums = jnp.pad(
        vector_sums.transpose(1, 0, 2), ((0, 0), (0, 2), (0, 128 - shard_rows))
    ).reshape(zs, 2, 2, 8, 128)

    def blocks(part):
        return part.astype(BF).reshape(zs, 2, 2, -1, part.shape[1])

    (vector_sums, sum_query, sum_key, sum_value, sum_self_output, sum_memory, crest) = (
        scatter_all(
            [
                vector_sums,
                blocks(part_query),
                blocks(part_key),
                blocks(part_value),
                blocks(part_self_output),
                blocks(part_memory),
            ],
            ["x", "x", "y", "x", "y", "z"],
            crest,
            zs,
        )
    )
    vector_sums = vector_sums[:, :shard_rows]
    peaks = crest[0, :heads_here]
    factor = jnp.sqrt(threshold[0] / jnp.maximum(peaks, threshold[0]))
    columns = jnp.repeat(factor, HEAD_DIM)[None, :]

    def side_by_side(kept, got):
        low = jnp.where(x_at == 0, kept, got).astype(F32)
        high = jnp.where(x_at == 0, got, kept).astype(F32)
        return jnp.concatenate([low, high], axis=1)

    down_sum = side_by_side(down_keep, down_got).T
    gate_sum = side_by_side(gates_keep[:, :ff], gates_got[:, :ff])
    up_sum = side_by_side(gates_keep[:, ff:], gates_got[:, ff:])
    return (
        result,
        grad_stream,
        vector_sums[0],
        vector_sums[1],
        sum_query,
        sum_key,
        sum_value,
        sum_self_output.T,
        vector_sums[2],
        vector_sums[3],
        sum_cross_query,
        sum_memory[:, :inner],
        sum_memory[:, inner:],
        sum_cross_output.T,
        vector_sums[4],
        vector_sums[5],
        gate_sum,
        up_sum,
        down_sum,
        peaks,
        self_query.astype(F32) * columns,
        self_key.astype(F32) * columns,
        cross_query.astype(F32) * columns,
        cross_key.astype(F32) * columns,
    )


def solution(mesh):
    count = mesh.shape["dp"]
    mesh = Mesh(
        mesh.devices.reshape(count // 4, 2, 2, mesh.shape["tensor"]), ("z", "y", "x", "tensor")
    )
    dp = ("z", "y", "x")
    both = P(dp + ("tensor",), None)
    split = P(dp)
    row_major = P(dp, "tensor")
    column_major = P("tensor", dp)
    in_specs = (
        both,
        both,
        P(dp, None, None),
        P(dp, None),
        split,
        P(),
        split,
        split,
        row_major,
        row_major,
        row_major,
        column_major,
        split,
        split,
        row_major,
        row_major,
        row_major,
        column_major,
        split,
        split,
        row_major,
        row_major,
        column_major,
    )
    out_specs = (
        both,
        both,
        split,
        split,
        row_major,
        row_major,
        row_major,
        column_major,
        split,
        split,
        row_major,
        row_major,
        row_major,
        column_major,
        split,
        split,
        row_major,
        row_major,
        column_major,
        P("tensor"),
        row_major,
        row_major,
        row_major,
        row_major,
    )
    return jax.shard_map(
        per_device, mesh=mesh, in_specs=in_specs, out_specs=out_specs, check_vma=False
    )
```

```python
import functools

import jax
import jax.numpy as jnp
from jax import lax
from jax.experimental import pallas as pl
from jax.experimental.pallas import tpu as pltpu
from jax.sharding import Mesh
from jax.sharding import PartitionSpec as P

HEAD_DIM = 64
ROT_DIM = 32
EPSILON = 1e-05
NEGATIVE = -1e30
BF = jnp.bfloat16
F32 = jnp.float32


def swap(value, axis):
    return lax.ppermute(value, axis, [(0, 1), (1, 0)])


def pick(value, index, dim):
    return lax.dynamic_index_in_dim(value, index, dim, keepdims=False)


class Lanes:
    def __init__(self, send_sems, recv_sems, local_sems, zs):
        self.send_sems, self.recv_sems, self.local_sems = send_sems, recv_sems, local_sems
        self.used = self.used_local = 0
        self.z = lax.axis_index("z")
        self.y = lax.axis_index("y")
        self.x = lax.axis_index("x")
        self.zs = zs

    def local(self):
        self.used_local += 1
        return self.local_sems.at[self.used_local - 1]

    def copy(self, source, target, device):
        return self.copies([source], target, device)[0]

    def copies(self, sources, target, device):
        slot = self.used
        self.used += 1
        return [
            pltpu.make_async_remote_copy(
                src_ref=source,
                dst_ref=target,
                send_sem=self.send_sems.at[slot],
                recv_sem=self.recv_sems.at[slot],
                device_id=device,
                device_id_type=pl.DeviceIdType.MESH,
            )
            for source in sources
        ]


def guarded(condition, action):
    if condition is None:
        action()
    else:
        pl.when(condition)(action)


class Move:
    def __init__(self, copy, sends, receives):
        self.copy_, self.sends, self.receives = copy, sends, receives

    def start(self):
        guarded(self.sends, self.copy_.start)

    def arrived(self):
        guarded(self.receives, self.copy_.wait_recv)

    def sent(self):
        guarded(self.sends, self.copy_.wait_send)


class Gather:
    def __init__(self, lanes, whole):
        zs, z, y, x = lanes.zs, lanes.z, lanes.y, lanes.x
        own = whole.at[z, y, x]

        def block(zz, yy):
            return whole.at[zz, yy, x]

        def along(source, target, axis, to, sends=None, receives=None):
            return Move(lanes.copy(source, target, {axis: to}), sends, receives)

        self.first = [
            along(own, block(z, y), "y", 1 - y),
            along(own, block(z, y), "x", 1 - x),
        ]
        self.far = [[along(block(z, 1 - y), block(z, 1 - y), "x", 1 - x)]]
        self.steps = []
        for k in range(zs - 1):
            right, left = jnp.maximum(z - k, 0), jnp.minimum(z + k, zs - 1)
            step = []
            for zz, to, sends, receives, got in (
                (right, z + 1, (z >= k) & (z < zs - 1), z >= k + 1, jnp.maximum(z - 1 - k, 0)),
                (left, z - 1, (z + k < zs) & (z > 0), z + k + 1 < zs, jnp.minimum(z + 1 + k, zs - 1)),
            ):
                source = own if k == 0 else block(zz, y)
                move = along(source, block(zz, y), "z", to, sends, receives)
                follow = [
                    along(block(got, y), block(got, y), "y", 1 - y, receives, receives),
                    along(block(got, y), block(got, y), "x", 1 - x, receives, receives),
                    along(block(got, 1 - y), block(got, 1 - y), "x", 1 - x, receives, receives),
                ]
                step.append((move, follow))
            self.steps.append(step)

    def begin(self):
        for move, _ in self.steps[0]:
            move.start()
        for move in self.first:
            move.start()

    def step(self, k, side):
        move, follow = self.steps[k][side]
        move.arrived()
        if k + 1 < len(self.steps):
            self.steps[k + 1][side][0].start()
        follow[0].start()
        follow[1].start()

    def far_first(self):
        self.first[0].arrived()
        self.far[0][0].start()

    def far_step(self, k, side):
        _, follow = self.steps[k][side]
        follow[0].arrived()
        follow[2].start()

    def landed(self):
        self.first[1].arrived()
        self.far[0][0].arrived()
        for step in self.steps:
            for _, follow in step:
                follow[1].arrived()
                follow[2].arrived()

    def sent(self):
        for move in self.first + self.far[0]:
            move.sent()
        for step in self.steps:
            for move, follow in step:
                move.sent()
                for other in follow:
                    other.sent()


class PairGather:
    def __init__(self, lanes, shard, whole, y_first):
        zs, z, y, x = lanes.zs, lanes.z, lanes.y, lanes.x
        ff = whole.shape[-1]
        kept = shard.at[:, pl.ds(pl.multiple_of(x * ff, ff), ff)]
        sent = shard.at[:, pl.ds(pl.multiple_of((1 - x) * ff, ff), ff)]
        self.y_first = y_first

        def along(piece, axis, to, sends=None, receives=None):
            return Move(lanes.copy(piece, piece, {axis: to}), sends, receives)

        self.swap = Move(lanes.copy(sent, whole.at[z, y, x], {"x": 1 - x}), None, None)
        self.local = pltpu.make_async_copy(kept, whole.at[z, y, x], lanes.local())
        self.own_y = along(whole.at[z, y], "y", 1 - y)
        self.steps = []
        for k in range(zs - 1):
            step = []
            for zz, to, sends, receives, got in (
                (jnp.maximum(z - k, 0), z + 1, (z >= k) & (z < zs - 1), z >= k + 1, jnp.maximum(z - 1 - k, 0)),
                (jnp.minimum(z + k, zs - 1), z - 1, (z + k < zs) & (z > 0), z + k + 1 < zs, jnp.minimum(z + 1 + k, zs - 1)),
            ):
                piece = whole.at[zz] if y_first else whole.at[zz, y]
                move = along(piece, "z", to, sends, receives)
                follow = [] if y_first else [along(whole.at[got, y], "y", 1 - y, receives, receives)]
                step.append((move, follow))
            self.steps.append(step)

    def begin(self):
        self.swap.start()
        self.local.start()

    def far_first(self):
        self.swap.arrived()
        self.local.wait()
        self.own_y.start()
        if not self.y_first:
            for move, _ in self.steps[0]:
                move.start()

    def own_y_arrived(self):
        self.own_y.arrived()
        if self.y_first:
            for move, _ in self.steps[0]:
                move.start()

    def step(self, k, side):
        move, follow = self.steps[k][side]
        move.arrived()
        if k + 1 < len(self.steps):
            self.steps[k + 1][side][0].start()
        for other in follow:
            other.start()

    def landed(self):
        if not self.y_first:
            self.own_y.arrived()
        for step in self.steps:
            for move, follow in step:
                for other in follow:
                    other.arrived()

    def sent(self):
        self.swap.sent()
        self.own_y.sent()
        for step in self.steps:
            for move, follow in step:
                move.sent()
                for other in follow:
                    other.sent()


def greet(zs, mates=False):
    z, y, x = lax.axis_index("z"), lax.axis_index("y"), lax.axis_index("x")
    barrier = pltpu.get_barrier_semaphore()

    def signal(device):
        pl.semaphore_signal(barrier, inc=1, device_id=device, device_id_type=pl.DeviceIdType.MESH)

    signal({"x": 1 - x})
    signal({"y": 1 - y})
    pl.when(z > 0)(lambda: signal({"z": z - 1}))
    pl.when(z < zs - 1)(lambda: signal({"z": z + 1}))
    if mates:
        signal({"tensor": 1 - lax.axis_index("tensor")})
    peers = (3 if mates else 2) + (z > 0).astype(jnp.int32) + (z < zs - 1).astype(jnp.int32)
    pl.semaphore_wait(barrier, peers)


def gather_kernel(zs, groups, pairs, *refs):
    shards = sum(groups)
    owns, pair_in = refs[:shards], refs[shards : shards + pairs]
    refs = refs[shards + pairs :]
    outs = refs[: len(groups) + pairs]
    lanes = Lanes(*refs[len(groups) + pairs :], zs)
    z, y, x = lanes.z, lanes.y, lanes.x
    pieces, at = [], 0
    for count, whole in zip(groups, outs):
        width = whole.shape[-1] // count
        for i in range(count):
            target = whole.at[z, y, x, :, pl.ds(i * width, width)]
            pieces.append(pltpu.make_async_copy(owns[at], target, lanes.local()))
            at += 1
    for piece in pieces:
        piece.start()
    greet(zs)
    gathers = [Gather(lanes, whole) for whole in outs[: len(groups)]]
    quarters = [
        PairGather(lanes, pair_in[i], outs[len(groups) + i], i == 0) for i in range(pairs)
    ]
    for quarter in quarters:
        quarter.begin()
    for piece in pieces:
        piece.wait()
    for gather in gathers:
        gather.begin()
    for quarter in quarters:
        quarter.far_first()
    for gather in gathers:
        gather.far_first()
    for k, side in [(k, side) for k in range(zs - 1) for side in range(2)]:
        for gather in gathers:
            gather.step(k, side)
        for quarter in quarters:
            if quarter.y_first:
                if k == 0 and side == 0:
                    quarter.own_y_arrived()
            else:
                quarter.step(k, side)
        for gather in gathers:
            gather.far_step(k, side)
        for quarter in quarters:
            if quarter.y_first:
                quarter.step(k, side)
    for item in gathers + quarters:
        item.landed()
        item.sent()


def gather_all(groups, quarters, zs):
    flat = [shard for group in groups for shard in group] + list(quarters)
    outs = []
    for group in groups:
        columns = sum(shard.shape[1] for shard in group)
        outs.append(
            jax.ShapeDtypeStruct((zs, 2, 2, group[0].shape[0], columns), group[0].dtype)
        )
    for shard in quarters:
        outs.append(
            jax.ShapeDtypeStruct((zs, 2, 2, shard.shape[0], shard.shape[1] // 2), shard.dtype)
        )
    count, pairs = len(groups), len(quarters)
    moves = count * (3 + 8 * (zs - 1)) + pairs * (2 + 4 * (zs - 1))
    hbm = pl.BlockSpec(memory_space=pltpu.HBM)
    return pl.pallas_call(
        functools.partial(gather_kernel, zs, tuple(len(group) for group in groups), pairs),
        out_shape=outs,
        in_specs=[hbm] * len(flat),
        out_specs=[hbm] * len(outs),
        scratch_shapes=[
            pltpu.SemaphoreType.DMA((moves,)),
            pltpu.SemaphoreType.DMA((moves,)),
            pltpu.SemaphoreType.DMA((len(flat),)),
        ],
        compiler_params=pltpu.CompilerParams(collective_id=1, has_side_effects=True),
    )(*flat)


def plus(*terms):
    total = terms[0].astype(F32)
    for term in terms[1:]:
        total = total + term.astype(F32)
    return total


def ends_first(zs):
    order = []
    for i in range(zs // 2):
        order += [zs - 1 - i, i]
    return order


class Line:
    def __init__(self, lanes, part, from_left, from_right):
        zs, z = lanes.zs, lanes.z
        self.zs, self.z, self.part = zs, z, part
        self.from_left, self.from_right = from_left, from_right
        self.right, self.left = {}, {}
        for d in ends_first(zs):
            after, before = jnp.minimum(z + 1, zs - 1), jnp.maximum(z - 1, 0)
            self.right[d] = lanes.copies(
                (part.at[d], from_left.at[d]), from_left.at[d], {"z": after}
            )
            self.left[d] = lanes.copies(
                (part.at[d], from_right.at[d]), from_right.at[d], {"z": before}
            )

    def pass_on(self, d):
        for moves, inbox, sends, edge in (
            (self.right[d], self.from_left, self.z < d, self.z == 0),
            (self.left[d], self.from_right, self.z > d, self.z == self.zs - 1),
        ):

            @pl.when(sends & edge)
            def _():
                moves[0].start()

            @pl.when(sends & jnp.logical_not(edge))
            def _():
                moves[1].wait_recv()
                inbox[d] = plus(self.part[d], inbox[d]).astype(inbox.dtype)
                moves[1].start()

    def total(self, sink):
        for d in range(self.zs):

            @pl.when(self.z == d)
            def _():
                terms = [self.part[d]]
                if d > 0:
                    self.right[d][0].wait_recv()
                    terms.append(self.from_left[d])
                if d < self.zs - 1:
                    self.left[d][0].wait_recv()
                    terms.append(self.from_right[d])
                sink[...] = plus(*terms).astype(sink.dtype)

    def finish(self):
        for d in ends_first(self.zs):
            pl.when(self.z < d)(self.right[d][0].wait_send)
            pl.when(self.z > d)(self.left[d][0].wait_send)


class Scatter:
    def __init__(self, lanes, part, held, out, first):
        zs, z, y, x = lanes.zs, lanes.z, lanes.y, lanes.x
        got, near, from_left, from_right, ready = held
        second = "y" if first == "x" else "x"
        self.lanes, self.part, self.got, self.near, self.ready, self.out = (
            lanes, part, got, near, ready, out,
        )
        f, s = (x, y) if first == "x" else (y, x)
        self.f, self.s = f, s

        def block(zz, a, b):
            return part.at[zz, b, a] if first == "x" else part.at[zz, a, b]

        self.block = block
        self.one, self.two = {}, {}
        for zz in ends_first(zs):
            for j, b in enumerate((1 - s, s)):
                self.one[zz, j] = Move(
                    lanes.copy(block(zz, 1 - f, b), got.at[zz, j], {first: 1 - f}), None, None
                )
        for zz in ends_first(zs):
            self.two[zz] = Move(
                lanes.copy(got.at[zz, 0], near.at[zz], {second: 1 - s}), None, None
            )
        self.line = Line(lanes, ready, from_left, from_right)

    def begin(self, zz):
        for j in range(2):
            self.one[zz, j].start()

    def second(self, zz):
        self.one[zz, 0].arrived()
        mine, got = self.block(zz, self.f, 1 - self.s), self.got
        got[zz, 0] = plus(mine[...], got[zz, 0]).astype(got.dtype)
        self.two[zz].start()

    def third(self, zz):
        self.one[zz, 1].arrived()
        self.two[zz].arrived()
        mine = self.block(zz, self.f, self.s)
        self.ready[zz] = plus(mine[...], self.got[zz, 1], self.near[zz]).astype(self.ready.dtype)
        self.line.pass_on(zz)

    def finish(self):
        self.line.total(self.out)
        self.line.finish()
        for move in list(self.one.values()) + list(self.two.values()):
            move.sent()


class ScatterZ:
    def __init__(self, lanes, part, held, out):
        y, x = lanes.y, lanes.x
        from_left, from_right, held_z, near, last = held
        self.lanes, self.sum_z, self.near, self.last, self.out = lanes, held_z, near, last, out
        self.line = Line(lanes, part, from_left, from_right)
        self.two = Move(lanes.copy(held_z.at[1 - y], near, {"y": 1 - y}), None, None)
        self.three = Move(lanes.copy(near.at[1 - x], last, {"x": 1 - x}), None, None)

    def pass_on(self, d):
        self.line.pass_on(d)

    def total(self):
        self.line.total(self.sum_z)
        self.two.start()

    def after(self):
        self.two.arrived()
        self.near[...] = plus(self.sum_z[self.lanes.y], self.near[...]).astype(self.near.dtype)
        self.three.start()

    def finish(self):
        self.three.arrived()
        self.out[...] = plus(self.near[self.lanes.x], self.last[...]).astype(self.out.dtype)
        self.line.finish()
        self.two.sent()
        self.three.sent()


class Crest:
    def __init__(self, lanes, own, held, out):
        zs, z, y, x = lanes.zs, lanes.z, lanes.y, lanes.x
        near_x, near_y, mine_x, mine_y, right, left, inbox_r, inbox_l = (
            held.at[i] for i in range(8)
        )
        self.zs, self.z, self.own, self.out = zs, z, own, out
        self.near_x, self.near_y, self.mine_x, self.mine_y = near_x, near_y, mine_x, mine_y
        self.ways = (
            (right, inbox_r, z > 0, z < zs - 1),
            (left, inbox_l, z < zs - 1, z > 0),
        )
        self.one = Move(lanes.copy(own, near_x, {"x": 1 - x}), None, None)
        self.two = Move(lanes.copy(mine_x, near_y, {"y": 1 - y}), None, None)
        self.moves = [
            Move(lanes.copy(right, inbox_r, {"z": jnp.minimum(z + 1, zs - 1)}), z < zs - 1, z > 0),
            Move(lanes.copy(left, inbox_l, {"z": jnp.maximum(z - 1, 0)}), z > 0, z < zs - 1),
        ]

    def second(self):
        self.one.arrived()
        self.mine_x[...] = jnp.maximum(self.own[...], self.near_x[...])
        self.two.start()

    def finish(self):
        self.two.arrived()
        self.mine_y[...] = jnp.maximum(self.mine_x[...], self.near_y[...])
        self.out[...] = self.mine_y[...]
        for move, (held, inbox, has_before, has_after) in zip(self.moves, self.ways):

            @pl.when(has_before)
            def _():
                move.copy_.wait_recv()
                self.out[...] = jnp.maximum(self.out[...], inbox[...])
                held[...] = jnp.maximum(self.mine_y[...], inbox[...])

            @pl.when(jnp.logical_not(has_before))
            def _():
                held[...] = self.mine_y[...]

            move.start()
        for move in [self.one, self.two] + self.moves:
            move.sent()


def scatter_kernel(zs, orders, *refs):
    count = len(orders)
    parts, crest_in, refs = refs[:count], refs[count], refs[count + 1 :]
    outs, crest_out, rest = refs[:count], refs[count], list(refs[count + 1 :])
    send_sems, recv_sems = rest[:2]
    rest = rest[2:]
    lanes = Lanes(send_sems, recv_sems, None, zs)
    greet(zs)
    full, zfirst = [], []
    for i, order in enumerate(orders):
        held, rest = rest[:5], rest[5:]
        if order == "z":
            zfirst.append(ScatterZ(lanes, parts[i], held, outs[i]))
        else:
            full.append(Scatter(lanes, parts[i], held, outs[i], order))
    crest = Crest(lanes, crest_in, rest[0], crest_out)
    crest.one.start()
    order = ends_first(zs)
    for i in range(zs + 3):
        for item in full:
            if i < zs:
                item.begin(order[i])
        if i == 1:
            crest.second()
        if i < zs:
            for item in zfirst:
                item.pass_on(order[i])
        for item in full:
            if 2 <= i < zs + 2:
                item.second(order[i - 2])
        if i == zs:
            for item in zfirst:
                item.total()
        for item in full:
            if 3 <= i:
                item.third(order[i - 3])
    crest.finish()
    for item in zfirst:
        item.after()
    for item in full:
        item.finish()
    for item in zfirst:
        item.finish()


def scatter_all(parts, orders, crest, zs):
    scratch, moves = [], 4
    for part, order in zip(parts, orders):
        block = part.shape[3:]
        if order == "z":
            shapes = [(zs, 2, 2) + block] * 2 + [(2, 2) + block, (2,) + block, block]
            moves += 2 * zs + 2
        else:
            shapes = [(zs, 2) + block] + [(zs,) + block] * 4
            moves += 5 * zs
        scratch += [pltpu.VMEM(shape, part.dtype) for shape in shapes]
    vmem = pl.BlockSpec(memory_space=pltpu.VMEM)
    return pl.pallas_call(
        functools.partial(scatter_kernel, zs, orders),
        out_shape=[jax.ShapeDtypeStruct(part.shape[3:], F32) for part in parts]
        + [jax.ShapeDtypeStruct(crest.shape, F32)],
        in_specs=[vmem] * (len(parts) + 1),
        out_specs=[vmem] * (len(parts) + 1),
        scratch_shapes=[pltpu.SemaphoreType.DMA((moves,)), pltpu.SemaphoreType.DMA((moves,))]
        + scratch
        + [pltpu.VMEM((8,) + crest.shape, F32)],
        compiler_params=pltpu.CompilerParams(
            collective_id=2, has_side_effects=True, vmem_limit_bytes=56 * 2**20
        ),
    )(*parts, crest)


def nn(left, right):
    return lax.dot_general(left, right, (((1,), (0,)), ((), ())), preferred_element_type=F32)


def nt(left, right):
    return lax.dot_general(left, right, (((1,), (1,)), ((), ())), preferred_element_type=F32)


def tn(left, right):
    return lax.dot_general(left, right, (((0,), (0,)), ((), ())), preferred_element_type=F32)


def reduce_full(left, right, zs):
    held = tn(left, right).astype(BF).reshape(zs * 2, 2, -1, right.shape[1])
    at = lax.axis_index("x")
    got = swap(pick(held, 1 - at, 1), "x")
    held = (pick(held, at, 1).astype(F32) + got.astype(F32)).astype(BF)
    held = held.reshape(zs, 2, -1, right.shape[1])
    at = lax.axis_index("y")
    got = swap(pick(held, 1 - at, 1), "y")
    held = (pick(held, at, 1).astype(F32) + got.astype(F32)).astype(BF)
    return lax.psum_scatter(held, "z", scatter_dimension=0, tiled=False)


def reduce_pair(left, right, zs):
    held = tn(left, right).astype(BF).reshape(zs, 2, -1, right.shape[1])
    at = lax.axis_index("y")
    got = swap(pick(held, 1 - at, 1), "y")
    held = (pick(held, at, 1).astype(F32) + got.astype(F32)).astype(BF)
    held = lax.psum_scatter(held, "z", scatter_dimension=0, tiled=False)
    held = held.reshape(2, -1, right.shape[1])
    at = lax.axis_index("x")
    got = swap(pick(held, 1 - at, 0), "x")
    return pick(held, at, 0), got


def norm_forward(stream, gain_vec, bias_vec):
    average = jnp.mean(stream, axis=-1, keepdims=True)
    centred = stream - average
    inverse = lax.rsqrt(jnp.mean(centred * centred, axis=-1, keepdims=True) + EPSILON)
    unit_rows = centred * inverse
    return (unit_rows * gain_vec + bias_vec, unit_rows, inverse)


def unit_rows_of(stream):
    _, unit_rows, inverse = norm_forward(stream, 1.0, 0.0)
    return unit_rows, inverse


def norm_backward(incoming, unit_rows, inverse, gain_vec):
    gain_grad = jnp.sum(incoming * unit_rows, axis=0)
    bias_grad = jnp.sum(incoming, axis=0)
    scaled = incoming * gain_vec
    stream_grad = inverse * (
        scaled
        - jnp.mean(scaled, axis=-1, keepdims=True)
        - unit_rows * jnp.mean(scaled * unit_rows, axis=-1, keepdims=True)
    )
    return (stream_grad, gain_grad, bias_grad)


def turn_tables(positions):
    rates = 10000.0 ** (-jnp.arange(0, ROT_DIM, 2).astype(F32) / ROT_DIM)
    angles = positions[:, None] * rates[None, :]
    cosine, sine = jnp.cos(angles), jnp.sin(angles)
    rest = jnp.ones((positions.shape[0], HEAD_DIM - ROT_DIM), F32)
    zero, none = jnp.zeros_like(rest), jnp.zeros_like(sine)
    return (
        jnp.concatenate([cosine, cosine, rest] * 2, axis=1),
        jnp.concatenate([-sine, none, zero] * 2, axis=1),
        jnp.concatenate([none, sine, zero] * 2, axis=1),
    )


def turn(field, cosine, sine_a, sine_b, direction):
    half = ROT_DIM // 2
    width = field.shape[-1]
    ahead = pltpu.roll(field, width - half, 1)
    behind = pltpu.roll(field, half, 1)
    return field * cosine + direction * (ahead * sine_a + behind * sine_b)


def head_lanes(shape, which):
    lanes = lax.broadcasted_iota(jnp.int32, shape, 1)
    return (lanes >= which * HEAD_DIM) & (lanes < (which + 1) * HEAD_DIM)


def attend_tile(query, keys, values, bias):
    scores = nt(query, keys) + bias
    top = jnp.max(scores, axis=-1, keepdims=True)
    weights = jnp.exp(scores - top)
    total = jnp.sum(weights, axis=-1, keepdims=True)
    return nn(weights.astype(BF), values) / total, top


def attend_kernel(q_ref, k_ref, v_ref, bias_ref, mixed_ref, peak_ref):
    rows = q_ref.shape[0]
    tile = rows // 3 if rows % 3 == 0 and (rows // 3) % 16 == 0 else rows
    keys, values, bias = k_ref[...], v_ref[...], bias_ref[...]
    peaks = [None, None]
    for start in range(0, rows, tile):
        query = q_ref[start : start + tile, :] * BF(HEAD_DIM ** (-0.5))
        outs = []
        for which in range(2):
            one = jnp.where(head_lanes(query.shape, which), query, jnp.zeros_like(query))
            out, top = attend_tile(one, keys, values, bias)
            outs.append(out)
            top = jnp.max(top, axis=0, keepdims=True)
            peaks[which] = top if peaks[which] is None else jnp.maximum(peaks[which], top)
        mixed = jnp.where(head_lanes(outs[0].shape, 0), outs[0], outs[1])
        mixed_ref[start : start + tile, :] = mixed.astype(BF)
    spot = head_lanes((8, 2 * HEAD_DIM), 0)
    peak_ref[0] = jnp.where(
        spot, jnp.broadcast_to(peaks[0], spot.shape), jnp.broadcast_to(peaks[1], spot.shape)
    )


def attend(query, keys, values, bias, offsets):
    rows, tokens = query.shape[0], keys.shape[0]
    pairs = bias.shape[0]
    wide = 2 * HEAD_DIM
    mixed, peak = pl.pallas_call(
        attend_kernel,
        grid=(pairs,),
        out_shape=[
            jax.ShapeDtypeStruct((rows, pairs * wide), BF),
            jax.ShapeDtypeStruct((pairs, 8, wide), F32),
        ],
        in_specs=[
            pl.BlockSpec((rows, wide), lambda j: (0, offsets[0] + j)),
            pl.BlockSpec((tokens, wide), lambda j: (0, offsets[1] + j)),
            pl.BlockSpec((tokens, wide), lambda j: (0, offsets[2] + j)),
            pl.BlockSpec((1, tokens), lambda j: (0, 0)),
        ],
        out_specs=[
            pl.BlockSpec((rows, wide), lambda j: (0, j)),
            pl.BlockSpec((1, 8, wide), lambda j: (j, 0, 0)),
        ],
        compiler_params=pltpu.CompilerParams(vmem_limit_bytes=48 * 2**20),
        cost_estimate=pl.CostEstimate(
            flops=8 * rows * tokens * pairs * wide,
            bytes_accessed=4 * (rows + tokens) * pairs * wide,
            transcendentals=2 * pairs * rows * tokens,
        ),
    )(query, keys, values, bias[:1])
    return mixed, peak[:, 0, ::HEAD_DIM].reshape(-1)


def attend_back_kernel(turned, q_ref, k_ref, v_ref, g_ref, bias_ref, *refs):
    if turned:
        cos_ref, sa_ref, sb_ref = refs[:3]
        refs = refs[3:]
    dq_ref, dk_ref, dv_ref, dk_acc, dv_acc = refs
    rows = q_ref.shape[0]
    tile = rows // 3 if rows % 3 == 0 and (rows // 3) % 128 == 0 else rows
    scale = BF(HEAD_DIM ** (-0.5))
    keys, values, bias = k_ref[...], v_ref[...], bias_ref[...]
    for start in range(0, rows, tile):
        part = slice(start, start + tile)
        query, grad = q_ref[part, :] * scale, g_ref[part, :]
        dq = None
        for which in range(2):
            mine = head_lanes(query.shape, which)
            one = jnp.where(mine, query, jnp.zeros_like(query))
            out = jnp.where(mine, grad, jnp.zeros_like(grad))
            scores = nt(keys, one) + bias
            weights = jnp.exp(scores - jnp.max(scores, axis=0, keepdims=True))
            weights = weights * (1.0 / jnp.sum(weights, axis=0, keepdims=True))
            slope = nt(values, out)
            slope = weights * (slope - jnp.sum(weights * slope, axis=0, keepdims=True))
            slope = slope.astype(BF)
            dv = nn(weights.astype(BF), out)
            dk = nn(slope, one)
            other = jnp.where(head_lanes(keys.shape, which), keys, jnp.zeros_like(keys))
            piece = tn(slope, other * scale)
            dq = piece if dq is None else dq + piece
            if start == 0 and which == 0:
                dv_acc[...] = dv
                dk_acc[...] = dk
            else:
                dv_acc[...] += dv
                dk_acc[...] += dk
        if turned:
            dq = turn(dq, cos_ref[part, :], sa_ref[part, :], sb_ref[part, :], -1.0)
        dq_ref[part, :] = dq.astype(BF)
    dk = dk_acc[...]
    if turned:
        dk = turn(dk, cos_ref[...], sa_ref[...], sb_ref[...], -1.0)
    dk_ref[...] = dk.astype(BF)
    dv_ref[...] = dv_acc[...].astype(BF)


def attend_back(query, keys, values, grad, bias_column, offsets, turns):
    rows, tokens = query.shape[0], keys.shape[0]
    wide = 2 * HEAD_DIM
    pairs = grad.shape[1] // wide
    ins = [query, keys, values, grad, bias_column]
    specs = [
        pl.BlockSpec((rows, wide), lambda j: (0, offsets[0] + j)),
        pl.BlockSpec((tokens, wide), lambda j: (0, offsets[1] + j)),
        pl.BlockSpec((tokens, wide), lambda j: (0, offsets[2] + j)),
        pl.BlockSpec((rows, wide), lambda j: (0, j)),
        pl.BlockSpec((tokens, 1), lambda j: (0, 0)),
    ]
    if turns is not None:
        ins += list(turns)
        specs += [pl.BlockSpec((rows, wide), lambda j: (0, 0))] * 3
    return pl.pallas_call(
        functools.partial(attend_back_kernel, turns is not None),
        grid=(pairs,),
        out_shape=[
            jax.ShapeDtypeStruct((rows, pairs * wide), BF),
            jax.ShapeDtypeStruct((tokens, pairs * wide), BF),
            jax.ShapeDtypeStruct((tokens, pairs * wide), BF),
        ],
        in_specs=specs,
        out_specs=[
            pl.BlockSpec((rows, wide), lambda j: (0, j)),
            pl.BlockSpec((tokens, wide), lambda j: (0, j)),
            pl.BlockSpec((tokens, wide), lambda j: (0, j)),
        ],
        scratch_shapes=[pltpu.VMEM((tokens, wide), F32), pltpu.VMEM((tokens, wide), F32)],
        compiler_params=pltpu.CompilerParams(vmem_limit_bytes=48 * 2**20),
        cost_estimate=pl.CostEstimate(
            flops=20 * rows * tokens * pairs * wide,
            bytes_accessed=8 * (rows + tokens) * pairs * wide,
            transcendentals=2 * pairs * rows * tokens,
        ),
    )(*ins)


def project_kernel(turned, x_ref, w_ref, cos_ref, sa_ref, sb_ref, out_ref):
    wide = 2 * HEAD_DIM
    made = nn(x_ref[...], w_ref[...])

    @pl.when(pl.program_id(0) < turned)
    def _():
        for start in range(0, made.shape[1], wide):
            piece = turn(made[:, start : start + wide], cos_ref[...], sa_ref[...], sb_ref[...], 1.0)
            out_ref[:, start : start + wide] = piece.astype(BF)

    @pl.when(pl.program_id(0) >= turned)
    def _():
        out_ref[...] = made.astype(BF)


def project(rows, weight, turns, turned_columns):
    count, depth = rows.shape
    columns = weight.shape[1]
    block = 2 * HEAD_DIM * (2 if turned_columns % (4 * HEAD_DIM) == 0 else 1)
    table = pl.BlockSpec((count, 2 * HEAD_DIM), lambda j: (0, 0))
    return pl.pallas_call(
        functools.partial(project_kernel, turned_columns // block),
        grid=(columns // block,),
        out_shape=jax.ShapeDtypeStruct((count, columns), BF),
        in_specs=[
            pl.BlockSpec((count, depth), lambda j: (0, 0)),
            pl.BlockSpec((depth, block), lambda j: (0, j)),
            table,
            table,
            table,
        ],
        out_specs=pl.BlockSpec((count, block), lambda j: (0, j)),
        compiler_params=pltpu.CompilerParams(vmem_limit_bytes=48 * 2**20),
        cost_estimate=pl.CostEstimate(
            flops=2 * count * depth * columns,
            bytes_accessed=2 * (count * depth + depth * columns + count * columns),
            transcendentals=0,
        ),
    )(rows, weight, *turns)


PLAN = (
    100, 700, 0, 1000, 2000, 2001, 800, 1100, 2100, 2101, 3000, 2010, 2011, 3001, 1700, 600,
    2110, 2111, 3100, 2020, 2021, 1800, 3101, 3010, 3011, 2700, 2701, 200, 2120, 2121, 3020,
    3021, 300, 400, 3110, 3111, 2710, 2711, 500, 2200, 2201, 1600, 5800, 2720, 2721, 2300, 2301,
    2400, 2401, 2210, 2211, 3120, 3121, 2220, 2221, 2310, 2311, 2500, 2501, 2410, 2411, 1200,
    4000, 2320, 2321, 2600, 2601, 2420, 2421, 1300, 1400, 3200, 3201, 4100, -1, 4700, -1, -1,
    1500, 3300, 3301, -1, -1, 2800, 2801, -1, 3400, 3401, -1, -1, 2510, 2511, 3210, 3211, -1,
    -1, 3220, 3221, -1, 3310, 3311, -1, -1, 2610, 2611, -1, 3410, 3411, 3320, 3321, -1, -1,
    3420, 3421, 3500, 3501, 4200, -1, -1, 2810, 2811, -1, -1, -1, -1, 4300, 2620, 2621, 4400,
    -1, -1, 2520, 2521, -1, -1, -1, -1, -1, -1, -1, -1, -1, 3510, 3511, -1, 4600, -1, -1, 3520,
    3521, 4500, -1, -1, -1, -1, -1, 2820, 2821, -1,
)


def normalise(stream, gain_vec, bias_vec):
    average = jnp.mean(stream, axis=-1, keepdims=True)
    centred = stream - average
    inverse = lax.rsqrt(jnp.mean(centred * centred, axis=-1, keepdims=True) + EPSILON)
    return centred * inverse * gain_vec + bias_vec


def attend_pair(query, keys, values, bias, tile):
    outs_all, peaks = [], [None, None]
    for start in range(0, tile[0], tile[1]):
        rows = query(start, tile[1]) * BF(HEAD_DIM ** (-0.5))
        outs = []
        for which in range(2):
            one = jnp.where(head_lanes(rows.shape, which), rows, jnp.zeros_like(rows))
            out, top = attend_tile(one, keys, values, bias)
            outs.append(out)
            top = jnp.max(top, axis=0, keepdims=True)
            peaks[which] = top if peaks[which] is None else jnp.maximum(peaks[which], top)
        outs_all.append((start, jnp.where(head_lanes(outs[0].shape, 0), outs[0], outs[1])))
    return outs_all, peaks


def forward_kernel(zs, *refs):
    refs = list(refs)

    def take(count):
        taken_refs = refs[:count]
        del refs[:count]
        return taken_refs

    shards = take(9)
    quarters_in = take(3)
    inputs_hbm, cot_hbm, cos_ref, sa_ref, sb_ref, self_bias, cross_bias, memory = take(8)
    wholes = take(6)
    quarter_outs = take(3)
    outs = take(10)
    cot_out = take(1)[0]
    peak_out = take(1)[0]
    send_sems, recv_sems, local_sems = take(3)
    w_vec, w_in, w_so, w_cq, w_kv, w_co = take(6)
    (
        x_all, normed_self, taken, mixed_self, stream_cross, normed_cross,
        query_cross, taken_cross, mixed_cross, stream_feed, normed_feed,
        part_send, part_got, part_send2, part_got2, vectors,
    ) = take(16)
    lanes = Lanes(send_sems, recv_sems, local_sems, zs)
    z, y, x = lanes.z, lanes.y, lanes.x
    t = lax.axis_index("tensor")
    rows, width = inputs_hbm.shape
    wide = 2 * HEAD_DIM

    def local(source, target):
        return pltpu.make_async_copy(source, target, lanes.local())

    pieces, at = [], 0
    for count, whole in zip((1, 3, 1, 1, 2, 1), wholes):
        columns = whole.shape[-1] // count
        for i in range(count):
            target = whole.at[z, y, x, :, pl.ds(i * columns, columns)]
            pieces.append(local(shards[at], target))
            at += 1
    own_inputs = local(inputs_hbm, x_all.at[0])
    own_cot = local(cot_hbm, cot_out.at[0])
    for piece in pieces + [own_inputs, own_cot]:
        piece.start()
    greet(zs, True)

    def mate(source, target):
        return Move(lanes.copy(source, target, {"tensor": 1 - t}), None, None)

    def across(source, target):
        return Move(lanes.copy(source, target, {"x": 1 - x}), None, None)

    mate_inputs = mate(inputs_hbm, x_all.at[1])
    cot_moves = [
        mate(cot_hbm, cot_out.at[1]),
        across(cot_hbm, cot_out.at[2]),
        mate(cot_out.at[2], cot_out.at[3]),
    ]
    feed_moves = [
        mate(normed_feed.at[0], normed_feed.at[1]),
        across(normed_feed.at[0], normed_feed.at[2]),
        mate(normed_feed.at[2], normed_feed.at[3]),
    ]
    mate_self = mate(part_send, part_got)
    mate_normed = mate(normed_cross.at[0], normed_cross.at[1])
    mate_cross = mate(part_send2, part_got2)
    gathers = [Gather(lanes, whole) for whole in wholes]
    quarters = [
        PairGather(lanes, quarters_in[i], quarter_outs[i], i == 2) for i in range(3)
    ]
    loads = [
        local(whole, held)
        for whole, held in zip(wholes, (w_vec, w_in, w_so, w_cq, w_kv, w_co))
    ]
    results = (
        normed_self, taken, mixed_self, stream_cross, normed_cross,
        query_cross, taken_cross, mixed_cross, stream_feed, normed_feed,
    )
    saves = [local(held, out) for held, out in zip(results, outs)]

    mate_inputs.start()
    cot_moves[0].start()
    for piece in pieces:
        piece.wait()
    columns = w_in.shape[-1]
    inner = columns // 3
    pairs = inner // wide
    block = 2 * wide
    tile = 128 if rows % 128 == 0 else rows
    chunk = width // zs
    total = 2 * rows
    step = total // 3 if total % 3 == 0 and (total // 3) % 16 == 0 else total
    tops, ready = [], set()

    def vec(i):
        return vectors[i : i + 1, :]

    def need(*groups):
        assert ready.issuperset(groups)

    def tiles():
        return [slice(start, start + tile) for start in range(0, rows, tile)]

    def attend_all(query_ref, keys_at, values_at, kv_ref, bias_ref, mixed_ref):
        for j in range(pairs):
            lanes_at = j * wide
            bits, peaks = attend_pair(
                lambda start, count: query_ref[start : start + count, lanes_at : lanes_at + wide],
                kv_ref[:, keys_at + lanes_at : keys_at + lanes_at + wide],
                kv_ref[:, values_at + lanes_at : values_at + lanes_at + wide],
                bias_ref[...],
                (total, step),
            )
            for start, bit in bits:
                mixed_ref[start : start + step, lanes_at : lanes_at + wide] = bit.astype(BF)
            tops.append(peaks)
            yield

    def out_rows(mixed_ref, first, weight, zz):
        columns_here = weight[zz].reshape(-1, inner)
        return nt(mixed_ref[first : first + rows, :], columns_here)

    def out_project(mixed_ref, weight, move, send, got, base, target):
        for zz in range(zs):
            send[:, zz * chunk : (zz + 1) * chunk] = out_rows(mixed_ref, rows, weight, zz)
        move.start()
        yield
        for zz in range(zs):
            part = slice(zz * chunk, (zz + 1) * chunk)
            target[:, part] = out_rows(mixed_ref, 0, weight, zz) + base(part)
            yield
        move.arrived()
        for part in tiles():
            target[part, :] = target[part, :] + got[part, :]

    def compute():
        need(0, 1)
        own_inputs.wait()
        mate_inputs.arrived()
        loads[0].wait()
        vectors[...] = jnp.transpose(w_vec[...].reshape(width, w_vec.shape[-1]))
        for side in range(2):
            for part in tiles():
                made = normalise(x_all[side, part, :].astype(F32), vec(0), vec(1))
                at = side * rows + part.start
                normed_self[at : at + tile, :] = made.astype(BF)
        saves[0].start()
        loads[1].wait()
        yield
        for start in range(0, columns, block):
            made = nn(normed_self[...], w_in[..., start : start + block].reshape(width, block))
            for at in range(0, block, wide):
                piece = made[:, at : at + wide]
                if start + at < 2 * inner:
                    piece = turn(piece, cos_ref[...], sa_ref[...], sb_ref[...], 1.0)
                taken[:, start + at : start + at + wide] = piece.astype(BF)
            yield
        saves[1].start()
        yield from attend_all(taken, inner, 2 * inner, taken, self_bias, mixed_self)
        saves[2].start()
        need(2)
        loads[2].wait()
        yield from out_project(
            mixed_self, w_so, mate_self, part_send, part_got,
            lambda part: x_all[0, :, part].astype(F32), stream_cross,
        )
        saves[3].start()
        for part in tiles():
            made = normalise(stream_cross[part, :], vec(2), vec(3))
            normed_cross[0, part, :] = made.astype(BF)
        mate_normed.start()
        yield
        need(4)
        loads[4].wait()
        depth = memory.shape[1]
        for start in range(0, 2 * inner, block):
            weight = w_kv[..., start : start + block].reshape(depth, block)
            taken_cross[:, start : start + block] = nn(memory[...], weight).astype(BF)
        saves[6].start()
        yield
        need(3)
        loads[3].wait()
        yield
        for side in range(2):
            if side == 1:
                mate_normed.arrived()
                saves[4].start()
            for start in range(0, inner, block):
                weight = w_cq[..., start : start + block].reshape(width, block)
                made = nn(normed_cross[side], weight).astype(BF)
                query_cross[side * rows : (side + 1) * rows, start : start + block] = made
                yield
        saves[5].start()
        yield from attend_all(query_cross, 0, inner, taken_cross, cross_bias, mixed_cross)
        saves[7].start()
        need(5)
        loads[5].wait()
        yield from out_project(
            mixed_cross, w_co, mate_cross, part_send2, part_got2,
            lambda part: stream_cross[:, part], stream_feed,
        )
        saves[8].start()
        for part in tiles():
            made = normalise(stream_feed[part, :], vec(4), vec(5))
            normed_feed[0, part, :] = made.astype(BF)
        feed_moves[1].start()
        feed_moves[0].start()

    items = gathers + quarters
    names = ("begin", "far_first", "step", "far_step", "landed", "own_y_arrived")
    work = compute()
    for entry in PLAN:
        if entry < 0:
            next(work, None)
            continue
        kind, which, k, side = entry // 1000, entry // 100 % 10, entry // 10 % 10, entry % 10
        item = items[which]
        getattr(item, names[kind])(*((k, side) if kind in (2, 3) else ()))
        if kind == 0 and which == 4:
            cot_moves[1].start()
        if kind == 4:
            ready.add(which)
            if which < 6:
                loads[which].start()
    cot_moves[1].arrived()
    cot_moves[2].start()
    for _ in work:
        pass
    lane = lax.broadcasted_iota(jnp.int32, peak_out.shape, 1)
    crest = jnp.full(peak_out.shape, NEGATIVE, F32)
    for i, peaks in enumerate(tops):
        for which in range(2):
            head = (i % pairs) * 2 + which
            crest = jnp.where(lane == head, jnp.maximum(crest, peaks[which]), crest)
    peak_out[...] = crest
    feed_moves[1].arrived()
    feed_moves[2].start()
    for i, item in enumerate(items):
        if i not in ready:
            item.landed()
    feed_moves[0].arrived()
    feed_moves[2].arrived()
    saves[9].start()
    cot_moves[0].arrived()
    cot_moves[2].arrived()
    own_cot.wait()
    for item in gathers + quarters:
        item.sent()
    for move in [mate_inputs, mate_self, mate_normed, mate_cross] + cot_moves + feed_moves:
        move.sent()
    for save in saves:
        save.wait()


def forward(shards, quarters, inputs, cotangent, turns, self_bias, cross_bias, memory, zs):
    rows, width = inputs.shape
    seq_len, inner = 2 * rows, shards[1].shape[1]
    tokens = memory.shape[0]
    spread = []
    groups = ([shards[0]], shards[1:4], [shards[4]], [shards[5]], shards[6:8], [shards[8]])
    for group in groups:
        columns = sum(shard.shape[1] for shard in group)
        spread.append(jax.ShapeDtypeStruct((zs, 2, 2, group[0].shape[0], columns), group[0].dtype))
    for shard in quarters:
        spread.append(
            jax.ShapeDtypeStruct((zs, 2, 2, shard.shape[0], shard.shape[1] // 2), shard.dtype)
        )
    results = [
        jax.ShapeDtypeStruct((seq_len, width), BF),
        jax.ShapeDtypeStruct((seq_len, 3 * inner), BF),
        jax.ShapeDtypeStruct((seq_len, inner), BF),
        jax.ShapeDtypeStruct((rows, width), F32),
        jax.ShapeDtypeStruct((2, rows, width), BF),
        jax.ShapeDtypeStruct((seq_len, inner), BF),
        jax.ShapeDtypeStruct((tokens, 2 * inner), BF),
        jax.ShapeDtypeStruct((seq_len, inner), BF),
        jax.ShapeDtypeStruct((rows, width), F32),
        jax.ShapeDtypeStruct((4, rows, width), BF),
    ]
    cot_out = jax.ShapeDtypeStruct((4, rows, width), BF)
    peak = jax.ShapeDtypeStruct((8, 2 * HEAD_DIM), F32)
    moves = 6 * (3 + 8 * (zs - 1)) + 3 * (2 + 4 * (zs - 1)) + 10
    hbm = pl.BlockSpec(memory_space=pltpu.HBM)
    vmem = pl.BlockSpec(memory_space=pltpu.VMEM)
    held = [pltpu.VMEM(shape.shape, shape.dtype) for shape in spread[:6]]
    held += [pltpu.VMEM((2, rows, width), BF)]
    held += [pltpu.VMEM(shape.shape, shape.dtype) for shape in results]
    held += [pltpu.VMEM((rows, width), F32)] * 4
    held += [pltpu.VMEM((shards[0].shape[1], width), F32)]
    flops = 2 * seq_len * inner * (7 * width + 4 * seq_len) // 1
    made = pl.pallas_call(
        functools.partial(forward_kernel, zs),
        out_shape=spread + results + [cot_out, peak],
        in_specs=[hbm] * 14 + [vmem] * 6,
        out_specs=[hbm] * 20 + [vmem],
        scratch_shapes=[
            pltpu.SemaphoreType.DMA((moves,)),
            pltpu.SemaphoreType.DMA((moves,)),
            pltpu.SemaphoreType.DMA((9 + 2 + 3 + 6 + 10,)),
        ]
        + held,
        compiler_params=pltpu.CompilerParams(
            collective_id=1, has_side_effects=True, vmem_limit_bytes=62 * 2**20
        ),
        cost_estimate=pl.CostEstimate(flops=flops, bytes_accessed=10**8, transcendentals=10**7),
    )(*shards, *quarters, inputs, cotangent, *turns, self_bias, cross_bias, memory)
    return made[:9], made[9:19], made[19], made[20]


def pair_rows(own):
    return jnp.concatenate([own, swap(own, "tensor")], axis=0)


def group_rows(own):
    both = jnp.stack([own, swap(own, "x")])
    other = swap(both, "tensor")
    return jnp.concatenate([both[0], other[0], both[1], other[1]], axis=0)


def spread_pair(left, right_t):
    rows = left.shape[0] // 2
    got = swap(nt(left[rows:], right_t), "tensor")
    return nt(left[:rows], right_t) + got


def spread_group(product):
    quarter = product.rows // 4
    far_send = product(3 * quarter, quarter)
    far = product(2 * quarter, quarter) + swap(far_send, "tensor")
    got_far = swap(far.astype(BF), "x")
    near = product(0, quarter) + swap(product(quarter, quarter), "tensor")
    return near + got_far.astype(F32)


class Product:
    def __init__(self, terms, transposed):
        self.terms = terms
        self.transposed = transposed
        self.rows = terms[0][0].shape[0]

    def __call__(self, first, count):
        total = None
        for left, right in self.terms:
            part = (nt if self.transposed else nn)(left[first : first + count], right)
            total = part if total is None else total + part
        return total


def per_device(
    inputs,
    cotangent,
    context,
    context_live,
    lengths,
    threshold,
    self_gain,
    self_bias,
    self_query,
    self_key,
    self_value,
    self_output,
    cross_gain,
    cross_bias,
    cross_query,
    cross_key,
    cross_value,
    cross_output,
    feed_gain,
    feed_bias,
    gate_weight,
    up_weight,
    down_weight,
):
    zs = lax.axis_size("z")
    x_at = lax.axis_index("x")
    t_at = lax.axis_index("tensor")
    width = inputs.shape[1]
    rows = inputs.shape[0]
    seq_len = 2 * rows
    inner = self_query.shape[1]
    heads_here = inner // HEAD_DIM
    ff = gate_weight.shape[1] // 2
    shard_rows = self_query.shape[0]

    quarters = [gate_weight, up_weight, down_weight.T]
    vector_list = [self_gain, self_bias, cross_gain, cross_bias, feed_gain, feed_bias]
    stream = inputs.astype(F32)
    local = jnp.arange(rows)
    places = jnp.concatenate([t_at * rows + local, (1 - t_at) * rows + local])
    turns = turn_tables(places.astype(F32))
    self_bias_row = jnp.where(places < lengths[0], 0.0, NEGATIVE).astype(F32)
    tokens = context.shape[1]
    token_rows = -(-tokens // 128) * 128
    cross_bias_row = jnp.pad(
        jnp.where(context_live[0] > 0, 0.0, NEGATIVE).astype(F32),
        (0, token_rows - tokens),
        constant_values=NEGATIVE,
    )
    memory = jnp.pad(context[0], ((0, token_rows - tokens), (0, 0)))
    pairs = inner // (2 * HEAD_DIM)

    if shard_rows % 32 == 0:
        vectors = jnp.pad(jnp.stack(vector_list, axis=1).astype(F32), ((0, 0), (0, 122)))
        spread, made, cot_group, crest = forward(
            [
                vectors,
                self_query,
                self_key,
                self_value,
                self_output.T,
                cross_query,
                cross_key,
                cross_value,
                cross_output.T,
            ],
            quarters,
            inputs,
            cotangent,
            turns,
            self_bias_row[None],
            cross_bias_row[None],
            memory,
            zs,
        )
        norms, in_weight, self_out_t, cross_in, memory_weight, cross_out_t = spread[:6]
        norms = norms.reshape(width, -1).T
        (
            normed_self,
            taken,
            mixed_self,
            stream_cross,
            normed_cross,
            query_cross,
            taken_cross,
            mixed_cross,
            stream_feed,
            normed_feed,
        ) = made
        gate_full, up_full, down_t = spread[6:]
        normed_cross = normed_cross.reshape(seq_len, width)
        normed_feed, cot_group = (v.reshape(-1, width) for v in (normed_feed, cot_group))
    else:
        vectors = jnp.stack(vector_list).astype(F32)
        vectors = jnp.pad(vectors, ((0, 2), (0, 128 - shard_rows)))
        (norms, in_weight, self_out_t, cross_in, memory_weight, cross_out_t, gate_full, up_full, down_t) = (
            gather_all(
                [
                    [vectors],
                    [self_query, self_key, self_value],
                    [self_output.T],
                    [cross_query],
                    [cross_key, cross_value],
                    [cross_output.T],
                ],
                quarters,
                zs,
            )
        )
        norms = norms.reshape(-1, 8, 128)[:, :6, :shard_rows].transpose(1, 0, 2).reshape(6, width)
        in_weight, memory_weight = in_weight.reshape(width, -1), memory_weight.reshape(-1, 2 * inner)
        self_out_t, cross_in, cross_out_t, gate_full, up_full, down_t = (
            w.reshape(width, -1)
            for w in (self_out_t, cross_in, cross_out_t, gate_full, up_full, down_t)
        )
        cot_group = group_rows(cotangent)
        all_inputs = pair_rows(inputs)
        normed, _, _ = norm_forward(all_inputs.astype(F32), norms[0], norms[1])
        normed_self = normed.astype(BF)
        taken = project(normed_self, in_weight, turns, 2 * inner)
        self_bias_rows = jnp.broadcast_to(self_bias_row, (pairs, seq_len))
        mixed_self, peak_self = attend(taken, taken, taken, self_bias_rows, (0, pairs, 2 * pairs))
        stream_cross = stream + spread_pair(mixed_self, self_out_t)
        normed, _, _ = norm_forward(stream_cross, norms[2], norms[3])
        normed_cross = pair_rows(normed.astype(BF))
        query_cross = nn(normed_cross, cross_in).astype(BF)
        taken_cross = nn(memory, memory_weight).astype(BF)
        cross_bias_rows = jnp.broadcast_to(cross_bias_row, (pairs, token_rows))
        mixed_cross, peak_cross = attend(
            query_cross, taken_cross, taken_cross, cross_bias_rows, (0, 0, pairs)
        )
        stream_feed = stream_cross + spread_pair(mixed_cross, cross_out_t)
        normed, _, _ = norm_forward(stream_feed, norms[4], norms[5])
        normed_feed = group_rows(normed.astype(BF))
        crest = jnp.pad(
            jnp.maximum(peak_self, peak_cross)[None], ((0, 7), (0, 128 - heads_here))
        )
    in_weight, self_out_t, cross_in, cross_out_t, gate_full, up_full, down_t = (
        w.reshape(width, -1)
        for w in (in_weight, self_out_t, cross_in, cross_out_t, gate_full, up_full, down_t)
    )
    unit_cross, inverse_cross = unit_rows_of(stream_cross)
    unit_feed, inverse_feed = unit_rows_of(stream_feed)
    gate_pre = nn(normed_feed, gate_full)
    upward = nn(normed_feed, up_full)
    sigmoid_gate = jax.nn.sigmoid(gate_pre)
    hidden = (gate_pre * sigmoid_gate * upward).astype(BF)
    result = (stream_feed + spread_group(Product([(hidden, down_t)], True))).astype(BF)

    down_keep, down_got = reduce_pair(cot_group, hidden, zs)
    grad_hidden = nn(cot_group, down_t)
    grad_gate = grad_hidden * upward * sigmoid_gate * (1.0 + gate_pre * (1.0 - sigmoid_gate))
    grad_upward = grad_hidden * gate_pre * sigmoid_gate
    grad_gate = grad_gate.astype(BF)
    grad_upward = grad_upward.astype(BF)
    grad_normed = spread_group(Product([(grad_gate, gate_full), (grad_upward, up_full)], True))
    gate_keep, gate_got = reduce_pair(normed_feed, grad_gate, zs)
    up_keep, up_got = reduce_pair(normed_feed, grad_upward, zs)
    stream_part, grad_feed_gain, grad_feed_bias = norm_backward(
        grad_normed, unit_feed, inverse_feed, norms[4]
    )
    grad_stream = cotangent.astype(F32) + stream_part
    grad_full = pair_rows(grad_stream.astype(BF))
    sum_cross_output = reduce_full(grad_full, mixed_cross, zs).astype(F32)
    grad_mixed = nn(grad_full, cross_out_t).astype(BF)
    grad_query, grad_keys, grad_values = attend_back(
        query_cross, taken_cross, taken_cross, grad_mixed, cross_bias_row[:, None], (0, 0, pairs), None
    )
    grad_normed = spread_pair(grad_query, cross_in)
    sum_cross_query = reduce_full(normed_cross, grad_query, zs).astype(F32)
    part_memory = tn(memory, jnp.concatenate([grad_keys, grad_values], axis=1))
    stream_part, grad_cross_gain, grad_cross_bias = norm_backward(
        grad_normed, unit_cross, inverse_cross, norms[2]
    )
    grad_stream = grad_stream + stream_part
    grad_full = pair_rows(grad_stream.astype(BF))
    part_self_output = tn(grad_full, mixed_self)
    grad_mixed = nn(grad_full, self_out_t).astype(BF)
    grad_parts = attend_back(
        taken, taken, taken, grad_mixed, self_bias_row[:, None], (0, pairs, 2 * pairs), turns
    )
    grad_in = jnp.concatenate(grad_parts, axis=1)
    part_query, part_key, part_value = (tn(normed_self, part) for part in grad_parts)
    grad_normed = spread_pair(grad_in, in_weight)
    unit_self, inverse_self = unit_rows_of(stream)
    stream_part, grad_self_gain, grad_self_bias = norm_backward(
        grad_normed, unit_self, inverse_self, norms[0]
    )
    grad_stream = grad_stream + stream_part

    vector_sums = jnp.stack(
        [
            grad_self_gain,
            grad_self_bias,
            grad_cross_gain,
            grad_cross_bias,
            grad_feed_gain,
            grad_feed_bias,
        ]
    ).reshape(6, -1, shard_rows)
    vector_sums = vector_sums + swap(vector_sums, "tensor")
    vector_sums = jnp.pad(
        vector_sums.transpose(1, 0, 2), ((0, 0), (0, 2), (0, 128 - shard_rows))
    ).reshape(zs, 2, 2, 8, 128)

    def blocks(part):
        return part.astype(BF).reshape(zs, 2, 2, -1, part.shape[1])

    (vector_sums, sum_query, sum_key, sum_value, sum_self_output, sum_memory, crest) = (
        scatter_all(
            [
                vector_sums,
                blocks(part_query),
                blocks(part_key),
                blocks(part_value),
                blocks(part_self_output),
                blocks(part_memory),
            ],
            ["x", "x", "y", "x", "y", "z"],
            crest,
            zs,
        )
    )
    vector_sums = vector_sums[:, :shard_rows]
    peaks = crest[0, :heads_here]
    factor = jnp.sqrt(threshold[0] / jnp.maximum(peaks, threshold[0]))
    columns = jnp.repeat(factor, HEAD_DIM)[None, :]

    def side_by_side(kept, got):
        low = jnp.where(x_at == 0, kept, got).astype(F32)
        high = jnp.where(x_at == 0, got, kept).astype(F32)
        return jnp.concatenate([low, high], axis=1)

    down_sum = side_by_side(down_keep, down_got).T
    gate_sum = side_by_side(gate_keep, gate_got)
    up_sum = side_by_side(up_keep, up_got)
    return (
        result,
        grad_stream,
        vector_sums[0],
        vector_sums[1],
        sum_query,
        sum_key,
        sum_value,
        sum_self_output.T,
        vector_sums[2],
        vector_sums[3],
        sum_cross_query,
        sum_memory[:, :inner],
        sum_memory[:, inner:],
        sum_cross_output.T,
        vector_sums[4],
        vector_sums[5],
        gate_sum,
        up_sum,
        down_sum,
        peaks,
        self_query.astype(F32) * columns,
        self_key.astype(F32) * columns,
        cross_query.astype(F32) * columns,
        cross_key.astype(F32) * columns,
    )


def solution(mesh):
    count = mesh.shape["dp"]
    mesh = Mesh(
        mesh.devices.reshape(count // 4, 2, 2, mesh.shape["tensor"]), ("z", "y", "x", "tensor")
    )
    dp = ("z", "y", "x")
    both = P(dp + ("tensor",), None)
    split = P(dp)
    row_major = P(dp, "tensor")
    column_major = P("tensor", dp)
    in_specs = (
        both,
        both,
        P(dp, None, None),
        P(dp, None),
        split,
        P(),
        split,
        split,
        row_major,
        row_major,
        row_major,
        column_major,
        split,
        split,
        row_major,
        row_major,
        row_major,
        column_major,
        split,
        split,
        row_major,
        row_major,
        column_major,
    )
    out_specs = (
        both,
        both,
        split,
        split,
        row_major,
        row_major,
        row_major,
        column_major,
        split,
        split,
        row_major,
        row_major,
        row_major,
        column_major,
        split,
        split,
        row_major,
        row_major,
        column_major,
        P("tensor"),
        row_major,
        row_major,
        row_major,
        row_major,
    )
    return jax.shard_map(
        per_device, mesh=mesh, in_specs=in_specs, out_specs=out_specs, check_vma=False
    )
```

```python
import functools

import jax
import jax.numpy as jnp
from jax import lax
from jax.experimental import pallas as pl
from jax.experimental.pallas import tpu as pltpu
from jax.sharding import Mesh
from jax.sharding import PartitionSpec as P

HEAD_DIM = 64
ROT_DIM = 32
EPSILON = 1e-05
NEGATIVE = -1e30
BF = jnp.bfloat16
F32 = jnp.float32


def swap(value, axis):
    return lax.ppermute(value, axis, [(0, 1), (1, 0)])


def pick(value, index, dim):
    return lax.dynamic_index_in_dim(value, index, dim, keepdims=False)


class Lanes:
    def __init__(self, send_sems, recv_sems, local_sems, zs):
        self.send_sems, self.recv_sems, self.local_sems = send_sems, recv_sems, local_sems
        self.used = self.used_local = 0
        self.z = lax.axis_index("z")
        self.y = lax.axis_index("y")
        self.x = lax.axis_index("x")
        self.zs = zs

    def local(self):
        self.used_local += 1
        return self.local_sems.at[self.used_local - 1]

    def copy(self, source, target, device):
        return self.copies([source], target, device)[0]

    def copies(self, sources, target, device):
        slot = self.used
        self.used += 1
        return [
            pltpu.make_async_remote_copy(
                src_ref=source,
                dst_ref=target,
                send_sem=self.send_sems.at[slot],
                recv_sem=self.recv_sems.at[slot],
                device_id=device,
                device_id_type=pl.DeviceIdType.MESH,
            )
            for source in sources
        ]


def guarded(condition, action):
    if condition is None:
        action()
    else:
        pl.when(condition)(action)


class Move:
    def __init__(self, copy, sends, receives):
        self.copy_, self.sends, self.receives = copy, sends, receives

    def start(self):
        guarded(self.sends, self.copy_.start)

    def arrived(self):
        guarded(self.receives, self.copy_.wait_recv)

    def sent(self):
        guarded(self.sends, self.copy_.wait_send)


class Gather:
    def __init__(self, lanes, whole):
        zs, z, y, x = lanes.zs, lanes.z, lanes.y, lanes.x
        own = whole.at[z, y, x]

        def block(zz, yy):
            return whole.at[zz, yy, x]

        def along(source, target, axis, to, sends=None, receives=None):
            return Move(lanes.copy(source, target, {axis: to}), sends, receives)

        self.first = [
            along(own, block(z, y), "y", 1 - y),
            along(own, block(z, y), "x", 1 - x),
        ]
        self.far = [[along(block(z, 1 - y), block(z, 1 - y), "x", 1 - x)]]
        self.steps = []
        for k in range(zs - 1):
            right, left = jnp.maximum(z - k, 0), jnp.minimum(z + k, zs - 1)
            step = []
            for zz, to, sends, receives, got in (
                (right, z + 1, (z >= k) & (z < zs - 1), z >= k + 1, jnp.maximum(z - 1 - k, 0)),
                (left, z - 1, (z + k < zs) & (z > 0), z + k + 1 < zs, jnp.minimum(z + 1 + k, zs - 1)),
            ):
                source = own if k == 0 else block(zz, y)
                move = along(source, block(zz, y), "z", to, sends, receives)
                follow = [
                    along(block(got, y), block(got, y), "y", 1 - y, receives, receives),
                    along(block(got, y), block(got, y), "x", 1 - x, receives, receives),
                    along(block(got, 1 - y), block(got, 1 - y), "x", 1 - x, receives, receives),
                ]
                step.append((move, follow))
            self.steps.append(step)

    def begin(self):
        for move, _ in self.steps[0]:
            move.start()
        for move in self.first:
            move.start()

    def step(self, k, side):
        move, follow = self.steps[k][side]
        move.arrived()
        if k + 1 < len(self.steps):
            self.steps[k + 1][side][0].start()
        follow[0].start()
        follow[1].start()

    def far_first(self):
        self.first[0].arrived()
        self.far[0][0].start()

    def far_step(self, k, side):
        _, follow = self.steps[k][side]
        follow[0].arrived()
        follow[2].start()

    def landed(self):
        self.first[1].arrived()
        self.far[0][0].arrived()
        for step in self.steps:
            for _, follow in step:
                follow[1].arrived()
                follow[2].arrived()

    def sent(self):
        for move in self.first + self.far[0]:
            move.sent()
        for step in self.steps:
            for move, follow in step:
                move.sent()
                for other in follow:
                    other.sent()


class PairGather:
    def __init__(self, lanes, shard, whole, y_first):
        zs, z, y, x = lanes.zs, lanes.z, lanes.y, lanes.x
        ff = whole.shape[-1]
        kept = shard.at[:, pl.ds(pl.multiple_of(x * ff, ff), ff)]
        sent = shard.at[:, pl.ds(pl.multiple_of((1 - x) * ff, ff), ff)]
        self.y_first = y_first

        def along(piece, axis, to, sends=None, receives=None):
            return Move(lanes.copy(piece, piece, {axis: to}), sends, receives)

        self.swap = Move(lanes.copy(sent, whole.at[z, y, x], {"x": 1 - x}), None, None)
        self.local = pltpu.make_async_copy(kept, whole.at[z, y, x], lanes.local())
        self.own_y = along(whole.at[z, y], "y", 1 - y)
        self.steps = []
        for k in range(zs - 1):
            step = []
            for zz, to, sends, receives, got in (
                (jnp.maximum(z - k, 0), z + 1, (z >= k) & (z < zs - 1), z >= k + 1, jnp.maximum(z - 1 - k, 0)),
                (jnp.minimum(z + k, zs - 1), z - 1, (z + k < zs) & (z > 0), z + k + 1 < zs, jnp.minimum(z + 1 + k, zs - 1)),
            ):
                piece = whole.at[zz] if y_first else whole.at[zz, y]
                move = along(piece, "z", to, sends, receives)
                follow = [] if y_first else [along(whole.at[got, y], "y", 1 - y, receives, receives)]
                step.append((move, follow))
            self.steps.append(step)

    def begin(self):
        self.swap.start()
        self.local.start()

    def far_first(self):
        self.swap.arrived()
        self.local.wait()
        self.own_y.start()
        if not self.y_first:
            for move, _ in self.steps[0]:
                move.start()

    def own_y_arrived(self):
        self.own_y.arrived()
        if self.y_first:
            for move, _ in self.steps[0]:
                move.start()

    def step(self, k, side):
        move, follow = self.steps[k][side]
        move.arrived()
        if k + 1 < len(self.steps):
            self.steps[k + 1][side][0].start()
        for other in follow:
            other.start()

    def landed(self):
        if not self.y_first:
            self.own_y.arrived()
        for step in self.steps:
            for move, follow in step:
                for other in follow:
                    other.arrived()

    def sent(self):
        self.swap.sent()
        self.own_y.sent()
        for step in self.steps:
            for move, follow in step:
                move.sent()
                for other in follow:
                    other.sent()


def greet(zs, mates=False):
    z, y, x = lax.axis_index("z"), lax.axis_index("y"), lax.axis_index("x")
    barrier = pltpu.get_barrier_semaphore()

    def signal(device):
        pl.semaphore_signal(barrier, inc=1, device_id=device, device_id_type=pl.DeviceIdType.MESH)

    signal({"x": 1 - x})
    signal({"y": 1 - y})
    pl.when(z > 0)(lambda: signal({"z": z - 1}))
    pl.when(z < zs - 1)(lambda: signal({"z": z + 1}))
    if mates:
        signal({"tensor": 1 - lax.axis_index("tensor")})
    peers = (3 if mates else 2) + (z > 0).astype(jnp.int32) + (z < zs - 1).astype(jnp.int32)
    pl.semaphore_wait(barrier, peers)


def gather_kernel(zs, groups, pairs, *refs):
    shards = sum(groups)
    owns, pair_in = refs[:shards], refs[shards : shards + pairs]
    refs = refs[shards + pairs :]
    outs = refs[: len(groups) + pairs]
    lanes = Lanes(*refs[len(groups) + pairs :], zs)
    z, y, x = lanes.z, lanes.y, lanes.x
    pieces, at = [], 0
    for count, whole in zip(groups, outs):
        width = whole.shape[-1] // count
        for i in range(count):
            target = whole.at[z, y, x, :, pl.ds(i * width, width)]
            pieces.append(pltpu.make_async_copy(owns[at], target, lanes.local()))
            at += 1
    for piece in pieces:
        piece.start()
    greet(zs)
    gathers = [Gather(lanes, whole) for whole in outs[: len(groups)]]
    quarters = [
        PairGather(lanes, pair_in[i], outs[len(groups) + i], i == 0) for i in range(pairs)
    ]
    for quarter in quarters:
        quarter.begin()
    for piece in pieces:
        piece.wait()
    for gather in gathers:
        gather.begin()
    for quarter in quarters:
        quarter.far_first()
    for gather in gathers:
        gather.far_first()
    for k, side in [(k, side) for k in range(zs - 1) for side in range(2)]:
        for gather in gathers:
            gather.step(k, side)
        for quarter in quarters:
            if quarter.y_first:
                if k == 0 and side == 0:
                    quarter.own_y_arrived()
            else:
                quarter.step(k, side)
        for gather in gathers:
            gather.far_step(k, side)
        for quarter in quarters:
            if quarter.y_first:
                quarter.step(k, side)
    for item in gathers + quarters:
        item.landed()
        item.sent()


def gather_all(groups, quarters, zs):
    flat = [shard for group in groups for shard in group] + list(quarters)
    outs = []
    for group in groups:
        columns = sum(shard.shape[1] for shard in group)
        outs.append(
            jax.ShapeDtypeStruct((zs, 2, 2, group[0].shape[0], columns), group[0].dtype)
        )
    for shard in quarters:
        outs.append(
            jax.ShapeDtypeStruct((zs, 2, 2, shard.shape[0], shard.shape[1] // 2), shard.dtype)
        )
    count, pairs = len(groups), len(quarters)
    moves = count * (3 + 8 * (zs - 1)) + pairs * (2 + 4 * (zs - 1))
    hbm = pl.BlockSpec(memory_space=pltpu.HBM)
    return pl.pallas_call(
        functools.partial(gather_kernel, zs, tuple(len(group) for group in groups), pairs),
        out_shape=outs,
        in_specs=[hbm] * len(flat),
        out_specs=[hbm] * len(outs),
        scratch_shapes=[
            pltpu.SemaphoreType.DMA((moves,)),
            pltpu.SemaphoreType.DMA((moves,)),
            pltpu.SemaphoreType.DMA((len(flat),)),
        ],
        compiler_params=pltpu.CompilerParams(collective_id=1, has_side_effects=True),
    )(*flat)


def plus(*terms):
    total = terms[0].astype(F32)
    for term in terms[1:]:
        total = total + term.astype(F32)
    return total


def ends_first(zs):
    order = []
    for i in range(zs // 2):
        order += [zs - 1 - i, i]
    return order


class Line:
    def __init__(self, lanes, part, from_left, from_right):
        zs, z = lanes.zs, lanes.z
        self.zs, self.z, self.part = zs, z, part
        self.from_left, self.from_right = from_left, from_right
        self.right, self.left = {}, {}
        for d in ends_first(zs):
            after, before = jnp.minimum(z + 1, zs - 1), jnp.maximum(z - 1, 0)
            self.right[d] = lanes.copies(
                (part.at[d], from_left.at[d]), from_left.at[d], {"z": after}
            )
            self.left[d] = lanes.copies(
                (part.at[d], from_right.at[d]), from_right.at[d], {"z": before}
            )

    def pass_on(self, d):
        for moves, inbox, sends, edge in (
            (self.right[d], self.from_left, self.z < d, self.z == 0),
            (self.left[d], self.from_right, self.z > d, self.z == self.zs - 1),
        ):

            @pl.when(sends & edge)
            def _():
                moves[0].start()

            @pl.when(sends & jnp.logical_not(edge))
            def _():
                moves[1].wait_recv()
                inbox[d] = plus(self.part[d], inbox[d]).astype(inbox.dtype)
                moves[1].start()

    def total(self, sink):
        for d in range(self.zs):

            @pl.when(self.z == d)
            def _():
                terms = [self.part[d]]
                if d > 0:
                    self.right[d][0].wait_recv()
                    terms.append(self.from_left[d])
                if d < self.zs - 1:
                    self.left[d][0].wait_recv()
                    terms.append(self.from_right[d])
                sink[...] = plus(*terms).astype(sink.dtype)

    def finish(self):
        for d in ends_first(self.zs):
            pl.when(self.z < d)(self.right[d][0].wait_send)
            pl.when(self.z > d)(self.left[d][0].wait_send)


class Scatter:
    def __init__(self, lanes, part, held, out, first):
        zs, z, y, x = lanes.zs, lanes.z, lanes.y, lanes.x
        got, near, from_left, from_right, ready = held
        second = "y" if first == "x" else "x"
        self.lanes, self.part, self.got, self.near, self.ready, self.out = (
            lanes, part, got, near, ready, out,
        )
        f, s = (x, y) if first == "x" else (y, x)
        self.f, self.s = f, s

        def block(zz, a, b):
            return part.at[zz, b, a] if first == "x" else part.at[zz, a, b]

        self.block = block
        self.one, self.two = {}, {}
        for zz in ends_first(zs):
            for j, b in enumerate((1 - s, s)):
                self.one[zz, j] = Move(
                    lanes.copy(block(zz, 1 - f, b), got.at[zz, j], {first: 1 - f}), None, None
                )
        for zz in ends_first(zs):
            self.two[zz] = Move(
                lanes.copy(got.at[zz, 0], near.at[zz], {second: 1 - s}), None, None
            )
        self.line = Line(lanes, ready, from_left, from_right)

    def begin(self, zz):
        for j in range(2):
            self.one[zz, j].start()

    def second(self, zz):
        self.one[zz, 0].arrived()
        mine, got = self.block(zz, self.f, 1 - self.s), self.got
        got[zz, 0] = plus(mine[...], got[zz, 0]).astype(got.dtype)
        self.two[zz].start()

    def third(self, zz):
        self.one[zz, 1].arrived()
        self.two[zz].arrived()
        mine = self.block(zz, self.f, self.s)
        self.ready[zz] = plus(mine[...], self.got[zz, 1], self.near[zz]).astype(self.ready.dtype)
        self.line.pass_on(zz)

    def finish(self):
        self.line.total(self.out)
        self.line.finish()
        for move in list(self.one.values()) + list(self.two.values()):
            move.sent()


class ScatterZ:
    def __init__(self, lanes, part, held, out):
        y, x = lanes.y, lanes.x
        from_left, from_right, held_z, near, last = held
        self.lanes, self.sum_z, self.near, self.last, self.out = lanes, held_z, near, last, out
        self.line = Line(lanes, part, from_left, from_right)
        self.two = Move(lanes.copy(held_z.at[1 - y], near, {"y": 1 - y}), None, None)
        self.three = Move(lanes.copy(near.at[1 - x], last, {"x": 1 - x}), None, None)

    def pass_on(self, d):
        self.line.pass_on(d)

    def total(self):
        self.line.total(self.sum_z)
        self.two.start()

    def after(self):
        self.two.arrived()
        self.near[...] = plus(self.sum_z[self.lanes.y], self.near[...]).astype(self.near.dtype)
        self.three.start()

    def finish(self):
        self.three.arrived()
        self.out[...] = plus(self.near[self.lanes.x], self.last[...]).astype(self.out.dtype)
        self.line.finish()
        self.two.sent()
        self.three.sent()


class Crest:
    def __init__(self, lanes, own, held, out):
        zs, z, y, x = lanes.zs, lanes.z, lanes.y, lanes.x
        near_x, near_y, mine_x, mine_y, right, left, inbox_r, inbox_l = (
            held.at[i] for i in range(8)
        )
        self.zs, self.z, self.own, self.out = zs, z, own, out
        self.near_x, self.near_y, self.mine_x, self.mine_y = near_x, near_y, mine_x, mine_y
        self.ways = (
            (right, inbox_r, z > 0, z < zs - 1),
            (left, inbox_l, z < zs - 1, z > 0),
        )
        self.one = Move(lanes.copy(own, near_x, {"x": 1 - x}), None, None)
        self.two = Move(lanes.copy(mine_x, near_y, {"y": 1 - y}), None, None)
        self.moves = [
            Move(lanes.copy(right, inbox_r, {"z": jnp.minimum(z + 1, zs - 1)}), z < zs - 1, z > 0),
            Move(lanes.copy(left, inbox_l, {"z": jnp.maximum(z - 1, 0)}), z > 0, z < zs - 1),
        ]

    def second(self):
        self.one.arrived()
        self.mine_x[...] = jnp.maximum(self.own[...], self.near_x[...])
        self.two.start()

    def finish(self):
        self.two.arrived()
        self.mine_y[...] = jnp.maximum(self.mine_x[...], self.near_y[...])
        self.out[...] = self.mine_y[...]
        for move, (held, inbox, has_before, has_after) in zip(self.moves, self.ways):

            @pl.when(has_before)
            def _():
                move.copy_.wait_recv()
                self.out[...] = jnp.maximum(self.out[...], inbox[...])
                held[...] = jnp.maximum(self.mine_y[...], inbox[...])

            @pl.when(jnp.logical_not(has_before))
            def _():
                held[...] = self.mine_y[...]

            move.start()
        for move in [self.one, self.two] + self.moves:
            move.sent()


def scatter_kernel(zs, orders, *refs):
    count = len(orders)
    parts, crest_in, refs = refs[:count], refs[count], refs[count + 1 :]
    outs, crest_out, rest = refs[:count], refs[count], list(refs[count + 1 :])
    send_sems, recv_sems = rest[:2]
    rest = rest[2:]
    lanes = Lanes(send_sems, recv_sems, None, zs)
    greet(zs)
    full, zfirst = [], []
    for i, order in enumerate(orders):
        held, rest = rest[:5], rest[5:]
        if order == "z":
            zfirst.append(ScatterZ(lanes, parts[i], held, outs[i]))
        else:
            full.append(Scatter(lanes, parts[i], held, outs[i], order))
    crest = Crest(lanes, crest_in, rest[0], crest_out)
    crest.one.start()
    order = ends_first(zs)
    for i in range(zs + 3):
        for item in full:
            if i < zs:
                item.begin(order[i])
        if i == 1:
            crest.second()
        if i < zs:
            for item in zfirst:
                item.pass_on(order[i])
        for item in full:
            if 2 <= i < zs + 2:
                item.second(order[i - 2])
        if i == zs:
            for item in zfirst:
                item.total()
        for item in full:
            if 3 <= i:
                item.third(order[i - 3])
    crest.finish()
    for item in zfirst:
        item.after()
    for item in full:
        item.finish()
    for item in zfirst:
        item.finish()


def scatter_all(parts, orders, crest, zs):
    scratch, moves = [], 4
    for part, order in zip(parts, orders):
        block = part.shape[3:]
        if order == "z":
            shapes = [(zs, 2, 2) + block] * 2 + [(2, 2) + block, (2,) + block, block]
            moves += 2 * zs + 2
        else:
            shapes = [(zs, 2) + block] + [(zs,) + block] * 4
            moves += 5 * zs
        scratch += [pltpu.VMEM(shape, part.dtype) for shape in shapes]
    vmem = pl.BlockSpec(memory_space=pltpu.VMEM)
    return pl.pallas_call(
        functools.partial(scatter_kernel, zs, orders),
        out_shape=[jax.ShapeDtypeStruct(part.shape[3:], F32) for part in parts]
        + [jax.ShapeDtypeStruct(crest.shape, F32)],
        in_specs=[vmem] * (len(parts) + 1),
        out_specs=[vmem] * (len(parts) + 1),
        scratch_shapes=[pltpu.SemaphoreType.DMA((moves,)), pltpu.SemaphoreType.DMA((moves,))]
        + scratch
        + [pltpu.VMEM((8,) + crest.shape, F32)],
        compiler_params=pltpu.CompilerParams(
            collective_id=2, has_side_effects=True, vmem_limit_bytes=56 * 2**20
        ),
    )(*parts, crest)


def nn(left, right):
    return lax.dot_general(left, right, (((1,), (0,)), ((), ())), preferred_element_type=F32)


def nt(left, right):
    return lax.dot_general(left, right, (((1,), (1,)), ((), ())), preferred_element_type=F32)


def tn(left, right):
    return lax.dot_general(left, right, (((0,), (0,)), ((), ())), preferred_element_type=F32)


def after(value, *others):
    return lax.optimization_barrier((value, others))[0]


class FullSum:
    def __init__(self, left, right, zs):
        self.zs = zs
        held = tn(left, right).astype(BF)
        self.held = held.reshape(2 * zs, 2, -1, held.shape[1])
        self.x, self.y = lax.axis_index("x"), lax.axis_index("y")
        self.got = swap(pick(self.held, 1 - self.x, 1), "x")

    def second(self, *others):
        got = after(self.got, others)
        held = pick(self.held, self.x, 1).astype(F32) + got.astype(F32)
        self.held = held.astype(BF).reshape(self.zs, 2, -1, held.shape[-1])
        self.got = swap(pick(self.held, 1 - self.y, 1), "y")

    def third(self, *others):
        got = after(self.got, others)
        held = pick(self.held, self.y, 1).astype(F32) + got.astype(F32)
        return lax.psum_scatter(held.astype(BF), "z", scatter_dimension=0, tiled=False)


class PairSum:
    def __init__(self, left, right, zs):
        held = tn(left, right).astype(BF)
        self.held = held.reshape(zs, 2, -1, held.shape[1])
        self.y = lax.axis_index("y")
        self.got = swap(pick(self.held, 1 - self.y, 1), "y")

    def second(self, *others):
        got = after(self.got, others)
        held = pick(self.held, self.y, 1).astype(F32) + got.astype(F32)
        held = lax.psum_scatter(held.astype(BF), "z", scatter_dimension=0, tiled=False)
        self.held = held.reshape(2, -1, held.shape[-1])

    def third(self):
        at = lax.axis_index("x")
        return pick(self.held, at, 0), swap(pick(self.held, 1 - at, 0), "x")


def norm_forward(stream, gain_vec, bias_vec):
    average = jnp.mean(stream, axis=-1, keepdims=True)
    centred = stream - average
    inverse = lax.rsqrt(jnp.mean(centred * centred, axis=-1, keepdims=True) + EPSILON)
    unit_rows = centred * inverse
    return (unit_rows * gain_vec + bias_vec, unit_rows, inverse)


def unit_rows_of(stream):
    _, unit_rows, inverse = norm_forward(stream, 1.0, 0.0)
    return unit_rows, inverse


def norm_backward(incoming, unit_rows, inverse, gain_vec):
    gain_grad = jnp.sum(incoming * unit_rows, axis=0)
    bias_grad = jnp.sum(incoming, axis=0)
    scaled = incoming * gain_vec
    stream_grad = inverse * (
        scaled
        - jnp.mean(scaled, axis=-1, keepdims=True)
        - unit_rows * jnp.mean(scaled * unit_rows, axis=-1, keepdims=True)
    )
    return (stream_grad, gain_grad, bias_grad)


def turn_tables(positions):
    rates = 10000.0 ** (-jnp.arange(0, ROT_DIM, 2).astype(F32) / ROT_DIM)
    angles = positions[:, None] * rates[None, :]
    cosine, sine = jnp.cos(angles), jnp.sin(angles)
    rest = jnp.ones((positions.shape[0], HEAD_DIM - ROT_DIM), F32)
    zero, none = jnp.zeros_like(rest), jnp.zeros_like(sine)
    return (
        jnp.concatenate([cosine, cosine, rest] * 2, axis=1),
        jnp.concatenate([-sine, none, zero] * 2, axis=1),
        jnp.concatenate([none, sine, zero] * 2, axis=1),
    )


def turn(field, cosine, sine_a, sine_b, direction):
    half = ROT_DIM // 2
    width = field.shape[-1]
    ahead = pltpu.roll(field, width - half, 1)
    behind = pltpu.roll(field, half, 1)
    return field * cosine + direction * (ahead * sine_a + behind * sine_b)


def head_lanes(shape, which):
    lanes = lax.broadcasted_iota(jnp.int32, shape, 1)
    return (lanes >= which * HEAD_DIM) & (lanes < (which + 1) * HEAD_DIM)


def attend_tile(query, keys, values, bias):
    scores = nt(query, keys) + bias
    top = jnp.max(scores, axis=-1, keepdims=True)
    weights = jnp.exp(scores - top)
    total = jnp.sum(weights, axis=-1, keepdims=True)
    return nn(weights.astype(BF), values) / total, top


def attend_kernel(q_ref, k_ref, v_ref, bias_ref, mixed_ref, peak_ref):
    rows = q_ref.shape[0]
    tile = rows // 3 if rows % 3 == 0 and (rows // 3) % 16 == 0 else rows
    keys, values, bias = k_ref[...], v_ref[...], bias_ref[...]
    peaks = [None, None]
    for start in range(0, rows, tile):
        query = q_ref[start : start + tile, :] * BF(HEAD_DIM ** (-0.5))
        outs = []
        for which in range(2):
            one = jnp.where(head_lanes(query.shape, which), query, jnp.zeros_like(query))
            out, top = attend_tile(one, keys, values, bias)
            outs.append(out)
            top = jnp.max(top, axis=0, keepdims=True)
            peaks[which] = top if peaks[which] is None else jnp.maximum(peaks[which], top)
        mixed = jnp.where(head_lanes(outs[0].shape, 0), outs[0], outs[1])
        mixed_ref[start : start + tile, :] = mixed.astype(BF)
    spot = head_lanes((8, 2 * HEAD_DIM), 0)
    peak_ref[0] = jnp.where(
        spot, jnp.broadcast_to(peaks[0], spot.shape), jnp.broadcast_to(peaks[1], spot.shape)
    )


def attend(query, keys, values, bias, offsets):
    rows, tokens = query.shape[0], keys.shape[0]
    pairs = bias.shape[0]
    wide = 2 * HEAD_DIM
    mixed, peak = pl.pallas_call(
        attend_kernel,
        grid=(pairs,),
        out_shape=[
            jax.ShapeDtypeStruct((rows, pairs * wide), BF),
            jax.ShapeDtypeStruct((pairs, 8, wide), F32),
        ],
        in_specs=[
            pl.BlockSpec((rows, wide), lambda j: (0, offsets[0] + j)),
            pl.BlockSpec((tokens, wide), lambda j: (0, offsets[1] + j)),
            pl.BlockSpec((tokens, wide), lambda j: (0, offsets[2] + j)),
            pl.BlockSpec((1, tokens), lambda j: (0, 0)),
        ],
        out_specs=[
            pl.BlockSpec((rows, wide), lambda j: (0, j)),
            pl.BlockSpec((1, 8, wide), lambda j: (j, 0, 0)),
        ],
        compiler_params=pltpu.CompilerParams(vmem_limit_bytes=48 * 2**20),
        cost_estimate=pl.CostEstimate(
            flops=8 * rows * tokens * pairs * wide,
            bytes_accessed=4 * (rows + tokens) * pairs * wide,
            transcendentals=2 * pairs * rows * tokens,
        ),
    )(query, keys, values, bias[:1])
    return mixed, peak[:, 0, ::HEAD_DIM].reshape(-1)


def attend_back_kernel(turned, q_ref, k_ref, v_ref, g_ref, bias_ref, *refs):
    if turned:
        cos_ref, sa_ref, sb_ref = refs[:3]
        refs = refs[3:]
    dq_ref, dk_ref, dv_ref, dk_acc, dv_acc = refs
    rows = q_ref.shape[0]
    tile = rows // 3 if rows % 3 == 0 and (rows // 3) % 128 == 0 else rows
    scale = BF(HEAD_DIM ** (-0.5))
    keys, values, bias = k_ref[...], v_ref[...], bias_ref[...]
    for start in range(0, rows, tile):
        part = slice(start, start + tile)
        query, grad = q_ref[part, :] * scale, g_ref[part, :]
        dq = None
        for which in range(2):
            mine = head_lanes(query.shape, which)
            one = jnp.where(mine, query, jnp.zeros_like(query))
            out = jnp.where(mine, grad, jnp.zeros_like(grad))
            scores = nt(keys, one) + bias
            weights = jnp.exp(scores - jnp.max(scores, axis=0, keepdims=True))
            weights = weights * (1.0 / jnp.sum(weights, axis=0, keepdims=True))
            slope = nt(values, out)
            slope = weights * (slope - jnp.sum(weights * slope, axis=0, keepdims=True))
            slope = slope.astype(BF)
            dv = nn(weights.astype(BF), out)
            dk = nn(slope, one)
            other = jnp.where(head_lanes(keys.shape, which), keys, jnp.zeros_like(keys))
            piece = tn(slope, other * scale)
            dq = piece if dq is None else dq + piece
            if start == 0 and which == 0:
                dv_acc[...] = dv
                dk_acc[...] = dk
            else:
                dv_acc[...] += dv
                dk_acc[...] += dk
        if turned:
            dq = turn(dq, cos_ref[part, :], sa_ref[part, :], sb_ref[part, :], -1.0)
        dq_ref[part, :] = dq.astype(BF)
    dk = dk_acc[...]
    if turned:
        dk = turn(dk, cos_ref[...], sa_ref[...], sb_ref[...], -1.0)
    dk_ref[...] = dk.astype(BF)
    dv_ref[...] = dv_acc[...].astype(BF)


def attend_back(query, keys, values, grad, bias_column, offsets, turns):
    rows, tokens = query.shape[0], keys.shape[0]
    wide = 2 * HEAD_DIM
    pairs = grad.shape[1] // wide
    ins = [query, keys, values, grad, bias_column]
    specs = [
        pl.BlockSpec((rows, wide), lambda j: (0, offsets[0] + j)),
        pl.BlockSpec((tokens, wide), lambda j: (0, offsets[1] + j)),
        pl.BlockSpec((tokens, wide), lambda j: (0, offsets[2] + j)),
        pl.BlockSpec((rows, wide), lambda j: (0, j)),
        pl.BlockSpec((tokens, 1), lambda j: (0, 0)),
    ]
    if turns is not None:
        ins += list(turns)
        specs += [pl.BlockSpec((rows, wide), lambda j: (0, 0))] * 3
    return pl.pallas_call(
        functools.partial(attend_back_kernel, turns is not None),
        grid=(pairs,),
        out_shape=[
            jax.ShapeDtypeStruct((rows, pairs * wide), BF),
            jax.ShapeDtypeStruct((tokens, pairs * wide), BF),
            jax.ShapeDtypeStruct((tokens, pairs * wide), BF),
        ],
        in_specs=specs,
        out_specs=[
            pl.BlockSpec((rows, wide), lambda j: (0, j)),
            pl.BlockSpec((tokens, wide), lambda j: (0, j)),
            pl.BlockSpec((tokens, wide), lambda j: (0, j)),
        ],
        scratch_shapes=[pltpu.VMEM((tokens, wide), F32), pltpu.VMEM((tokens, wide), F32)],
        compiler_params=pltpu.CompilerParams(vmem_limit_bytes=48 * 2**20),
        cost_estimate=pl.CostEstimate(
            flops=20 * rows * tokens * pairs * wide,
            bytes_accessed=8 * (rows + tokens) * pairs * wide,
            transcendentals=2 * pairs * rows * tokens,
        ),
    )(*ins)


def project_kernel(turned, x_ref, w_ref, cos_ref, sa_ref, sb_ref, out_ref):
    wide = 2 * HEAD_DIM
    made = nn(x_ref[...], w_ref[...])

    @pl.when(pl.program_id(0) < turned)
    def _():
        for start in range(0, made.shape[1], wide):
            piece = turn(made[:, start : start + wide], cos_ref[...], sa_ref[...], sb_ref[...], 1.0)
            out_ref[:, start : start + wide] = piece.astype(BF)

    @pl.when(pl.program_id(0) >= turned)
    def _():
        out_ref[...] = made.astype(BF)


def project(rows, weight, turns, turned_columns):
    count, depth = rows.shape
    columns = weight.shape[1]
    block = 2 * HEAD_DIM * (2 if turned_columns % (4 * HEAD_DIM) == 0 else 1)
    table = pl.BlockSpec((count, 2 * HEAD_DIM), lambda j: (0, 0))
    return pl.pallas_call(
        functools.partial(project_kernel, turned_columns // block),
        grid=(columns // block,),
        out_shape=jax.ShapeDtypeStruct((count, columns), BF),
        in_specs=[
            pl.BlockSpec((count, depth), lambda j: (0, 0)),
            pl.BlockSpec((depth, block), lambda j: (0, j)),
            table,
            table,
            table,
        ],
        out_specs=pl.BlockSpec((count, block), lambda j: (0, j)),
        compiler_params=pltpu.CompilerParams(vmem_limit_bytes=48 * 2**20),
        cost_estimate=pl.CostEstimate(
            flops=2 * count * depth * columns,
            bytes_accessed=2 * (count * depth + depth * columns + count * columns),
            transcendentals=0,
        ),
    )(rows, weight, *turns)


PLAN = (
    100, 0, 1000, 2000, 2001, 1100, 2100, 2101, 3000, 2010, 2011, 3001, 800, 2110, 2111, 3100,
    2020, 2021, 400, 700, 3101, 2120, 2121, 3010, 3011, 3020, 3021, 2400, 2401, 600, 200, 2410,
    2411, 2420, 2421, 3110, 3111, 2200, 2201, 1400, 3120, 3121, 2210, 2211, 3400, 1800, 3401,
    2220, 2221, 3410, 3411, 500, 1200, 2800, 2801, 3420, 3421, 3200, 3201, 1700, 3210, 3211,
    3220, 3221, 2500, 2501, 2810, 2811, 300, 4000, 2820, 2821, 1500, 2510, 2511, 2520, 2521,
    2300, 2301, 1600, 2310, 2311, 2320, 2321, 2600, 2601, 5700, 4100, -1, -1, -1, 2610, 2611,
    -1, -1, 3500, 3501, 4800, -1, -1, 3510, 3511, -1, 1300, -1, 3520, 3521, -1, 4400, -1, -1,
    -1, 4200, 2700, 2701, 3300, 3301, -1, 3310, 3311, -1, 3320, 3321, -1, 2620, 2621, -1, -1,
    -1, -1, -1, -1, -1, 4500, 2710, 2711, 4300, -1, -1, -1, 4600, -1, -1, -1, -1, -1, -1, -1,
    -1, -1, -1, 2720, 2721, -1, -1, -1, -1, -1, -1,
)


def normalise(stream, gain_vec, bias_vec):
    average = jnp.mean(stream, axis=-1, keepdims=True)
    centred = stream - average
    inverse = lax.rsqrt(jnp.mean(centred * centred, axis=-1, keepdims=True) + EPSILON)
    return centred * inverse * gain_vec + bias_vec


def forward_kernel(zs, *refs):
    refs = list(refs)

    def take(count):
        taken_refs = refs[:count]
        del refs[:count]
        return taken_refs

    shards = take(9)
    quarters_in = take(3)
    inputs_hbm, cot_hbm, cos_ref, sa_ref, sb_ref, self_bias, cross_bias, memory = take(8)
    wholes = take(6)
    quarter_outs = take(3)
    outs = take(10)
    cot_out = take(1)[0]
    peak_out = take(1)[0]
    send_sems, recv_sems, local_sems = take(3)
    w_vec, w_in, w_so, w_cq, w_kv, w_co = take(6)
    (
        x_all, normed_self, taken, mixed_self, stream_cross, normed_cross,
        query_cross, taken_cross, mixed_cross, stream_feed, normed_feed,
        part_send, part_got, vectors, crest,
    ) = take(15)
    lanes = Lanes(send_sems, recv_sems, local_sems, zs)
    z, y, x = lanes.z, lanes.y, lanes.x
    t = lax.axis_index("tensor")
    rows, width = inputs_hbm.shape
    wide = 2 * HEAD_DIM

    def local(source, target):
        return pltpu.make_async_copy(source, target, lanes.local())

    pieces, at = [], 0
    for count, whole in zip((1, 3, 1, 1, 2, 1), wholes):
        columns = whole.shape[-1] // count
        for i in range(count):
            target = whole.at[z, y, x, :, pl.ds(i * columns, columns)]
            pieces.append(local(shards[at], target))
            at += 1
    own_inputs = local(inputs_hbm, x_all.at[0])
    own_cot = local(cot_hbm, cot_out.at[0])
    for piece in pieces + [own_inputs, own_cot]:
        piece.start()
    greet(zs, True)

    def mate(source, target):
        return Move(lanes.copy(source, target, {"tensor": 1 - t}), None, None)

    def across(source, target):
        return Move(lanes.copy(source, target, {"x": 1 - x}), None, None)

    mate_inputs = mate(inputs_hbm, x_all.at[1])
    cot_moves = [
        mate(cot_hbm, cot_out.at[1]),
        across(cot_hbm, cot_out.at[2]),
        mate(cot_out.at[2], cot_out.at[3]),
    ]
    feed_moves = [mate(normed_feed.at[0], normed_feed.at[1])]
    mate_self = mate(part_send, part_got)
    mate_normed = mate(normed_cross.at[0], normed_cross.at[1])
    mate_cross = mate(part_send, part_got)
    gathers = [Gather(lanes, whole) for whole in wholes]
    quarters = [
        PairGather(lanes, quarters_in[i], quarter_outs[i], i == 1) for i in range(3)
    ]
    loads = [
        local(whole, held)
        for whole, held in zip(wholes, (w_vec, w_in, w_so, w_cq, w_kv, w_co))
    ]
    results = (
        normed_self, taken, mixed_self, stream_cross, normed_cross,
        query_cross, taken_cross, mixed_cross, stream_feed, normed_feed,
    )
    saves = [local(held, out) for held, out in zip(results, outs)]

    mate_inputs.start()
    cot_moves[0].start()
    for piece in pieces:
        piece.wait()
    columns = w_in.shape[-1]
    inner = columns // 3
    pairs = inner // wide
    block = 2 * wide
    tile = 128 if rows % 128 == 0 else rows
    chunk = width // zs
    total = 2 * rows
    step = total // 3 if total % 3 == 0 and (total // 3) % 16 == 0 else total
    ready = set()

    def vec(i):
        return vectors[i : i + 1, :]

    def need(*groups):
        assert ready.issuperset(groups)

    def over(count, size, body):
        @pl.loop(0, count // size)
        def _(i):
            body(pl.ds(pl.multiple_of(i * size, size), size), i)

    def attend_all(query_ref, keys_at, values_at, kv_ref, bias_ref, mixed_ref):
        lane = lax.broadcasted_iota(jnp.int32, (8, wide), 1)
        for j in range(pairs):
            at = slice(j * wide, (j + 1) * wide)
            keys_in = slice(keys_at + j * wide, keys_at + (j + 1) * wide)
            values_in = slice(values_at + j * wide, values_at + (j + 1) * wide)

            def body(part, _):
                query = query_ref[part, at] * BF(HEAD_DIM ** (-0.5))
                outs = []
                for which in range(2):
                    mine = head_lanes(query.shape, which)
                    one = jnp.where(mine, query, jnp.zeros_like(query))
                    out, top = attend_tile(
                        one, kv_ref[:, keys_in], kv_ref[:, values_in], bias_ref[...]
                    )
                    outs.append(out)
                    top = jnp.broadcast_to(jnp.max(top, axis=0, keepdims=True), lane.shape)
                    best = jnp.where(lane == 2 * j + which, top, NEGATIVE)
                    crest[...] = jnp.maximum(crest[...], best)
                made = jnp.where(head_lanes(outs[0].shape, 0), outs[0], outs[1])
                mixed_ref[part, at] = made.astype(BF)

            over(total, step, body)
            yield

    def out_project(mixed_ref, weight, move, send, got, base, target):
        for zz in range(zs):
            cols = slice(zz * chunk, (zz + 1) * chunk)

            def body(part, i):
                left = mixed_ref[pl.ds(pl.multiple_of(rows + i * tile, tile), tile), :]
                send[part, cols] = nt(left, weight[zz].reshape(-1, inner)).astype(BF)

            over(rows, tile, body)
        move.start()
        yield
        for zz in range(zs):
            cols = slice(zz * chunk, (zz + 1) * chunk)

            def body(part, _):
                made = nt(mixed_ref[part, :], weight[zz].reshape(-1, inner))
                target[part, cols] = made + base(part, cols)

            over(rows, tile, body)
            yield
        move.arrived()

        def body(part, _):
            target[part, :] = target[part, :] + got[part, :].astype(F32)

        over(rows, tile, body)

    def compute():
        need(0, 1)
        own_inputs.wait()
        mate_inputs.arrived()
        loads[0].wait()
        vectors[...] = jnp.transpose(w_vec[...].reshape(width, w_vec.shape[-1]))
        crest[...] = jnp.full(crest.shape, NEGATIVE, F32)
        for side in range(2):

            def body(part, i):
                made = normalise(x_all[side, part, :].astype(F32), vec(0), vec(1))
                at = pl.multiple_of(side * rows + i * tile, tile)
                normed_self[pl.ds(at, tile), :] = made.astype(BF)

            over(rows, tile, body)
        saves[0].start()
        loads[1].wait()
        yield
        for start in range(0, columns, block):

            def body(part, _):
                weight = w_in[..., start : start + block].reshape(width, block)
                made = nn(normed_self[part, :], weight)
                for at in range(0, block, wide):
                    piece = made[:, at : at + wide]
                    if start + at < 2 * inner:
                        piece = turn(piece, cos_ref[part, :], sa_ref[part, :], sb_ref[part, :], 1.0)
                    taken[part, start + at : start + at + wide] = piece.astype(BF)

            over(total, step, body)
            yield
        saves[1].start()
        yield from attend_all(taken, inner, 2 * inner, taken, self_bias, mixed_self)
        saves[2].start()
        need(2)
        loads[2].wait()
        yield from out_project(
            mixed_self, w_so, mate_self, part_send, part_got,
            lambda part, cols: x_all[0, part, cols].astype(F32), stream_cross,
        )
        saves[3].start()

        def second_norm(part, _):
            made = normalise(stream_cross[part, :], vec(2), vec(3))
            normed_cross[0, part, :] = made.astype(BF)

        over(rows, tile, second_norm)
        mate_normed.start()
        yield
        need(4)
        loads[4].wait()
        depth = memory.shape[1]
        for start in range(0, 2 * inner, block):
            weight = w_kv[..., start : start + block].reshape(depth, block)
            taken_cross[:, start : start + block] = nn(memory[...], weight).astype(BF)
        saves[6].start()
        yield
        need(3)
        loads[3].wait()
        yield
        for side in range(2):
            if side == 1:
                mate_normed.arrived()
                saves[4].start()
            for start in range(0, inner, block):

                def body(part, i):
                    weight = w_cq[..., start : start + block].reshape(width, block)
                    made = nn(normed_cross[side, part, :], weight).astype(BF)
                    at = pl.multiple_of(side * rows + i * tile, tile)
                    query_cross[pl.ds(at, tile), start : start + block] = made

                over(rows, tile, body)
                yield
        saves[5].start()
        yield from attend_all(query_cross, 0, inner, taken_cross, cross_bias, mixed_cross)
        saves[7].start()
        need(5)
        loads[5].wait()
        mate_self.sent()
        yield from out_project(
            mixed_cross, w_co, mate_cross, part_send, part_got,
            lambda part, cols: stream_cross[part, cols], stream_feed,
        )
        saves[8].start()

        def third_norm(part, _):
            made = normalise(stream_feed[part, :], vec(4), vec(5))
            normed_feed[0, part, :] = made.astype(BF)

        over(rows, tile, third_norm)
        feed_moves[0].start()

    items = gathers + quarters
    names = ("begin", "far_first", "step", "far_step", "landed", "own_y_arrived")
    work = compute()
    for entry in PLAN:
        if entry < 0:
            next(work, None)
            continue
        kind, which, k, side = entry // 1000, entry // 100 % 10, entry // 10 % 10, entry % 10
        item = items[which]
        getattr(item, names[kind])(*((k, side) if kind in (2, 3) else ()))
        if kind == 0 and which == 4:
            cot_moves[1].start()
        if kind == 4:
            ready.add(which)
            if which < 6:
                loads[which].start()
    cot_moves[1].arrived()
    cot_moves[2].start()
    for _ in work:
        pass
    peak_out[...] = crest[...]
    for i, item in enumerate(items):
        if i not in ready:
            item.landed()
    feed_moves[0].arrived()
    saves[9].start()
    cot_moves[0].arrived()
    cot_moves[2].arrived()
    own_cot.wait()
    for item in gathers + quarters:
        item.sent()
    for move in [mate_inputs, mate_normed, mate_cross] + cot_moves + feed_moves:
        move.sent()
    for save in saves:
        save.wait()


def forward(shards, quarters, inputs, cotangent, turns, self_bias, cross_bias, memory, zs):
    rows, width = inputs.shape
    seq_len, inner = 2 * rows, shards[1].shape[1]
    tokens = memory.shape[0]
    spread = []
    groups = ([shards[0]], shards[1:4], [shards[4]], [shards[5]], shards[6:8], [shards[8]])
    for group in groups:
        columns = sum(shard.shape[1] for shard in group)
        spread.append(jax.ShapeDtypeStruct((zs, 2, 2, group[0].shape[0], columns), group[0].dtype))
    for shard in quarters:
        spread.append(
            jax.ShapeDtypeStruct((zs, 2, 2, shard.shape[0], shard.shape[1] // 2), shard.dtype)
        )
    results = [
        jax.ShapeDtypeStruct((seq_len, width), BF),
        jax.ShapeDtypeStruct((seq_len, 3 * inner), BF),
        jax.ShapeDtypeStruct((seq_len, inner), BF),
        jax.ShapeDtypeStruct((rows, width), F32),
        jax.ShapeDtypeStruct((2, rows, width), BF),
        jax.ShapeDtypeStruct((seq_len, inner), BF),
        jax.ShapeDtypeStruct((tokens, 2 * inner), BF),
        jax.ShapeDtypeStruct((seq_len, inner), BF),
        jax.ShapeDtypeStruct((rows, width), F32),
        jax.ShapeDtypeStruct((2, rows, width), BF),
    ]
    cot_out = jax.ShapeDtypeStruct((4, rows, width), BF)
    peak = jax.ShapeDtypeStruct((8, 2 * HEAD_DIM), F32)
    moves = 6 * (3 + 8 * (zs - 1)) + 3 * (2 + 4 * (zs - 1)) + 8
    hbm = pl.BlockSpec(memory_space=pltpu.HBM)
    vmem = pl.BlockSpec(memory_space=pltpu.VMEM)
    held = [pltpu.VMEM(shape.shape, shape.dtype) for shape in spread[:6]]
    held += [pltpu.VMEM((2, rows, width), BF)]
    held += [pltpu.VMEM(shape.shape, shape.dtype) for shape in results]
    held += [pltpu.VMEM((rows, width), BF)] * 2
    held += [pltpu.VMEM((shards[0].shape[1], width), F32), pltpu.VMEM(peak.shape, F32)]
    flops = 2 * seq_len * inner * (7 * width + 4 * seq_len) // 1
    made = pl.pallas_call(
        functools.partial(forward_kernel, zs),
        out_shape=spread + results + [cot_out, peak],
        in_specs=[hbm] * 14 + [vmem] * 6,
        out_specs=[hbm] * 20 + [vmem],
        scratch_shapes=[
            pltpu.SemaphoreType.DMA((moves,)),
            pltpu.SemaphoreType.DMA((moves,)),
            pltpu.SemaphoreType.DMA((9 + 2 + 3 + 6 + 10,)),
        ]
        + held,
        compiler_params=pltpu.CompilerParams(
            collective_id=1, has_side_effects=True, vmem_limit_bytes=62 * 2**20
        ),
        cost_estimate=pl.CostEstimate(flops=flops, bytes_accessed=10**8, transcendentals=10**7),
    )(*shards, *quarters, inputs, cotangent, *turns, self_bias, cross_bias, memory)
    return made[:9], made[9:19], made[19], made[20]


def pair_rows(own):
    return jnp.concatenate([own, swap(own, "tensor")], axis=0)


def group_rows(own):
    both = jnp.stack([own, swap(own, "x")])
    other = swap(both, "tensor")
    return jnp.concatenate([both[0], other[0], both[1], other[1]], axis=0)


def spread_pair(left, right_t):
    rows = left.shape[0] // 2
    got = swap(nt(left[rows:], right_t), "tensor")
    return nt(left[:rows], right_t) + got


def spread_group(product):
    quarter = product.rows // 4
    far_send = product(3 * quarter, quarter)
    far = product(2 * quarter, quarter) + swap(far_send, "tensor")
    got_far = swap(far.astype(BF), "x")
    near = product(0, quarter) + swap(product(quarter, quarter), "tensor")
    return near + got_far.astype(F32)


class Product:
    def __init__(self, terms, transposed):
        self.terms = terms
        self.transposed = transposed
        self.rows = terms[0][0].shape[0]

    def __call__(self, first, count):
        total = None
        for left, right in self.terms:
            part = (nt if self.transposed else nn)(left[first : first + count], right)
            total = part if total is None else total + part
        return total


def per_device(
    inputs,
    cotangent,
    context,
    context_live,
    lengths,
    threshold,
    self_gain,
    self_bias,
    self_query,
    self_key,
    self_value,
    self_output,
    cross_gain,
    cross_bias,
    cross_query,
    cross_key,
    cross_value,
    cross_output,
    feed_gain,
    feed_bias,
    gate_weight,
    up_weight,
    down_weight,
):
    zs = lax.axis_size("z")
    x_at = lax.axis_index("x")
    t_at = lax.axis_index("tensor")
    width = inputs.shape[1]
    rows = inputs.shape[0]
    seq_len = 2 * rows
    inner = self_query.shape[1]
    heads_here = inner // HEAD_DIM
    ff = gate_weight.shape[1] // 2
    shard_rows = self_query.shape[0]

    quarters = [gate_weight, up_weight, down_weight.T]
    vector_list = [self_gain, self_bias, cross_gain, cross_bias, feed_gain, feed_bias]
    stream = inputs.astype(F32)
    local = jnp.arange(rows)
    places = jnp.concatenate([t_at * rows + local, (1 - t_at) * rows + local])
    turns = turn_tables(places.astype(F32))
    self_bias_row = jnp.where(places < lengths[0], 0.0, NEGATIVE).astype(F32)
    tokens = context.shape[1]
    token_rows = -(-tokens // 128) * 128
    cross_bias_row = jnp.pad(
        jnp.where(context_live[0] > 0, 0.0, NEGATIVE).astype(F32),
        (0, token_rows - tokens),
        constant_values=NEGATIVE,
    )
    memory = jnp.pad(context[0], ((0, token_rows - tokens), (0, 0)))
    pairs = inner // (2 * HEAD_DIM)

    if shard_rows % 32 == 0:
        vectors = jnp.pad(jnp.stack(vector_list, axis=1).astype(F32), ((0, 0), (0, 122)))
        spread, made, cot_group, crest = forward(
            [
                vectors,
                self_query,
                self_key,
                self_value,
                self_output.T,
                cross_query,
                cross_key,
                cross_value,
                cross_output.T,
            ],
            quarters,
            inputs,
            cotangent,
            turns,
            self_bias_row[None],
            cross_bias_row[None],
            memory,
            zs,
        )
        norms, in_weight, self_out_t, cross_in, memory_weight, cross_out_t = spread[:6]
        norms = norms.reshape(width, -1).T
        (
            normed_self,
            taken,
            mixed_self,
            stream_cross,
            normed_cross,
            query_cross,
            taken_cross,
            mixed_cross,
            stream_feed,
            normed_feed,
        ) = made
        gate_full, up_full, down_t = spread[6:]
        normed_cross = normed_cross.reshape(seq_len, width)
        near_feed, cot_group = (v.reshape(-1, width) for v in (normed_feed, cot_group))
    else:
        vectors = jnp.stack(vector_list).astype(F32)
        vectors = jnp.pad(vectors, ((0, 2), (0, 128 - shard_rows)))
        (norms, in_weight, self_out_t, cross_in, memory_weight, cross_out_t, gate_full, up_full, down_t) = (
            gather_all(
                [
                    [vectors],
                    [self_query, self_key, self_value],
                    [self_output.T],
                    [cross_query],
                    [cross_key, cross_value],
                    [cross_output.T],
                ],
                quarters,
                zs,
            )
        )
        norms = norms.reshape(-1, 8, 128)[:, :6, :shard_rows].transpose(1, 0, 2).reshape(6, width)
        in_weight, memory_weight = in_weight.reshape(width, -1), memory_weight.reshape(-1, 2 * inner)
        self_out_t, cross_in, cross_out_t, gate_full, up_full, down_t = (
            w.reshape(width, -1)
            for w in (self_out_t, cross_in, cross_out_t, gate_full, up_full, down_t)
        )
        cot_group = group_rows(cotangent)
        all_inputs = pair_rows(inputs)
        normed, _, _ = norm_forward(all_inputs.astype(F32), norms[0], norms[1])
        normed_self = normed.astype(BF)
        taken = project(normed_self, in_weight, turns, 2 * inner)
        self_bias_rows = jnp.broadcast_to(self_bias_row, (pairs, seq_len))
        mixed_self, peak_self = attend(taken, taken, taken, self_bias_rows, (0, pairs, 2 * pairs))
        stream_cross = stream + spread_pair(mixed_self, self_out_t)
        normed, _, _ = norm_forward(stream_cross, norms[2], norms[3])
        normed_cross = pair_rows(normed.astype(BF))
        query_cross = nn(normed_cross, cross_in).astype(BF)
        taken_cross = nn(memory, memory_weight).astype(BF)
        cross_bias_rows = jnp.broadcast_to(cross_bias_row, (pairs, token_rows))
        mixed_cross, peak_cross = attend(
            query_cross, taken_cross, taken_cross, cross_bias_rows, (0, 0, pairs)
        )
        stream_feed = stream_cross + spread_pair(mixed_cross, cross_out_t)
        normed, _, _ = norm_forward(stream_feed, norms[4], norms[5])
        near_feed = pair_rows(normed.astype(BF))
        crest = jnp.pad(
            jnp.maximum(peak_self, peak_cross)[None], ((0, 7), (0, 128 - heads_here))
        )
    in_weight, self_out_t, cross_in, cross_out_t, gate_full, up_full, down_t = (
        w.reshape(width, -1)
        for w in (in_weight, self_out_t, cross_in, cross_out_t, gate_full, up_full, down_t)
    )
    unit_cross, inverse_cross = unit_rows_of(stream_cross)
    unit_feed, inverse_feed = unit_rows_of(stream_feed)
    far_feed = pair_rows(swap(near_feed[:rows], "x"))

    def feed_half(normed, cot_rows):
        gate_pre = nn(normed, gate_full)
        upward = nn(normed, up_full)
        sigmoid_gate = jax.nn.sigmoid(gate_pre)
        hidden = (gate_pre * sigmoid_gate * upward).astype(BF)
        grad_hidden = nn(cot_rows, down_t)
        grad_gate = grad_hidden * upward * sigmoid_gate * (1.0 + gate_pre * (1.0 - sigmoid_gate))
        grad_upward = grad_hidden * gate_pre * sigmoid_gate
        return hidden, grad_gate.astype(BF), grad_upward.astype(BF)

    def feed_back(grad_gate, grad_upward):
        return nt(grad_gate, gate_full) + nt(grad_upward, up_full)

    hidden_near, gate_near, up_near = feed_half(near_feed, cot_group[:seq_len])
    far_feed, gate_near, up_near, hidden_near = lax.optimization_barrier(
        (far_feed, gate_near, up_near, hidden_near)
    )
    hidden_far, gate_far, up_far = feed_half(far_feed, cot_group[seq_len:])
    far_sum = feed_back(gate_far[:rows], up_far[:rows]) + swap(
        feed_back(gate_far[rows:], up_far[rows:]), "tensor"
    )
    far_sum = far_sum.astype(BF)
    got_far = swap(far_sum, "x")
    normed_feed = jnp.concatenate([near_feed, far_feed], axis=0)
    hidden = jnp.concatenate([hidden_near, hidden_far], axis=0)
    grad_gate = jnp.concatenate([gate_near, gate_far], axis=0)
    grad_upward = jnp.concatenate([up_near, up_far], axis=0)
    down_pair = PairSum(after(cot_group, far_sum), hidden, zs)
    gate_pair = PairSum(after(normed_feed, far_sum), grad_gate, zs)
    grad_normed = feed_back(gate_near[:rows], up_near[:rows]) + swap(
        feed_back(gate_near[rows:], up_near[rows:]), "tensor"
    )
    grad_normed, got_far = after((grad_normed, got_far), gate_pair.got, down_pair.got)
    grad_normed = grad_normed + got_far.astype(F32)
    stream_part, grad_feed_gain, grad_feed_bias = norm_backward(
        grad_normed, unit_feed, inverse_feed, norms[4]
    )
    grad_stream = cotangent.astype(F32) + stream_part
    grad_full = pair_rows(grad_stream.astype(BF))
    up_pair = PairSum(after(normed_feed, grad_full), grad_upward, zs)
    down_pair.second(grad_full)
    cross_output_sum = FullSum(grad_full, mixed_cross, zs)
    grad_mixed = nn(grad_full, cross_out_t).astype(BF)
    grad_query, grad_keys, grad_values = attend_back(
        query_cross, taken_cross, taken_cross, grad_mixed, cross_bias_row[:, None], (0, 0, pairs), None
    )
    gate_pair.second(grad_query)
    grad_normed = spread_pair(grad_query, cross_in)
    cross_query_sum = FullSum(normed_cross, grad_query, zs)
    part_memory = tn(memory, jnp.concatenate([grad_keys, grad_values], axis=1))
    stream_part, grad_cross_gain, grad_cross_bias = norm_backward(
        grad_normed, unit_cross, inverse_cross, norms[2]
    )
    grad_stream = grad_stream + stream_part
    grad_full = pair_rows(grad_stream.astype(BF))
    up_pair.second(grad_full)
    part_self_output = tn(grad_full, mixed_self)
    grad_mixed = nn(grad_full, self_out_t).astype(BF)
    cross_output_sum.second(grad_mixed)
    cross_query_sum.second(grad_mixed)
    grad_parts = attend_back(
        taken, taken, taken, grad_mixed, self_bias_row[:, None], (0, pairs, 2 * pairs), turns
    )
    grad_in = jnp.concatenate(grad_parts, axis=1)
    sum_cross_output = cross_output_sum.third(grad_in).astype(F32)
    sum_cross_query = cross_query_sum.third(grad_in).astype(F32)
    part_query, part_key, part_value = (tn(normed_self, part) for part in grad_parts)
    grad_normed = spread_pair(grad_in, in_weight)
    unit_self, inverse_self = unit_rows_of(stream)
    stream_part, grad_self_gain, grad_self_bias = norm_backward(
        grad_normed, unit_self, inverse_self, norms[0]
    )
    grad_stream = grad_stream + stream_part

    vector_sums = jnp.stack(
        [
            grad_self_gain,
            grad_self_bias,
            grad_cross_gain,
            grad_cross_bias,
            grad_feed_gain,
            grad_feed_bias,
        ]
    ).reshape(6, -1, shard_rows)
    vector_sums = vector_sums + swap(vector_sums, "tensor")
    vector_sums = jnp.pad(
        vector_sums.transpose(1, 0, 2), ((0, 0), (0, 2), (0, 128 - shard_rows))
    ).reshape(zs, 2, 2, 8, 128)

    def blocks(part):
        return part.astype(BF).reshape(zs, 2, 2, -1, part.shape[1])

    (vector_sums, sum_query, sum_key, sum_value, sum_self_output, sum_memory, crest) = (
        scatter_all(
            [
                vector_sums,
                blocks(part_query),
                blocks(part_key),
                blocks(part_value),
                blocks(part_self_output),
                blocks(part_memory),
            ],
            ["x", "x", "y", "x", "y", "z"],
            crest,
            zs,
        )
    )
    vector_sums = vector_sums[:, :shard_rows]
    peaks = crest[0, :heads_here]
    factor = jnp.sqrt(threshold[0] / jnp.maximum(peaks, threshold[0]))
    columns = jnp.repeat(factor, HEAD_DIM)[None, :]
    result = stream_feed + spread_group(Product([(hidden, down_t)], True))
    result = result.astype(BF)
    down_keep, down_got = down_pair.third()
    gate_keep, gate_got = gate_pair.third()
    up_keep, up_got = up_pair.third()

    def side_by_side(kept, got):
        low = jnp.where(x_at == 0, kept, got).astype(F32)
        high = jnp.where(x_at == 0, got, kept).astype(F32)
        return jnp.concatenate([low, high], axis=1)

    down_sum = side_by_side(down_keep, down_got).T
    gate_sum = side_by_side(gate_keep, gate_got)
    up_sum = side_by_side(up_keep, up_got)
    return (
        result,
        grad_stream,
        vector_sums[0],
        vector_sums[1],
        sum_query,
        sum_key,
        sum_value,
        sum_self_output.T,
        vector_sums[2],
        vector_sums[3],
        sum_cross_query,
        sum_memory[:, :inner],
        sum_memory[:, inner:],
        sum_cross_output.T,
        vector_sums[4],
        vector_sums[5],
        gate_sum,
        up_sum,
        down_sum,
        peaks,
        self_query.astype(F32) * columns,
        self_key.astype(F32) * columns,
        cross_query.astype(F32) * columns,
        cross_key.astype(F32) * columns,
    )


def solution(mesh):
    count = mesh.shape["dp"]
    mesh = Mesh(
        mesh.devices.reshape(count // 4, 2, 2, mesh.shape["tensor"]), ("z", "y", "x", "tensor")
    )
    dp = ("z", "y", "x")
    both = P(dp + ("tensor",), None)
    split = P(dp)
    row_major = P(dp, "tensor")
    column_major = P("tensor", dp)
    in_specs = (
        both,
        both,
        P(dp, None, None),
        P(dp, None),
        split,
        P(),
        split,
        split,
        row_major,
        row_major,
        row_major,
        column_major,
        split,
        split,
        row_major,
        row_major,
        row_major,
        column_major,
        split,
        split,
        row_major,
        row_major,
        column_major,
    )
    out_specs = (
        both,
        both,
        split,
        split,
        row_major,
        row_major,
        row_major,
        column_major,
        split,
        split,
        row_major,
        row_major,
        row_major,
        column_major,
        split,
        split,
        row_major,
        row_major,
        column_major,
        P("tensor"),
        row_major,
        row_major,
        row_major,
        row_major,
    )
    return jax.shard_map(
        per_device, mesh=mesh, in_specs=in_specs, out_specs=out_specs, check_vma=False
    )
```

```python
import functools

import jax
import jax.numpy as jnp
from jax import lax
from jax.experimental import pallas as pl
from jax.experimental.pallas import tpu as pltpu
from jax.sharding import Mesh
from jax.sharding import PartitionSpec as P

HEAD_DIM = 64
ROT_DIM = 32
EPSILON = 1e-05
NEGATIVE = -1e30
BF = jnp.bfloat16
F32 = jnp.float32


def swap(value, axis):
    return lax.ppermute(value, axis, [(0, 1), (1, 0)])


def pick(value, index, dim):
    return lax.dynamic_index_in_dim(value, index, dim, keepdims=False)


class Lanes:
    def __init__(self, send_sems, recv_sems, local_sems, zs):
        self.send_sems, self.recv_sems, self.local_sems = send_sems, recv_sems, local_sems
        self.used = self.used_local = 0
        self.z = lax.axis_index("z")
        self.y = lax.axis_index("y")
        self.x = lax.axis_index("x")
        self.zs = zs

    def local(self):
        self.used_local += 1
        return self.local_sems.at[self.used_local - 1]

    def copy(self, source, target, device):
        return self.copies([source], target, device)[0]

    def copies(self, sources, target, device):
        slot = self.used
        self.used += 1
        return [
            pltpu.make_async_remote_copy(
                src_ref=source,
                dst_ref=target,
                send_sem=self.send_sems.at[slot],
                recv_sem=self.recv_sems.at[slot],
                device_id=device,
                device_id_type=pl.DeviceIdType.MESH,
            )
            for source in sources
        ]


def guarded(condition, action):
    if condition is None:
        action()
    else:
        pl.when(condition)(action)


class Move:
    def __init__(self, copy, sends, receives):
        self.copy_, self.sends, self.receives = copy, sends, receives

    def start(self):
        guarded(self.sends, self.copy_.start)

    def arrived(self):
        guarded(self.receives, self.copy_.wait_recv)

    def sent(self):
        guarded(self.sends, self.copy_.wait_send)


class Gather:
    def __init__(self, lanes, whole):
        zs, z, y, x = lanes.zs, lanes.z, lanes.y, lanes.x
        own = whole.at[z, y, x]

        def block(zz, yy):
            return whole.at[zz, yy, x]

        def along(source, target, axis, to, sends=None, receives=None):
            return Move(lanes.copy(source, target, {axis: to}), sends, receives)

        self.first = [
            along(own, block(z, y), "y", 1 - y),
            along(own, block(z, y), "x", 1 - x),
        ]
        self.far = [[along(block(z, 1 - y), block(z, 1 - y), "x", 1 - x)]]
        self.steps = []
        for k in range(zs - 1):
            right, left = jnp.maximum(z - k, 0), jnp.minimum(z + k, zs - 1)
            step = []
            for zz, to, sends, receives, got in (
                (right, z + 1, (z >= k) & (z < zs - 1), z >= k + 1, jnp.maximum(z - 1 - k, 0)),
                (left, z - 1, (z + k < zs) & (z > 0), z + k + 1 < zs, jnp.minimum(z + 1 + k, zs - 1)),
            ):
                source = own if k == 0 else block(zz, y)
                move = along(source, block(zz, y), "z", to, sends, receives)
                follow = [
                    along(block(got, y), block(got, y), "y", 1 - y, receives, receives),
                    along(block(got, y), block(got, y), "x", 1 - x, receives, receives),
                    along(block(got, 1 - y), block(got, 1 - y), "x", 1 - x, receives, receives),
                ]
                step.append((move, follow))
            self.steps.append(step)

    def begin(self):
        for move, _ in self.steps[0]:
            move.start()
        for move in self.first:
            move.start()

    def step(self, k, side):
        move, follow = self.steps[k][side]
        move.arrived()
        if k + 1 < len(self.steps):
            self.steps[k + 1][side][0].start()
        follow[0].start()
        follow[1].start()

    def far_first(self):
        self.first[0].arrived()
        self.far[0][0].start()

    def far_step(self, k, side):
        _, follow = self.steps[k][side]
        follow[0].arrived()
        follow[2].start()

    def landed(self):
        self.first[1].arrived()
        self.far[0][0].arrived()
        for step in self.steps:
            for _, follow in step:
                follow[1].arrived()
                follow[2].arrived()

    def sent(self):
        for move in self.first + self.far[0]:
            move.sent()
        for step in self.steps:
            for move, follow in step:
                move.sent()
                for other in follow:
                    other.sent()


class PairGather:
    def __init__(self, lanes, shard, whole, y_first):
        zs, z, y, x = lanes.zs, lanes.z, lanes.y, lanes.x
        ff = whole.shape[-1]
        kept = shard.at[:, pl.ds(pl.multiple_of(x * ff, ff), ff)]
        sent = shard.at[:, pl.ds(pl.multiple_of((1 - x) * ff, ff), ff)]
        self.y_first = y_first

        def along(piece, axis, to, sends=None, receives=None):
            return Move(lanes.copy(piece, piece, {axis: to}), sends, receives)

        self.swap = Move(lanes.copy(sent, whole.at[z, y, x], {"x": 1 - x}), None, None)
        self.local = pltpu.make_async_copy(kept, whole.at[z, y, x], lanes.local())
        self.own_y = along(whole.at[z, y], "y", 1 - y)
        self.steps = []
        for k in range(zs - 1):
            step = []
            for zz, to, sends, receives, got in (
                (jnp.maximum(z - k, 0), z + 1, (z >= k) & (z < zs - 1), z >= k + 1, jnp.maximum(z - 1 - k, 0)),
                (jnp.minimum(z + k, zs - 1), z - 1, (z + k < zs) & (z > 0), z + k + 1 < zs, jnp.minimum(z + 1 + k, zs - 1)),
            ):
                piece = whole.at[zz] if y_first else whole.at[zz, y]
                move = along(piece, "z", to, sends, receives)
                follow = [] if y_first else [along(whole.at[got, y], "y", 1 - y, receives, receives)]
                step.append((move, follow))
            self.steps.append(step)

    def begin(self):
        self.swap.start()
        self.local.start()

    def far_first(self):
        self.swap.arrived()
        self.local.wait()
        self.own_y.start()
        if not self.y_first:
            for move, _ in self.steps[0]:
                move.start()

    def own_y_arrived(self):
        self.own_y.arrived()
        if self.y_first:
            for move, _ in self.steps[0]:
                move.start()

    def step(self, k, side):
        move, follow = self.steps[k][side]
        move.arrived()
        if k + 1 < len(self.steps):
            self.steps[k + 1][side][0].start()
        for other in follow:
            other.start()

    def landed(self):
        if not self.y_first:
            self.own_y.arrived()
        for step in self.steps:
            for move, follow in step:
                for other in follow:
                    other.arrived()

    def sent(self):
        self.swap.sent()
        self.own_y.sent()
        for step in self.steps:
            for move, follow in step:
                move.sent()
                for other in follow:
                    other.sent()


def greet(zs, mates=False):
    z, y, x = lax.axis_index("z"), lax.axis_index("y"), lax.axis_index("x")
    barrier = pltpu.get_barrier_semaphore()

    def signal(device):
        pl.semaphore_signal(barrier, inc=1, device_id=device, device_id_type=pl.DeviceIdType.MESH)

    signal({"x": 1 - x})
    signal({"y": 1 - y})
    pl.when(z > 0)(lambda: signal({"z": z - 1}))
    pl.when(z < zs - 1)(lambda: signal({"z": z + 1}))
    if mates:
        signal({"tensor": 1 - lax.axis_index("tensor")})
    peers = (3 if mates else 2) + (z > 0).astype(jnp.int32) + (z < zs - 1).astype(jnp.int32)
    pl.semaphore_wait(barrier, peers)


def gather_kernel(zs, groups, pairs, *refs):
    shards = sum(groups)
    owns, pair_in = refs[:shards], refs[shards : shards + pairs]
    refs = refs[shards + pairs :]
    outs = refs[: len(groups) + pairs]
    lanes = Lanes(*refs[len(groups) + pairs :], zs)
    z, y, x = lanes.z, lanes.y, lanes.x
    pieces, at = [], 0
    for count, whole in zip(groups, outs):
        width = whole.shape[-1] // count
        for i in range(count):
            target = whole.at[z, y, x, :, pl.ds(i * width, width)]
            pieces.append(pltpu.make_async_copy(owns[at], target, lanes.local()))
            at += 1
    for piece in pieces:
        piece.start()
    greet(zs)
    gathers = [Gather(lanes, whole) for whole in outs[: len(groups)]]
    quarters = [
        PairGather(lanes, pair_in[i], outs[len(groups) + i], i == 0) for i in range(pairs)
    ]
    for quarter in quarters:
        quarter.begin()
    for piece in pieces:
        piece.wait()
    for gather in gathers:
        gather.begin()
    for quarter in quarters:
        quarter.far_first()
    for gather in gathers:
        gather.far_first()
    for k, side in [(k, side) for k in range(zs - 1) for side in range(2)]:
        for gather in gathers:
            gather.step(k, side)
        for quarter in quarters:
            if quarter.y_first:
                if k == 0 and side == 0:
                    quarter.own_y_arrived()
            else:
                quarter.step(k, side)
        for gather in gathers:
            gather.far_step(k, side)
        for quarter in quarters:
            if quarter.y_first:
                quarter.step(k, side)
    for item in gathers + quarters:
        item.landed()
        item.sent()


def gather_all(groups, quarters, zs):
    flat = [shard for group in groups for shard in group] + list(quarters)
    outs = []
    for group in groups:
        columns = sum(shard.shape[1] for shard in group)
        outs.append(
            jax.ShapeDtypeStruct((zs, 2, 2, group[0].shape[0], columns), group[0].dtype)
        )
    for shard in quarters:
        outs.append(
            jax.ShapeDtypeStruct((zs, 2, 2, shard.shape[0], shard.shape[1] // 2), shard.dtype)
        )
    count, pairs = len(groups), len(quarters)
    moves = count * (3 + 8 * (zs - 1)) + pairs * (2 + 4 * (zs - 1))
    hbm = pl.BlockSpec(memory_space=pltpu.HBM)
    return pl.pallas_call(
        functools.partial(gather_kernel, zs, tuple(len(group) for group in groups), pairs),
        out_shape=outs,
        in_specs=[hbm] * len(flat),
        out_specs=[hbm] * len(outs),
        scratch_shapes=[
            pltpu.SemaphoreType.DMA((moves,)),
            pltpu.SemaphoreType.DMA((moves,)),
            pltpu.SemaphoreType.DMA((len(flat),)),
        ],
        compiler_params=pltpu.CompilerParams(collective_id=1, has_side_effects=True),
    )(*flat)


def plus(*terms):
    total = terms[0].astype(F32)
    for term in terms[1:]:
        total = total + term.astype(F32)
    return total


def ends_first(zs):
    order = []
    for i in range(zs // 2):
        order += [zs - 1 - i, i]
    return order


class Line:
    def __init__(self, lanes, part, from_left, from_right):
        zs, z = lanes.zs, lanes.z
        self.zs, self.z, self.part = zs, z, part
        self.from_left, self.from_right = from_left, from_right
        self.right, self.left = {}, {}
        for d in ends_first(zs):
            after, before = jnp.minimum(z + 1, zs - 1), jnp.maximum(z - 1, 0)
            self.right[d] = lanes.copies(
                (part.at[d], from_left.at[d]), from_left.at[d], {"z": after}
            )
            self.left[d] = lanes.copies(
                (part.at[d], from_right.at[d]), from_right.at[d], {"z": before}
            )

    def pass_on(self, d):
        for moves, inbox, sends, edge in (
            (self.right[d], self.from_left, self.z < d, self.z == 0),
            (self.left[d], self.from_right, self.z > d, self.z == self.zs - 1),
        ):

            @pl.when(sends & edge)
            def _():
                moves[0].start()

            @pl.when(sends & jnp.logical_not(edge))
            def _():
                moves[1].wait_recv()
                inbox[d] = plus(self.part[d], inbox[d]).astype(inbox.dtype)
                moves[1].start()

    def total(self, sink):
        for d in range(self.zs):

            @pl.when(self.z == d)
            def _():
                terms = [self.part[d]]
                if d > 0:
                    self.right[d][0].wait_recv()
                    terms.append(self.from_left[d])
                if d < self.zs - 1:
                    self.left[d][0].wait_recv()
                    terms.append(self.from_right[d])
                sink[...] = plus(*terms).astype(sink.dtype)

    def finish(self):
        for d in ends_first(self.zs):
            pl.when(self.z < d)(self.right[d][0].wait_send)
            pl.when(self.z > d)(self.left[d][0].wait_send)


class Scatter:
    def __init__(self, lanes, part, held, out, first):
        zs, z, y, x = lanes.zs, lanes.z, lanes.y, lanes.x
        got, near, from_left, from_right, ready = held
        second = "y" if first == "x" else "x"
        self.lanes, self.part, self.got, self.near, self.ready, self.out = (
            lanes, part, got, near, ready, out,
        )
        f, s = (x, y) if first == "x" else (y, x)
        self.f, self.s = f, s

        def block(zz, a, b):
            return part.at[zz, b, a] if first == "x" else part.at[zz, a, b]

        self.block = block
        self.one, self.two = {}, {}
        for zz in ends_first(zs):
            for j, b in enumerate((1 - s, s)):
                self.one[zz, j] = Move(
                    lanes.copy(block(zz, 1 - f, b), got.at[zz, j], {first: 1 - f}), None, None
                )
        for zz in ends_first(zs):
            self.two[zz] = Move(
                lanes.copy(got.at[zz, 0], near.at[zz], {second: 1 - s}), None, None
            )
        self.line = Line(lanes, ready, from_left, from_right)

    def begin(self, zz):
        for j in range(2):
            self.one[zz, j].start()

    def second(self, zz):
        self.one[zz, 0].arrived()
        mine, got = self.block(zz, self.f, 1 - self.s), self.got
        got[zz, 0] = plus(mine[...], got[zz, 0]).astype(got.dtype)
        self.two[zz].start()

    def third(self, zz):
        self.one[zz, 1].arrived()
        self.two[zz].arrived()
        mine = self.block(zz, self.f, self.s)
        self.ready[zz] = plus(mine[...], self.got[zz, 1], self.near[zz]).astype(self.ready.dtype)
        self.line.pass_on(zz)

    def finish(self):
        self.line.total(self.out)
        self.line.finish()
        for move in list(self.one.values()) + list(self.two.values()):
            move.sent()


class ScatterZ:
    def __init__(self, lanes, part, held, out):
        y, x = lanes.y, lanes.x
        from_left, from_right, held_z, near, last = held
        self.lanes, self.sum_z, self.near, self.last, self.out = lanes, held_z, near, last, out
        self.line = Line(lanes, part, from_left, from_right)
        self.two = Move(lanes.copy(held_z.at[1 - y], near, {"y": 1 - y}), None, None)
        self.three = Move(lanes.copy(near.at[1 - x], last, {"x": 1 - x}), None, None)

    def pass_on(self, d):
        self.line.pass_on(d)

    def total(self):
        self.line.total(self.sum_z)
        self.two.start()

    def after(self):
        self.two.arrived()
        self.near[...] = plus(self.sum_z[self.lanes.y], self.near[...]).astype(self.near.dtype)
        self.three.start()

    def finish(self):
        self.three.arrived()
        self.out[...] = plus(self.near[self.lanes.x], self.last[...]).astype(self.out.dtype)
        self.line.finish()
        self.two.sent()
        self.three.sent()


class Crest:
    def __init__(self, lanes, own, held, out):
        zs, z, y, x = lanes.zs, lanes.z, lanes.y, lanes.x
        near_x, near_y, mine_x, mine_y, right, left, inbox_r, inbox_l = (
            held.at[i] for i in range(8)
        )
        self.zs, self.z, self.own, self.out = zs, z, own, out
        self.near_x, self.near_y, self.mine_x, self.mine_y = near_x, near_y, mine_x, mine_y
        self.ways = (
            (right, inbox_r, z > 0, z < zs - 1),
            (left, inbox_l, z < zs - 1, z > 0),
        )
        self.one = Move(lanes.copy(own, near_x, {"x": 1 - x}), None, None)
        self.two = Move(lanes.copy(mine_x, near_y, {"y": 1 - y}), None, None)
        self.moves = [
            Move(lanes.copy(right, inbox_r, {"z": jnp.minimum(z + 1, zs - 1)}), z < zs - 1, z > 0),
            Move(lanes.copy(left, inbox_l, {"z": jnp.maximum(z - 1, 0)}), z > 0, z < zs - 1),
        ]

    def second(self):
        self.one.arrived()
        self.mine_x[...] = jnp.maximum(self.own[...], self.near_x[...])
        self.two.start()

    def finish(self):
        self.two.arrived()
        self.mine_y[...] = jnp.maximum(self.mine_x[...], self.near_y[...])
        self.out[...] = self.mine_y[...]
        for move, (held, inbox, has_before, has_after) in zip(self.moves, self.ways):

            @pl.when(has_before)
            def _():
                move.copy_.wait_recv()
                self.out[...] = jnp.maximum(self.out[...], inbox[...])
                held[...] = jnp.maximum(self.mine_y[...], inbox[...])

            @pl.when(jnp.logical_not(has_before))
            def _():
                held[...] = self.mine_y[...]

            move.start()
        for move in [self.one, self.two] + self.moves:
            move.sent()


def scatter_kernel(zs, orders, *refs):
    count = len(orders)
    parts, crest_in, refs = refs[:count], refs[count], refs[count + 1 :]
    outs, crest_out, rest = refs[:count], refs[count], list(refs[count + 1 :])
    send_sems, recv_sems = rest[:2]
    rest = rest[2:]
    lanes = Lanes(send_sems, recv_sems, None, zs)
    greet(zs)
    full, zfirst = [], []
    for i, order in enumerate(orders):
        held, rest = rest[:5], rest[5:]
        if order == "z":
            zfirst.append(ScatterZ(lanes, parts[i], held, outs[i]))
        else:
            full.append(Scatter(lanes, parts[i], held, outs[i], order))
    crest = Crest(lanes, crest_in, rest[0], crest_out)
    crest.one.start()
    order = ends_first(zs)
    for i in range(zs + 3):
        for item in full:
            if i < zs:
                item.begin(order[i])
        if i == 1:
            crest.second()
        if i < zs:
            for item in zfirst:
                item.pass_on(order[i])
        for item in full:
            if 2 <= i < zs + 2:
                item.second(order[i - 2])
        if i == zs:
            for item in zfirst:
                item.total()
        for item in full:
            if 3 <= i:
                item.third(order[i - 3])
    crest.finish()
    for item in zfirst:
        item.after()
    for item in full:
        item.finish()
    for item in zfirst:
        item.finish()


def scatter_all(parts, orders, crest, zs):
    scratch, moves = [], 4
    for part, order in zip(parts, orders):
        block = part.shape[3:]
        if order == "z":
            shapes = [(zs, 2, 2) + block] * 2 + [(2, 2) + block, (2,) + block, block]
            moves += 2 * zs + 2
        else:
            shapes = [(zs, 2) + block] + [(zs,) + block] * 4
            moves += 5 * zs
        scratch += [pltpu.VMEM(shape, part.dtype) for shape in shapes]
    vmem = pl.BlockSpec(memory_space=pltpu.VMEM)
    return pl.pallas_call(
        functools.partial(scatter_kernel, zs, orders),
        out_shape=[jax.ShapeDtypeStruct(part.shape[3:], F32) for part in parts]
        + [jax.ShapeDtypeStruct(crest.shape, F32)],
        in_specs=[vmem] * (len(parts) + 1),
        out_specs=[vmem] * (len(parts) + 1),
        scratch_shapes=[pltpu.SemaphoreType.DMA((moves,)), pltpu.SemaphoreType.DMA((moves,))]
        + scratch
        + [pltpu.VMEM((8,) + crest.shape, F32)],
        compiler_params=pltpu.CompilerParams(
            collective_id=2, has_side_effects=True, vmem_limit_bytes=56 * 2**20
        ),
    )(*parts, crest)


def nn(left, right):
    return lax.dot_general(left, right, (((1,), (0,)), ((), ())), preferred_element_type=F32)


def nt(left, right):
    return lax.dot_general(left, right, (((1,), (1,)), ((), ())), preferred_element_type=F32)


def tn(left, right):
    return lax.dot_general(left, right, (((0,), (0,)), ((), ())), preferred_element_type=F32)


def after(value, *others):
    return lax.optimization_barrier((value, others))[0]


class FullSum:
    def __init__(self, left, right, zs):
        self.zs = zs
        held = tn(left, right).astype(BF)
        self.held = held.reshape(2 * zs, 2, -1, held.shape[1])
        self.x, self.y = lax.axis_index("x"), lax.axis_index("y")
        self.got = swap(pick(self.held, 1 - self.x, 1), "x")

    def second(self, *others):
        got = after(self.got, others)
        held = pick(self.held, self.x, 1).astype(F32) + got.astype(F32)
        self.held = held.astype(BF).reshape(self.zs, 2, -1, held.shape[-1])
        self.got = swap(pick(self.held, 1 - self.y, 1), "y")

    def third(self, *others):
        got = after(self.got, others)
        held = pick(self.held, self.y, 1).astype(F32) + got.astype(F32)
        return lax.psum_scatter(held.astype(BF), "z", scatter_dimension=0, tiled=False)


class PairSum:
    def __init__(self, left, right, zs):
        held = tn(left, right).astype(BF)
        self.held = held.reshape(zs, 2, -1, held.shape[1])
        self.y = lax.axis_index("y")
        self.got = swap(pick(self.held, 1 - self.y, 1), "y")

    def second(self, *others):
        got = after(self.got, others)
        held = pick(self.held, self.y, 1).astype(F32) + got.astype(F32)
        held = lax.psum_scatter(held.astype(BF), "z", scatter_dimension=0, tiled=False)
        self.held = held.reshape(2, -1, held.shape[-1])

    def third(self):
        at = lax.axis_index("x")
        return pick(self.held, at, 0), swap(pick(self.held, 1 - at, 0), "x")


def norm_forward(stream, gain_vec, bias_vec):
    average = jnp.mean(stream, axis=-1, keepdims=True)
    centred = stream - average
    inverse = lax.rsqrt(jnp.mean(centred * centred, axis=-1, keepdims=True) + EPSILON)
    unit_rows = centred * inverse
    return (unit_rows * gain_vec + bias_vec, unit_rows, inverse)


def unit_rows_of(stream):
    _, unit_rows, inverse = norm_forward(stream, 1.0, 0.0)
    return unit_rows, inverse


def norm_backward(incoming, unit_rows, inverse, gain_vec):
    gain_grad = jnp.sum(incoming * unit_rows, axis=0)
    bias_grad = jnp.sum(incoming, axis=0)
    scaled = incoming * gain_vec
    stream_grad = inverse * (
        scaled
        - jnp.mean(scaled, axis=-1, keepdims=True)
        - unit_rows * jnp.mean(scaled * unit_rows, axis=-1, keepdims=True)
    )
    return (stream_grad, gain_grad, bias_grad)


def turn_tables(positions):
    rates = 10000.0 ** (-jnp.arange(0, ROT_DIM, 2).astype(F32) / ROT_DIM)
    angles = positions[:, None] * rates[None, :]
    cosine, sine = jnp.cos(angles), jnp.sin(angles)
    rest = jnp.ones((positions.shape[0], HEAD_DIM - ROT_DIM), F32)
    zero, none = jnp.zeros_like(rest), jnp.zeros_like(sine)
    return (
        jnp.concatenate([cosine, cosine, rest] * 2, axis=1),
        jnp.concatenate([-sine, none, zero] * 2, axis=1),
        jnp.concatenate([none, sine, zero] * 2, axis=1),
    )


def turn(field, cosine, sine_a, sine_b, direction):
    half = ROT_DIM // 2
    width = field.shape[-1]
    ahead = pltpu.roll(field, width - half, 1)
    behind = pltpu.roll(field, half, 1)
    return field * cosine + direction * (ahead * sine_a + behind * sine_b)


def head_lanes(shape, which):
    lanes = lax.broadcasted_iota(jnp.int32, shape, 1)
    return (lanes >= which * HEAD_DIM) & (lanes < (which + 1) * HEAD_DIM)


def attend_tile(query, keys, values, bias):
    scores = nt(query, keys) + bias
    top = jnp.max(scores, axis=-1, keepdims=True)
    weights = jnp.exp(scores - top)
    total = jnp.sum(weights, axis=-1, keepdims=True)
    return nn(weights.astype(BF), values) / total, top


def attend_kernel(q_ref, k_ref, v_ref, bias_ref, mixed_ref, peak_ref):
    rows = q_ref.shape[0]
    tile = rows // 3 if rows % 3 == 0 and (rows // 3) % 16 == 0 else rows
    keys, values, bias = k_ref[...], v_ref[...], bias_ref[...]
    peaks = [None, None]
    for start in range(0, rows, tile):
        query = q_ref[start : start + tile, :] * BF(HEAD_DIM ** (-0.5))
        outs = []
        for which in range(2):
            one = jnp.where(head_lanes(query.shape, which), query, jnp.zeros_like(query))
            out, top = attend_tile(one, keys, values, bias)
            outs.append(out)
            top = jnp.max(top, axis=0, keepdims=True)
            peaks[which] = top if peaks[which] is None else jnp.maximum(peaks[which], top)
        mixed = jnp.where(head_lanes(outs[0].shape, 0), outs[0], outs[1])
        mixed_ref[start : start + tile, :] = mixed.astype(BF)
    spot = head_lanes((8, 2 * HEAD_DIM), 0)
    peak_ref[0] = jnp.where(
        spot, jnp.broadcast_to(peaks[0], spot.shape), jnp.broadcast_to(peaks[1], spot.shape)
    )


def attend(query, keys, values, bias, offsets):
    rows, tokens = query.shape[0], keys.shape[0]
    pairs = bias.shape[0]
    wide = 2 * HEAD_DIM
    mixed, peak = pl.pallas_call(
        attend_kernel,
        grid=(pairs,),
        out_shape=[
            jax.ShapeDtypeStruct((rows, pairs * wide), BF),
            jax.ShapeDtypeStruct((pairs, 8, wide), F32),
        ],
        in_specs=[
            pl.BlockSpec((rows, wide), lambda j: (0, offsets[0] + j)),
            pl.BlockSpec((tokens, wide), lambda j: (0, offsets[1] + j)),
            pl.BlockSpec((tokens, wide), lambda j: (0, offsets[2] + j)),
            pl.BlockSpec((1, tokens), lambda j: (0, 0)),
        ],
        out_specs=[
            pl.BlockSpec((rows, wide), lambda j: (0, j)),
            pl.BlockSpec((1, 8, wide), lambda j: (j, 0, 0)),
        ],
        compiler_params=pltpu.CompilerParams(vmem_limit_bytes=48 * 2**20),
        cost_estimate=pl.CostEstimate(
            flops=8 * rows * tokens * pairs * wide,
            bytes_accessed=4 * (rows + tokens) * pairs * wide,
            transcendentals=2 * pairs * rows * tokens,
        ),
    )(query, keys, values, bias[:1])
    return mixed, peak[:, 0, ::HEAD_DIM].reshape(-1)


def attend_back_kernel(turned, q_ref, k_ref, v_ref, g_ref, bias_ref, *refs):
    if turned:
        cos_ref, sa_ref, sb_ref = refs[:3]
        refs = refs[3:]
    dq_ref, dk_ref, dv_ref, dk_acc, dv_acc = refs
    rows = q_ref.shape[0]
    tile = rows // 3 if rows % 3 == 0 and (rows // 3) % 128 == 0 else rows
    scale = BF(HEAD_DIM ** (-0.5))
    keys, values, bias = k_ref[...], v_ref[...], bias_ref[...]
    for start in range(0, rows, tile):
        part = slice(start, start + tile)
        query, grad = q_ref[part, :] * scale, g_ref[part, :]
        dq = None
        for which in range(2):
            mine = head_lanes(query.shape, which)
            one = jnp.where(mine, query, jnp.zeros_like(query))
            out = jnp.where(mine, grad, jnp.zeros_like(grad))
            scores = nt(keys, one) + bias
            weights = jnp.exp(scores - jnp.max(scores, axis=0, keepdims=True))
            weights = weights * (1.0 / jnp.sum(weights, axis=0, keepdims=True))
            slope = nt(values, out)
            slope = weights * (slope - jnp.sum(weights * slope, axis=0, keepdims=True))
            slope = slope.astype(BF)
            dv = nn(weights.astype(BF), out)
            dk = nn(slope, one)
            other = jnp.where(head_lanes(keys.shape, which), keys, jnp.zeros_like(keys))
            piece = tn(slope, other * scale)
            dq = piece if dq is None else dq + piece
            if start == 0 and which == 0:
                dv_acc[...] = dv
                dk_acc[...] = dk
            else:
                dv_acc[...] += dv
                dk_acc[...] += dk
        if turned:
            dq = turn(dq, cos_ref[part, :], sa_ref[part, :], sb_ref[part, :], -1.0)
        dq_ref[part, :] = dq.astype(BF)
    dk = dk_acc[...]
    if turned:
        dk = turn(dk, cos_ref[...], sa_ref[...], sb_ref[...], -1.0)
    dk_ref[...] = dk.astype(BF)
    dv_ref[...] = dv_acc[...].astype(BF)


def attend_back(query, keys, values, grad, bias_column, offsets, turns):
    rows, tokens = query.shape[0], keys.shape[0]
    wide = 2 * HEAD_DIM
    pairs = grad.shape[1] // wide
    ins = [query, keys, values, grad, bias_column]
    specs = [
        pl.BlockSpec((rows, wide), lambda j: (0, offsets[0] + j)),
        pl.BlockSpec((tokens, wide), lambda j: (0, offsets[1] + j)),
        pl.BlockSpec((tokens, wide), lambda j: (0, offsets[2] + j)),
        pl.BlockSpec((rows, wide), lambda j: (0, j)),
        pl.BlockSpec((tokens, 1), lambda j: (0, 0)),
    ]
    if turns is not None:
        ins += list(turns)
        specs += [pl.BlockSpec((rows, wide), lambda j: (0, 0))] * 3
    return pl.pallas_call(
        functools.partial(attend_back_kernel, turns is not None),
        grid=(pairs,),
        out_shape=[
            jax.ShapeDtypeStruct((rows, pairs * wide), BF),
            jax.ShapeDtypeStruct((tokens, pairs * wide), BF),
            jax.ShapeDtypeStruct((tokens, pairs * wide), BF),
        ],
        in_specs=specs,
        out_specs=[
            pl.BlockSpec((rows, wide), lambda j: (0, j)),
            pl.BlockSpec((tokens, wide), lambda j: (0, j)),
            pl.BlockSpec((tokens, wide), lambda j: (0, j)),
        ],
        scratch_shapes=[pltpu.VMEM((tokens, wide), F32), pltpu.VMEM((tokens, wide), F32)],
        compiler_params=pltpu.CompilerParams(vmem_limit_bytes=48 * 2**20),
        cost_estimate=pl.CostEstimate(
            flops=20 * rows * tokens * pairs * wide,
            bytes_accessed=8 * (rows + tokens) * pairs * wide,
            transcendentals=2 * pairs * rows * tokens,
        ),
    )(*ins)


def project_kernel(turned, x_ref, w_ref, cos_ref, sa_ref, sb_ref, out_ref):
    wide = 2 * HEAD_DIM
    made = nn(x_ref[...], w_ref[...])

    @pl.when(pl.program_id(0) < turned)
    def _():
        for start in range(0, made.shape[1], wide):
            piece = turn(made[:, start : start + wide], cos_ref[...], sa_ref[...], sb_ref[...], 1.0)
            out_ref[:, start : start + wide] = piece.astype(BF)

    @pl.when(pl.program_id(0) >= turned)
    def _():
        out_ref[...] = made.astype(BF)


def project(rows, weight, turns, turned_columns):
    count, depth = rows.shape
    columns = weight.shape[1]
    block = 2 * HEAD_DIM * (2 if turned_columns % (4 * HEAD_DIM) == 0 else 1)
    table = pl.BlockSpec((count, 2 * HEAD_DIM), lambda j: (0, 0))
    return pl.pallas_call(
        functools.partial(project_kernel, turned_columns // block),
        grid=(columns // block,),
        out_shape=jax.ShapeDtypeStruct((count, columns), BF),
        in_specs=[
            pl.BlockSpec((count, depth), lambda j: (0, 0)),
            pl.BlockSpec((depth, block), lambda j: (0, j)),
            table,
            table,
            table,
        ],
        out_specs=pl.BlockSpec((count, block), lambda j: (0, j)),
        compiler_params=pltpu.CompilerParams(vmem_limit_bytes=48 * 2**20),
        cost_estimate=pl.CostEstimate(
            flops=2 * count * depth * columns,
            bytes_accessed=2 * (count * depth + depth * columns + count * columns),
            transcendentals=0,
        ),
    )(rows, weight, *turns)


PLAN = (
    0, 100, 200, 800, 300, 700, 400, 2000, 2100, 2101, 2010, 1700, 1100, 2001, 2110, 2111, 600,
    3010, 1400, 1800, 2210, 500, 2120, 3100, 3101, 2121, 2200, 2201, 2211, 2011, 2701, 2410,
    3001, 3121, 2020, 2400, 2700, 2711, 2720, 2710, 2220, 3110, 1600, 3120, 5800, 3111, 2021,
    3000, 3021, 3020, 1000, 2221, 2401, 4100, 3011, 1500, 2301, 2721, 2411, 2500, 3410, 4000,
    -1, 2300, 2501, -1, -1, 1200, 3221, -1, 2600, 3220, -1, -1, 2311, 3401, 2321, -1, -1, 3210,
    3201, 1300, 3211, -1, 2801, -1, 2511, 3200, -1, 2421, 2510, 2420, -1, 3500, -1, 3301, 2310,
    3321, 3421, 2520, -1, 2610, 2601, -1, 3300, -1, 3411, 3400, 2800, 4200, 3511, -1, -1, 3310,
    3420, 2521, -1, 2320, 3311, -1, 3510, -1, 2620, -1, 3320, 4400, 2611, -1, 4300, -1, 3520,
    -1, 3521, -1, -1, 3501, 2811, -1, -1, 2810, -1, -1, -1, -1, -1, -1, 2621, 4500, -1, -1,
    4700, -1, -1, -1, -1, -1, 2821, 2820, 4600,
)


def normalise(stream, gain_vec, bias_vec):
    average = jnp.mean(stream, axis=-1, keepdims=True)
    centred = stream - average
    inverse = lax.rsqrt(jnp.mean(centred * centred, axis=-1, keepdims=True) + EPSILON)
    return centred * inverse * gain_vec + bias_vec


def forward_kernel(zs, *refs):
    refs = list(refs)

    def take(count):
        taken_refs = refs[:count]
        del refs[:count]
        return taken_refs

    shards = take(9)
    quarters_in = take(3)
    inputs_hbm, cot_hbm, cos_ref, sa_ref, sb_ref, self_bias, cross_bias, memory = take(8)
    wholes = take(6)
    quarter_outs = take(3)
    outs = take(10)
    cot_out = take(1)[0]
    peak_out = take(1)[0]
    send_sems, recv_sems, local_sems = take(3)
    w_vec, w_in, w_so, w_cq, w_kv, w_co = take(6)
    (
        x_all, normed_self, taken, mixed_self, stream_cross, normed_cross,
        query_cross, taken_cross, mixed_cross, stream_feed, normed_feed,
        part_send, part_got, vectors, crest,
    ) = take(15)
    lanes = Lanes(send_sems, recv_sems, local_sems, zs)
    z, y, x = lanes.z, lanes.y, lanes.x
    t = lax.axis_index("tensor")
    rows, width = inputs_hbm.shape
    wide = 2 * HEAD_DIM

    def local(source, target):
        return pltpu.make_async_copy(source, target, lanes.local())

    pieces, at = [], 0
    for count, whole in zip((1, 3, 1, 1, 2, 1), wholes):
        columns = whole.shape[-1] // count
        for i in range(count):
            target = whole.at[z, y, x, :, pl.ds(i * columns, columns)]
            pieces.append(local(shards[at], target))
            at += 1
    own_inputs = local(inputs_hbm, x_all.at[0])
    own_cot = local(cot_hbm, cot_out.at[0])
    for piece in pieces + [own_inputs, own_cot]:
        piece.start()
    greet(zs, True)

    def mate(source, target):
        return Move(lanes.copy(source, target, {"tensor": 1 - t}), None, None)

    def across(source, target):
        return Move(lanes.copy(source, target, {"x": 1 - x}), None, None)

    mate_inputs = mate(inputs_hbm, x_all.at[1])
    cot_moves = [
        mate(cot_hbm, cot_out.at[1]),
        across(cot_hbm, cot_out.at[2]),
        mate(cot_out.at[2], cot_out.at[3]),
    ]
    feed_moves = [mate(normed_feed.at[0], normed_feed.at[1])]
    mate_self = mate(part_send, part_got)
    mate_normed = mate(normed_cross.at[0], normed_cross.at[1])
    mate_cross = mate(part_send, part_got)
    gathers = [Gather(lanes, whole) for whole in wholes]
    quarters = [
        PairGather(lanes, quarters_in[i], quarter_outs[i], i == 2) for i in range(3)
    ]
    loads = [
        local(whole, held)
        for whole, held in zip(wholes, (w_vec, w_in, w_so, w_cq, w_kv, w_co))
    ]
    results = (
        normed_self, taken, mixed_self, stream_cross, normed_cross,
        query_cross, taken_cross, mixed_cross, stream_feed, normed_feed,
    )
    saves = [local(held, out) for held, out in zip(results, outs)]

    mate_inputs.start()
    cot_moves[0].start()
    for piece in pieces:
        piece.wait()
    columns = w_in.shape[-1]
    inner = columns // 3
    pairs = inner // wide
    block = 2 * wide
    tile = 128 if rows % 128 == 0 else rows
    chunk = width // zs
    total = 2 * rows
    step = total // 3 if total % 3 == 0 and (total // 3) % 16 == 0 else total
    ready = set()

    def vec(i):
        return vectors[i : i + 1, :]

    def need(*groups):
        assert ready.issuperset(groups)

    def over(count, size, body):
        @pl.loop(0, count // size)
        def _(i):
            body(pl.ds(pl.multiple_of(i * size, size), size), i)

    def attend_all(query_ref, keys_at, values_at, kv_ref, bias_ref, mixed_ref):
        lane = lax.broadcasted_iota(jnp.int32, (8, wide), 1)
        for j in range(pairs):
            at = slice(j * wide, (j + 1) * wide)
            keys_in = slice(keys_at + j * wide, keys_at + (j + 1) * wide)
            values_in = slice(values_at + j * wide, values_at + (j + 1) * wide)

            def body(part, _):
                query = query_ref[part, at] * BF(HEAD_DIM ** (-0.5))
                outs = []
                for which in range(2):
                    mine = head_lanes(query.shape, which)
                    one = jnp.where(mine, query, jnp.zeros_like(query))
                    out, top = attend_tile(
                        one, kv_ref[:, keys_in], kv_ref[:, values_in], bias_ref[...]
                    )
                    outs.append(out)
                    top = jnp.broadcast_to(jnp.max(top, axis=0, keepdims=True), lane.shape)
                    best = jnp.where(lane == 2 * j + which, top, NEGATIVE)
                    crest[...] = jnp.maximum(crest[...], best)
                made = jnp.where(head_lanes(outs[0].shape, 0), outs[0], outs[1])
                mixed_ref[part, at] = made.astype(BF)

            over(total, step, body)
            yield

    def out_project(mixed_ref, weight, move, send, got, base, target):
        for zz in range(zs):
            cols = slice(zz * chunk, (zz + 1) * chunk)

            def body(part, i):
                left = mixed_ref[pl.ds(pl.multiple_of(rows + i * tile, tile), tile), :]
                send[part, cols] = nt(left, weight[zz].reshape(-1, inner)).astype(BF)

            over(rows, tile, body)
        move.start()
        yield
        for zz in range(zs):
            cols = slice(zz * chunk, (zz + 1) * chunk)

            def body(part, _):
                made = nt(mixed_ref[part, :], weight[zz].reshape(-1, inner))
                target[part, cols] = made + base(part, cols)

            over(rows, tile, body)
            yield
        move.arrived()

        def body(part, _):
            target[part, :] = target[part, :] + got[part, :].astype(F32)

        over(rows, tile, body)

    def compute():
        need(0, 1)
        own_inputs.wait()
        mate_inputs.arrived()
        loads[0].wait()
        vectors[...] = jnp.transpose(w_vec[...].reshape(width, w_vec.shape[-1]))
        crest[...] = jnp.full(crest.shape, NEGATIVE, F32)
        for side in range(2):

            def body(part, i):
                made = normalise(x_all[side, part, :].astype(F32), vec(0), vec(1))
                at = pl.multiple_of(side * rows + i * tile, tile)
                normed_self[pl.ds(at, tile), :] = made.astype(BF)

            over(rows, tile, body)
        saves[0].start()
        loads[1].wait()
        yield
        for start in range(0, columns, block):

            def body(part, _):
                weight = w_in[..., start : start + block].reshape(width, block)
                made = nn(normed_self[part, :], weight)
                for at in range(0, block, wide):
                    piece = made[:, at : at + wide]
                    if start + at < 2 * inner:
                        piece = turn(piece, cos_ref[part, :], sa_ref[part, :], sb_ref[part, :], 1.0)
                    taken[part, start + at : start + at + wide] = piece.astype(BF)

            over(total, step, body)
            yield
        saves[1].start()
        yield from attend_all(taken, inner, 2 * inner, taken, self_bias, mixed_self)
        saves[2].start()
        need(2)
        loads[2].wait()
        yield from out_project(
            mixed_self, w_so, mate_self, part_send, part_got,
            lambda part, cols: x_all[0, part, cols].astype(F32), stream_cross,
        )
        saves[3].start()

        def second_norm(part, _):
            made = normalise(stream_cross[part, :], vec(2), vec(3))
            normed_cross[0, part, :] = made.astype(BF)

        over(rows, tile, second_norm)
        mate_normed.start()
        yield
        need(4)
        loads[4].wait()
        depth = memory.shape[1]
        for start in range(0, 2 * inner, block):
            weight = w_kv[..., start : start + block].reshape(depth, block)
            taken_cross[:, start : start + block] = nn(memory[...], weight).astype(BF)
        saves[6].start()
        yield
        need(3)
        loads[3].wait()
        yield
        for side in range(2):
            if side == 1:
                mate_normed.arrived()
                saves[4].start()
            for start in range(0, inner, block):

                def body(part, i):
                    weight = w_cq[..., start : start + block].reshape(width, block)
                    made = nn(normed_cross[side, part, :], weight).astype(BF)
                    at = pl.multiple_of(side * rows + i * tile, tile)
                    query_cross[pl.ds(at, tile), start : start + block] = made

                over(rows, tile, body)
                yield
        saves[5].start()
        yield from attend_all(query_cross, 0, inner, taken_cross, cross_bias, mixed_cross)
        saves[7].start()
        need(5)
        loads[5].wait()
        mate_self.sent()
        yield from out_project(
            mixed_cross, w_co, mate_cross, part_send, part_got,
            lambda part, cols: stream_cross[part, cols], stream_feed,
        )
        saves[8].start()

        def third_norm(part, _):
            made = normalise(stream_feed[part, :], vec(4), vec(5))
            normed_feed[0, part, :] = made.astype(BF)

        over(rows, tile, third_norm)
        feed_moves[0].start()

    items = gathers + quarters
    names = ("begin", "far_first", "step", "far_step", "landed", "own_y_arrived")
    work = compute()
    for entry in PLAN:
        if entry < 0:
            next(work, None)
            continue
        kind, which, k, side = entry // 1000, entry // 100 % 10, entry // 10 % 10, entry % 10
        item = items[which]
        getattr(item, names[kind])(*((k, side) if kind in (2, 3) else ()))
        if kind == 0 and which == 4:
            cot_moves[1].start()
        if kind == 4:
            ready.add(which)
            if which < 6:
                loads[which].start()
    cot_moves[1].arrived()
    cot_moves[2].start()
    for _ in work:
        pass
    peak_out[...] = crest[...]
    for i, item in enumerate(items):
        if i not in ready:
            item.landed()
    feed_moves[0].arrived()
    saves[9].start()
    cot_moves[0].arrived()
    cot_moves[2].arrived()
    own_cot.wait()
    for item in gathers + quarters:
        item.sent()
    for move in [mate_inputs, mate_normed, mate_cross] + cot_moves + feed_moves:
        move.sent()
    for save in saves:
        save.wait()


def forward(shards, quarters, inputs, cotangent, turns, self_bias, cross_bias, memory, zs):
    rows, width = inputs.shape
    seq_len, inner = 2 * rows, shards[1].shape[1]
    tokens = memory.shape[0]
    spread = []
    groups = ([shards[0]], shards[1:4], [shards[4]], [shards[5]], shards[6:8], [shards[8]])
    for group in groups:
        columns = sum(shard.shape[1] for shard in group)
        spread.append(jax.ShapeDtypeStruct((zs, 2, 2, group[0].shape[0], columns), group[0].dtype))
    for shard in quarters:
        spread.append(
            jax.ShapeDtypeStruct((zs, 2, 2, shard.shape[0], shard.shape[1] // 2), shard.dtype)
        )
    results = [
        jax.ShapeDtypeStruct((seq_len, width), BF),
        jax.ShapeDtypeStruct((seq_len, 3 * inner), BF),
        jax.ShapeDtypeStruct((seq_len, inner), BF),
        jax.ShapeDtypeStruct((rows, width), F32),
        jax.ShapeDtypeStruct((2, rows, width), BF),
        jax.ShapeDtypeStruct((seq_len, inner), BF),
        jax.ShapeDtypeStruct((tokens, 2 * inner), BF),
        jax.ShapeDtypeStruct((seq_len, inner), BF),
        jax.ShapeDtypeStruct((rows, width), F32),
        jax.ShapeDtypeStruct((2, rows, width), BF),
    ]
    cot_out = jax.ShapeDtypeStruct((4, rows, width), BF)
    peak = jax.ShapeDtypeStruct((8, 2 * HEAD_DIM), F32)
    moves = 6 * (3 + 8 * (zs - 1)) + 3 * (2 + 4 * (zs - 1)) + 8
    hbm = pl.BlockSpec(memory_space=pltpu.HBM)
    vmem = pl.BlockSpec(memory_space=pltpu.VMEM)
    held = [pltpu.VMEM(shape.shape, shape.dtype) for shape in spread[:6]]
    held += [pltpu.VMEM((2, rows, width), BF)]
    held += [pltpu.VMEM(shape.shape, shape.dtype) for shape in results]
    held += [pltpu.VMEM((rows, width), BF)] * 2
    held += [pltpu.VMEM((shards[0].shape[1], width), F32), pltpu.VMEM(peak.shape, F32)]
    flops = 2 * seq_len * inner * (7 * width + 4 * seq_len) // 1
    made = pl.pallas_call(
        functools.partial(forward_kernel, zs),
        out_shape=spread + results + [cot_out, peak],
        in_specs=[hbm] * 14 + [vmem] * 6,
        out_specs=[hbm] * 20 + [vmem],
        scratch_shapes=[
            pltpu.SemaphoreType.DMA((moves,)),
            pltpu.SemaphoreType.DMA((moves,)),
            pltpu.SemaphoreType.DMA((9 + 2 + 3 + 6 + 10,)),
        ]
        + held,
        compiler_params=pltpu.CompilerParams(
            collective_id=1, has_side_effects=True, vmem_limit_bytes=62 * 2**20
        ),
        cost_estimate=pl.CostEstimate(flops=flops, bytes_accessed=10**8, transcendentals=10**7),
    )(*shards, *quarters, inputs, cotangent, *turns, self_bias, cross_bias, memory)
    return made[:9], made[9:19], made[19], made[20]


def pair_rows(own):
    return jnp.concatenate([own, swap(own, "tensor")], axis=0)


def group_rows(own):
    both = jnp.stack([own, swap(own, "x")])
    other = swap(both, "tensor")
    return jnp.concatenate([both[0], other[0], both[1], other[1]], axis=0)


def spread_pair(left, right_t):
    rows = left.shape[0] // 2
    got = swap(nt(left[rows:], right_t), "tensor")
    return nt(left[:rows], right_t) + got


def spread_group(product):
    quarter = product.rows // 4
    far_send = product(3 * quarter, quarter)
    far = product(2 * quarter, quarter) + swap(far_send, "tensor")
    got_far = swap(far.astype(BF), "x")
    near = product(0, quarter) + swap(product(quarter, quarter), "tensor")
    return near + got_far.astype(F32)


class Product:
    def __init__(self, terms, transposed):
        self.terms = terms
        self.transposed = transposed
        self.rows = terms[0][0].shape[0]

    def __call__(self, first, count):
        total = None
        for left, right in self.terms:
            part = (nt if self.transposed else nn)(left[first : first + count], right)
            total = part if total is None else total + part
        return total


def per_device(
    inputs,
    cotangent,
    context,
    context_live,
    lengths,
    threshold,
    self_gain,
    self_bias,
    self_query,
    self_key,
    self_value,
    self_output,
    cross_gain,
    cross_bias,
    cross_query,
    cross_key,
    cross_value,
    cross_output,
    feed_gain,
    feed_bias,
    gate_weight,
    up_weight,
    down_weight,
):
    zs = lax.axis_size("z")
    x_at = lax.axis_index("x")
    t_at = lax.axis_index("tensor")
    width = inputs.shape[1]
    rows = inputs.shape[0]
    seq_len = 2 * rows
    inner = self_query.shape[1]
    heads_here = inner // HEAD_DIM
    ff = gate_weight.shape[1] // 2
    shard_rows = self_query.shape[0]

    quarters = [gate_weight, up_weight, down_weight.T]
    vector_list = [self_gain, self_bias, cross_gain, cross_bias, feed_gain, feed_bias]
    stream = inputs.astype(F32)
    local = jnp.arange(rows)
    places = jnp.concatenate([t_at * rows + local, (1 - t_at) * rows + local])
    turns = turn_tables(places.astype(F32))
    self_bias_row = jnp.where(places < lengths[0], 0.0, NEGATIVE).astype(F32)
    tokens = context.shape[1]
    token_rows = -(-tokens // 128) * 128
    cross_bias_row = jnp.pad(
        jnp.where(context_live[0] > 0, 0.0, NEGATIVE).astype(F32),
        (0, token_rows - tokens),
        constant_values=NEGATIVE,
    )
    memory = jnp.pad(context[0], ((0, token_rows - tokens), (0, 0)))
    pairs = inner // (2 * HEAD_DIM)

    if shard_rows % 32 == 0:
        vectors = jnp.pad(jnp.stack(vector_list, axis=1).astype(F32), ((0, 0), (0, 122)))
        spread, made, cot_group, crest = forward(
            [
                vectors,
                self_query,
                self_key,
                self_value,
                self_output.T,
                cross_query,
                cross_key,
                cross_value,
                cross_output.T,
            ],
            quarters,
            inputs,
            cotangent,
            turns,
            self_bias_row[None],
            cross_bias_row[None],
            memory,
            zs,
        )
        norms, in_weight, self_out_t, cross_in, memory_weight, cross_out_t = spread[:6]
        norms = norms.reshape(width, -1).T
        (
            normed_self,
            taken,
            mixed_self,
            stream_cross,
            normed_cross,
            query_cross,
            taken_cross,
            mixed_cross,
            stream_feed,
            normed_feed,
        ) = made
        gate_full, up_full, down_t = spread[6:]
        normed_cross = normed_cross.reshape(seq_len, width)
        near_feed, cot_group = (v.reshape(-1, width) for v in (normed_feed, cot_group))
    else:
        vectors = jnp.stack(vector_list).astype(F32)
        vectors = jnp.pad(vectors, ((0, 2), (0, 128 - shard_rows)))
        (norms, in_weight, self_out_t, cross_in, memory_weight, cross_out_t, gate_full, up_full, down_t) = (
            gather_all(
                [
                    [vectors],
                    [self_query, self_key, self_value],
                    [self_output.T],
                    [cross_query],
                    [cross_key, cross_value],
                    [cross_output.T],
                ],
                quarters,
                zs,
            )
        )
        norms = norms.reshape(-1, 8, 128)[:, :6, :shard_rows].transpose(1, 0, 2).reshape(6, width)
        in_weight, memory_weight = in_weight.reshape(width, -1), memory_weight.reshape(-1, 2 * inner)
        self_out_t, cross_in, cross_out_t, gate_full, up_full, down_t = (
            w.reshape(width, -1)
            for w in (self_out_t, cross_in, cross_out_t, gate_full, up_full, down_t)
        )
        cot_group = group_rows(cotangent)
        all_inputs = pair_rows(inputs)
        normed, _, _ = norm_forward(all_inputs.astype(F32), norms[0], norms[1])
        normed_self = normed.astype(BF)
        taken = project(normed_self, in_weight, turns, 2 * inner)
        self_bias_rows = jnp.broadcast_to(self_bias_row, (pairs, seq_len))
        mixed_self, peak_self = attend(taken, taken, taken, self_bias_rows, (0, pairs, 2 * pairs))
        stream_cross = stream + spread_pair(mixed_self, self_out_t)
        normed, _, _ = norm_forward(stream_cross, norms[2], norms[3])
        normed_cross = pair_rows(normed.astype(BF))
        query_cross = nn(normed_cross, cross_in).astype(BF)
        taken_cross = nn(memory, memory_weight).astype(BF)
        cross_bias_rows = jnp.broadcast_to(cross_bias_row, (pairs, token_rows))
        mixed_cross, peak_cross = attend(
            query_cross, taken_cross, taken_cross, cross_bias_rows, (0, 0, pairs)
        )
        stream_feed = stream_cross + spread_pair(mixed_cross, cross_out_t)
        normed, _, _ = norm_forward(stream_feed, norms[4], norms[5])
        near_feed = pair_rows(normed.astype(BF))
        crest = jnp.pad(
            jnp.maximum(peak_self, peak_cross)[None], ((0, 7), (0, 128 - heads_here))
        )
    in_weight, self_out_t, cross_in, cross_out_t, gate_full, up_full, down_t = (
        w.reshape(width, -1)
        for w in (in_weight, self_out_t, cross_in, cross_out_t, gate_full, up_full, down_t)
    )
    unit_cross, inverse_cross = unit_rows_of(stream_cross)
    unit_feed, inverse_feed = unit_rows_of(stream_feed)
    far_own = swap(near_feed[:rows], "x")

    def feed_half(normed, cot_rows):
        gate_pre = nn(normed, gate_full)
        upward = nn(normed, up_full)
        sigmoid_gate = jax.nn.sigmoid(gate_pre)
        hidden = (gate_pre * sigmoid_gate * upward).astype(BF)
        grad_hidden = nn(cot_rows, down_t)
        grad_gate = grad_hidden * upward * sigmoid_gate * (1.0 + gate_pre * (1.0 - sigmoid_gate))
        grad_upward = grad_hidden * gate_pre * sigmoid_gate
        return hidden, grad_gate.astype(BF), grad_upward.astype(BF)

    def feed_back(grad_gate, grad_upward):
        return nt(grad_gate, gate_full) + nt(grad_upward, up_full)

    hidden_near, gate_near, up_near = feed_half(near_feed, cot_group[:seq_len])
    far_own, hidden_near, gate_near, up_near = lax.optimization_barrier(
        (far_own, hidden_near, gate_near, up_near)
    )
    far_feed = pair_rows(far_own)
    hidden_far, gate_far, up_far = feed_half(far_feed, cot_group[seq_len:])
    far_sum = feed_back(gate_far[:rows], up_far[:rows]) + swap(
        feed_back(gate_far[rows:], up_far[rows:]), "tensor"
    )
    far_sum = far_sum.astype(BF)
    got_far = swap(far_sum, "x")
    normed_feed = jnp.concatenate([near_feed, far_feed], axis=0)
    hidden = jnp.concatenate([hidden_near, hidden_far], axis=0)
    grad_gate = jnp.concatenate([gate_near, gate_far], axis=0)
    grad_upward = jnp.concatenate([up_near, up_far], axis=0)
    down_pair = PairSum(after(cot_group, far_sum), hidden, zs)
    gate_pair = PairSum(after(normed_feed, far_sum), grad_gate, zs)
    grad_normed = feed_back(gate_near[:rows], up_near[:rows]) + swap(
        feed_back(gate_near[rows:], up_near[rows:]), "tensor"
    )
    got_far = after(got_far, grad_normed, gate_pair.held, down_pair.held)
    grad_normed = grad_normed + got_far.astype(F32)
    stream_part, grad_feed_gain, grad_feed_bias = norm_backward(
        grad_normed, unit_feed, inverse_feed, norms[4]
    )
    grad_stream = cotangent.astype(F32) + stream_part
    grad_full = pair_rows(grad_stream.astype(BF))
    up_pair = PairSum(after(normed_feed, grad_full), grad_upward, zs)
    down_pair.second(grad_full)
    cross_output_sum = FullSum(grad_full, mixed_cross, zs)
    grad_mixed = nn(grad_full, cross_out_t).astype(BF)
    grad_query, grad_keys, grad_values = attend_back(
        query_cross, taken_cross, taken_cross, grad_mixed, cross_bias_row[:, None], (0, 0, pairs), None
    )
    gate_pair.second(grad_query)
    grad_normed = spread_pair(grad_query, cross_in)
    cross_query_sum = FullSum(normed_cross, grad_query, zs)
    part_memory = tn(memory, jnp.concatenate([grad_keys, grad_values], axis=1))
    stream_part, grad_cross_gain, grad_cross_bias = norm_backward(
        grad_normed, unit_cross, inverse_cross, norms[2]
    )
    grad_stream = grad_stream + stream_part
    grad_full = pair_rows(grad_stream.astype(BF))
    up_pair.second(grad_full)
    part_self_output = tn(grad_full, mixed_self)
    grad_mixed = nn(grad_full, self_out_t).astype(BF)
    grad_parts = attend_back(
        taken, taken, taken, grad_mixed, self_bias_row[:, None], (0, pairs, 2 * pairs), turns
    )
    grad_in = jnp.concatenate(grad_parts, axis=1)
    cross_output_sum.second(grad_in)
    cross_query_sum.second(grad_in)
    part_query, part_key, part_value = (
        tn(normed_self, part).astype(BF) for part in grad_parts
    )
    sum_cross_output = cross_output_sum.third(part_query, part_key).astype(F32)
    sum_cross_query = cross_query_sum.third(part_query, part_key).astype(F32)
    grad_normed = spread_pair(grad_in, in_weight)
    unit_self, inverse_self = unit_rows_of(stream)
    stream_part, grad_self_gain, grad_self_bias = norm_backward(
        grad_normed, unit_self, inverse_self, norms[0]
    )
    grad_stream = grad_stream + stream_part

    vector_sums = jnp.stack(
        [
            grad_self_gain,
            grad_self_bias,
            grad_cross_gain,
            grad_cross_bias,
            grad_feed_gain,
            grad_feed_bias,
        ]
    ).reshape(6, -1, shard_rows)
    vector_sums = vector_sums + swap(vector_sums, "tensor")
    vector_sums = jnp.pad(
        vector_sums.transpose(1, 0, 2), ((0, 0), (0, 2), (0, 128 - shard_rows))
    ).reshape(zs, 2, 2, 8, 128)

    def blocks(part):
        return part.astype(BF).reshape(zs, 2, 2, -1, part.shape[1])

    (vector_sums, sum_query, sum_key, sum_value, sum_self_output, sum_memory, crest) = (
        scatter_all(
            [
                vector_sums,
                blocks(part_query),
                blocks(part_key),
                blocks(part_value),
                blocks(part_self_output),
                blocks(part_memory),
            ],
            ["x", "x", "y", "x", "y", "z"],
            crest,
            zs,
        )
    )
    vector_sums = vector_sums[:, :shard_rows]
    peaks = crest[0, :heads_here]
    factor = jnp.sqrt(threshold[0] / jnp.maximum(peaks, threshold[0]))
    columns = jnp.repeat(factor, HEAD_DIM)[None, :]
    result = stream_feed + spread_group(Product([(hidden, down_t)], True))
    result = result.astype(BF)
    down_keep, down_got = down_pair.third()
    gate_keep, gate_got = gate_pair.third()
    up_keep, up_got = up_pair.third()

    def side_by_side(kept, got):
        low = jnp.where(x_at == 0, kept, got).astype(F32)
        high = jnp.where(x_at == 0, got, kept).astype(F32)
        return jnp.concatenate([low, high], axis=1)

    down_sum = side_by_side(down_keep, down_got).T
    gate_sum = side_by_side(gate_keep, gate_got)
    up_sum = side_by_side(up_keep, up_got)
    return (
        result,
        grad_stream,
        vector_sums[0],
        vector_sums[1],
        sum_query,
        sum_key,
        sum_value,
        sum_self_output.T,
        vector_sums[2],
        vector_sums[3],
        sum_cross_query,
        sum_memory[:, :inner],
        sum_memory[:, inner:],
        sum_cross_output.T,
        vector_sums[4],
        vector_sums[5],
        gate_sum,
        up_sum,
        down_sum,
        peaks,
        self_query.astype(F32) * columns,
        self_key.astype(F32) * columns,
        cross_query.astype(F32) * columns,
        cross_key.astype(F32) * columns,
    )


def solution(mesh):
    count = mesh.shape["dp"]
    mesh = Mesh(
        mesh.devices.reshape(count // 4, 2, 2, mesh.shape["tensor"]), ("z", "y", "x", "tensor")
    )
    dp = ("z", "y", "x")
    both = P(dp + ("tensor",), None)
    split = P(dp)
    row_major = P(dp, "tensor")
    column_major = P("tensor", dp)
    in_specs = (
        both,
        both,
        P(dp, None, None),
        P(dp, None),
        split,
        P(),
        split,
        split,
        row_major,
        row_major,
        row_major,
        column_major,
        split,
        split,
        row_major,
        row_major,
        row_major,
        column_major,
        split,
        split,
        row_major,
        row_major,
        column_major,
    )
    out_specs = (
        both,
        both,
        split,
        split,
        row_major,
        row_major,
        row_major,
        column_major,
        split,
        split,
        row_major,
        row_major,
        row_major,
        column_major,
        split,
        split,
        row_major,
        row_major,
        column_major,
        P("tensor"),
        row_major,
        row_major,
        row_major,
        row_major,
    )
    return jax.shard_map(
        per_device, mesh=mesh, in_specs=in_specs, out_specs=out_specs, check_vma=False
    )
```

```python
import functools

import jax
import jax.numpy as jnp
from jax import lax
from jax.experimental import pallas as pl
from jax.experimental.pallas import tpu as pltpu
from jax.sharding import Mesh
from jax.sharding import PartitionSpec as P

HEAD_DIM = 64
ROT_DIM = 32
EPSILON = 1e-05
NEGATIVE = -1e30
BF = jnp.bfloat16
F32 = jnp.float32


def swap(value, axis):
    return lax.ppermute(value, axis, [(0, 1), (1, 0)])


def pick(value, index, dim):
    return lax.dynamic_index_in_dim(value, index, dim, keepdims=False)


class Lanes:
    def __init__(self, send_sems, recv_sems, local_sems, zs):
        self.send_sems, self.recv_sems, self.local_sems = send_sems, recv_sems, local_sems
        self.used = self.used_local = 0
        self.z = lax.axis_index("z")
        self.y = lax.axis_index("y")
        self.x = lax.axis_index("x")
        self.zs = zs

    def local(self):
        self.used_local += 1
        return self.local_sems.at[self.used_local - 1]

    def copy(self, source, target, device):
        return self.copies([source], target, device)[0]

    def copies(self, sources, target, device):
        slot = self.used
        self.used += 1
        return [
            pltpu.make_async_remote_copy(
                src_ref=source,
                dst_ref=target,
                send_sem=self.send_sems.at[slot],
                recv_sem=self.recv_sems.at[slot],
                device_id=device,
                device_id_type=pl.DeviceIdType.MESH,
            )
            for source in sources
        ]


def guarded(condition, action):
    if condition is None:
        action()
    else:
        pl.when(condition)(action)


class Move:
    def __init__(self, copy, sends, receives):
        self.copy_, self.sends, self.receives = copy, sends, receives

    def start(self):
        guarded(self.sends, self.copy_.start)

    def arrived(self):
        guarded(self.receives, self.copy_.wait_recv)

    def sent(self):
        guarded(self.sends, self.copy_.wait_send)


class Gather:
    def __init__(self, lanes, whole):
        zs, z, y, x = lanes.zs, lanes.z, lanes.y, lanes.x
        own = whole.at[z, y, x]

        def block(zz, yy):
            return whole.at[zz, yy, x]

        def along(source, target, axis, to, sends=None, receives=None):
            return Move(lanes.copy(source, target, {axis: to}), sends, receives)

        self.first = [
            along(own, block(z, y), "y", 1 - y),
            along(own, block(z, y), "x", 1 - x),
        ]
        self.far = [[along(block(z, 1 - y), block(z, 1 - y), "x", 1 - x)]]
        self.steps = []
        for k in range(zs - 1):
            right, left = jnp.maximum(z - k, 0), jnp.minimum(z + k, zs - 1)
            step = []
            for zz, to, sends, receives, got in (
                (right, z + 1, (z >= k) & (z < zs - 1), z >= k + 1, jnp.maximum(z - 1 - k, 0)),
                (left, z - 1, (z + k < zs) & (z > 0), z + k + 1 < zs, jnp.minimum(z + 1 + k, zs - 1)),
            ):
                source = own if k == 0 else block(zz, y)
                move = along(source, block(zz, y), "z", to, sends, receives)
                follow = [
                    along(block(got, y), block(got, y), "y", 1 - y, receives, receives),
                    along(block(got, y), block(got, y), "x", 1 - x, receives, receives),
                    along(block(got, 1 - y), block(got, 1 - y), "x", 1 - x, receives, receives),
                ]
                step.append((move, follow))
            self.steps.append(step)

    def begin(self):
        for move, _ in self.steps[0]:
            move.start()
        for move in self.first:
            move.start()

    def step(self, k, side):
        move, follow = self.steps[k][side]
        move.arrived()
        if k + 1 < len(self.steps):
            self.steps[k + 1][side][0].start()
        follow[0].start()
        follow[1].start()

    def far_first(self):
        self.first[0].arrived()
        self.far[0][0].start()

    def far_step(self, k, side):
        _, follow = self.steps[k][side]
        follow[0].arrived()
        follow[2].start()

    def landed(self):
        self.first[1].arrived()
        self.far[0][0].arrived()
        for step in self.steps:
            for _, follow in step:
                follow[1].arrived()
                follow[2].arrived()

    def sent(self):
        for move in self.first + self.far[0]:
            move.sent()
        for step in self.steps:
            for move, follow in step:
                move.sent()
                for other in follow:
                    other.sent()


class PairGather:
    def __init__(self, lanes, shard, whole, y_first):
        zs, z, y, x = lanes.zs, lanes.z, lanes.y, lanes.x
        ff = whole.shape[-1]
        kept = shard.at[:, pl.ds(pl.multiple_of(x * ff, ff), ff)]
        sent = shard.at[:, pl.ds(pl.multiple_of((1 - x) * ff, ff), ff)]
        self.y_first = y_first

        def along(piece, axis, to, sends=None, receives=None):
            return Move(lanes.copy(piece, piece, {axis: to}), sends, receives)

        self.swap = Move(lanes.copy(sent, whole.at[z, y, x], {"x": 1 - x}), None, None)
        self.local = pltpu.make_async_copy(kept, whole.at[z, y, x], lanes.local())
        self.own_y = along(whole.at[z, y], "y", 1 - y)
        self.steps = []
        for k in range(zs - 1):
            step = []
            for zz, to, sends, receives, got in (
                (jnp.maximum(z - k, 0), z + 1, (z >= k) & (z < zs - 1), z >= k + 1, jnp.maximum(z - 1 - k, 0)),
                (jnp.minimum(z + k, zs - 1), z - 1, (z + k < zs) & (z > 0), z + k + 1 < zs, jnp.minimum(z + 1 + k, zs - 1)),
            ):
                piece = whole.at[zz] if y_first else whole.at[zz, y]
                move = along(piece, "z", to, sends, receives)
                follow = [] if y_first else [along(whole.at[got, y], "y", 1 - y, receives, receives)]
                step.append((move, follow))
            self.steps.append(step)

    def begin(self):
        self.swap.start()
        self.local.start()

    def far_first(self):
        self.swap.arrived()
        self.local.wait()
        self.own_y.start()
        if not self.y_first:
            for move, _ in self.steps[0]:
                move.start()

    def own_y_arrived(self):
        self.own_y.arrived()
        if self.y_first:
            for move, _ in self.steps[0]:
                move.start()

    def step(self, k, side):
        move, follow = self.steps[k][side]
        move.arrived()
        if k + 1 < len(self.steps):
            self.steps[k + 1][side][0].start()
        for other in follow:
            other.start()

    def landed(self):
        if not self.y_first:
            self.own_y.arrived()
        for step in self.steps:
            for move, follow in step:
                for other in follow:
                    other.arrived()

    def sent(self):
        self.swap.sent()
        self.own_y.sent()
        for step in self.steps:
            for move, follow in step:
                move.sent()
                for other in follow:
                    other.sent()


def greet(zs, mates=False):
    z, y, x = lax.axis_index("z"), lax.axis_index("y"), lax.axis_index("x")
    barrier = pltpu.get_barrier_semaphore()

    def signal(device):
        pl.semaphore_signal(barrier, inc=1, device_id=device, device_id_type=pl.DeviceIdType.MESH)

    signal({"x": 1 - x})
    signal({"y": 1 - y})
    pl.when(z > 0)(lambda: signal({"z": z - 1}))
    pl.when(z < zs - 1)(lambda: signal({"z": z + 1}))
    if mates:
        signal({"tensor": 1 - lax.axis_index("tensor")})
    peers = (3 if mates else 2) + (z > 0).astype(jnp.int32) + (z < zs - 1).astype(jnp.int32)
    pl.semaphore_wait(barrier, peers)


def gather_kernel(zs, groups, pairs, *refs):
    shards = sum(groups)
    owns, pair_in = refs[:shards], refs[shards : shards + pairs]
    refs = refs[shards + pairs :]
    outs = refs[: len(groups) + pairs]
    lanes = Lanes(*refs[len(groups) + pairs :], zs)
    z, y, x = lanes.z, lanes.y, lanes.x
    pieces, at = [], 0
    for count, whole in zip(groups, outs):
        width = whole.shape[-1] // count
        for i in range(count):
            target = whole.at[z, y, x, :, pl.ds(i * width, width)]
            pieces.append(pltpu.make_async_copy(owns[at], target, lanes.local()))
            at += 1
    for piece in pieces:
        piece.start()
    greet(zs)
    gathers = [Gather(lanes, whole) for whole in outs[: len(groups)]]
    quarters = [
        PairGather(lanes, pair_in[i], outs[len(groups) + i], i == 0) for i in range(pairs)
    ]
    for quarter in quarters:
        quarter.begin()
    for piece in pieces:
        piece.wait()
    for gather in gathers:
        gather.begin()
    for quarter in quarters:
        quarter.far_first()
    for gather in gathers:
        gather.far_first()
    for k, side in [(k, side) for k in range(zs - 1) for side in range(2)]:
        for gather in gathers:
            gather.step(k, side)
        for quarter in quarters:
            if quarter.y_first:
                if k == 0 and side == 0:
                    quarter.own_y_arrived()
            else:
                quarter.step(k, side)
        for gather in gathers:
            gather.far_step(k, side)
        for quarter in quarters:
            if quarter.y_first:
                quarter.step(k, side)
    for item in gathers + quarters:
        item.landed()
        item.sent()


def gather_all(groups, quarters, zs):
    flat = [shard for group in groups for shard in group] + list(quarters)
    outs = []
    for group in groups:
        columns = sum(shard.shape[1] for shard in group)
        outs.append(
            jax.ShapeDtypeStruct((zs, 2, 2, group[0].shape[0], columns), group[0].dtype)
        )
    for shard in quarters:
        outs.append(
            jax.ShapeDtypeStruct((zs, 2, 2, shard.shape[0], shard.shape[1] // 2), shard.dtype)
        )
    count, pairs = len(groups), len(quarters)
    moves = count * (3 + 8 * (zs - 1)) + pairs * (2 + 4 * (zs - 1))
    hbm = pl.BlockSpec(memory_space=pltpu.HBM)
    return pl.pallas_call(
        functools.partial(gather_kernel, zs, tuple(len(group) for group in groups), pairs),
        out_shape=outs,
        in_specs=[hbm] * len(flat),
        out_specs=[hbm] * len(outs),
        scratch_shapes=[
            pltpu.SemaphoreType.DMA((moves,)),
            pltpu.SemaphoreType.DMA((moves,)),
            pltpu.SemaphoreType.DMA((len(flat),)),
        ],
        compiler_params=pltpu.CompilerParams(collective_id=1, has_side_effects=True),
    )(*flat)


def plus(*terms):
    total = terms[0].astype(F32)
    for term in terms[1:]:
        total = total + term.astype(F32)
    return total


def ends_first(zs):
    order = []
    for i in range(zs // 2):
        order += [zs - 1 - i, i]
    return order


class Line:
    def __init__(self, lanes, part, from_left, from_right):
        zs, z = lanes.zs, lanes.z
        self.zs, self.z, self.part = zs, z, part
        self.from_left, self.from_right = from_left, from_right
        self.right, self.left = {}, {}
        for d in ends_first(zs):
            after, before = jnp.minimum(z + 1, zs - 1), jnp.maximum(z - 1, 0)
            self.right[d] = lanes.copies(
                (part.at[d], from_left.at[d]), from_left.at[d], {"z": after}
            )
            self.left[d] = lanes.copies(
                (part.at[d], from_right.at[d]), from_right.at[d], {"z": before}
            )

    def pass_on(self, d):
        for moves, inbox, sends, edge in (
            (self.right[d], self.from_left, self.z < d, self.z == 0),
            (self.left[d], self.from_right, self.z > d, self.z == self.zs - 1),
        ):

            @pl.when(sends & edge)
            def _():
                moves[0].start()

            @pl.when(sends & jnp.logical_not(edge))
            def _():
                moves[1].wait_recv()
                inbox[d] = plus(self.part[d], inbox[d]).astype(inbox.dtype)
                moves[1].start()

    def total(self, sink):
        for d in range(self.zs):

            @pl.when(self.z == d)
            def _():
                terms = [self.part[d]]
                if d > 0:
                    self.right[d][0].wait_recv()
                    terms.append(self.from_left[d])
                if d < self.zs - 1:
                    self.left[d][0].wait_recv()
                    terms.append(self.from_right[d])
                sink[...] = plus(*terms).astype(sink.dtype)

    def finish(self):
        for d in ends_first(self.zs):
            pl.when(self.z < d)(self.right[d][0].wait_send)
            pl.when(self.z > d)(self.left[d][0].wait_send)


class Scatter:
    def __init__(self, lanes, part, held, out, first):
        zs, z, y, x = lanes.zs, lanes.z, lanes.y, lanes.x
        got, near, from_left, from_right, ready = held
        second = "y" if first == "x" else "x"
        self.lanes, self.part, self.got, self.near, self.ready, self.out = (
            lanes, part, got, near, ready, out,
        )
        f, s = (x, y) if first == "x" else (y, x)
        self.f, self.s = f, s

        def block(zz, a, b):
            return part.at[zz, b, a] if first == "x" else part.at[zz, a, b]

        self.block = block
        self.one, self.two = {}, {}
        for zz in ends_first(zs):
            for j, b in enumerate((1 - s, s)):
                self.one[zz, j] = Move(
                    lanes.copy(block(zz, 1 - f, b), got.at[zz, j], {first: 1 - f}), None, None
                )
        for zz in ends_first(zs):
            self.two[zz] = Move(
                lanes.copy(got.at[zz, 0], near.at[zz], {second: 1 - s}), None, None
            )
        self.line = Line(lanes, ready, from_left, from_right)

    def begin(self, zz):
        for j in range(2):
            self.one[zz, j].start()

    def second(self, zz):
        self.one[zz, 0].arrived()
        mine, got = self.block(zz, self.f, 1 - self.s), self.got
        got[zz, 0] = plus(mine[...], got[zz, 0]).astype(got.dtype)
        self.two[zz].start()

    def third(self, zz):
        self.one[zz, 1].arrived()
        self.two[zz].arrived()
        mine = self.block(zz, self.f, self.s)
        self.ready[zz] = plus(mine[...], self.got[zz, 1], self.near[zz]).astype(self.ready.dtype)
        self.line.pass_on(zz)

    def finish(self):
        self.line.total(self.out)
        self.line.finish()
        for move in list(self.one.values()) + list(self.two.values()):
            move.sent()


class ScatterZ:
    def __init__(self, lanes, part, held, out):
        y, x = lanes.y, lanes.x
        from_left, from_right, held_z, near, last = held
        self.lanes, self.sum_z, self.near, self.last, self.out = lanes, held_z, near, last, out
        self.line = Line(lanes, part, from_left, from_right)
        self.two = Move(lanes.copy(held_z.at[1 - y], near, {"y": 1 - y}), None, None)
        self.three = Move(lanes.copy(near.at[1 - x], last, {"x": 1 - x}), None, None)

    def pass_on(self, d):
        self.line.pass_on(d)

    def total(self):
        self.line.total(self.sum_z)
        self.two.start()

    def after(self):
        self.two.arrived()
        self.near[...] = plus(self.sum_z[self.lanes.y], self.near[...]).astype(self.near.dtype)
        self.three.start()

    def finish(self):
        self.three.arrived()
        self.out[...] = plus(self.near[self.lanes.x], self.last[...]).astype(self.out.dtype)
        self.line.finish()
        self.two.sent()
        self.three.sent()


class Crest:
    def __init__(self, lanes, own, held, out):
        zs, z, y, x = lanes.zs, lanes.z, lanes.y, lanes.x
        near_x, near_y, mine_x, mine_y, right, left, inbox_r, inbox_l = (
            held.at[i] for i in range(8)
        )
        self.zs, self.z, self.own, self.out = zs, z, own, out
        self.near_x, self.near_y, self.mine_x, self.mine_y = near_x, near_y, mine_x, mine_y
        self.ways = (
            (right, inbox_r, z > 0, z < zs - 1),
            (left, inbox_l, z < zs - 1, z > 0),
        )
        self.one = Move(lanes.copy(own, near_x, {"x": 1 - x}), None, None)
        self.two = Move(lanes.copy(mine_x, near_y, {"y": 1 - y}), None, None)
        self.moves = [
            Move(lanes.copy(right, inbox_r, {"z": jnp.minimum(z + 1, zs - 1)}), z < zs - 1, z > 0),
            Move(lanes.copy(left, inbox_l, {"z": jnp.maximum(z - 1, 0)}), z > 0, z < zs - 1),
        ]

    def second(self):
        self.one.arrived()
        self.mine_x[...] = jnp.maximum(self.own[...], self.near_x[...])
        self.two.start()

    def finish(self):
        self.two.arrived()
        self.mine_y[...] = jnp.maximum(self.mine_x[...], self.near_y[...])
        self.out[...] = self.mine_y[...]
        for move, (held, inbox, has_before, has_after) in zip(self.moves, self.ways):

            @pl.when(has_before)
            def _():
                move.copy_.wait_recv()
                self.out[...] = jnp.maximum(self.out[...], inbox[...])
                held[...] = jnp.maximum(self.mine_y[...], inbox[...])

            @pl.when(jnp.logical_not(has_before))
            def _():
                held[...] = self.mine_y[...]

            move.start()
        for move in [self.one, self.two] + self.moves:
            move.sent()


def scatter_kernel(zs, orders, *refs):
    count = len(orders)
    parts, crest_in, refs = refs[:count], refs[count], refs[count + 1 :]
    outs, crest_out, rest = refs[:count], refs[count], list(refs[count + 1 :])
    send_sems, recv_sems = rest[:2]
    rest = rest[2:]
    lanes = Lanes(send_sems, recv_sems, None, zs)
    greet(zs)
    full, zfirst = [], []
    for i, order in enumerate(orders):
        held, rest = rest[:5], rest[5:]
        if order == "z":
            zfirst.append(ScatterZ(lanes, parts[i], held, outs[i]))
        else:
            full.append(Scatter(lanes, parts[i], held, outs[i], order))
    crest = Crest(lanes, crest_in, rest[0], crest_out)
    crest.one.start()
    order = ends_first(zs)
    for i in range(zs + 3):
        for item in full:
            if i < zs:
                item.begin(order[i])
        if i == 1:
            crest.second()
        if i < zs:
            for item in zfirst:
                item.pass_on(order[i])
        for item in full:
            if 2 <= i < zs + 2:
                item.second(order[i - 2])
        if i == zs:
            for item in zfirst:
                item.total()
        for item in full:
            if 3 <= i:
                item.third(order[i - 3])
    crest.finish()
    for item in zfirst:
        item.after()
    for item in full:
        item.finish()
    for item in zfirst:
        item.finish()


def scatter_all(parts, orders, crest, zs):
    scratch, moves = [], 4
    for part, order in zip(parts, orders):
        block = part.shape[3:]
        if order == "z":
            shapes = [(zs, 2, 2) + block] * 2 + [(2, 2) + block, (2,) + block, block]
            moves += 2 * zs + 2
        else:
            shapes = [(zs, 2) + block] + [(zs,) + block] * 4
            moves += 5 * zs
        scratch += [pltpu.VMEM(shape, part.dtype) for shape in shapes]
    vmem = pl.BlockSpec(memory_space=pltpu.VMEM)
    return pl.pallas_call(
        functools.partial(scatter_kernel, zs, orders),
        out_shape=[jax.ShapeDtypeStruct(part.shape[3:], F32) for part in parts]
        + [jax.ShapeDtypeStruct(crest.shape, F32)],
        in_specs=[vmem] * (len(parts) + 1),
        out_specs=[vmem] * (len(parts) + 1),
        scratch_shapes=[pltpu.SemaphoreType.DMA((moves,)), pltpu.SemaphoreType.DMA((moves,))]
        + scratch
        + [pltpu.VMEM((8,) + crest.shape, F32)],
        compiler_params=pltpu.CompilerParams(
            collective_id=2, has_side_effects=True, vmem_limit_bytes=56 * 2**20
        ),
    )(*parts, crest)


def nn(left, right):
    return lax.dot_general(left, right, (((1,), (0,)), ((), ())), preferred_element_type=F32)


def nt(left, right):
    return lax.dot_general(left, right, (((1,), (1,)), ((), ())), preferred_element_type=F32)


def tn(left, right):
    return lax.dot_general(left, right, (((0,), (0,)), ((), ())), preferred_element_type=F32)


def after(value, *others):
    return lax.optimization_barrier((value, others))[0]


class FullSum:
    def __init__(self, left, right, zs):
        self.zs = zs
        held = tn(left, right).astype(BF)
        self.held = held.reshape(2 * zs, 2, -1, held.shape[1])
        self.x, self.y = lax.axis_index("x"), lax.axis_index("y")
        self.got = swap(pick(self.held, 1 - self.x, 1), "x")

    def second(self, *others):
        got = after(self.got, others)
        held = pick(self.held, self.x, 1).astype(F32) + got.astype(F32)
        self.held = held.astype(BF).reshape(self.zs, 2, -1, held.shape[-1])
        self.got = swap(pick(self.held, 1 - self.y, 1), "y")

    def third(self, *others):
        got = after(self.got, others)
        held = pick(self.held, self.y, 1).astype(F32) + got.astype(F32)
        return lax.psum_scatter(held.astype(BF), "z", scatter_dimension=0, tiled=False)


class PairSum:
    def __init__(self, left, right, zs):
        held = tn(left, right).astype(BF)
        self.held = held.reshape(zs, 2, -1, held.shape[1])
        self.y = lax.axis_index("y")
        self.sent = pick(self.held, 1 - self.y, 1)
        self.got = swap(self.sent, "y")

    def second(self, *others):
        got = after(self.got, others)
        held = pick(self.held, self.y, 1).astype(F32) + got.astype(F32)
        held = lax.psum_scatter(held.astype(BF), "z", scatter_dimension=0, tiled=False)
        self.held = held.reshape(2, -1, held.shape[-1])

    def third(self):
        at = lax.axis_index("x")
        return pick(self.held, at, 0), swap(pick(self.held, 1 - at, 0), "x")


def norm_forward(stream, gain_vec, bias_vec):
    average = jnp.mean(stream, axis=-1, keepdims=True)
    centred = stream - average
    inverse = lax.rsqrt(jnp.mean(centred * centred, axis=-1, keepdims=True) + EPSILON)
    unit_rows = centred * inverse
    return (unit_rows * gain_vec + bias_vec, unit_rows, inverse)


def unit_rows_of(stream):
    _, unit_rows, inverse = norm_forward(stream, 1.0, 0.0)
    return unit_rows, inverse


def norm_backward(incoming, unit_rows, inverse, gain_vec):
    gain_grad = jnp.sum(incoming * unit_rows, axis=0)
    bias_grad = jnp.sum(incoming, axis=0)
    scaled = incoming * gain_vec
    stream_grad = inverse * (
        scaled
        - jnp.mean(scaled, axis=-1, keepdims=True)
        - unit_rows * jnp.mean(scaled * unit_rows, axis=-1, keepdims=True)
    )
    return (stream_grad, gain_grad, bias_grad)


def turn_tables(positions):
    rates = 10000.0 ** (-jnp.arange(0, ROT_DIM, 2).astype(F32) / ROT_DIM)
    angles = positions[:, None] * rates[None, :]
    cosine, sine = jnp.cos(angles), jnp.sin(angles)
    rest = jnp.ones((positions.shape[0], HEAD_DIM - ROT_DIM), F32)
    zero, none = jnp.zeros_like(rest), jnp.zeros_like(sine)
    return (
        jnp.concatenate([cosine, cosine, rest] * 2, axis=1),
        jnp.concatenate([-sine, none, zero] * 2, axis=1),
        jnp.concatenate([none, sine, zero] * 2, axis=1),
    )


def turn(field, cosine, sine_a, sine_b, direction):
    half = ROT_DIM // 2
    width = field.shape[-1]
    ahead = pltpu.roll(field, width - half, 1)
    behind = pltpu.roll(field, half, 1)
    return field * cosine + direction * (ahead * sine_a + behind * sine_b)


def head_lanes(shape, which):
    lanes = lax.broadcasted_iota(jnp.int32, shape, 1)
    return (lanes >= which * HEAD_DIM) & (lanes < (which + 1) * HEAD_DIM)


def attend_tile(query, keys, values, bias):
    scores = nt(query, keys) + bias
    top = jnp.max(scores, axis=-1, keepdims=True)
    weights = jnp.exp(scores - top)
    total = jnp.sum(weights, axis=-1, keepdims=True)
    return nn(weights.astype(BF), values) / total, top


def attend_kernel(q_ref, k_ref, v_ref, bias_ref, mixed_ref, peak_ref):
    rows = q_ref.shape[0]
    tile = rows // 3 if rows % 3 == 0 and (rows // 3) % 16 == 0 else rows
    keys, values, bias = k_ref[...], v_ref[...], bias_ref[...]
    peaks = [None, None]
    for start in range(0, rows, tile):
        query = q_ref[start : start + tile, :] * BF(HEAD_DIM ** (-0.5))
        outs = []
        for which in range(2):
            one = jnp.where(head_lanes(query.shape, which), query, jnp.zeros_like(query))
            out, top = attend_tile(one, keys, values, bias)
            outs.append(out)
            top = jnp.max(top, axis=0, keepdims=True)
            peaks[which] = top if peaks[which] is None else jnp.maximum(peaks[which], top)
        mixed = jnp.where(head_lanes(outs[0].shape, 0), outs[0], outs[1])
        mixed_ref[start : start + tile, :] = mixed.astype(BF)
    spot = head_lanes((8, 2 * HEAD_DIM), 0)
    peak_ref[0] = jnp.where(
        spot, jnp.broadcast_to(peaks[0], spot.shape), jnp.broadcast_to(peaks[1], spot.shape)
    )


def attend(query, keys, values, bias, offsets):
    rows, tokens = query.shape[0], keys.shape[0]
    pairs = bias.shape[0]
    wide = 2 * HEAD_DIM
    mixed, peak = pl.pallas_call(
        attend_kernel,
        grid=(pairs,),
        out_shape=[
            jax.ShapeDtypeStruct((rows, pairs * wide), BF),
            jax.ShapeDtypeStruct((pairs, 8, wide), F32),
        ],
        in_specs=[
            pl.BlockSpec((rows, wide), lambda j: (0, offsets[0] + j)),
            pl.BlockSpec((tokens, wide), lambda j: (0, offsets[1] + j)),
            pl.BlockSpec((tokens, wide), lambda j: (0, offsets[2] + j)),
            pl.BlockSpec((1, tokens), lambda j: (0, 0)),
        ],
        out_specs=[
            pl.BlockSpec((rows, wide), lambda j: (0, j)),
            pl.BlockSpec((1, 8, wide), lambda j: (j, 0, 0)),
        ],
        compiler_params=pltpu.CompilerParams(vmem_limit_bytes=48 * 2**20),
        cost_estimate=pl.CostEstimate(
            flops=8 * rows * tokens * pairs * wide,
            bytes_accessed=4 * (rows + tokens) * pairs * wide,
            transcendentals=2 * pairs * rows * tokens,
        ),
    )(query, keys, values, bias[:1])
    return mixed, peak[:, 0, ::HEAD_DIM].reshape(-1)


def attend_back_kernel(turned, q_ref, k_ref, v_ref, g_ref, bias_ref, *refs):
    if turned:
        cos_ref, sa_ref, sb_ref = refs[:3]
        refs = refs[3:]
    dq_ref, dk_ref, dv_ref, dk_acc, dv_acc = refs
    rows = q_ref.shape[0]
    tile = rows // 3 if rows % 3 == 0 and (rows // 3) % 128 == 0 else rows
    scale = BF(HEAD_DIM ** (-0.5))
    keys, values, bias = k_ref[...], v_ref[...], bias_ref[...]
    for start in range(0, rows, tile):
        part = slice(start, start + tile)
        query, grad = q_ref[part, :] * scale, g_ref[part, :]
        dq = None
        for which in range(2):
            mine = head_lanes(query.shape, which)
            one = jnp.where(mine, query, jnp.zeros_like(query))
            out = jnp.where(mine, grad, jnp.zeros_like(grad))
            scores = nt(keys, one) + bias
            weights = jnp.exp(scores - jnp.max(scores, axis=0, keepdims=True))
            weights = weights * (1.0 / jnp.sum(weights, axis=0, keepdims=True))
            slope = nt(values, out)
            slope = weights * (slope - jnp.sum(weights * slope, axis=0, keepdims=True))
            slope = slope.astype(BF)
            dv = nn(weights.astype(BF), out)
            dk = nn(slope, one)
            other = jnp.where(head_lanes(keys.shape, which), keys, jnp.zeros_like(keys))
            piece = tn(slope, other * scale)
            dq = piece if dq is None else dq + piece
            if start == 0 and which == 0:
                dv_acc[...] = dv
                dk_acc[...] = dk
            else:
                dv_acc[...] += dv
                dk_acc[...] += dk
        if turned:
            dq = turn(dq, cos_ref[part, :], sa_ref[part, :], sb_ref[part, :], -1.0)
        dq_ref[part, :] = dq.astype(BF)
    dk = dk_acc[...]
    if turned:
        dk = turn(dk, cos_ref[...], sa_ref[...], sb_ref[...], -1.0)
    dk_ref[...] = dk.astype(BF)
    dv_ref[...] = dv_acc[...].astype(BF)


def attend_back(query, keys, values, grad, bias_column, offsets, turns):
    rows, tokens = query.shape[0], keys.shape[0]
    wide = 2 * HEAD_DIM
    pairs = grad.shape[1] // wide
    ins = [query, keys, values, grad, bias_column]
    specs = [
        pl.BlockSpec((rows, wide), lambda j: (0, offsets[0] + j)),
        pl.BlockSpec((tokens, wide), lambda j: (0, offsets[1] + j)),
        pl.BlockSpec((tokens, wide), lambda j: (0, offsets[2] + j)),
        pl.BlockSpec((rows, wide), lambda j: (0, j)),
        pl.BlockSpec((tokens, 1), lambda j: (0, 0)),
    ]
    if turns is not None:
        ins += list(turns)
        specs += [pl.BlockSpec((rows, wide), lambda j: (0, 0))] * 3
    return pl.pallas_call(
        functools.partial(attend_back_kernel, turns is not None),
        grid=(pairs,),
        out_shape=[
            jax.ShapeDtypeStruct((rows, pairs * wide), BF),
            jax.ShapeDtypeStruct((tokens, pairs * wide), BF),
            jax.ShapeDtypeStruct((tokens, pairs * wide), BF),
        ],
        in_specs=specs,
        out_specs=[
            pl.BlockSpec((rows, wide), lambda j: (0, j)),
            pl.BlockSpec((tokens, wide), lambda j: (0, j)),
            pl.BlockSpec((tokens, wide), lambda j: (0, j)),
        ],
        scratch_shapes=[pltpu.VMEM((tokens, wide), F32), pltpu.VMEM((tokens, wide), F32)],
        compiler_params=pltpu.CompilerParams(vmem_limit_bytes=48 * 2**20),
        cost_estimate=pl.CostEstimate(
            flops=20 * rows * tokens * pairs * wide,
            bytes_accessed=8 * (rows + tokens) * pairs * wide,
            transcendentals=2 * pairs * rows * tokens,
        ),
    )(*ins)


def project_kernel(turned, x_ref, w_ref, cos_ref, sa_ref, sb_ref, out_ref):
    wide = 2 * HEAD_DIM
    made = nn(x_ref[...], w_ref[...])

    @pl.when(pl.program_id(0) < turned)
    def _():
        for start in range(0, made.shape[1], wide):
            piece = turn(made[:, start : start + wide], cos_ref[...], sa_ref[...], sb_ref[...], 1.0)
            out_ref[:, start : start + wide] = piece.astype(BF)

    @pl.when(pl.program_id(0) >= turned)
    def _():
        out_ref[...] = made.astype(BF)


def project(rows, weight, turns, turned_columns):
    count, depth = rows.shape
    columns = weight.shape[1]
    block = 2 * HEAD_DIM * (2 if turned_columns % (4 * HEAD_DIM) == 0 else 1)
    table = pl.BlockSpec((count, 2 * HEAD_DIM), lambda j: (0, 0))
    return pl.pallas_call(
        functools.partial(project_kernel, turned_columns // block),
        grid=(columns // block,),
        out_shape=jax.ShapeDtypeStruct((count, columns), BF),
        in_specs=[
            pl.BlockSpec((count, depth), lambda j: (0, 0)),
            pl.BlockSpec((depth, block), lambda j: (0, j)),
            table,
            table,
            table,
        ],
        out_specs=pl.BlockSpec((count, block), lambda j: (0, j)),
        compiler_params=pltpu.CompilerParams(vmem_limit_bytes=48 * 2**20),
        cost_estimate=pl.CostEstimate(
            flops=2 * count * depth * columns,
            bytes_accessed=2 * (count * depth + depth * columns + count * columns),
            transcendentals=0,
        ),
    )(rows, weight, *turns)


PLAN = (
    0, 100, 300, 400, 500, 200, 2000, 1100, 2020, 2010, 2001, 3010, 1000, 1300, 3000, 2011,
    2101, 3011, 1500, 3001, 2220, 2021, 3021, 2100, 2200, 2300, 2110, 2201, 3020, 2210, 1400,
    2111, 2121, 2221, 2120, 2211, 3101, 2301, 5500, 4000, -1, -1, 2400, 3201, 2310, 3110, -1,
    1200, 3111, 3120, -1, -1, -1, 2401, 2410, 2311, 3100, 3200, -1, -1, -1, 3121, -1, -1, -1,
    -1, 2411, 3221, -1, 2421, 2501, 3211, 2500, 2320, -1, -1, 3210, 3220, 4100, 2420, 6000, -1,
    -1, -1, -1, -1, -1, 2510, 2511, 4200, -1, -1, -1, -1, -1, -1, 2321, -1, -1, -1, -1, -1, -1,
    -1, -1, -1, -1, -1, -1, -1, -1, 2521, 7000, 2520,
)


def normalise(stream, gain_vec, bias_vec):
    average = jnp.mean(stream, axis=-1, keepdims=True)
    centred = stream - average
    inverse = lax.rsqrt(jnp.mean(centred * centred, axis=-1, keepdims=True) + EPSILON)
    return centred * inverse * gain_vec + bias_vec


def forward_kernel(zs, *refs):
    refs = list(refs)

    def take(count):
        taken_refs = refs[:count]
        del refs[:count]
        return taken_refs

    shards = take(9)
    quarters_in = take(3)
    inputs_hbm, cot_hbm, cos_ref, sa_ref, sb_ref, self_bias, cross_bias, memory = take(8)
    wholes = take(3)
    quarter_outs = take(3)
    outs = take(15)
    cot_out = take(1)[0]
    peak_out = take(1)[0]
    send_sems, recv_sems, local_sems = take(3)
    w_in, w_a, w_b = take(3)
    (
        x_all, normed_self, taken, mixed_self, stream_cross, normed_cross,
        query_cross, taken_cross, mixed_cross, stream_feed, normed_feed,
        part_send, part_got, vectors, crest,
    ) = take(15)
    lanes = Lanes(send_sems, recv_sems, local_sems, zs)
    z, y, x = lanes.z, lanes.y, lanes.x
    t = lax.axis_index("tensor")
    rows, width = inputs_hbm.shape
    wide = 2 * HEAD_DIM

    def local(source, target):
        return pltpu.make_async_copy(source, target, lanes.local())

    rows_here, inner = shards[1].shape
    rows_kv = shards[6].shape[0]

    def spot(whole, row, count, column, wide_):
        return whole.at[z, y, x, pl.ds(row, count), pl.ds(column, wide_)]

    places = [
        spot(wholes[0], 0, rows_here, 3 * inner, shards[0].shape[1]),
        spot(wholes[0], 0, rows_here, 0, inner),
        spot(wholes[0], 0, rows_here, inner, inner),
        spot(wholes[0], 0, rows_here, 2 * inner, inner),
        spot(wholes[1], 0, rows_here, 0, inner),
        spot(wholes[1], 0, rows_here, inner, inner),
        spot(wholes[2], 0, rows_kv, 0, inner),
        spot(wholes[2], rows_kv, rows_kv, 0, inner),
        spot(wholes[2], 0, rows_here, inner, inner),
    ]
    pieces = [local(shard, place) for shard, place in zip(shards, places)]
    own_inputs = local(inputs_hbm, x_all.at[0])
    own_cot = local(cot_hbm, cot_out.at[0])
    for piece in pieces + [own_inputs, own_cot]:
        piece.start()
    greet(zs, True)

    def mate(source, target):
        return Move(lanes.copy(source, target, {"tensor": 1 - t}), None, None)

    def across(source, target):
        return Move(lanes.copy(source, target, {"x": 1 - x}), None, None)

    mate_inputs = mate(inputs_hbm, x_all.at[1])
    cot_moves = [
        mate(cot_hbm, cot_out.at[1]),
        across(cot_hbm, cot_out.at[2]),
        mate(cot_out.at[2], cot_out.at[3]),
    ]
    feed_moves = [mate(normed_feed.at[0], normed_feed.at[1])]
    mate_self = mate(part_send, part_got)
    mate_normed = mate(normed_cross.at[0], normed_cross.at[1])
    mate_cross = mate(part_send, part_got)
    gathers = [Gather(lanes, whole) for whole in wholes]
    quarters = [
        PairGather(lanes, quarters_in[i], quarter_outs[i], i == 2) for i in range(3)
    ]
    loads = [
        local(whole, held)
        for whole, held in zip(wholes, (w_in, w_a, w_b))
    ]
    results = (
        normed_self, taken, mixed_self, stream_cross, normed_cross,
        query_cross, taken_cross, mixed_cross, stream_feed, normed_feed,
        w_in.at[:, :, :, :, pl.ds(0, 3 * inner)],
        w_a.at[:, :, :, :, pl.ds(0, inner)],
        w_a.at[:, :, :, :, pl.ds(inner, inner)],
        w_b.at[:, :, :, :, pl.ds(inner, inner)],
        vectors,
    )
    saves = [local(held, out) for held, out in zip(results, outs)]

    mate_inputs.start()
    cot_moves[0].start()
    for piece in pieces:
        piece.wait()
    columns = 3 * inner
    pairs = inner // wide
    block = 2 * wide
    tile = 128 if rows % 128 == 0 else rows
    chunk = width // zs
    total = 2 * rows
    step = total // 3 if total % 3 == 0 and (total // 3) % 16 == 0 else total
    ready = set()

    def vec(i):
        return vectors[i : i + 1, :]

    def need(*groups):
        assert ready.issuperset(groups)

    def over(count, size, body):
        @pl.loop(0, count // size)
        def _(i):
            body(pl.ds(pl.multiple_of(i * size, size), size), i)

    def attend_all(query_ref, keys_at, values_at, kv_ref, bias_ref, mixed_ref):
        lane = lax.broadcasted_iota(jnp.int32, (8, wide), 1)
        for j in range(pairs):
            at = slice(j * wide, (j + 1) * wide)
            keys_in = slice(keys_at + j * wide, keys_at + (j + 1) * wide)
            values_in = slice(values_at + j * wide, values_at + (j + 1) * wide)

            def body(part, _):
                query = query_ref[part, at] * BF(HEAD_DIM ** (-0.5))
                outs = []
                for which in range(2):
                    mine = head_lanes(query.shape, which)
                    one = jnp.where(mine, query, jnp.zeros_like(query))
                    out, top = attend_tile(
                        one, kv_ref[:, keys_in], kv_ref[:, values_in], bias_ref[...]
                    )
                    outs.append(out)
                    top = jnp.broadcast_to(jnp.max(top, axis=0, keepdims=True), lane.shape)
                    best = jnp.where(lane == 2 * j + which, top, NEGATIVE)
                    crest[...] = jnp.maximum(crest[...], best)
                made = jnp.where(head_lanes(outs[0].shape, 0), outs[0], outs[1])
                mixed_ref[part, at] = made.astype(BF)

            over(total, step, body)
            yield

    def out_project(mixed_ref, weight, move, send, got, base, target):
        for zz in range(zs):
            cols = slice(zz * chunk, (zz + 1) * chunk)

            def body(part, i):
                left = mixed_ref[pl.ds(pl.multiple_of(rows + i * tile, tile), tile), :]
                send[part, cols] = nt(left, weight(zz)).astype(BF)

            over(rows, tile, body)
        move.start()
        yield
        for zz in range(zs):
            cols = slice(zz * chunk, (zz + 1) * chunk)

            def body(part, _):
                made = nt(mixed_ref[part, :], weight(zz))
                target[part, cols] = made + base(part, cols)

            over(rows, tile, body)
            yield
        move.arrived()

        def body(part, _):
            target[part, :] = target[part, :] + got[part, :].astype(F32)

        over(rows, tile, body)

    def compute():
        need(0)
        own_inputs.wait()
        mate_inputs.arrived()
        loads[0].wait()
        tail = w_in[..., columns : w_in.shape[-1]].reshape(width, w_in.shape[-1] - columns)
        vectors[...] = jnp.transpose(tail.astype(F32))
        saves[10].start()
        saves[14].start()
        crest[...] = jnp.full(crest.shape, NEGATIVE, F32)
        for side in range(2):

            def body(part, i):
                made = normalise(x_all[side, part, :].astype(F32), vec(0), vec(1))
                at = pl.multiple_of(side * rows + i * tile, tile)
                normed_self[pl.ds(at, tile), :] = made.astype(BF)

            over(rows, tile, body)
        saves[0].start()
        yield
        for start in range(0, columns, block):

            def body(part, _):
                weight = w_in[..., start : start + block].reshape(width, block)
                made = nn(normed_self[part, :], weight)
                for at in range(0, block, wide):
                    piece = made[:, at : at + wide]
                    if start + at < 2 * inner:
                        piece = turn(piece, cos_ref[part, :], sa_ref[part, :], sb_ref[part, :], 1.0)
                    taken[part, start + at : start + at + wide] = piece.astype(BF)

            over(total, step, body)
            yield
        saves[1].start()
        yield from attend_all(taken, inner, 2 * inner, taken, self_bias, mixed_self)
        saves[2].start()
        need(1)
        loads[1].wait()
        saves[11].start()
        saves[12].start()
        yield from out_project(
            mixed_self, lambda zz: w_a[zz, :, :, :, 0:inner].reshape(-1, inner), mate_self, part_send, part_got,
            lambda part, cols: x_all[0, part, cols].astype(F32), stream_cross,
        )
        saves[3].start()

        def second_norm(part, _):
            made = normalise(stream_cross[part, :], vec(2), vec(3))
            normed_cross[0, part, :] = made.astype(BF)

        over(rows, tile, second_norm)
        mate_normed.start()
        yield
        need(2)
        loads[2].wait()
        saves[13].start()
        depth = memory.shape[1]
        for side in range(2):
            for start in range(0, inner, block):
                part = slice(side * rows_kv, (side + 1) * rows_kv)
                weight = w_b[:, :, :, part, start : start + block].reshape(depth, block)
                at = side * inner + start
                taken_cross[:, at : at + block] = nn(memory[...], weight).astype(BF)
        saves[6].start()
        yield
        yield
        for side in range(2):
            if side == 1:
                mate_normed.arrived()
                saves[4].start()
            for start in range(0, inner, block):

                def body(part, i):
                    weight = w_a[..., inner + start : inner + start + block].reshape(width, block)
                    made = nn(normed_cross[side, part, :], weight).astype(BF)
                    at = pl.multiple_of(side * rows + i * tile, tile)
                    query_cross[pl.ds(at, tile), start : start + block] = made

                over(rows, tile, body)
                yield
        saves[5].start()
        yield from attend_all(query_cross, 0, inner, taken_cross, cross_bias, mixed_cross)
        saves[7].start()
        mate_self.sent()
        yield from out_project(
            mixed_cross, lambda zz: w_b[zz, :, :, :, inner : 2 * inner].reshape(-1, inner), mate_cross, part_send, part_got,
            lambda part, cols: stream_cross[part, cols], stream_feed,
        )
        saves[8].start()

        def third_norm(part, _):
            made = normalise(stream_feed[part, :], vec(4), vec(5))
            normed_feed[0, part, :] = made.astype(BF)

        over(rows, tile, third_norm)
        feed_moves[0].start()

    items = gathers + quarters
    names = ("begin", "far_first", "step", "far_step", "landed", "own_y_arrived")
    work = compute()
    for entry in PLAN:
        if entry < 0:
            next(work, None)
            continue
        kind, which, k, side = entry // 1000, entry // 100 % 10, entry // 10 % 10, entry % 10
        if kind == 6:
            cot_moves[1].start()
            continue
        if kind == 7:
            cot_moves[1].arrived()
            cot_moves[2].start()
            continue
        item = items[which]
        getattr(item, names[kind])(*((k, side) if kind in (2, 3) else ()))
        if kind == 4:
            ready.add(which)
            if which < 3:
                loads[which].start()
    for _ in work:
        pass
    peak_out[...] = crest[...]
    for i, item in enumerate(items):
        if i not in ready:
            item.landed()
    feed_moves[0].arrived()
    saves[9].start()
    cot_moves[0].arrived()
    cot_moves[2].arrived()
    own_cot.wait()
    for item in gathers + quarters:
        item.sent()
    for move in [mate_inputs, mate_normed, mate_cross] + cot_moves + feed_moves:
        move.sent()
    for save in saves:
        save.wait()


def forward(shards, quarters, inputs, cotangent, turns, self_bias, cross_bias, memory, zs):
    rows, width = inputs.shape
    seq_len, inner = 2 * rows, shards[1].shape[1]
    tokens = memory.shape[0]
    spread = []
    count = shards[1].shape[0]
    for columns in (3 * inner + shards[0].shape[1], 2 * inner, 2 * inner):
        spread.append(jax.ShapeDtypeStruct((zs, 2, 2, count, columns), BF))
    for shard in quarters:
        spread.append(
            jax.ShapeDtypeStruct((zs, 2, 2, shard.shape[0], shard.shape[1] // 2), shard.dtype)
        )
    results = [
        jax.ShapeDtypeStruct((seq_len, width), BF),
        jax.ShapeDtypeStruct((seq_len, 3 * inner), BF),
        jax.ShapeDtypeStruct((seq_len, inner), BF),
        jax.ShapeDtypeStruct((rows, width), F32),
        jax.ShapeDtypeStruct((2, rows, width), BF),
        jax.ShapeDtypeStruct((seq_len, inner), BF),
        jax.ShapeDtypeStruct((tokens, 2 * inner), BF),
        jax.ShapeDtypeStruct((seq_len, inner), BF),
        jax.ShapeDtypeStruct((rows, width), F32),
        jax.ShapeDtypeStruct((2, rows, width), BF),
    ]
    saved = [
        jax.ShapeDtypeStruct((zs, 2, 2, count, columns), BF)
        for columns in (3 * inner, inner, inner, inner)
    ]
    saved.append(jax.ShapeDtypeStruct((shards[0].shape[1], width), F32))
    cot_out = jax.ShapeDtypeStruct((4, rows, width), BF)
    peak = jax.ShapeDtypeStruct((8, 2 * HEAD_DIM), F32)
    moves = 3 * (3 + 8 * (zs - 1)) + 3 * (2 + 4 * (zs - 1)) + 8
    hbm = pl.BlockSpec(memory_space=pltpu.HBM)
    vmem = pl.BlockSpec(memory_space=pltpu.VMEM)
    held = [pltpu.VMEM(shape.shape, shape.dtype) for shape in spread[:3]]
    held += [pltpu.VMEM((2, rows, width), BF)]
    held += [pltpu.VMEM(shape.shape, shape.dtype) for shape in results]
    held += [pltpu.VMEM((rows, width), BF)] * 2
    held += [pltpu.VMEM((shards[0].shape[1], width), F32), pltpu.VMEM(peak.shape, F32)]
    flops = 2 * seq_len * inner * (7 * width + 4 * seq_len) // 1
    made = pl.pallas_call(
        functools.partial(forward_kernel, zs),
        out_shape=spread + results + saved + [cot_out, peak],
        in_specs=[hbm] * 14 + [vmem] * 6,
        out_specs=[hbm] * 22 + [vmem],
        scratch_shapes=[
            pltpu.SemaphoreType.DMA((moves,)),
            pltpu.SemaphoreType.DMA((moves,)),
            pltpu.SemaphoreType.DMA((9 + 2 + 3 + 3 + 15,)),
        ]
        + held,
        compiler_params=pltpu.CompilerParams(
            collective_id=1, has_side_effects=True, vmem_limit_bytes=62 * 2**20
        ),
        cost_estimate=pl.CostEstimate(flops=flops, bytes_accessed=10**8, transcendentals=10**7),
    )(*shards, *quarters, inputs, cotangent, *turns, self_bias, cross_bias, memory)
    return made[3:6], made[6:16], made[16:21], made[21], made[22]


def pair_rows(own):
    return jnp.concatenate([own, swap(own, "tensor")], axis=0)


def group_rows(own):
    both = jnp.stack([own, swap(own, "x")])
    other = swap(both, "tensor")
    return jnp.concatenate([both[0], other[0], both[1], other[1]], axis=0)


def spread_pair(left, right_t):
    rows = left.shape[0] // 2
    got = swap(nt(left[rows:], right_t), "tensor")
    return nt(left[:rows], right_t) + got


def spread_group(product):
    quarter = product.rows // 4
    far_send = product(3 * quarter, quarter)
    far = product(2 * quarter, quarter) + swap(far_send, "tensor")
    got_far = swap(far.astype(BF), "x")
    near = product(0, quarter) + swap(product(quarter, quarter), "tensor")
    return near + got_far.astype(F32)


class Product:
    def __init__(self, terms, transposed):
        self.terms = terms
        self.transposed = transposed
        self.rows = terms[0][0].shape[0]

    def __call__(self, first, count):
        total = None
        for left, right in self.terms:
            part = (nt if self.transposed else nn)(left[first : first + count], right)
            total = part if total is None else total + part
        return total


def per_device(
    inputs,
    cotangent,
    context,
    context_live,
    lengths,
    threshold,
    self_gain,
    self_bias,
    self_query,
    self_key,
    self_value,
    self_output,
    cross_gain,
    cross_bias,
    cross_query,
    cross_key,
    cross_value,
    cross_output,
    feed_gain,
    feed_bias,
    gate_weight,
    up_weight,
    down_weight,
):
    zs = lax.axis_size("z")
    x_at = lax.axis_index("x")
    t_at = lax.axis_index("tensor")
    width = inputs.shape[1]
    rows = inputs.shape[0]
    seq_len = 2 * rows
    inner = self_query.shape[1]
    heads_here = inner // HEAD_DIM
    ff = gate_weight.shape[1] // 2
    shard_rows = self_query.shape[0]

    quarters = [gate_weight, up_weight, down_weight.T]
    vector_list = [self_gain, self_bias, cross_gain, cross_bias, feed_gain, feed_bias]
    stream = inputs.astype(F32)
    local = jnp.arange(rows)
    places = jnp.concatenate([t_at * rows + local, (1 - t_at) * rows + local])
    turns = turn_tables(places.astype(F32))
    self_bias_row = jnp.where(places < lengths[0], 0.0, NEGATIVE).astype(F32)
    tokens = context.shape[1]
    token_rows = -(-tokens // 128) * 128
    cross_bias_row = jnp.pad(
        jnp.where(context_live[0] > 0, 0.0, NEGATIVE).astype(F32),
        (0, token_rows - tokens),
        constant_values=NEGATIVE,
    )
    memory = jnp.pad(context[0], ((0, token_rows - tokens), (0, 0)))
    pairs = inner // (2 * HEAD_DIM)

    if shard_rows % 32 == 0:
        vectors = jnp.pad(jnp.stack(vector_list, axis=1), ((0, 0), (0, 122)))
        spread, made, saved, cot_group, crest = forward(
            [
                vectors,
                self_query,
                self_key,
                self_value,
                self_output.T,
                cross_query,
                cross_key,
                cross_value,
                cross_output.T,
            ],
            quarters,
            inputs,
            cotangent,
            turns,
            self_bias_row[None],
            cross_bias_row[None],
            memory,
            zs,
        )
        in_weight, self_out_t, cross_in, cross_out_t, norms = saved
        (
            normed_self,
            taken,
            mixed_self,
            stream_cross,
            normed_cross,
            query_cross,
            taken_cross,
            mixed_cross,
            stream_feed,
            normed_feed,
        ) = made
        gate_full, up_full, down_t = spread
        normed_cross = normed_cross.reshape(seq_len, width)
        near_feed, cot_group = (v.reshape(-1, width) for v in (normed_feed, cot_group))
    else:
        vectors = jnp.stack(vector_list).astype(F32)
        vectors = jnp.pad(vectors, ((0, 2), (0, 128 - shard_rows)))
        (norms, in_weight, self_out_t, cross_in, memory_weight, cross_out_t, gate_full, up_full, down_t) = (
            gather_all(
                [
                    [vectors],
                    [self_query, self_key, self_value],
                    [self_output.T],
                    [cross_query],
                    [cross_key, cross_value],
                    [cross_output.T],
                ],
                quarters,
                zs,
            )
        )
        norms = norms.reshape(-1, 8, 128)[:, :6, :shard_rows].transpose(1, 0, 2).reshape(6, width)
        in_weight, memory_weight = in_weight.reshape(width, -1), memory_weight.reshape(-1, 2 * inner)
        self_out_t, cross_in, cross_out_t, gate_full, up_full, down_t = (
            w.reshape(width, -1)
            for w in (self_out_t, cross_in, cross_out_t, gate_full, up_full, down_t)
        )
        cot_group = group_rows(cotangent)
        all_inputs = pair_rows(inputs)
        normed, _, _ = norm_forward(all_inputs.astype(F32), norms[0], norms[1])
        normed_self = normed.astype(BF)
        taken = project(normed_self, in_weight, turns, 2 * inner)
        self_bias_rows = jnp.broadcast_to(self_bias_row, (pairs, seq_len))
        mixed_self, peak_self = attend(taken, taken, taken, self_bias_rows, (0, pairs, 2 * pairs))
        stream_cross = stream + spread_pair(mixed_self, self_out_t)
        normed, _, _ = norm_forward(stream_cross, norms[2], norms[3])
        normed_cross = pair_rows(normed.astype(BF))
        query_cross = nn(normed_cross, cross_in).astype(BF)
        taken_cross = nn(memory, memory_weight).astype(BF)
        cross_bias_rows = jnp.broadcast_to(cross_bias_row, (pairs, token_rows))
        mixed_cross, peak_cross = attend(
            query_cross, taken_cross, taken_cross, cross_bias_rows, (0, 0, pairs)
        )
        stream_feed = stream_cross + spread_pair(mixed_cross, cross_out_t)
        normed, _, _ = norm_forward(stream_feed, norms[4], norms[5])
        near_feed = pair_rows(normed.astype(BF))
        crest = jnp.pad(
            jnp.maximum(peak_self, peak_cross)[None], ((0, 7), (0, 128 - heads_here))
        )
    in_weight, self_out_t, cross_in, cross_out_t, gate_full, up_full, down_t = (
        w.reshape(width, -1)
        for w in (in_weight, self_out_t, cross_in, cross_out_t, gate_full, up_full, down_t)
    )
    unit_cross, inverse_cross = unit_rows_of(stream_cross)
    unit_feed, inverse_feed = unit_rows_of(stream_feed)
    far_own = swap(near_feed[:rows], "x")

    def feed_half(normed, cot_rows):
        gate_pre = nn(normed, gate_full)
        upward = nn(normed, up_full)
        sigmoid_gate = jax.nn.sigmoid(gate_pre)
        hidden = (gate_pre * sigmoid_gate * upward).astype(BF)
        grad_hidden = nn(cot_rows, down_t)
        grad_gate = grad_hidden * upward * sigmoid_gate * (1.0 + gate_pre * (1.0 - sigmoid_gate))
        grad_upward = grad_hidden * gate_pre * sigmoid_gate
        return hidden, grad_gate.astype(BF), grad_upward.astype(BF)

    def feed_back(grad_gate, grad_upward):
        return nt(grad_gate, gate_full) + nt(grad_upward, up_full)

    hidden_near, gate_near, up_near = feed_half(near_feed, cot_group[:seq_len])
    far_own, hidden_near, gate_near, up_near = lax.optimization_barrier(
        (far_own, hidden_near, gate_near, up_near)
    )
    far_feed = pair_rows(far_own)
    hidden_far, gate_far, up_far = feed_half(far_feed, cot_group[seq_len:])
    far_sum = feed_back(gate_far[:rows], up_far[:rows]) + swap(
        feed_back(gate_far[rows:], up_far[rows:]), "tensor"
    )
    far_sum = far_sum.astype(BF)
    got_far = swap(far_sum, "x")
    normed_feed = jnp.concatenate([near_feed, far_feed], axis=0)
    hidden = jnp.concatenate([hidden_near, hidden_far], axis=0)
    grad_gate = jnp.concatenate([gate_near, gate_far], axis=0)
    grad_upward = jnp.concatenate([up_near, up_far], axis=0)
    down_pair = PairSum(after(cot_group, far_sum), hidden, zs)
    gate_pair = PairSum(after(normed_feed, far_sum), grad_gate, zs)
    grad_normed = feed_back(gate_near[:rows], up_near[:rows]) + swap(
        feed_back(gate_near[rows:], up_near[rows:]), "tensor"
    )
    got_far = after(got_far, grad_normed, gate_pair.sent, down_pair.sent)
    grad_normed = grad_normed + got_far.astype(F32)
    stream_part, grad_feed_gain, grad_feed_bias = norm_backward(
        grad_normed, unit_feed, inverse_feed, norms[4]
    )
    grad_stream = cotangent.astype(F32) + stream_part
    grad_full = pair_rows(grad_stream.astype(BF))
    up_pair = PairSum(after(normed_feed, grad_full), grad_upward, zs)
    cross_output_sum = FullSum(grad_full, mixed_cross, zs)
    grad_mixed = nn(grad_full, cross_out_t).astype(BF)
    grad_query, grad_keys, grad_values = attend_back(
        query_cross, taken_cross, taken_cross, grad_mixed, cross_bias_row[:, None], (0, 0, pairs), None
    )
    down_pair.second(grad_query)
    grad_normed = spread_pair(grad_query, cross_in)
    cross_query_sum = FullSum(normed_cross, grad_query, zs)
    part_memory = tn(memory, jnp.concatenate([grad_keys, grad_values], axis=1))
    stream_part, grad_cross_gain, grad_cross_bias = norm_backward(
        grad_normed, unit_cross, inverse_cross, norms[2]
    )
    grad_stream = grad_stream + stream_part
    grad_full = pair_rows(grad_stream.astype(BF))
    gate_pair.second(grad_full)
    part_self_output = tn(grad_full, mixed_self)
    grad_mixed = nn(grad_full, self_out_t).astype(BF)
    grad_parts = attend_back(
        taken, taken, taken, grad_mixed, self_bias_row[:, None], (0, pairs, 2 * pairs), turns
    )
    grad_in = jnp.concatenate(grad_parts, axis=1)
    up_pair.second(grad_in)
    cross_output_sum.second(grad_in)
    cross_query_sum.second(grad_in)
    part_in = tn(normed_self, grad_in[:, : 2 * inner]).astype(BF)
    part_value = tn(normed_self, grad_parts[2]).astype(BF)
    grad_normed = spread_pair(grad_in, in_weight)
    sum_cross_output = cross_output_sum.third(grad_normed).astype(F32)
    sum_cross_query = cross_query_sum.third(grad_normed).astype(F32)
    unit_self, inverse_self = unit_rows_of(stream)
    stream_part, grad_self_gain, grad_self_bias = norm_backward(
        grad_normed, unit_self, inverse_self, norms[0]
    )
    grad_stream = grad_stream + stream_part

    vector_sums = jnp.stack(
        [
            grad_self_gain,
            grad_self_bias,
            grad_cross_gain,
            grad_cross_bias,
            grad_feed_gain,
            grad_feed_bias,
        ]
    ).reshape(6, -1, shard_rows)
    vector_sums = vector_sums + swap(vector_sums, "tensor")
    vector_sums = jnp.pad(
        vector_sums.transpose(1, 0, 2), ((0, 0), (0, 2), (0, 128 - shard_rows))
    ).reshape(zs, 2, 2, 8, 128)

    def blocks(part):
        return part.astype(BF).reshape(zs, 2, 2, -1, part.shape[1])

    vector_sums, sum_in, sum_value, sum_self_output, sum_memory, crest = scatter_all(
        [
            vector_sums,
            blocks(part_in),
            blocks(part_value),
            blocks(part_self_output),
            blocks(part_memory),
        ],
        ["z", "x", "y", "y", "z"],
        crest,
        zs,
    )
    vector_sums = vector_sums[:, :shard_rows]
    peaks = crest[0, :heads_here]
    factor = jnp.sqrt(threshold[0] / jnp.maximum(peaks, threshold[0]))
    columns = jnp.repeat(factor, HEAD_DIM)[None, :]
    result = stream_feed + spread_group(Product([(hidden, down_t)], True))
    result = result.astype(BF)
    down_keep, down_got = down_pair.third()
    gate_keep, gate_got = gate_pair.third()
    up_keep, up_got = up_pair.third()

    def side_by_side(kept, got):
        low = jnp.where(x_at == 0, kept, got).astype(F32)
        high = jnp.where(x_at == 0, got, kept).astype(F32)
        return jnp.concatenate([low, high], axis=1)

    down_sum = side_by_side(down_keep, down_got).T
    gate_sum = side_by_side(gate_keep, gate_got)
    up_sum = side_by_side(up_keep, up_got)
    return (
        result,
        grad_stream,
        vector_sums[0],
        vector_sums[1],
        sum_in[:, :inner],
        sum_in[:, inner:],
        sum_value,
        sum_self_output.T,
        vector_sums[2],
        vector_sums[3],
        sum_cross_query,
        sum_memory[:, :inner],
        sum_memory[:, inner:],
        sum_cross_output.T,
        vector_sums[4],
        vector_sums[5],
        gate_sum,
        up_sum,
        down_sum,
        peaks,
        self_query.astype(F32) * columns,
        self_key.astype(F32) * columns,
        cross_query.astype(F32) * columns,
        cross_key.astype(F32) * columns,
    )


def solution(mesh):
    count = mesh.shape["dp"]
    mesh = Mesh(
        mesh.devices.reshape(count // 4, 2, 2, mesh.shape["tensor"]), ("z", "y", "x", "tensor")
    )
    dp = ("z", "y", "x")
    both = P(dp + ("tensor",), None)
    split = P(dp)
    row_major = P(dp, "tensor")
    column_major = P("tensor", dp)
    in_specs = (
        both,
        both,
        P(dp, None, None),
        P(dp, None),
        split,
        P(),
        split,
        split,
        row_major,
        row_major,
        row_major,
        column_major,
        split,
        split,
        row_major,
        row_major,
        row_major,
        column_major,
        split,
        split,
        row_major,
        row_major,
        column_major,
    )
    out_specs = (
        both,
        both,
        split,
        split,
        row_major,
        row_major,
        row_major,
        column_major,
        split,
        split,
        row_major,
        row_major,
        row_major,
        column_major,
        split,
        split,
        row_major,
        row_major,
        column_major,
        P("tensor"),
        row_major,
        row_major,
        row_major,
        row_major,
    )
    return jax.shard_map(
        per_device, mesh=mesh, in_specs=in_specs, out_specs=out_specs, check_vma=False
    )
```

```python
import functools

import jax
import jax.numpy as jnp
from jax import lax
from jax.experimental import pallas as pl
from jax.experimental.pallas import tpu as pltpu
from jax.sharding import Mesh
from jax.sharding import PartitionSpec as P

HEAD_DIM = 64
ROT_DIM = 32
EPSILON = 1e-05
NEGATIVE = -1e30
BF = jnp.bfloat16
F32 = jnp.float32


def swap(value, axis):
    return lax.ppermute(value, axis, [(0, 1), (1, 0)])


def pick(value, index, dim):
    return lax.dynamic_index_in_dim(value, index, dim, keepdims=False)


class Lanes:
    def __init__(self, send_sems, recv_sems, local_sems, zs):
        self.send_sems, self.recv_sems, self.local_sems = send_sems, recv_sems, local_sems
        self.used = self.used_local = 0
        self.z = lax.axis_index("z")
        self.y = lax.axis_index("y")
        self.x = lax.axis_index("x")
        self.zs = zs

    def local(self):
        self.used_local += 1
        return self.local_sems.at[self.used_local - 1]

    def copy(self, source, target, device):
        return self.copies([source], target, device)[0]

    def copies(self, sources, target, device):
        slot = self.used
        self.used += 1
        return [
            pltpu.make_async_remote_copy(
                src_ref=source,
                dst_ref=target,
                send_sem=self.send_sems.at[slot],
                recv_sem=self.recv_sems.at[slot],
                device_id=device,
                device_id_type=pl.DeviceIdType.MESH,
            )
            for source in sources
        ]


def guarded(condition, action):
    if condition is None:
        action()
    else:
        pl.when(condition)(action)


class Move:
    def __init__(self, copy, sends, receives):
        self.copy_, self.sends, self.receives = copy, sends, receives

    def start(self):
        guarded(self.sends, self.copy_.start)

    def arrived(self):
        guarded(self.receives, self.copy_.wait_recv)

    def sent(self):
        guarded(self.sends, self.copy_.wait_send)


class Gather:
    def __init__(self, lanes, whole):
        zs, z, y, x = lanes.zs, lanes.z, lanes.y, lanes.x
        own = whole.at[z, y, x]

        def block(zz, yy):
            return whole.at[zz, yy, x]

        def along(source, target, axis, to, sends=None, receives=None):
            return Move(lanes.copy(source, target, {axis: to}), sends, receives)

        self.first = [
            along(own, block(z, y), "y", 1 - y),
            along(own, block(z, y), "x", 1 - x),
        ]
        self.far = [[along(block(z, 1 - y), block(z, 1 - y), "x", 1 - x)]]
        self.steps = []
        for k in range(zs - 1):
            right, left = jnp.maximum(z - k, 0), jnp.minimum(z + k, zs - 1)
            step = []
            for zz, to, sends, receives, got in (
                (right, z + 1, (z >= k) & (z < zs - 1), z >= k + 1, jnp.maximum(z - 1 - k, 0)),
                (left, z - 1, (z + k < zs) & (z > 0), z + k + 1 < zs, jnp.minimum(z + 1 + k, zs - 1)),
            ):
                source = own if k == 0 else block(zz, y)
                move = along(source, block(zz, y), "z", to, sends, receives)
                follow = [
                    along(block(got, y), block(got, y), "y", 1 - y, receives, receives),
                    along(block(got, y), block(got, y), "x", 1 - x, receives, receives),
                    along(block(got, 1 - y), block(got, 1 - y), "x", 1 - x, receives, receives),
                ]
                step.append((move, follow))
            self.steps.append(step)

    def begin(self):
        for move, _ in self.steps[0]:
            move.start()
        for move in self.first:
            move.start()

    def step(self, k, side):
        move, follow = self.steps[k][side]
        move.arrived()
        if k + 1 < len(self.steps):
            self.steps[k + 1][side][0].start()
        follow[0].start()
        follow[1].start()

    def far_first(self):
        self.first[0].arrived()
        self.far[0][0].start()

    def far_step(self, k, side):
        _, follow = self.steps[k][side]
        follow[0].arrived()
        follow[2].start()

    def landed(self):
        self.first[1].arrived()
        self.far[0][0].arrived()
        for step in self.steps:
            for _, follow in step:
                follow[1].arrived()
                follow[2].arrived()

    def sent(self):
        for move in self.first + self.far[0]:
            move.sent()
        for step in self.steps:
            for move, follow in step:
                move.sent()
                for other in follow:
                    other.sent()


class PairGather:
    def __init__(self, lanes, shard, whole, y_first):
        zs, z, y, x = lanes.zs, lanes.z, lanes.y, lanes.x
        ff = whole.shape[-1]
        kept = shard.at[:, pl.ds(pl.multiple_of(x * ff, ff), ff)]
        sent = shard.at[:, pl.ds(pl.multiple_of((1 - x) * ff, ff), ff)]
        self.y_first = y_first

        def along(piece, axis, to, sends=None, receives=None):
            return Move(lanes.copy(piece, piece, {axis: to}), sends, receives)

        self.swap = Move(lanes.copy(sent, whole.at[z, y, x], {"x": 1 - x}), None, None)
        self.local = pltpu.make_async_copy(kept, whole.at[z, y, x], lanes.local())
        self.own_y = along(whole.at[z, y], "y", 1 - y)
        self.steps = []
        for k in range(zs - 1):
            step = []
            for zz, to, sends, receives, got in (
                (jnp.maximum(z - k, 0), z + 1, (z >= k) & (z < zs - 1), z >= k + 1, jnp.maximum(z - 1 - k, 0)),
                (jnp.minimum(z + k, zs - 1), z - 1, (z + k < zs) & (z > 0), z + k + 1 < zs, jnp.minimum(z + 1 + k, zs - 1)),
            ):
                piece = whole.at[zz] if y_first else whole.at[zz, y]
                move = along(piece, "z", to, sends, receives)
                follow = [] if y_first else [along(whole.at[got, y], "y", 1 - y, receives, receives)]
                step.append((move, follow))
            self.steps.append(step)

    def begin(self):
        self.swap.start()
        self.local.start()

    def far_first(self):
        self.swap.arrived()
        self.local.wait()
        self.own_y.start()
        if not self.y_first:
            for move, _ in self.steps[0]:
                move.start()

    def own_y_arrived(self):
        self.own_y.arrived()
        if self.y_first:
            for move, _ in self.steps[0]:
                move.start()

    def step(self, k, side):
        move, follow = self.steps[k][side]
        move.arrived()
        if k + 1 < len(self.steps):
            self.steps[k + 1][side][0].start()
        for other in follow:
            other.start()

    def landed(self):
        if not self.y_first:
            self.own_y.arrived()
        for step in self.steps:
            for move, follow in step:
                for other in follow:
                    other.arrived()

    def sent(self):
        self.swap.sent()
        self.own_y.sent()
        for step in self.steps:
            for move, follow in step:
                move.sent()
                for other in follow:
                    other.sent()


def greet(zs, mates=False):
    z, y, x = lax.axis_index("z"), lax.axis_index("y"), lax.axis_index("x")
    barrier = pltpu.get_barrier_semaphore()

    def signal(device):
        pl.semaphore_signal(barrier, inc=1, device_id=device, device_id_type=pl.DeviceIdType.MESH)

    signal({"x": 1 - x})
    signal({"y": 1 - y})
    pl.when(z > 0)(lambda: signal({"z": z - 1}))
    pl.when(z < zs - 1)(lambda: signal({"z": z + 1}))
    if mates:
        signal({"tensor": 1 - lax.axis_index("tensor")})
    peers = (3 if mates else 2) + (z > 0).astype(jnp.int32) + (z < zs - 1).astype(jnp.int32)
    pl.semaphore_wait(barrier, peers)


def gather_kernel(zs, groups, pairs, *refs):
    shards = sum(groups)
    owns, pair_in = refs[:shards], refs[shards : shards + pairs]
    refs = refs[shards + pairs :]
    outs = refs[: len(groups) + pairs]
    lanes = Lanes(*refs[len(groups) + pairs :], zs)
    z, y, x = lanes.z, lanes.y, lanes.x
    pieces, at = [], 0
    for count, whole in zip(groups, outs):
        width = whole.shape[-1] // count
        for i in range(count):
            target = whole.at[z, y, x, :, pl.ds(i * width, width)]
            pieces.append(pltpu.make_async_copy(owns[at], target, lanes.local()))
            at += 1
    for piece in pieces:
        piece.start()
    greet(zs)
    gathers = [Gather(lanes, whole) for whole in outs[: len(groups)]]
    quarters = [
        PairGather(lanes, pair_in[i], outs[len(groups) + i], i == 0) for i in range(pairs)
    ]
    for quarter in quarters:
        quarter.begin()
    for piece in pieces:
        piece.wait()
    for gather in gathers:
        gather.begin()
    for quarter in quarters:
        quarter.far_first()
    for gather in gathers:
        gather.far_first()
    for k, side in [(k, side) for k in range(zs - 1) for side in range(2)]:
        for gather in gathers:
            gather.step(k, side)
        for quarter in quarters:
            if quarter.y_first:
                if k == 0 and side == 0:
                    quarter.own_y_arrived()
            else:
                quarter.step(k, side)
        for gather in gathers:
            gather.far_step(k, side)
        for quarter in quarters:
            if quarter.y_first:
                quarter.step(k, side)
    for item in gathers + quarters:
        item.landed()
        item.sent()


def gather_all(groups, quarters, zs):
    flat = [shard for group in groups for shard in group] + list(quarters)
    outs = []
    for group in groups:
        columns = sum(shard.shape[1] for shard in group)
        outs.append(
            jax.ShapeDtypeStruct((zs, 2, 2, group[0].shape[0], columns), group[0].dtype)
        )
    for shard in quarters:
        outs.append(
            jax.ShapeDtypeStruct((zs, 2, 2, shard.shape[0], shard.shape[1] // 2), shard.dtype)
        )
    count, pairs = len(groups), len(quarters)
    moves = count * (3 + 8 * (zs - 1)) + pairs * (2 + 4 * (zs - 1))
    hbm = pl.BlockSpec(memory_space=pltpu.HBM)
    return pl.pallas_call(
        functools.partial(gather_kernel, zs, tuple(len(group) for group in groups), pairs),
        out_shape=outs,
        in_specs=[hbm] * len(flat),
        out_specs=[hbm] * len(outs),
        scratch_shapes=[
            pltpu.SemaphoreType.DMA((moves,)),
            pltpu.SemaphoreType.DMA((moves,)),
            pltpu.SemaphoreType.DMA((len(flat),)),
        ],
        compiler_params=pltpu.CompilerParams(collective_id=1, has_side_effects=True),
    )(*flat)


def plus(*terms):
    total = terms[0].astype(F32)
    for term in terms[1:]:
        total = total + term.astype(F32)
    return total


def ends_first(zs):
    order = []
    for i in range(zs // 2):
        order += [zs - 1 - i, i]
    return order


class Line:
    def __init__(self, lanes, part, from_left, from_right):
        zs, z = lanes.zs, lanes.z
        self.zs, self.z, self.part = zs, z, part
        self.from_left, self.from_right = from_left, from_right
        self.right, self.left = {}, {}
        for d in ends_first(zs):
            after, before = jnp.minimum(z + 1, zs - 1), jnp.maximum(z - 1, 0)
            self.right[d] = lanes.copies(
                (part.at[d], from_left.at[d]), from_left.at[d], {"z": after}
            )
            self.left[d] = lanes.copies(
                (part.at[d], from_right.at[d]), from_right.at[d], {"z": before}
            )

    def pass_on(self, d):
        for moves, inbox, sends, edge in (
            (self.right[d], self.from_left, self.z < d, self.z == 0),
            (self.left[d], self.from_right, self.z > d, self.z == self.zs - 1),
        ):

            @pl.when(sends & edge)
            def _():
                moves[0].start()

            @pl.when(sends & jnp.logical_not(edge))
            def _():
                moves[1].wait_recv()
                inbox[d] = plus(self.part[d], inbox[d]).astype(inbox.dtype)
                moves[1].start()

    def total(self, sink):
        for d in range(self.zs):

            @pl.when(self.z == d)
            def _():
                terms = [self.part[d]]
                if d > 0:
                    self.right[d][0].wait_recv()
                    terms.append(self.from_left[d])
                if d < self.zs - 1:
                    self.left[d][0].wait_recv()
                    terms.append(self.from_right[d])
                sink[...] = plus(*terms).astype(sink.dtype)

    def finish(self):
        for d in ends_first(self.zs):
            pl.when(self.z < d)(self.right[d][0].wait_send)
            pl.when(self.z > d)(self.left[d][0].wait_send)


class Scatter:
    def __init__(self, lanes, part, held, out, first):
        zs, z, y, x = lanes.zs, lanes.z, lanes.y, lanes.x
        got, near, from_left, from_right, ready = held
        second = "y" if first == "x" else "x"
        self.lanes, self.part, self.got, self.near, self.ready, self.out = (
            lanes, part, got, near, ready, out,
        )
        f, s = (x, y) if first == "x" else (y, x)
        self.f, self.s = f, s

        def block(zz, a, b):
            return part.at[zz, b, a] if first == "x" else part.at[zz, a, b]

        self.block = block
        self.one, self.two = {}, {}
        for zz in ends_first(zs):
            for j, b in enumerate((1 - s, s)):
                self.one[zz, j] = Move(
                    lanes.copy(block(zz, 1 - f, b), got.at[zz, j], {first: 1 - f}), None, None
                )
        for zz in ends_first(zs):
            self.two[zz] = Move(
                lanes.copy(got.at[zz, 0], near.at[zz], {second: 1 - s}), None, None
            )
        self.line = Line(lanes, ready, from_left, from_right)

    def begin(self, zz):
        for j in range(2):
            self.one[zz, j].start()

    def second(self, zz):
        self.one[zz, 0].arrived()
        mine, got = self.block(zz, self.f, 1 - self.s), self.got
        got[zz, 0] = plus(mine[...], got[zz, 0]).astype(got.dtype)
        self.two[zz].start()

    def third(self, zz):
        self.one[zz, 1].arrived()
        self.two[zz].arrived()
        mine = self.block(zz, self.f, self.s)
        self.ready[zz] = plus(mine[...], self.got[zz, 1], self.near[zz]).astype(self.ready.dtype)
        self.line.pass_on(zz)

    def finish(self):
        self.line.total(self.out)
        self.line.finish()
        for move in list(self.one.values()) + list(self.two.values()):
            move.sent()


class ScatterZ:
    def __init__(self, lanes, part, held, out):
        y, x = lanes.y, lanes.x
        from_left, from_right, held_z, near, last = held
        self.lanes, self.sum_z, self.near, self.last, self.out = lanes, held_z, near, last, out
        self.line = Line(lanes, part, from_left, from_right)
        self.two = Move(lanes.copy(held_z.at[1 - y], near, {"y": 1 - y}), None, None)
        self.three = Move(lanes.copy(near.at[1 - x], last, {"x": 1 - x}), None, None)

    def pass_on(self, d):
        self.line.pass_on(d)

    def total(self):
        self.line.total(self.sum_z)
        self.two.start()

    def after(self):
        self.two.arrived()
        self.near[...] = plus(self.sum_z[self.lanes.y], self.near[...]).astype(self.near.dtype)
        self.three.start()

    def finish(self):
        self.three.arrived()
        self.out[...] = plus(self.near[self.lanes.x], self.last[...]).astype(self.out.dtype)
        self.line.finish()
        self.two.sent()
        self.three.sent()


class Crest:
    def __init__(self, lanes, own, held, out):
        zs, z, y, x = lanes.zs, lanes.z, lanes.y, lanes.x
        near_x, near_y, mine_x, mine_y, right, left, inbox_r, inbox_l = (
            held.at[i] for i in range(8)
        )
        self.zs, self.z, self.own, self.out = zs, z, own, out
        self.near_x, self.near_y, self.mine_x, self.mine_y = near_x, near_y, mine_x, mine_y
        self.ways = (
            (right, inbox_r, z > 0, z < zs - 1),
            (left, inbox_l, z < zs - 1, z > 0),
        )
        self.one = Move(lanes.copy(own, near_x, {"x": 1 - x}), None, None)
        self.two = Move(lanes.copy(mine_x, near_y, {"y": 1 - y}), None, None)
        self.moves = [
            Move(lanes.copy(right, inbox_r, {"z": jnp.minimum(z + 1, zs - 1)}), z < zs - 1, z > 0),
            Move(lanes.copy(left, inbox_l, {"z": jnp.maximum(z - 1, 0)}), z > 0, z < zs - 1),
        ]

    def second(self):
        self.one.arrived()
        self.mine_x[...] = jnp.maximum(self.own[...], self.near_x[...])
        self.two.start()

    def finish(self):
        self.two.arrived()
        self.mine_y[...] = jnp.maximum(self.mine_x[...], self.near_y[...])
        self.out[...] = self.mine_y[...]
        for move, (held, inbox, has_before, has_after) in zip(self.moves, self.ways):

            @pl.when(has_before)
            def _():
                move.copy_.wait_recv()
                self.out[...] = jnp.maximum(self.out[...], inbox[...])
                held[...] = jnp.maximum(self.mine_y[...], inbox[...])

            @pl.when(jnp.logical_not(has_before))
            def _():
                held[...] = self.mine_y[...]

            move.start()
        for move in [self.one, self.two] + self.moves:
            move.sent()


class LastNorm:
    def __init__(self, lanes, given, held, out, local_sems):
        grad_hbm, weight_hbm, self.inputs, self.stream, self.gain, self.others = given
        (
            self.grad, self.weight, self.send, self.got, self.normed,
            self.rows8, self.got8, self.tall, self.blocks,
        ) = held
        self.out, self.zs = out, lanes.zs
        mate = {"tensor": 1 - lax.axis_index("tensor")}
        self.loads = [
            pltpu.make_async_copy(grad_hbm, self.grad, local_sems.at[0]),
            pltpu.make_async_copy(weight_hbm, self.weight, local_sems.at[1]),
        ]
        self.mate_part = Move(lanes.copy(self.send, self.got, mate), None, None)
        self.mate_rows = Move(lanes.copy(self.rows8, self.got8, mate), None, None)

    def pieces(self):
        rows, width = self.out.shape
        tile = 128 if rows % 128 == 0 else rows
        chunk = width // self.zs

        def over(body):
            @pl.loop(0, rows // tile)
            def _(i):
                body(pl.multiple_of(i * tile, tile))

        def part_of(first, zz):
            weight = self.weight[zz].reshape(chunk, self.weight.shape[-1])
            return nt(self.grad[pl.ds(first, tile), :], weight)

        self.loads[0].wait()
        self.loads[1].wait()
        for zz in range(self.zs):
            cols = slice(zz * chunk, (zz + 1) * chunk)

            def body(at):
                made = part_of(pl.multiple_of(rows + at, tile), zz)
                self.send[pl.ds(at, tile), cols] = made.astype(BF)

            over(body)
            yield
        self.mate_part.start()
        for zz in range(self.zs):
            cols = slice(zz * chunk, (zz + 1) * chunk)

            def body(at):
                self.normed[pl.ds(at, tile), cols] = part_of(at, zz)

            over(body)
            yield
        self.mate_part.arrived()
        self.rows8[...] = self.others[...]

        def body(at):
            part = pl.ds(at, tile)
            incoming = self.normed[part, :] + self.got[part, :].astype(F32)
            stream = self.inputs[part, :].astype(F32)
            centred = stream - jnp.mean(stream, axis=-1, keepdims=True)
            inverse = lax.rsqrt(jnp.mean(centred * centred, axis=-1, keepdims=True) + EPSILON)
            unit = centred * inverse
            scaled = incoming * self.gain[...]
            slope = scaled - jnp.mean(scaled, axis=-1, keepdims=True)
            slope = slope - unit * jnp.mean(scaled * unit, axis=-1, keepdims=True)
            self.out[part, :] = self.stream[part, :] + inverse * slope
            self.rows8[0:1, :] += jnp.sum(incoming * unit, axis=0, keepdims=True)
            self.rows8[1:2, :] += jnp.sum(incoming, axis=0, keepdims=True)

        over(body)
        self.mate_rows.start()
        self.tall[...] = jnp.zeros_like(self.tall)
        yield
        self.mate_rows.arrived()
        self.tall[0:8, :] = self.rows8[...] + self.got8[...]
        turned = jnp.transpose(self.tall[...]).astype(BF)
        self.blocks[...] = turned.reshape(self.blocks.shape)
        yield

    def finish(self):
        self.mate_part.sent()
        self.mate_rows.sent()


def scatter_kernel(zs, orders, fused, *refs):
    refs = list(refs)

    def take(number):
        taken = refs[:number]
        del refs[:number]
        return taken

    count = len(orders)
    parts = take(count - 1 if fused else count)
    crest_in = take(1)[0]
    given = take(6) if fused else None
    outs = take(count)
    crest_out = take(1)[0]
    norm_out = take(1)[0] if fused else None
    send_sems, recv_sems, local_sems = take(3)
    lanes = Lanes(send_sems, recv_sems, None, zs)
    norm = None
    pieces = iter(())
    if fused:
        norm = LastNorm(lanes, given, take(9), norm_out, local_sems)
        for load in norm.loads:
            load.start()
        parts = [norm.blocks] + parts
        pieces = norm.pieces()
    greet(zs, fused)
    full, zfirst = [], []
    for i, order in enumerate(orders):
        held = take(5)
        if order == "z":
            zfirst.append(ScatterZ(lanes, parts[i], held, outs[i]))
        else:
            full.append(Scatter(lanes, parts[i], held, outs[i], order))
    late = [zfirst.pop(0)] if fused else []
    crest = Crest(lanes, crest_in, take(1)[0], crest_out)
    crest.one.start()
    order = ends_first(zs)
    for i in range(zs + 3):
        for item in full:
            if i < zs:
                item.begin(order[i])
        if i == 1:
            crest.second()
        if i < zs:
            for item in zfirst:
                item.pass_on(order[i])
        for _ in range((0, 4, 4, 1, 1)[i] if i < 5 else 0):
            next(pieces, None)
        for item in full:
            if 2 <= i < zs + 2:
                item.second(order[i - 2])
        if i == zs:
            for item in zfirst:
                item.total()
            for _ in pieces:
                pass
            for item in late:
                for d in order:
                    item.pass_on(d)
        for item in full:
            if 3 <= i:
                item.third(order[i - 3])
    for item in late:
        item.total()
    crest.finish()
    for item in zfirst + late:
        item.after()
    for item in full:
        item.finish()
    for item in zfirst + late:
        item.finish()
    if fused:
        norm.finish()


def scatter_all(parts, orders, crest, zs, given=None):
    scratch, moves = [], 4
    shapes_in = [(part.shape, part.dtype) for part in parts]
    extra_in, extra_out = [], []
    vmem = pl.BlockSpec(memory_space=pltpu.VMEM)
    specs = [vmem] * (len(parts) + 1)
    if given is not None:
        grad, weight, inputs = given[:3]
        rows, width = inputs.shape
        blocks = (zs, 2, 2, weight.shape[3], 128)
        shapes_in = [(blocks, BF)] + shapes_in
        extra_in = list(given)
        extra_out = [jax.ShapeDtypeStruct((rows, width), F32)]
        hbm = pl.BlockSpec(memory_space=pltpu.HBM)
        specs += [hbm, hbm] + [vmem] * 4
        moves += 2
        scratch += [
            pltpu.VMEM(grad.shape, grad.dtype),
            pltpu.VMEM(weight.shape, weight.dtype),
            pltpu.VMEM((rows, width), BF),
            pltpu.VMEM((rows, width), BF),
            pltpu.VMEM((rows, width), F32),
            pltpu.VMEM((8, width), F32),
            pltpu.VMEM((8, width), F32),
            pltpu.VMEM((128, width), F32),
            pltpu.VMEM(blocks, BF),
        ]
    for (shape, dtype), order in zip(shapes_in, orders):
        block = shape[3:]
        if order == "z":
            shapes = [(zs, 2, 2) + block] * 2 + [(2, 2) + block, (2,) + block, block]
            moves += 2 * zs + 2
        else:
            shapes = [(zs, 2) + block] + [(zs,) + block] * 4
            moves += 5 * zs
        scratch += [pltpu.VMEM(shape, dtype) for shape in shapes]
    outs = [jax.ShapeDtypeStruct(shape[3:], F32) for shape, _ in shapes_in]
    outs += [jax.ShapeDtypeStruct(crest.shape, F32)] + extra_out
    return pl.pallas_call(
        functools.partial(scatter_kernel, zs, orders, given is not None),
        out_shape=outs,
        in_specs=specs,
        out_specs=[vmem] * len(outs),
        scratch_shapes=[
            pltpu.SemaphoreType.DMA((moves,)),
            pltpu.SemaphoreType.DMA((moves,)),
            pltpu.SemaphoreType.DMA((2,)),
        ]
        + scratch
        + [pltpu.VMEM((8,) + crest.shape, F32)],
        compiler_params=pltpu.CompilerParams(
            collective_id=2, has_side_effects=True, vmem_limit_bytes=62 * 2**20
        ),
    )(*parts, crest, *extra_in)


def nn(left, right):
    return lax.dot_general(left, right, (((1,), (0,)), ((), ())), preferred_element_type=F32)


def nt(left, right):
    return lax.dot_general(left, right, (((1,), (1,)), ((), ())), preferred_element_type=F32)


def tn(left, right):
    return lax.dot_general(left, right, (((0,), (0,)), ((), ())), preferred_element_type=F32)


def after(value, *others):
    return lax.optimization_barrier((value, others))[0]


class FullSum:
    def __init__(self, left, right, zs):
        self.zs = zs
        held = tn(left, right).astype(BF)
        self.held = held.reshape(2 * zs, 2, -1, held.shape[1])
        self.x, self.y = lax.axis_index("x"), lax.axis_index("y")
        self.sent = pick(self.held, 1 - self.x, 1)
        self.got = swap(self.sent, "x")

    def second(self, *others):
        got = after(self.got, others)
        held = pick(self.held, self.x, 1).astype(F32) + got.astype(F32)
        self.held = held.astype(BF).reshape(self.zs, 2, -1, held.shape[-1])
        self.got = swap(pick(self.held, 1 - self.y, 1), "y")

    def third(self, *others):
        got = after(self.got, others)
        held = pick(self.held, self.y, 1).astype(F32) + got.astype(F32)
        return lax.psum_scatter(held.astype(BF), "z", scatter_dimension=0, tiled=False)


class PairSum:
    def __init__(self, left, right, zs):
        held = tn(left, right).astype(BF)
        self.held = held.reshape(zs, 2, -1, held.shape[1])
        self.y = lax.axis_index("y")
        self.sent = pick(self.held, 1 - self.y, 1)
        self.got = swap(self.sent, "y")

    def second(self, *others):
        got = after(self.got, others)
        held = pick(self.held, self.y, 1).astype(F32) + got.astype(F32)
        held = lax.psum_scatter(held.astype(BF), "z", scatter_dimension=0, tiled=False)
        self.held = held.reshape(2, -1, held.shape[-1])

    def third(self):
        at = lax.axis_index("x")
        return pick(self.held, at, 0), swap(pick(self.held, 1 - at, 0), "x")


def norm_forward(stream, gain_vec, bias_vec):
    average = jnp.mean(stream, axis=-1, keepdims=True)
    centred = stream - average
    inverse = lax.rsqrt(jnp.mean(centred * centred, axis=-1, keepdims=True) + EPSILON)
    unit_rows = centred * inverse
    return (unit_rows * gain_vec + bias_vec, unit_rows, inverse)


def unit_rows_of(stream):
    _, unit_rows, inverse = norm_forward(stream, 1.0, 0.0)
    return unit_rows, inverse


def norm_backward(incoming, unit_rows, inverse, gain_vec):
    gain_grad = jnp.sum(incoming * unit_rows, axis=0)
    bias_grad = jnp.sum(incoming, axis=0)
    scaled = incoming * gain_vec
    stream_grad = inverse * (
        scaled
        - jnp.mean(scaled, axis=-1, keepdims=True)
        - unit_rows * jnp.mean(scaled * unit_rows, axis=-1, keepdims=True)
    )
    return (stream_grad, gain_grad, bias_grad)


def turn_tables(positions):
    rates = 10000.0 ** (-jnp.arange(0, ROT_DIM, 2).astype(F32) / ROT_DIM)
    angles = positions[:, None] * rates[None, :]
    cosine, sine = jnp.cos(angles), jnp.sin(angles)
    rest = jnp.ones((positions.shape[0], HEAD_DIM - ROT_DIM), F32)
    zero, none = jnp.zeros_like(rest), jnp.zeros_like(sine)
    return (
        jnp.concatenate([cosine, cosine, rest] * 2, axis=1),
        jnp.concatenate([-sine, none, zero] * 2, axis=1),
        jnp.concatenate([none, sine, zero] * 2, axis=1),
    )


def turn(field, cosine, sine_a, sine_b, direction):
    half = ROT_DIM // 2
    width = field.shape[-1]
    ahead = pltpu.roll(field, width - half, 1)
    behind = pltpu.roll(field, half, 1)
    return field * cosine + direction * (ahead * sine_a + behind * sine_b)


def head_lanes(shape, which):
    lanes = lax.broadcasted_iota(jnp.int32, shape, 1)
    return (lanes >= which * HEAD_DIM) & (lanes < (which + 1) * HEAD_DIM)


def attend_tile(query, keys, values, bias):
    scores = nt(query, keys) + bias
    top = jnp.max(scores, axis=-1, keepdims=True)
    weights = jnp.exp(scores - top)
    total = jnp.sum(weights, axis=-1, keepdims=True)
    return nn(weights.astype(BF), values) / total, top


def attend_kernel(q_ref, k_ref, v_ref, bias_ref, mixed_ref, peak_ref):
    rows = q_ref.shape[0]
    tile = rows // 3 if rows % 3 == 0 and (rows // 3) % 16 == 0 else rows
    keys, values, bias = k_ref[...], v_ref[...], bias_ref[...]
    peaks = [None, None]
    for start in range(0, rows, tile):
        query = q_ref[start : start + tile, :] * BF(HEAD_DIM ** (-0.5))
        outs = []
        for which in range(2):
            one = jnp.where(head_lanes(query.shape, which), query, jnp.zeros_like(query))
            out, top = attend_tile(one, keys, values, bias)
            outs.append(out)
            top = jnp.max(top, axis=0, keepdims=True)
            peaks[which] = top if peaks[which] is None else jnp.maximum(peaks[which], top)
        mixed = jnp.where(head_lanes(outs[0].shape, 0), outs[0], outs[1])
        mixed_ref[start : start + tile, :] = mixed.astype(BF)
    spot = head_lanes((8, 2 * HEAD_DIM), 0)
    peak_ref[0] = jnp.where(
        spot, jnp.broadcast_to(peaks[0], spot.shape), jnp.broadcast_to(peaks[1], spot.shape)
    )


def attend(query, keys, values, bias, offsets):
    rows, tokens = query.shape[0], keys.shape[0]
    pairs = bias.shape[0]
    wide = 2 * HEAD_DIM
    mixed, peak = pl.pallas_call(
        attend_kernel,
        grid=(pairs,),
        out_shape=[
            jax.ShapeDtypeStruct((rows, pairs * wide), BF),
            jax.ShapeDtypeStruct((pairs, 8, wide), F32),
        ],
        in_specs=[
            pl.BlockSpec((rows, wide), lambda j: (0, offsets[0] + j)),
            pl.BlockSpec((tokens, wide), lambda j: (0, offsets[1] + j)),
            pl.BlockSpec((tokens, wide), lambda j: (0, offsets[2] + j)),
            pl.BlockSpec((1, tokens), lambda j: (0, 0)),
        ],
        out_specs=[
            pl.BlockSpec((rows, wide), lambda j: (0, j)),
            pl.BlockSpec((1, 8, wide), lambda j: (j, 0, 0)),
        ],
        compiler_params=pltpu.CompilerParams(vmem_limit_bytes=48 * 2**20),
        cost_estimate=pl.CostEstimate(
            flops=8 * rows * tokens * pairs * wide,
            bytes_accessed=4 * (rows + tokens) * pairs * wide,
            transcendentals=2 * pairs * rows * tokens,
        ),
    )(query, keys, values, bias[:1])
    return mixed, peak[:, 0, ::HEAD_DIM].reshape(-1)


def attend_back_kernel(turned, q_ref, k_ref, v_ref, g_ref, bias_ref, *refs):
    if turned:
        cos_ref, sa_ref, sb_ref = refs[:3]
        refs = refs[3:]
    dq_ref, dk_ref, dv_ref, dk_acc, dv_acc = refs
    rows = q_ref.shape[0]
    tile = rows // 3 if rows % 3 == 0 and (rows // 3) % 128 == 0 else rows
    scale = BF(HEAD_DIM ** (-0.5))
    keys, values, bias = k_ref[...], v_ref[...], bias_ref[...]
    for start in range(0, rows, tile):
        part = slice(start, start + tile)
        query, grad = q_ref[part, :] * scale, g_ref[part, :]
        dq = None
        for which in range(2):
            mine = head_lanes(query.shape, which)
            one = jnp.where(mine, query, jnp.zeros_like(query))
            out = jnp.where(mine, grad, jnp.zeros_like(grad))
            scores = nt(keys, one) + bias
            weights = jnp.exp(scores - jnp.max(scores, axis=0, keepdims=True))
            weights = weights * (1.0 / jnp.sum(weights, axis=0, keepdims=True))
            slope = nt(values, out)
            slope = weights * (slope - jnp.sum(weights * slope, axis=0, keepdims=True))
            slope = slope.astype(BF)
            dv = nn(weights.astype(BF), out)
            dk = nn(slope, one)
            other = jnp.where(head_lanes(keys.shape, which), keys, jnp.zeros_like(keys))
            piece = tn(slope, other * scale)
            dq = piece if dq is None else dq + piece
            if start == 0 and which == 0:
                dv_acc[...] = dv
                dk_acc[...] = dk
            else:
                dv_acc[...] += dv
                dk_acc[...] += dk
        if turned:
            dq = turn(dq, cos_ref[part, :], sa_ref[part, :], sb_ref[part, :], -1.0)
        dq_ref[part, :] = dq.astype(BF)
    dk = dk_acc[...]
    if turned:
        dk = turn(dk, cos_ref[...], sa_ref[...], sb_ref[...], -1.0)
    dk_ref[...] = dk.astype(BF)
    dv_ref[...] = dv_acc[...].astype(BF)


def attend_back(query, keys, values, grad, bias_column, offsets, turns):
    rows, tokens = query.shape[0], keys.shape[0]
    wide = 2 * HEAD_DIM
    pairs = grad.shape[1] // wide
    ins = [query, keys, values, grad, bias_column]
    specs = [
        pl.BlockSpec((rows, wide), lambda j: (0, offsets[0] + j)),
        pl.BlockSpec((tokens, wide), lambda j: (0, offsets[1] + j)),
        pl.BlockSpec((tokens, wide), lambda j: (0, offsets[2] + j)),
        pl.BlockSpec((rows, wide), lambda j: (0, j)),
        pl.BlockSpec((tokens, 1), lambda j: (0, 0)),
    ]
    if turns is not None:
        ins += list(turns)
        specs += [pl.BlockSpec((rows, wide), lambda j: (0, 0))] * 3
    return pl.pallas_call(
        functools.partial(attend_back_kernel, turns is not None),
        grid=(pairs,),
        out_shape=[
            jax.ShapeDtypeStruct((rows, pairs * wide), BF),
            jax.ShapeDtypeStruct((tokens, pairs * wide), BF),
            jax.ShapeDtypeStruct((tokens, pairs * wide), BF),
        ],
        in_specs=specs,
        out_specs=[
            pl.BlockSpec((rows, wide), lambda j: (0, j)),
            pl.BlockSpec((tokens, wide), lambda j: (0, j)),
            pl.BlockSpec((tokens, wide), lambda j: (0, j)),
        ],
        scratch_shapes=[pltpu.VMEM((tokens, wide), F32), pltpu.VMEM((tokens, wide), F32)],
        compiler_params=pltpu.CompilerParams(vmem_limit_bytes=48 * 2**20),
        cost_estimate=pl.CostEstimate(
            flops=20 * rows * tokens * pairs * wide,
            bytes_accessed=8 * (rows + tokens) * pairs * wide,
            transcendentals=2 * pairs * rows * tokens,
        ),
    )(*ins)


def project_kernel(turned, x_ref, w_ref, cos_ref, sa_ref, sb_ref, out_ref):
    wide = 2 * HEAD_DIM
    made = nn(x_ref[...], w_ref[...])

    @pl.when(pl.program_id(0) < turned)
    def _():
        for start in range(0, made.shape[1], wide):
            piece = turn(made[:, start : start + wide], cos_ref[...], sa_ref[...], sb_ref[...], 1.0)
            out_ref[:, start : start + wide] = piece.astype(BF)

    @pl.when(pl.program_id(0) >= turned)
    def _():
        out_ref[...] = made.astype(BF)


def project(rows, weight, turns, turned_columns):
    count, depth = rows.shape
    columns = weight.shape[1]
    block = 2 * HEAD_DIM * (2 if turned_columns % (4 * HEAD_DIM) == 0 else 1)
    table = pl.BlockSpec((count, 2 * HEAD_DIM), lambda j: (0, 0))
    return pl.pallas_call(
        functools.partial(project_kernel, turned_columns // block),
        grid=(columns // block,),
        out_shape=jax.ShapeDtypeStruct((count, columns), BF),
        in_specs=[
            pl.BlockSpec((count, depth), lambda j: (0, 0)),
            pl.BlockSpec((depth, block), lambda j: (0, j)),
            table,
            table,
            table,
        ],
        out_specs=pl.BlockSpec((count, block), lambda j: (0, j)),
        compiler_params=pltpu.CompilerParams(vmem_limit_bytes=48 * 2**20),
        cost_estimate=pl.CostEstimate(
            flops=2 * count * depth * columns,
            bytes_accessed=2 * (count * depth + depth * columns + count * columns),
            transcendentals=0,
        ),
    )(rows, weight, *turns)


PLAN = (
    0, 100, 300, 400, 500, 200, 2000, 1100, 2020, 2010, 2001, 3010, 1000, 1300, 3000, 2011,
    2101, 3011, 1500, 3001, 2220, 2021, 3021, 2100, 2200, 2300, 2110, 2201, 3020, 2210, 1400,
    2111, 2121, 2221, 2120, 2211, 3101, 2301, 5500, 4000, -1, -1, 2400, 3201, 2310, 3110, -1,
    1200, 3111, 3120, -1, -1, -1, 2401, 2410, 2311, 3100, 3200, -1, -1, -1, 3121, -1, -1, -1,
    -1, 2411, 3221, -1, 2421, 2501, 3211, 2500, 2320, -1, -1, 3210, 3220, 4100, 2420, 6000, -1,
    -1, -1, -1, -1, -1, 2510, 2511, 4200, -1, -1, -1, -1, -1, -1, 2321, -1, -1, -1, -1, -1, -1,
    -1, -1, -1, -1, -1, -1, -1, -1, 2521, 7000, 2520,
)


def normalise(stream, gain_vec, bias_vec):
    average = jnp.mean(stream, axis=-1, keepdims=True)
    centred = stream - average
    inverse = lax.rsqrt(jnp.mean(centred * centred, axis=-1, keepdims=True) + EPSILON)
    return centred * inverse * gain_vec + bias_vec


def forward_kernel(zs, *refs):
    refs = list(refs)

    def take(count):
        taken_refs = refs[:count]
        del refs[:count]
        return taken_refs

    shards = take(9)
    quarters_in = take(3)
    inputs_hbm, cot_hbm, cos_ref, sa_ref, sb_ref, self_bias, cross_bias, memory = take(8)
    wholes = take(3)
    quarter_outs = take(3)
    outs = take(15)
    cot_out = take(1)[0]
    peak_out = take(1)[0]
    send_sems, recv_sems, local_sems = take(3)
    w_in, w_a, w_b = take(3)
    (
        x_all, normed_self, taken, mixed_self, stream_cross, normed_cross,
        query_cross, taken_cross, mixed_cross, stream_feed, normed_feed,
        part_send, part_got, vectors, crest,
    ) = take(15)
    lanes = Lanes(send_sems, recv_sems, local_sems, zs)
    z, y, x = lanes.z, lanes.y, lanes.x
    t = lax.axis_index("tensor")
    rows, width = inputs_hbm.shape
    wide = 2 * HEAD_DIM

    def local(source, target):
        return pltpu.make_async_copy(source, target, lanes.local())

    rows_here, inner = shards[1].shape
    rows_kv = shards[6].shape[0]

    def spot(whole, row, count, column, wide_):
        return whole.at[z, y, x, pl.ds(row, count), pl.ds(column, wide_)]

    places = [
        spot(wholes[0], 0, rows_here, 3 * inner, shards[0].shape[1]),
        spot(wholes[0], 0, rows_here, 0, inner),
        spot(wholes[0], 0, rows_here, inner, inner),
        spot(wholes[0], 0, rows_here, 2 * inner, inner),
        spot(wholes[1], 0, rows_here, 0, inner),
        spot(wholes[1], 0, rows_here, inner, inner),
        spot(wholes[2], 0, rows_kv, 0, inner),
        spot(wholes[2], rows_kv, rows_kv, 0, inner),
        spot(wholes[2], 0, rows_here, inner, inner),
    ]
    pieces = [local(shard, place) for shard, place in zip(shards, places)]
    own_inputs = local(inputs_hbm, x_all.at[0])
    own_cot = local(cot_hbm, cot_out.at[0])
    for piece in pieces + [own_inputs, own_cot]:
        piece.start()
    greet(zs, True)

    def mate(source, target):
        return Move(lanes.copy(source, target, {"tensor": 1 - t}), None, None)

    def across(source, target):
        return Move(lanes.copy(source, target, {"x": 1 - x}), None, None)

    mate_inputs = mate(inputs_hbm, x_all.at[1])
    cot_moves = [
        mate(cot_hbm, cot_out.at[1]),
        across(cot_hbm, cot_out.at[2]),
        mate(cot_out.at[2], cot_out.at[3]),
    ]
    feed_moves = [mate(normed_feed.at[0], normed_feed.at[1])]
    mate_self = mate(part_send, part_got)
    mate_normed = mate(normed_cross.at[0], normed_cross.at[1])
    mate_cross = mate(part_send, part_got)
    gathers = [Gather(lanes, whole) for whole in wholes]
    quarters = [
        PairGather(lanes, quarters_in[i], quarter_outs[i], i == 2) for i in range(3)
    ]
    loads = [
        local(whole, held)
        for whole, held in zip(wholes, (w_in, w_a, w_b))
    ]
    results = (
        normed_self, taken, mixed_self, stream_cross, normed_cross,
        query_cross, taken_cross, mixed_cross, stream_feed, normed_feed,
        w_in.at[:, :, :, :, pl.ds(0, 3 * inner)],
        w_a.at[:, :, :, :, pl.ds(0, inner)],
        w_a.at[:, :, :, :, pl.ds(inner, inner)],
        w_b.at[:, :, :, :, pl.ds(inner, inner)],
        vectors,
    )
    saves = [local(held, out) for held, out in zip(results, outs)]

    mate_inputs.start()
    cot_moves[0].start()
    for piece in pieces:
        piece.wait()
    columns = 3 * inner
    pairs = inner // wide
    block = 2 * wide
    tile = 128 if rows % 128 == 0 else rows
    chunk = width // zs
    total = 2 * rows
    step = total // 3 if total % 3 == 0 and (total // 3) % 16 == 0 else total
    ready = set()

    def vec(i):
        return vectors[i : i + 1, :]

    def need(*groups):
        assert ready.issuperset(groups)

    def over(count, size, body):
        @pl.loop(0, count // size)
        def _(i):
            body(pl.ds(pl.multiple_of(i * size, size), size), i)

    def attend_all(query_ref, keys_at, values_at, kv_ref, bias_ref, mixed_ref):
        lane = lax.broadcasted_iota(jnp.int32, (8, wide), 1)
        for j in range(pairs):
            at = slice(j * wide, (j + 1) * wide)
            keys_in = slice(keys_at + j * wide, keys_at + (j + 1) * wide)
            values_in = slice(values_at + j * wide, values_at + (j + 1) * wide)

            def body(part, _):
                query = query_ref[part, at] * BF(HEAD_DIM ** (-0.5))
                outs = []
                for which in range(2):
                    mine = head_lanes(query.shape, which)
                    one = jnp.where(mine, query, jnp.zeros_like(query))
                    out, top = attend_tile(
                        one, kv_ref[:, keys_in], kv_ref[:, values_in], bias_ref[...]
                    )
                    outs.append(out)
                    top = jnp.broadcast_to(jnp.max(top, axis=0, keepdims=True), lane.shape)
                    best = jnp.where(lane == 2 * j + which, top, NEGATIVE)
                    crest[...] = jnp.maximum(crest[...], best)
                made = jnp.where(head_lanes(outs[0].shape, 0), outs[0], outs[1])
                mixed_ref[part, at] = made.astype(BF)

            over(total, step, body)
            yield

    def out_project(mixed_ref, weight, move, send, got, base, target):
        for zz in range(zs):
            cols = slice(zz * chunk, (zz + 1) * chunk)

            def body(part, i):
                left = mixed_ref[pl.ds(pl.multiple_of(rows + i * tile, tile), tile), :]
                send[part, cols] = nt(left, weight(zz)).astype(BF)

            over(rows, tile, body)
        move.start()
        yield
        for zz in range(zs):
            cols = slice(zz * chunk, (zz + 1) * chunk)

            def body(part, _):
                made = nt(mixed_ref[part, :], weight(zz))
                target[part, cols] = made + base(part, cols)

            over(rows, tile, body)
            yield
        move.arrived()

        def body(part, _):
            target[part, :] = target[part, :] + got[part, :].astype(F32)

        over(rows, tile, body)

    def compute():
        need(0)
        own_inputs.wait()
        mate_inputs.arrived()
        loads[0].wait()
        tail = w_in[..., columns : w_in.shape[-1]].reshape(width, w_in.shape[-1] - columns)
        vectors[...] = jnp.transpose(tail.astype(F32))
        saves[10].start()
        saves[14].start()
        crest[...] = jnp.full(crest.shape, NEGATIVE, F32)
        for side in range(2):

            def body(part, i):
                made = normalise(x_all[side, part, :].astype(F32), vec(0), vec(1))
                at = pl.multiple_of(side * rows + i * tile, tile)
                normed_self[pl.ds(at, tile), :] = made.astype(BF)

            over(rows, tile, body)
        saves[0].start()
        yield
        for start in range(0, columns, block):

            def body(part, _):
                weight = w_in[..., start : start + block].reshape(width, block)
                made = nn(normed_self[part, :], weight)
                for at in range(0, block, wide):
                    piece = made[:, at : at + wide]
                    if start + at < 2 * inner:
                        piece = turn(piece, cos_ref[part, :], sa_ref[part, :], sb_ref[part, :], 1.0)
                    taken[part, start + at : start + at + wide] = piece.astype(BF)

            over(total, step, body)
            yield
        saves[1].start()
        yield from attend_all(taken, inner, 2 * inner, taken, self_bias, mixed_self)
        saves[2].start()
        need(1)
        loads[1].wait()
        saves[11].start()
        saves[12].start()
        yield from out_project(
            mixed_self, lambda zz: w_a[zz, :, :, :, 0:inner].reshape(-1, inner), mate_self, part_send, part_got,
            lambda part, cols: x_all[0, part, cols].astype(F32), stream_cross,
        )
        saves[3].start()

        def second_norm(part, _):
            made = normalise(stream_cross[part, :], vec(2), vec(3))
            normed_cross[0, part, :] = made.astype(BF)

        over(rows, tile, second_norm)
        mate_normed.start()
        yield
        need(2)
        loads[2].wait()
        saves[13].start()
        depth = memory.shape[1]
        for side in range(2):
            for start in range(0, inner, block):
                part = slice(side * rows_kv, (side + 1) * rows_kv)
                weight = w_b[:, :, :, part, start : start + block].reshape(depth, block)
                at = side * inner + start
                taken_cross[:, at : at + block] = nn(memory[...], weight).astype(BF)
        saves[6].start()
        yield
        yield
        for side in range(2):
            if side == 1:
                mate_normed.arrived()
                saves[4].start()
            for start in range(0, inner, block):

                def body(part, i):
                    weight = w_a[..., inner + start : inner + start + block].reshape(width, block)
                    made = nn(normed_cross[side, part, :], weight).astype(BF)
                    at = pl.multiple_of(side * rows + i * tile, tile)
                    query_cross[pl.ds(at, tile), start : start + block] = made

                over(rows, tile, body)
                yield
        saves[5].start()
        yield from attend_all(query_cross, 0, inner, taken_cross, cross_bias, mixed_cross)
        saves[7].start()
        mate_self.sent()
        yield from out_project(
            mixed_cross, lambda zz: w_b[zz, :, :, :, inner : 2 * inner].reshape(-1, inner), mate_cross, part_send, part_got,
            lambda part, cols: stream_cross[part, cols], stream_feed,
        )
        saves[8].start()

        def third_norm(part, _):
            made = normalise(stream_feed[part, :], vec(4), vec(5))
            normed_feed[0, part, :] = made.astype(BF)

        over(rows, tile, third_norm)
        feed_moves[0].start()

    items = gathers + quarters
    names = ("begin", "far_first", "step", "far_step", "landed", "own_y_arrived")
    work = compute()
    for entry in PLAN:
        if entry < 0:
            next(work, None)
            continue
        kind, which, k, side = entry // 1000, entry // 100 % 10, entry // 10 % 10, entry % 10
        if kind == 6:
            cot_moves[1].start()
            continue
        if kind == 7:
            cot_moves[1].arrived()
            cot_moves[2].start()
            continue
        item = items[which]
        getattr(item, names[kind])(*((k, side) if kind in (2, 3) else ()))
        if kind == 4:
            ready.add(which)
            if which < 3:
                loads[which].start()
    for _ in work:
        pass
    peak_out[...] = crest[...]
    for i, item in enumerate(items):
        if i not in ready:
            item.landed()
    feed_moves[0].arrived()
    saves[9].start()
    cot_moves[0].arrived()
    cot_moves[2].arrived()
    own_cot.wait()
    for item in gathers + quarters:
        item.sent()
    for move in [mate_inputs, mate_normed, mate_cross] + cot_moves + feed_moves:
        move.sent()
    for save in saves:
        save.wait()


def forward(shards, quarters, inputs, cotangent, turns, self_bias, cross_bias, memory, zs):
    rows, width = inputs.shape
    seq_len, inner = 2 * rows, shards[1].shape[1]
    tokens = memory.shape[0]
    spread = []
    count = shards[1].shape[0]
    for columns in (3 * inner + shards[0].shape[1], 2 * inner, 2 * inner):
        spread.append(jax.ShapeDtypeStruct((zs, 2, 2, count, columns), BF))
    for shard in quarters:
        spread.append(
            jax.ShapeDtypeStruct((zs, 2, 2, shard.shape[0], shard.shape[1] // 2), shard.dtype)
        )
    results = [
        jax.ShapeDtypeStruct((seq_len, width), BF),
        jax.ShapeDtypeStruct((seq_len, 3 * inner), BF),
        jax.ShapeDtypeStruct((seq_len, inner), BF),
        jax.ShapeDtypeStruct((rows, width), F32),
        jax.ShapeDtypeStruct((2, rows, width), BF),
        jax.ShapeDtypeStruct((seq_len, inner), BF),
        jax.ShapeDtypeStruct((tokens, 2 * inner), BF),
        jax.ShapeDtypeStruct((seq_len, inner), BF),
        jax.ShapeDtypeStruct((rows, width), F32),
        jax.ShapeDtypeStruct((2, rows, width), BF),
    ]
    saved = [
        jax.ShapeDtypeStruct((zs, 2, 2, count, columns), BF)
        for columns in (3 * inner, inner, inner, inner)
    ]
    saved.append(jax.ShapeDtypeStruct((shards[0].shape[1], width), F32))
    cot_out = jax.ShapeDtypeStruct((4, rows, width), BF)
    peak = jax.ShapeDtypeStruct((8, 2 * HEAD_DIM), F32)
    moves = 3 * (3 + 8 * (zs - 1)) + 3 * (2 + 4 * (zs - 1)) + 8
    hbm = pl.BlockSpec(memory_space=pltpu.HBM)
    vmem = pl.BlockSpec(memory_space=pltpu.VMEM)
    held = [pltpu.VMEM(shape.shape, shape.dtype) for shape in spread[:3]]
    held += [pltpu.VMEM((2, rows, width), BF)]
    held += [pltpu.VMEM(shape.shape, shape.dtype) for shape in results]
    held += [pltpu.VMEM((rows, width), BF)] * 2
    held += [pltpu.VMEM((shards[0].shape[1], width), F32), pltpu.VMEM(peak.shape, F32)]
    flops = 2 * seq_len * inner * (7 * width + 4 * seq_len) // 1
    made = pl.pallas_call(
        functools.partial(forward_kernel, zs),
        out_shape=spread + results + saved + [cot_out, peak],
        in_specs=[hbm] * 14 + [vmem] * 6,
        out_specs=[hbm] * 22 + [vmem],
        scratch_shapes=[
            pltpu.SemaphoreType.DMA((moves,)),
            pltpu.SemaphoreType.DMA((moves,)),
            pltpu.SemaphoreType.DMA((9 + 2 + 3 + 3 + 15,)),
        ]
        + held,
        compiler_params=pltpu.CompilerParams(
            collective_id=1, has_side_effects=True, vmem_limit_bytes=62 * 2**20
        ),
        cost_estimate=pl.CostEstimate(flops=flops, bytes_accessed=10**8, transcendentals=10**7),
    )(*shards, *quarters, inputs, cotangent, *turns, self_bias, cross_bias, memory)
    return made[3:6], made[6:16], made[16:21], made[21], made[22]


def pair_rows(own):
    return jnp.concatenate([own, swap(own, "tensor")], axis=0)


def group_rows(own):
    both = jnp.stack([own, swap(own, "x")])
    other = swap(both, "tensor")
    return jnp.concatenate([both[0], other[0], both[1], other[1]], axis=0)


def spread_pair(left, right_t):
    rows = left.shape[0] // 2
    got = swap(nt(left[rows:], right_t), "tensor")
    return nt(left[:rows], right_t) + got


def spread_group(product):
    quarter = product.rows // 4
    far_send = product(3 * quarter, quarter)
    far = product(2 * quarter, quarter) + swap(far_send, "tensor")
    got_far = swap(far.astype(BF), "x")
    near = product(0, quarter) + swap(product(quarter, quarter), "tensor")
    return near + got_far.astype(F32)


class Product:
    def __init__(self, terms, transposed):
        self.terms = terms
        self.transposed = transposed
        self.rows = terms[0][0].shape[0]

    def __call__(self, first, count):
        total = None
        for left, right in self.terms:
            part = (nt if self.transposed else nn)(left[first : first + count], right)
            total = part if total is None else total + part
        return total


def per_device(
    inputs,
    cotangent,
    context,
    context_live,
    lengths,
    threshold,
    self_gain,
    self_bias,
    self_query,
    self_key,
    self_value,
    self_output,
    cross_gain,
    cross_bias,
    cross_query,
    cross_key,
    cross_value,
    cross_output,
    feed_gain,
    feed_bias,
    gate_weight,
    up_weight,
    down_weight,
):
    zs = lax.axis_size("z")
    x_at = lax.axis_index("x")
    t_at = lax.axis_index("tensor")
    width = inputs.shape[1]
    rows = inputs.shape[0]
    seq_len = 2 * rows
    inner = self_query.shape[1]
    heads_here = inner // HEAD_DIM
    ff = gate_weight.shape[1] // 2
    shard_rows = self_query.shape[0]

    quarters = [gate_weight, up_weight, down_weight.T]
    vector_list = [self_gain, self_bias, cross_gain, cross_bias, feed_gain, feed_bias]
    stream = inputs.astype(F32)
    local = jnp.arange(rows)
    places = jnp.concatenate([t_at * rows + local, (1 - t_at) * rows + local])
    turns = turn_tables(places.astype(F32))
    self_bias_row = jnp.where(places < lengths[0], 0.0, NEGATIVE).astype(F32)
    tokens = context.shape[1]
    token_rows = -(-tokens // 128) * 128
    cross_bias_row = jnp.pad(
        jnp.where(context_live[0] > 0, 0.0, NEGATIVE).astype(F32),
        (0, token_rows - tokens),
        constant_values=NEGATIVE,
    )
    memory = jnp.pad(context[0], ((0, token_rows - tokens), (0, 0)))
    pairs = inner // (2 * HEAD_DIM)

    if shard_rows % 32 == 0:
        vectors = jnp.pad(jnp.stack(vector_list, axis=1), ((0, 0), (0, 122)))
        spread, made, saved, cot_group, crest = forward(
            [
                vectors,
                self_query,
                self_key,
                self_value,
                self_output.T,
                cross_query,
                cross_key,
                cross_value,
                cross_output.T,
            ],
            quarters,
            inputs,
            cotangent,
            turns,
            self_bias_row[None],
            cross_bias_row[None],
            memory,
            zs,
        )
        in_weight, self_out_t, cross_in, cross_out_t, norms = saved
        (
            normed_self,
            taken,
            mixed_self,
            stream_cross,
            normed_cross,
            query_cross,
            taken_cross,
            mixed_cross,
            stream_feed,
            normed_feed,
        ) = made
        gate_full, up_full, down_t = spread
        normed_cross = normed_cross.reshape(seq_len, width)
        near_feed, cot_group = (v.reshape(-1, width) for v in (normed_feed, cot_group))
    else:
        vectors = jnp.stack(vector_list).astype(F32)
        vectors = jnp.pad(vectors, ((0, 2), (0, 128 - shard_rows)))
        (norms, in_weight, self_out_t, cross_in, memory_weight, cross_out_t, gate_full, up_full, down_t) = (
            gather_all(
                [
                    [vectors],
                    [self_query, self_key, self_value],
                    [self_output.T],
                    [cross_query],
                    [cross_key, cross_value],
                    [cross_output.T],
                ],
                quarters,
                zs,
            )
        )
        norms = norms.reshape(-1, 8, 128)[:, :6, :shard_rows].transpose(1, 0, 2).reshape(6, width)
        in_weight, memory_weight = in_weight.reshape(width, -1), memory_weight.reshape(-1, 2 * inner)
        self_out_t, cross_in, cross_out_t, gate_full, up_full, down_t = (
            w.reshape(width, -1)
            for w in (self_out_t, cross_in, cross_out_t, gate_full, up_full, down_t)
        )
        cot_group = group_rows(cotangent)
        all_inputs = pair_rows(inputs)
        normed, _, _ = norm_forward(all_inputs.astype(F32), norms[0], norms[1])
        normed_self = normed.astype(BF)
        taken = project(normed_self, in_weight, turns, 2 * inner)
        self_bias_rows = jnp.broadcast_to(self_bias_row, (pairs, seq_len))
        mixed_self, peak_self = attend(taken, taken, taken, self_bias_rows, (0, pairs, 2 * pairs))
        stream_cross = stream + spread_pair(mixed_self, self_out_t)
        normed, _, _ = norm_forward(stream_cross, norms[2], norms[3])
        normed_cross = pair_rows(normed.astype(BF))
        query_cross = nn(normed_cross, cross_in).astype(BF)
        taken_cross = nn(memory, memory_weight).astype(BF)
        cross_bias_rows = jnp.broadcast_to(cross_bias_row, (pairs, token_rows))
        mixed_cross, peak_cross = attend(
            query_cross, taken_cross, taken_cross, cross_bias_rows, (0, 0, pairs)
        )
        stream_feed = stream_cross + spread_pair(mixed_cross, cross_out_t)
        normed, _, _ = norm_forward(stream_feed, norms[4], norms[5])
        near_feed = pair_rows(normed.astype(BF))
        crest = jnp.pad(
            jnp.maximum(peak_self, peak_cross)[None], ((0, 7), (0, 128 - heads_here))
        )
    in_weight, self_out_t, cross_in, cross_out_t, gate_full, up_full, down_t = (
        w.reshape(width, -1)
        for w in (in_weight, self_out_t, cross_in, cross_out_t, gate_full, up_full, down_t)
    )
    unit_cross, inverse_cross = unit_rows_of(stream_cross)
    unit_feed, inverse_feed = unit_rows_of(stream_feed)
    far_own = swap(near_feed[:rows], "x")

    def feed_half(normed, cot_rows):
        gate_pre = nn(normed, gate_full)
        upward = nn(normed, up_full)
        sigmoid_gate = jax.nn.sigmoid(gate_pre)
        hidden = (gate_pre * sigmoid_gate * upward).astype(BF)
        grad_hidden = nn(cot_rows, down_t)
        grad_gate = grad_hidden * upward * sigmoid_gate * (1.0 + gate_pre * (1.0 - sigmoid_gate))
        grad_upward = grad_hidden * gate_pre * sigmoid_gate
        return hidden, grad_gate.astype(BF), grad_upward.astype(BF)

    def feed_back(grad_gate, grad_upward):
        return nt(grad_gate, gate_full) + nt(grad_upward, up_full)

    hidden_near, gate_near, up_near = feed_half(near_feed, cot_group[:seq_len])
    far_own, hidden_near, gate_near, up_near = lax.optimization_barrier(
        (far_own, hidden_near, gate_near, up_near)
    )
    far_feed = pair_rows(far_own)
    hidden_far, gate_far, up_far = feed_half(far_feed, cot_group[seq_len:])
    far_sum = feed_back(gate_far[:rows], up_far[:rows]) + swap(
        feed_back(gate_far[rows:], up_far[rows:]), "tensor"
    )
    far_sum = far_sum.astype(BF)
    got_far = swap(far_sum, "x")
    normed_feed = jnp.concatenate([near_feed, far_feed], axis=0)
    hidden = jnp.concatenate([hidden_near, hidden_far], axis=0)
    grad_gate = jnp.concatenate([gate_near, gate_far], axis=0)
    grad_upward = jnp.concatenate([up_near, up_far], axis=0)
    down_pair = PairSum(after(cot_group, far_sum), hidden, zs)
    gate_pair = PairSum(after(normed_feed, far_sum), grad_gate, zs)
    grad_normed = feed_back(gate_near[:rows], up_near[:rows]) + swap(
        feed_back(gate_near[rows:], up_near[rows:]), "tensor"
    )
    got_far = after(got_far, grad_normed, gate_pair.sent, down_pair.sent)
    grad_normed = grad_normed + got_far.astype(F32)
    stream_part, grad_feed_gain, grad_feed_bias = norm_backward(
        grad_normed, unit_feed, inverse_feed, norms[4]
    )
    grad_stream = cotangent.astype(F32) + stream_part
    grad_full = pair_rows(grad_stream.astype(BF))
    up_pair = PairSum(after(normed_feed, grad_full), grad_upward, zs)
    cross_output_sum = FullSum(grad_full, mixed_cross, zs)
    grad_mixed = after(nn(grad_full, cross_out_t).astype(BF), cross_output_sum.sent)
    grad_query, grad_keys, grad_values = attend_back(
        query_cross, taken_cross, taken_cross, grad_mixed, cross_bias_row[:, None], (0, 0, pairs), None
    )
    down_pair.second(grad_query)
    grad_normed = spread_pair(grad_query, cross_in)
    cross_query_sum = FullSum(normed_cross, grad_query, zs)
    part_memory = tn(memory, jnp.concatenate([grad_keys, grad_values], axis=1))
    stream_part, grad_cross_gain, grad_cross_bias = norm_backward(
        grad_normed, unit_cross, inverse_cross, norms[2]
    )
    grad_stream = grad_stream + stream_part
    grad_full = pair_rows(grad_stream.astype(BF))
    gate_pair.second(grad_full)
    cross_output_sum.second(grad_full)
    part_self_output = tn(grad_full, mixed_self)
    grad_mixed = after(nn(grad_full, self_out_t).astype(BF), cross_query_sum.sent)
    grad_parts = attend_back(
        taken, taken, taken, grad_mixed, self_bias_row[:, None], (0, pairs, 2 * pairs), turns
    )
    grad_in = jnp.concatenate(grad_parts, axis=1)
    up_pair.second(grad_in)
    cross_query_sum.second(grad_in)
    sum_cross_output = cross_output_sum.third(grad_in).astype(F32)
    part_in = tn(normed_self, grad_in[:, : 2 * inner]).astype(BF)
    part_value = tn(normed_self, grad_parts[2]).astype(BF)
    sum_cross_query = cross_query_sum.third(part_value).astype(F32)
    def blocks(part):
        return part.astype(BF).reshape(zs, 2, 2, -1, part.shape[1])

    if shard_rows % 32 == 0:
        none = jnp.zeros_like(grad_feed_gain)
        other_sums = jnp.stack(
            [none, none, grad_cross_gain, grad_cross_bias, grad_feed_gain, grad_feed_bias, none, none]
        )
        vector_sums, sum_in, sum_value, sum_self_output, sum_memory, crest, grad_stream = (
            scatter_all(
                [
                    blocks(part_in),
                    blocks(part_value),
                    blocks(part_self_output),
                    blocks(part_memory),
                ],
                ["z", "x", "y", "y", "z"],
                crest,
                zs,
                (
                    grad_in,
                    in_weight.reshape(zs, 2, 2, shard_rows, -1),
                    inputs,
                    grad_stream,
                    norms[:1],
                    other_sums,
                ),
            )
        )
        vector_sums = vector_sums.T
    else:
        grad_normed = spread_pair(grad_in, in_weight)
        unit_self, inverse_self = unit_rows_of(stream)
        stream_part, grad_self_gain, grad_self_bias = norm_backward(
            grad_normed, unit_self, inverse_self, norms[0]
        )
        grad_stream = grad_stream + stream_part

        vector_sums = jnp.stack(
            [
                grad_self_gain,
                grad_self_bias,
                grad_cross_gain,
                grad_cross_bias,
                grad_feed_gain,
                grad_feed_bias,
            ]
        ).reshape(6, -1, shard_rows)
        vector_sums = vector_sums + swap(vector_sums, "tensor")
        vector_sums = jnp.pad(
            vector_sums.transpose(1, 0, 2), ((0, 0), (0, 2), (0, 128 - shard_rows))
        ).reshape(zs, 2, 2, 8, 128)

        vector_sums, sum_in, sum_value, sum_self_output, sum_memory, crest = scatter_all(
            [
                vector_sums,
                blocks(part_in),
                blocks(part_value),
                blocks(part_self_output),
                blocks(part_memory),
            ],
            ["z", "x", "y", "y", "z"],
            crest,
            zs,
        )
        vector_sums = vector_sums[:, :shard_rows]
    peaks = crest[0, :heads_here]
    factor = jnp.sqrt(threshold[0] / jnp.maximum(peaks, threshold[0]))
    columns = jnp.repeat(factor, HEAD_DIM)[None, :]
    result = stream_feed + spread_group(Product([(hidden, down_t)], True))
    result = result.astype(BF)
    down_keep, down_got = down_pair.third()
    gate_keep, gate_got = gate_pair.third()
    up_keep, up_got = up_pair.third()

    def side_by_side(kept, got):
        low = jnp.where(x_at == 0, kept, got).astype(F32)
        high = jnp.where(x_at == 0, got, kept).astype(F32)
        return jnp.concatenate([low, high], axis=1)

    down_sum = side_by_side(down_keep, down_got).T
    gate_sum = side_by_side(gate_keep, gate_got)
    up_sum = side_by_side(up_keep, up_got)
    return (
        result,
        grad_stream,
        vector_sums[0],
        vector_sums[1],
        sum_in[:, :inner],
        sum_in[:, inner:],
        sum_value,
        sum_self_output.T,
        vector_sums[2],
        vector_sums[3],
        sum_cross_query,
        sum_memory[:, :inner],
        sum_memory[:, inner:],
        sum_cross_output.T,
        vector_sums[4],
        vector_sums[5],
        gate_sum,
        up_sum,
        down_sum,
        peaks,
        self_query.astype(F32) * columns,
        self_key.astype(F32) * columns,
        cross_query.astype(F32) * columns,
        cross_key.astype(F32) * columns,
    )


def solution(mesh):
    count = mesh.shape["dp"]
    mesh = Mesh(
        mesh.devices.reshape(count // 4, 2, 2, mesh.shape["tensor"]), ("z", "y", "x", "tensor")
    )
    dp = ("z", "y", "x")
    both = P(dp + ("tensor",), None)
    split = P(dp)
    row_major = P(dp, "tensor")
    column_major = P("tensor", dp)
    in_specs = (
        both,
        both,
        P(dp, None, None),
        P(dp, None),
        split,
        P(),
        split,
        split,
        row_major,
        row_major,
        row_major,
        column_major,
        split,
        split,
        row_major,
        row_major,
        row_major,
        column_major,
        split,
        split,
        row_major,
        row_major,
        column_major,
    )
    out_specs = (
        both,
        both,
        split,
        split,
        row_major,
        row_major,
        row_major,
        column_major,
        split,
        split,
        row_major,
        row_major,
        row_major,
        column_major,
        split,
        split,
        row_major,
        row_major,
        column_major,
        P("tensor"),
        row_major,
        row_major,
        row_major,
        row_major,
    )
    return jax.shard_map(
        per_device, mesh=mesh, in_specs=in_specs, out_specs=out_specs, check_vma=False
    )
```

```python
import functools

import jax
import jax.numpy as jnp
from jax import lax
from jax.experimental import pallas as pl
from jax.experimental.pallas import tpu as pltpu
from jax.sharding import Mesh
from jax.sharding import PartitionSpec as P

HEAD_DIM = 64
ROT_DIM = 32
EPSILON = 1e-05
NEGATIVE = -1e30
BF = jnp.bfloat16
F32 = jnp.float32


def swap(value, axis):
    return lax.ppermute(value, axis, [(0, 1), (1, 0)])


def pick(value, index, dim):
    return lax.dynamic_index_in_dim(value, index, dim, keepdims=False)


class Lanes:
    def __init__(self, send_sems, recv_sems, local_sems, zs):
        self.send_sems, self.recv_sems, self.local_sems = send_sems, recv_sems, local_sems
        self.used = self.used_local = 0
        self.z = lax.axis_index("z")
        self.y = lax.axis_index("y")
        self.x = lax.axis_index("x")
        self.zs = zs

    def local(self):
        self.used_local += 1
        return self.local_sems.at[self.used_local - 1]

    def copy(self, source, target, device):
        return self.copies([source], target, device)[0]

    def copies(self, sources, target, device):
        slot = self.used
        self.used += 1
        return [
            pltpu.make_async_remote_copy(
                src_ref=source,
                dst_ref=target,
                send_sem=self.send_sems.at[slot],
                recv_sem=self.recv_sems.at[slot],
                device_id=device,
                device_id_type=pl.DeviceIdType.MESH,
            )
            for source in sources
        ]


def guarded(condition, action):
    if condition is None:
        action()
    else:
        pl.when(condition)(action)


class Move:
    def __init__(self, copy, sends, receives):
        self.copy_, self.sends, self.receives = copy, sends, receives

    def start(self):
        guarded(self.sends, self.copy_.start)

    def arrived(self):
        guarded(self.receives, self.copy_.wait_recv)

    def sent(self):
        guarded(self.sends, self.copy_.wait_send)


class Gather:
    def __init__(self, lanes, whole):
        zs, z, y, x = lanes.zs, lanes.z, lanes.y, lanes.x
        own = whole.at[z, y, x]

        def block(zz, yy):
            return whole.at[zz, yy, x]

        def along(source, target, axis, to, sends=None, receives=None):
            return Move(lanes.copy(source, target, {axis: to}), sends, receives)

        self.first = [
            along(own, block(z, y), "y", 1 - y),
            along(own, block(z, y), "x", 1 - x),
        ]
        self.far = [[along(block(z, 1 - y), block(z, 1 - y), "x", 1 - x)]]
        self.steps = []
        for k in range(zs - 1):
            right, left = jnp.maximum(z - k, 0), jnp.minimum(z + k, zs - 1)
            step = []
            for zz, to, sends, receives, got in (
                (right, z + 1, (z >= k) & (z < zs - 1), z >= k + 1, jnp.maximum(z - 1 - k, 0)),
                (left, z - 1, (z + k < zs) & (z > 0), z + k + 1 < zs, jnp.minimum(z + 1 + k, zs - 1)),
            ):
                source = own if k == 0 else block(zz, y)
                move = along(source, block(zz, y), "z", to, sends, receives)
                follow = [
                    along(block(got, y), block(got, y), "y", 1 - y, receives, receives),
                    along(block(got, y), block(got, y), "x", 1 - x, receives, receives),
                    along(block(got, 1 - y), block(got, 1 - y), "x", 1 - x, receives, receives),
                ]
                step.append((move, follow))
            self.steps.append(step)

    def begin(self):
        for move, _ in self.steps[0]:
            move.start()
        for move in self.first:
            move.start()

    def step(self, k, side):
        move, follow = self.steps[k][side]
        move.arrived()
        if k + 1 < len(self.steps):
            self.steps[k + 1][side][0].start()
        follow[0].start()
        follow[1].start()

    def far_first(self):
        self.first[0].arrived()
        self.far[0][0].start()

    def far_step(self, k, side):
        _, follow = self.steps[k][side]
        follow[0].arrived()
        follow[2].start()

    def landed(self):
        self.first[1].arrived()
        self.far[0][0].arrived()
        for step in self.steps:
            for _, follow in step:
                follow[1].arrived()
                follow[2].arrived()

    def sent(self):
        for move in self.first + self.far[0]:
            move.sent()
        for step in self.steps:
            for move, follow in step:
                move.sent()
                for other in follow:
                    other.sent()


class PairGather:
    def __init__(self, lanes, shard, whole, y_first):
        zs, z, y, x = lanes.zs, lanes.z, lanes.y, lanes.x
        ff = whole.shape[-1]
        kept = shard.at[:, pl.ds(pl.multiple_of(x * ff, ff), ff)]
        sent = shard.at[:, pl.ds(pl.multiple_of((1 - x) * ff, ff), ff)]
        self.y_first = y_first

        def along(piece, axis, to, sends=None, receives=None):
            return Move(lanes.copy(piece, piece, {axis: to}), sends, receives)

        self.swap = Move(lanes.copy(sent, whole.at[z, y, x], {"x": 1 - x}), None, None)
        self.local = pltpu.make_async_copy(kept, whole.at[z, y, x], lanes.local())
        self.own_y = along(whole.at[z, y], "y", 1 - y)
        self.steps = []
        for k in range(zs - 1):
            step = []
            for zz, to, sends, receives, got in (
                (jnp.maximum(z - k, 0), z + 1, (z >= k) & (z < zs - 1), z >= k + 1, jnp.maximum(z - 1 - k, 0)),
                (jnp.minimum(z + k, zs - 1), z - 1, (z + k < zs) & (z > 0), z + k + 1 < zs, jnp.minimum(z + 1 + k, zs - 1)),
            ):
                piece = whole.at[zz] if y_first else whole.at[zz, y]
                move = along(piece, "z", to, sends, receives)
                follow = [] if y_first else [along(whole.at[got, y], "y", 1 - y, receives, receives)]
                step.append((move, follow))
            self.steps.append(step)

    def begin(self):
        self.swap.start()
        self.local.start()

    def far_first(self):
        self.swap.arrived()
        self.local.wait()
        self.own_y.start()
        if not self.y_first:
            for move, _ in self.steps[0]:
                move.start()

    def own_y_arrived(self):
        self.own_y.arrived()
        if self.y_first:
            for move, _ in self.steps[0]:
                move.start()

    def step(self, k, side):
        move, follow = self.steps[k][side]
        move.arrived()
        if k + 1 < len(self.steps):
            self.steps[k + 1][side][0].start()
        for other in follow:
            other.start()

    def landed(self):
        if not self.y_first:
            self.own_y.arrived()
        for step in self.steps:
            for move, follow in step:
                for other in follow:
                    other.arrived()

    def sent(self):
        self.swap.sent()
        self.own_y.sent()
        for step in self.steps:
            for move, follow in step:
                move.sent()
                for other in follow:
                    other.sent()


def greet(zs, mates=False):
    z, y, x = lax.axis_index("z"), lax.axis_index("y"), lax.axis_index("x")
    barrier = pltpu.get_barrier_semaphore()

    def signal(device):
        pl.semaphore_signal(barrier, inc=1, device_id=device, device_id_type=pl.DeviceIdType.MESH)

    signal({"x": 1 - x})
    signal({"y": 1 - y})
    pl.when(z > 0)(lambda: signal({"z": z - 1}))
    pl.when(z < zs - 1)(lambda: signal({"z": z + 1}))
    if mates:
        signal({"tensor": 1 - lax.axis_index("tensor")})
    peers = (3 if mates else 2) + (z > 0).astype(jnp.int32) + (z < zs - 1).astype(jnp.int32)
    pl.semaphore_wait(barrier, peers)


def gather_kernel(zs, groups, pairs, *refs):
    shards = sum(groups)
    owns, pair_in = refs[:shards], refs[shards : shards + pairs]
    refs = refs[shards + pairs :]
    outs = refs[: len(groups) + pairs]
    lanes = Lanes(*refs[len(groups) + pairs :], zs)
    z, y, x = lanes.z, lanes.y, lanes.x
    pieces, at = [], 0
    for count, whole in zip(groups, outs):
        width = whole.shape[-1] // count
        for i in range(count):
            target = whole.at[z, y, x, :, pl.ds(i * width, width)]
            pieces.append(pltpu.make_async_copy(owns[at], target, lanes.local()))
            at += 1
    for piece in pieces:
        piece.start()
    greet(zs)
    gathers = [Gather(lanes, whole) for whole in outs[: len(groups)]]
    quarters = [
        PairGather(lanes, pair_in[i], outs[len(groups) + i], i == 0) for i in range(pairs)
    ]
    for quarter in quarters:
        quarter.begin()
    for piece in pieces:
        piece.wait()
    for gather in gathers:
        gather.begin()
    for quarter in quarters:
        quarter.far_first()
    for gather in gathers:
        gather.far_first()
    for k, side in [(k, side) for k in range(zs - 1) for side in range(2)]:
        for gather in gathers:
            gather.step(k, side)
        for quarter in quarters:
            if quarter.y_first:
                if k == 0 and side == 0:
                    quarter.own_y_arrived()
            else:
                quarter.step(k, side)
        for gather in gathers:
            gather.far_step(k, side)
        for quarter in quarters:
            if quarter.y_first:
                quarter.step(k, side)
    for item in gathers + quarters:
        item.landed()
        item.sent()


def gather_all(groups, quarters, zs):
    flat = [shard for group in groups for shard in group] + list(quarters)
    outs = []
    for group in groups:
        columns = sum(shard.shape[1] for shard in group)
        outs.append(
            jax.ShapeDtypeStruct((zs, 2, 2, group[0].shape[0], columns), group[0].dtype)
        )
    for shard in quarters:
        outs.append(
            jax.ShapeDtypeStruct((zs, 2, 2, shard.shape[0], shard.shape[1] // 2), shard.dtype)
        )
    count, pairs = len(groups), len(quarters)
    moves = count * (3 + 8 * (zs - 1)) + pairs * (2 + 4 * (zs - 1))
    hbm = pl.BlockSpec(memory_space=pltpu.HBM)
    return pl.pallas_call(
        functools.partial(gather_kernel, zs, tuple(len(group) for group in groups), pairs),
        out_shape=outs,
        in_specs=[hbm] * len(flat),
        out_specs=[hbm] * len(outs),
        scratch_shapes=[
            pltpu.SemaphoreType.DMA((moves,)),
            pltpu.SemaphoreType.DMA((moves,)),
            pltpu.SemaphoreType.DMA((len(flat),)),
        ],
        compiler_params=pltpu.CompilerParams(collective_id=1, has_side_effects=True),
    )(*flat)


def plus(*terms):
    total = terms[0].astype(F32)
    for term in terms[1:]:
        total = total + term.astype(F32)
    return total


def ends_first(zs):
    order = []
    for i in range(zs // 2):
        order += [zs - 1 - i, i]
    return order


class Line:
    def __init__(self, lanes, part, from_left, from_right):
        zs, z = lanes.zs, lanes.z
        self.zs, self.z, self.part = zs, z, part
        self.from_left, self.from_right = from_left, from_right
        self.right, self.left = {}, {}
        for d in ends_first(zs):
            after, before = jnp.minimum(z + 1, zs - 1), jnp.maximum(z - 1, 0)
            self.right[d] = lanes.copies(
                (part(d), from_left.at[d]), from_left.at[d], {"z": after}
            )
            self.left[d] = lanes.copies(
                (part(d), from_right.at[d]), from_right.at[d], {"z": before}
            )

    def pass_on(self, d):
        for moves, inbox, sends, edge in (
            (self.right[d], self.from_left, self.z < d, self.z == 0),
            (self.left[d], self.from_right, self.z > d, self.z == self.zs - 1),
        ):

            @pl.when(sends & edge)
            def _():
                moves[0].start()

            @pl.when(sends & jnp.logical_not(edge))
            def _():
                moves[1].wait_recv()
                inbox[d] = plus(self.part(d)[...], inbox[d]).astype(inbox.dtype)
                moves[1].start()

    def total(self, sink):
        for d in range(self.zs):

            @pl.when(self.z == d)
            def _():
                terms = [self.part(d)[...]]
                if d > 0:
                    self.right[d][0].wait_recv()
                    terms.append(self.from_left[d])
                if d < self.zs - 1:
                    self.left[d][0].wait_recv()
                    terms.append(self.from_right[d])
                sink[...] = plus(*terms).astype(sink.dtype)

    def finish(self):
        for d in ends_first(self.zs):
            pl.when(self.z < d)(self.right[d][0].wait_send)
            pl.when(self.z > d)(self.left[d][0].wait_send)


class Scatter:
    def __init__(self, lanes, part, held, out, first):
        zs, z, y, x = lanes.zs, lanes.z, lanes.y, lanes.x
        got, near, from_left, from_right = held
        second = "y" if first == "x" else "x"
        self.lanes, self.part, self.got, self.near, self.out = lanes, part, got, near, out
        f, s = (x, y) if first == "x" else (y, x)
        self.f, self.s = f, s

        def block(zz, a, b):
            return part.at[zz, b, a] if first == "x" else part.at[zz, a, b]

        self.block = block
        self.one, self.two = {}, {}
        for zz in ends_first(zs):
            for j, b in enumerate((1 - s, s)):
                self.one[zz, j] = Move(
                    lanes.copy(block(zz, 1 - f, b), got.at[zz, j], {first: 1 - f}), None, None
                )
        for zz in ends_first(zs):
            self.two[zz] = Move(
                lanes.copy(got.at[zz, 0], near.at[zz], {second: 1 - s}), None, None
            )
        self.line = Line(lanes, lambda d: got.at[d, 1], from_left, from_right)

    def begin(self, zz):
        for j in range(2):
            self.one[zz, j].start()

    def second(self, zz):
        self.one[zz, 0].arrived()
        mine, got = self.block(zz, self.f, 1 - self.s), self.got
        got[zz, 0] = plus(mine[...], got[zz, 0]).astype(got.dtype)
        self.two[zz].start()

    def third(self, zz):
        self.one[zz, 1].arrived()
        self.two[zz].arrived()
        mine = self.block(zz, self.f, self.s)
        got = self.got
        got[zz, 1] = plus(mine[...], got[zz, 1], self.near[zz]).astype(got.dtype)
        self.line.pass_on(zz)

    def finish(self):
        self.line.total(self.out)
        self.line.finish()
        for move in list(self.one.values()) + list(self.two.values()):
            move.sent()


class ScatterZ:
    def __init__(self, lanes, part, held, out):
        y, x = lanes.y, lanes.x
        from_left, from_right, held_z, near, last = held
        self.lanes, self.sum_z, self.near, self.last, self.out = lanes, held_z, near, last, out
        self.line = Line(lanes, lambda d: part.at[d], from_left, from_right)
        self.two = Move(lanes.copy(held_z.at[1 - y], near, {"y": 1 - y}), None, None)
        self.three = Move(lanes.copy(near.at[1 - x], last, {"x": 1 - x}), None, None)

    def pass_on(self, d):
        self.line.pass_on(d)

    def total(self):
        self.line.total(self.sum_z)
        self.two.start()

    def after(self):
        self.two.arrived()
        self.near[...] = plus(self.sum_z[self.lanes.y], self.near[...]).astype(self.near.dtype)
        self.three.start()

    def finish(self):
        self.three.arrived()
        self.out[...] = plus(self.near[self.lanes.x], self.last[...]).astype(self.out.dtype)
        self.line.finish()
        self.two.sent()
        self.three.sent()


class Crest:
    def __init__(self, lanes, own, held, out):
        zs, z, y, x = lanes.zs, lanes.z, lanes.y, lanes.x
        near_x, near_y, mine_x, mine_y, right, left, inbox_r, inbox_l = (
            held.at[i] for i in range(8)
        )
        self.zs, self.z, self.own, self.out = zs, z, own, out
        self.near_x, self.near_y, self.mine_x, self.mine_y = near_x, near_y, mine_x, mine_y
        self.ways = (
            (right, inbox_r, z > 0, z < zs - 1),
            (left, inbox_l, z < zs - 1, z > 0),
        )
        self.one = Move(lanes.copy(own, near_x, {"x": 1 - x}), None, None)
        self.two = Move(lanes.copy(mine_x, near_y, {"y": 1 - y}), None, None)
        self.moves = [
            Move(lanes.copy(right, inbox_r, {"z": jnp.minimum(z + 1, zs - 1)}), z < zs - 1, z > 0),
            Move(lanes.copy(left, inbox_l, {"z": jnp.maximum(z - 1, 0)}), z > 0, z < zs - 1),
        ]

    def second(self):
        self.one.arrived()
        self.mine_x[...] = jnp.maximum(self.own[...], self.near_x[...])
        self.two.start()

    def finish(self):
        self.two.arrived()
        self.mine_y[...] = jnp.maximum(self.mine_x[...], self.near_y[...])
        self.out[...] = self.mine_y[...]
        for move, (held, inbox, has_before, has_after) in zip(self.moves, self.ways):

            @pl.when(has_before)
            def _():
                move.copy_.wait_recv()
                self.out[...] = jnp.maximum(self.out[...], inbox[...])
                held[...] = jnp.maximum(self.mine_y[...], inbox[...])

            @pl.when(jnp.logical_not(has_before))
            def _():
                held[...] = self.mine_y[...]

            move.start()
        for move in [self.one, self.two] + self.moves:
            move.sent()


class LastNorm:
    def __init__(self, lanes, given, held, out, local_sems):
        grad_hbm, weight_hbm, self.inputs, self.stream, self.gain, self.others = given
        (
            self.grad, self.weight, self.send, self.got,
            self.rows8, self.got8, self.tall, self.blocks,
        ) = held
        self.out, self.zs = out, lanes.zs
        mate = {"tensor": 1 - lax.axis_index("tensor")}
        self.loads = [pltpu.make_async_copy(grad_hbm, self.grad, local_sems.at[0])] + [
            pltpu.make_async_copy(
                weight_hbm.at[zz], self.weight.at[zz % 2], local_sems.at[1 + zz % 2]
            )
            for zz in range(lanes.zs)
        ]
        self.mate_part = Move(lanes.copy(self.send, self.got, mate), None, None)
        self.mate_rows = Move(lanes.copy(self.rows8, self.got8, mate), None, None)

    def pieces(self):
        rows, width = self.out.shape
        tile = 128 if rows % 128 == 0 else rows
        chunk = width // self.zs

        def over(body):
            @pl.loop(0, rows // tile)
            def _(i):
                body(pl.multiple_of(i * tile, tile))

        def part_of(first, zz):
            weight = self.weight[zz % 2].reshape(chunk, self.weight.shape[-1])
            return nt(self.grad[pl.ds(first, tile), :], weight)

        self.loads[0].wait()
        for zz in range(self.zs):
            cols = slice(zz * chunk, (zz + 1) * chunk)
            self.loads[1 + zz].wait()

            def body(at):
                made = part_of(pl.multiple_of(rows + at, tile), zz)
                self.send[pl.ds(at, tile), cols] = made.astype(BF)
                self.out[pl.ds(at, tile), cols] = part_of(at, zz)

            over(body)
            if zz + 2 < self.zs:
                self.loads[3 + zz].start()
            yield
        self.mate_part.start()
        self.mate_part.arrived()
        self.rows8[...] = self.others[...]

        def body(at):
            part = pl.ds(at, tile)
            incoming = self.out[part, :] + self.got[part, :].astype(F32)
            stream = self.inputs[part, :].astype(F32)
            centred = stream - jnp.mean(stream, axis=-1, keepdims=True)
            inverse = lax.rsqrt(jnp.mean(centred * centred, axis=-1, keepdims=True) + EPSILON)
            unit = centred * inverse
            scaled = incoming * self.gain[...]
            slope = scaled - jnp.mean(scaled, axis=-1, keepdims=True)
            slope = slope - unit * jnp.mean(scaled * unit, axis=-1, keepdims=True)
            self.out[part, :] = self.stream[part, :] + inverse * slope
            self.rows8[0:1, :] += jnp.sum(incoming * unit, axis=0, keepdims=True)
            self.rows8[1:2, :] += jnp.sum(incoming, axis=0, keepdims=True)

        over(body)
        self.mate_rows.start()
        self.tall[...] = jnp.zeros_like(self.tall)
        yield
        self.mate_rows.arrived()
        self.tall[0:8, :] = self.rows8[...] + self.got8[...]
        turned = jnp.transpose(self.tall[...]).astype(BF)
        self.blocks[...] = turned.reshape(self.blocks.shape)
        yield

    def finish(self):
        self.mate_part.sent()
        self.mate_rows.sent()


def scatter_kernel(zs, orders, fused, *refs):
    refs = list(refs)

    def take(number):
        taken = refs[:number]
        del refs[:number]
        return taken

    count = len(orders)
    parts = take(count - 1 if fused else count)
    crest_in = take(1)[0]
    given = take(6) if fused else None
    outs = take(count)
    crest_out = take(1)[0]
    norm_out = take(1)[0] if fused else None
    send_sems, recv_sems, local_sems = take(3)
    lanes = Lanes(send_sems, recv_sems, None, zs)
    norm = None
    pieces = iter(())
    if fused:
        norm = LastNorm(lanes, given, take(8), norm_out, local_sems)
        for load in norm.loads[:3]:
            load.start()
        parts = [norm.blocks] + parts
        pieces = norm.pieces()
    greet(zs, fused)
    full, zfirst = [], []
    for i, order in enumerate(orders):
        held = take(5 if order == "z" else 4)
        if order == "z":
            zfirst.append(ScatterZ(lanes, parts[i], held, outs[i]))
        else:
            full.append(Scatter(lanes, parts[i], held, outs[i], order))
    late = [zfirst.pop(0)] if fused else []
    crest = Crest(lanes, crest_in, take(1)[0], crest_out)
    crest.one.start()
    order = ends_first(zs)
    for i in range(zs + 3):
        for item in full:
            if i < zs:
                item.begin(order[i])
        if i == 1:
            crest.second()
        if i < zs:
            for item in zfirst:
                item.pass_on(order[i])
        for _ in range((0, 2, 2, 1, 1)[i] if i < 5 else 0):
            next(pieces, None)
        for item in full:
            if 2 <= i < zs + 2:
                item.second(order[i - 2])
        if i == zs:
            for item in zfirst:
                item.total()
            for _ in pieces:
                pass
            for item in late:
                for d in order:
                    item.pass_on(d)
        for item in full:
            if 3 <= i:
                item.third(order[i - 3])
    for item in late:
        item.total()
    crest.finish()
    for item in zfirst + late:
        item.after()
    for item in full:
        item.finish()
    for item in zfirst + late:
        item.finish()
    if fused:
        norm.finish()


def scatter_all(parts, orders, crest, zs, given=None):
    scratch, moves = [], 4
    shapes_in = [(part.shape, part.dtype) for part in parts]
    extra_in, extra_out = [], []
    vmem = pl.BlockSpec(memory_space=pltpu.VMEM)
    specs = [vmem] * (len(parts) + 1)
    if given is not None:
        grad, weight, inputs = given[:3]
        rows, width = inputs.shape
        blocks = (zs, 2, 2, weight.shape[3], 128)
        shapes_in = [(blocks, BF)] + shapes_in
        extra_in = list(given)
        extra_out = [jax.ShapeDtypeStruct((rows, width), F32)]
        hbm = pl.BlockSpec(memory_space=pltpu.HBM)
        specs += [hbm, hbm] + [vmem] * 4
        moves += 2
        scratch += [
            pltpu.VMEM(grad.shape, grad.dtype),
            pltpu.VMEM((2,) + weight.shape[1:], weight.dtype),
            pltpu.VMEM((rows, width), BF),
            pltpu.VMEM((rows, width), BF),
            pltpu.VMEM((8, width), F32),
            pltpu.VMEM((8, width), F32),
            pltpu.VMEM((128, width), F32),
            pltpu.VMEM(blocks, BF),
        ]
    for (shape, dtype), order in zip(shapes_in, orders):
        block = shape[3:]
        if order == "z":
            shapes = [(zs, 2, 2) + block] * 2 + [(2, 2) + block, (2,) + block, block]
            moves += 2 * zs + 2
        else:
            shapes = [(zs, 2) + block] + [(zs,) + block] * 3
            moves += 5 * zs
        scratch += [pltpu.VMEM(shape, dtype) for shape in shapes]
    outs = [jax.ShapeDtypeStruct(shape[3:], F32) for shape, _ in shapes_in]
    outs += [jax.ShapeDtypeStruct(crest.shape, F32)] + extra_out
    return pl.pallas_call(
        functools.partial(scatter_kernel, zs, orders, given is not None),
        out_shape=outs,
        in_specs=specs,
        out_specs=[vmem] * len(outs),
        scratch_shapes=[
            pltpu.SemaphoreType.DMA((moves,)),
            pltpu.SemaphoreType.DMA((moves,)),
            pltpu.SemaphoreType.DMA((3,)),
        ]
        + scratch
        + [pltpu.VMEM((8,) + crest.shape, F32)],
        compiler_params=pltpu.CompilerParams(
            collective_id=2, has_side_effects=True, vmem_limit_bytes=62 * 2**20
        ),
    )(*parts, crest, *extra_in)


def nn(left, right):
    return lax.dot_general(left, right, (((1,), (0,)), ((), ())), preferred_element_type=F32)


def nt(left, right):
    return lax.dot_general(left, right, (((1,), (1,)), ((), ())), preferred_element_type=F32)


def tn(left, right):
    return lax.dot_general(left, right, (((0,), (0,)), ((), ())), preferred_element_type=F32)


def after(value, *others):
    return lax.optimization_barrier((value, others))[0]


class PairSum:
    def __init__(self, left, right, zs):
        held = tn(left, right).astype(BF)
        self.held = held.reshape(zs, 2, -1, held.shape[1])
        self.y = lax.axis_index("y")
        self.sent = pick(self.held, 1 - self.y, 1)
        self.got = swap(self.sent, "y")

    def second(self, *others):
        got = after(self.got, others)
        held = pick(self.held, self.y, 1).astype(F32) + got.astype(F32)
        held = lax.psum_scatter(held.astype(BF), "z", scatter_dimension=0, tiled=False)
        self.held = held.reshape(2, -1, held.shape[-1])

    def third(self):
        at = lax.axis_index("x")
        return pick(self.held, at, 0), swap(pick(self.held, 1 - at, 0), "x")


def norm_forward(stream, gain_vec, bias_vec):
    average = jnp.mean(stream, axis=-1, keepdims=True)
    centred = stream - average
    inverse = lax.rsqrt(jnp.mean(centred * centred, axis=-1, keepdims=True) + EPSILON)
    unit_rows = centred * inverse
    return (unit_rows * gain_vec + bias_vec, unit_rows, inverse)


def unit_rows_of(stream):
    _, unit_rows, inverse = norm_forward(stream, 1.0, 0.0)
    return unit_rows, inverse


def norm_backward(incoming, unit_rows, inverse, gain_vec):
    gain_grad = jnp.sum(incoming * unit_rows, axis=0)
    bias_grad = jnp.sum(incoming, axis=0)
    scaled = incoming * gain_vec
    stream_grad = inverse * (
        scaled
        - jnp.mean(scaled, axis=-1, keepdims=True)
        - unit_rows * jnp.mean(scaled * unit_rows, axis=-1, keepdims=True)
    )
    return (stream_grad, gain_grad, bias_grad)


def turn_tables(positions):
    rates = 10000.0 ** (-jnp.arange(0, ROT_DIM, 2).astype(F32) / ROT_DIM)
    angles = positions[:, None] * rates[None, :]
    cosine, sine = jnp.cos(angles), jnp.sin(angles)
    rest = jnp.ones((positions.shape[0], HEAD_DIM - ROT_DIM), F32)
    zero, none = jnp.zeros_like(rest), jnp.zeros_like(sine)
    return (
        jnp.concatenate([cosine, cosine, rest] * 2, axis=1),
        jnp.concatenate([-sine, none, zero] * 2, axis=1),
        jnp.concatenate([none, sine, zero] * 2, axis=1),
    )


def turn(field, cosine, sine_a, sine_b, direction):
    half = ROT_DIM // 2
    width = field.shape[-1]
    ahead = pltpu.roll(field, width - half, 1)
    behind = pltpu.roll(field, half, 1)
    return field * cosine + direction * (ahead * sine_a + behind * sine_b)


def head_lanes(shape, which):
    lanes = lax.broadcasted_iota(jnp.int32, shape, 1)
    return (lanes >= which * HEAD_DIM) & (lanes < (which + 1) * HEAD_DIM)


def attend_tile(query, keys, values, bias):
    scores = nt(query, keys) + bias
    top = jnp.max(scores, axis=-1, keepdims=True)
    weights = jnp.exp(scores - top)
    total = jnp.sum(weights, axis=-1, keepdims=True)
    return nn(weights.astype(BF), values) / total, top


def attend_kernel(q_ref, k_ref, v_ref, bias_ref, mixed_ref, peak_ref):
    rows = q_ref.shape[0]
    tile = rows // 3 if rows % 3 == 0 and (rows // 3) % 16 == 0 else rows
    keys, values, bias = k_ref[...], v_ref[...], bias_ref[...]
    peaks = [None, None]
    for start in range(0, rows, tile):
        query = q_ref[start : start + tile, :] * BF(HEAD_DIM ** (-0.5))
        outs = []
        for which in range(2):
            one = jnp.where(head_lanes(query.shape, which), query, jnp.zeros_like(query))
            out, top = attend_tile(one, keys, values, bias)
            outs.append(out)
            top = jnp.max(top, axis=0, keepdims=True)
            peaks[which] = top if peaks[which] is None else jnp.maximum(peaks[which], top)
        mixed = jnp.where(head_lanes(outs[0].shape, 0), outs[0], outs[1])
        mixed_ref[start : start + tile, :] = mixed.astype(BF)
    spot = head_lanes((8, 2 * HEAD_DIM), 0)
    peak_ref[0] = jnp.where(
        spot, jnp.broadcast_to(peaks[0], spot.shape), jnp.broadcast_to(peaks[1], spot.shape)
    )


def attend(query, keys, values, bias, offsets):
    rows, tokens = query.shape[0], keys.shape[0]
    pairs = bias.shape[0]
    wide = 2 * HEAD_DIM
    mixed, peak = pl.pallas_call(
        attend_kernel,
        grid=(pairs,),
        out_shape=[
            jax.ShapeDtypeStruct((rows, pairs * wide), BF),
            jax.ShapeDtypeStruct((pairs, 8, wide), F32),
        ],
        in_specs=[
            pl.BlockSpec((rows, wide), lambda j: (0, offsets[0] + j)),
            pl.BlockSpec((tokens, wide), lambda j: (0, offsets[1] + j)),
            pl.BlockSpec((tokens, wide), lambda j: (0, offsets[2] + j)),
            pl.BlockSpec((1, tokens), lambda j: (0, 0)),
        ],
        out_specs=[
            pl.BlockSpec((rows, wide), lambda j: (0, j)),
            pl.BlockSpec((1, 8, wide), lambda j: (j, 0, 0)),
        ],
        compiler_params=pltpu.CompilerParams(vmem_limit_bytes=48 * 2**20),
        cost_estimate=pl.CostEstimate(
            flops=8 * rows * tokens * pairs * wide,
            bytes_accessed=4 * (rows + tokens) * pairs * wide,
            transcendentals=2 * pairs * rows * tokens,
        ),
    )(query, keys, values, bias[:1])
    return mixed, peak[:, 0, ::HEAD_DIM].reshape(-1)


def attend_back_kernel(turned, q_ref, k_ref, v_ref, g_ref, bias_ref, *refs):
    if turned:
        cos_ref, sa_ref, sb_ref = refs[:3]
        refs = refs[3:]
    dq_ref, dk_ref, dv_ref, dk_acc, dv_acc = refs
    rows = q_ref.shape[0]
    tile = rows // 3 if rows % 3 == 0 and (rows // 3) % 128 == 0 else rows
    scale = BF(HEAD_DIM ** (-0.5))
    keys, values, bias = k_ref[...], v_ref[...], bias_ref[...]
    for start in range(0, rows, tile):
        part = slice(start, start + tile)
        query, grad = q_ref[part, :] * scale, g_ref[part, :]
        dq = None
        for which in range(2):
            mine = head_lanes(query.shape, which)
            one = jnp.where(mine, query, jnp.zeros_like(query))
            out = jnp.where(mine, grad, jnp.zeros_like(grad))
            scores = nt(keys, one) + bias
            weights = jnp.exp(scores - jnp.max(scores, axis=0, keepdims=True))
            weights = weights * (1.0 / jnp.sum(weights, axis=0, keepdims=True))
            slope = nt(values, out)
            slope = weights * (slope - jnp.sum(weights * slope, axis=0, keepdims=True))
            slope = slope.astype(BF)
            dv = nn(weights.astype(BF), out)
            dk = nn(slope, one)
            other = jnp.where(head_lanes(keys.shape, which), keys, jnp.zeros_like(keys))
            piece = tn(slope, other * scale)
            dq = piece if dq is None else dq + piece
            if start == 0 and which == 0:
                dv_acc[...] = dv
                dk_acc[...] = dk
            else:
                dv_acc[...] += dv
                dk_acc[...] += dk
        if turned:
            dq = turn(dq, cos_ref[part, :], sa_ref[part, :], sb_ref[part, :], -1.0)
        dq_ref[part, :] = dq.astype(BF)
    dk = dk_acc[...]
    if turned:
        dk = turn(dk, cos_ref[...], sa_ref[...], sb_ref[...], -1.0)
    dk_ref[...] = dk.astype(BF)
    dv_ref[...] = dv_acc[...].astype(BF)


def attend_back(query, keys, values, grad, bias_column, offsets, turns):
    rows, tokens = query.shape[0], keys.shape[0]
    wide = 2 * HEAD_DIM
    pairs = grad.shape[1] // wide
    ins = [query, keys, values, grad, bias_column]
    specs = [
        pl.BlockSpec((rows, wide), lambda j: (0, offsets[0] + j)),
        pl.BlockSpec((tokens, wide), lambda j: (0, offsets[1] + j)),
        pl.BlockSpec((tokens, wide), lambda j: (0, offsets[2] + j)),
        pl.BlockSpec((rows, wide), lambda j: (0, j)),
        pl.BlockSpec((tokens, 1), lambda j: (0, 0)),
    ]
    if turns is not None:
        ins += list(turns)
        specs += [pl.BlockSpec((rows, wide), lambda j: (0, 0))] * 3
    return pl.pallas_call(
        functools.partial(attend_back_kernel, turns is not None),
        grid=(pairs,),
        out_shape=[
            jax.ShapeDtypeStruct((rows, pairs * wide), BF),
            jax.ShapeDtypeStruct((tokens, pairs * wide), BF),
            jax.ShapeDtypeStruct((tokens, pairs * wide), BF),
        ],
        in_specs=specs,
        out_specs=[
            pl.BlockSpec((rows, wide), lambda j: (0, j)),
            pl.BlockSpec((tokens, wide), lambda j: (0, j)),
            pl.BlockSpec((tokens, wide), lambda j: (0, j)),
        ],
        scratch_shapes=[pltpu.VMEM((tokens, wide), F32), pltpu.VMEM((tokens, wide), F32)],
        compiler_params=pltpu.CompilerParams(vmem_limit_bytes=48 * 2**20),
        cost_estimate=pl.CostEstimate(
            flops=20 * rows * tokens * pairs * wide,
            bytes_accessed=8 * (rows + tokens) * pairs * wide,
            transcendentals=2 * pairs * rows * tokens,
        ),
    )(*ins)


def project_kernel(turned, x_ref, w_ref, cos_ref, sa_ref, sb_ref, out_ref):
    wide = 2 * HEAD_DIM
    made = nn(x_ref[...], w_ref[...])

    @pl.when(pl.program_id(0) < turned)
    def _():
        for start in range(0, made.shape[1], wide):
            piece = turn(made[:, start : start + wide], cos_ref[...], sa_ref[...], sb_ref[...], 1.0)
            out_ref[:, start : start + wide] = piece.astype(BF)

    @pl.when(pl.program_id(0) >= turned)
    def _():
        out_ref[...] = made.astype(BF)


def project(rows, weight, turns, turned_columns):
    count, depth = rows.shape
    columns = weight.shape[1]
    block = 2 * HEAD_DIM * (2 if turned_columns % (4 * HEAD_DIM) == 0 else 1)
    table = pl.BlockSpec((count, 2 * HEAD_DIM), lambda j: (0, 0))
    return pl.pallas_call(
        functools.partial(project_kernel, turned_columns // block),
        grid=(columns // block,),
        out_shape=jax.ShapeDtypeStruct((count, columns), BF),
        in_specs=[
            pl.BlockSpec((count, depth), lambda j: (0, 0)),
            pl.BlockSpec((depth, block), lambda j: (0, j)),
            table,
            table,
            table,
        ],
        out_specs=pl.BlockSpec((count, block), lambda j: (0, j)),
        compiler_params=pltpu.CompilerParams(vmem_limit_bytes=48 * 2**20),
        cost_estimate=pl.CostEstimate(
            flops=2 * count * depth * columns,
            bytes_accessed=2 * (count * depth + depth * columns + count * columns),
            transcendentals=0,
        ),
    )(rows, weight, *turns)


PLAN = (
    0, 100, 300, 400, 500, 200, 2000, 1100, 2020, 2010, 2001, 3010, 1000, 1300, 3000, 2011,
    2101, 3011, 1500, 3001, 2220, 2021, 3021, 2100, 2200, 2300, 2110, 2201, 3020, 2210, 1400,
    2111, 2121, 2221, 2120, 2211, 3101, 2301, 5500, 4000, -1, -1, 2400, 3201, 2310, 3110, -1,
    1200, 3111, 3120, -1, -1, -1, 2401, 2410, 2311, 3100, 3200, -1, -1, -1, 3121, -1, -1, -1,
    -1, 2411, 3221, -1, 2421, 2501, 3211, 2500, 2320, -1, -1, 3210, 3220, 4100, 2420, 6000, -1,
    -1, -1, -1, -1, -1, 2510, 2511, 4200, -1, -1, -1, -1, -1, -1, 2321, -1, -1, -1, -1, -1, -1,
    -1, -1, -1, -1, -1, -1, -1, -1, 2521, 7000, 2520,
)


def normalise(stream, gain_vec, bias_vec):
    average = jnp.mean(stream, axis=-1, keepdims=True)
    centred = stream - average
    inverse = lax.rsqrt(jnp.mean(centred * centred, axis=-1, keepdims=True) + EPSILON)
    return centred * inverse * gain_vec + bias_vec


def forward_kernel(zs, *refs):
    refs = list(refs)

    def take(count):
        taken_refs = refs[:count]
        del refs[:count]
        return taken_refs

    shards = take(9)
    quarters_in = take(3)
    inputs_hbm, cot_hbm, cos_ref, sa_ref, sb_ref, self_bias, cross_bias, memory = take(8)
    wholes = take(3)
    quarter_outs = take(3)
    outs = take(15)
    cot_out = take(1)[0]
    peak_out = take(1)[0]
    send_sems, recv_sems, local_sems = take(3)
    w_in, w_a, w_b = take(3)
    (
        x_all, normed_self, taken, mixed_self, stream_cross, normed_cross,
        query_cross, taken_cross, mixed_cross, stream_feed, normed_feed,
        part_send, part_got, vectors, crest,
    ) = take(15)
    lanes = Lanes(send_sems, recv_sems, local_sems, zs)
    z, y, x = lanes.z, lanes.y, lanes.x
    t = lax.axis_index("tensor")
    rows, width = inputs_hbm.shape
    wide = 2 * HEAD_DIM

    def local(source, target):
        return pltpu.make_async_copy(source, target, lanes.local())

    rows_here, inner = shards[1].shape
    rows_kv = shards[6].shape[0]

    def spot(whole, row, count, column, wide_):
        return whole.at[z, y, x, pl.ds(row, count), pl.ds(column, wide_)]

    places = [
        spot(wholes[0], 0, rows_here, 3 * inner, shards[0].shape[1]),
        spot(wholes[0], 0, rows_here, 0, inner),
        spot(wholes[0], 0, rows_here, inner, inner),
        spot(wholes[0], 0, rows_here, 2 * inner, inner),
        spot(wholes[1], 0, rows_here, 0, inner),
        spot(wholes[1], 0, rows_here, inner, inner),
        spot(wholes[2], 0, rows_kv, 0, inner),
        spot(wholes[2], rows_kv, rows_kv, 0, inner),
        spot(wholes[2], 0, rows_here, inner, inner),
    ]
    pieces = [local(shard, place) for shard, place in zip(shards, places)]
    own_inputs = local(inputs_hbm, x_all.at[0])
    own_cot = local(cot_hbm, cot_out.at[0])
    for piece in pieces + [own_inputs, own_cot]:
        piece.start()
    greet(zs, True)

    def mate(source, target):
        return Move(lanes.copy(source, target, {"tensor": 1 - t}), None, None)

    def across(source, target):
        return Move(lanes.copy(source, target, {"x": 1 - x}), None, None)

    mate_inputs = mate(inputs_hbm, x_all.at[1])
    cot_moves = [
        mate(cot_hbm, cot_out.at[1]),
        across(cot_hbm, cot_out.at[2]),
        mate(cot_out.at[2], cot_out.at[3]),
    ]
    feed_moves = [mate(normed_feed.at[0], normed_feed.at[1])]
    mate_self = mate(part_send, part_got)
    mate_normed = mate(normed_cross.at[0], normed_cross.at[1])
    mate_cross = mate(part_send, part_got)
    gathers = [Gather(lanes, whole) for whole in wholes]
    quarters = [
        PairGather(lanes, quarters_in[i], quarter_outs[i], i == 2) for i in range(3)
    ]
    loads = [
        local(whole, held)
        for whole, held in zip(wholes, (w_in, w_a, w_b))
    ]
    results = (
        normed_self, taken, mixed_self, stream_cross, normed_cross,
        query_cross, taken_cross, mixed_cross, stream_feed, normed_feed,
        w_in.at[:, :, :, :, pl.ds(0, 3 * inner)],
        w_a.at[:, :, :, :, pl.ds(0, inner)],
        w_a.at[:, :, :, :, pl.ds(inner, inner)],
        w_b.at[:, :, :, :, pl.ds(inner, inner)],
        vectors,
    )
    saves = [local(held, out) for held, out in zip(results, outs)]

    mate_inputs.start()
    cot_moves[0].start()
    for piece in pieces:
        piece.wait()
    columns = 3 * inner
    pairs = inner // wide
    block = 2 * wide
    tile = 128 if rows % 128 == 0 else rows
    chunk = width // zs
    total = 2 * rows
    step = total // 3 if total % 3 == 0 and (total // 3) % 16 == 0 else total
    ready = set()

    def vec(i):
        return vectors[i : i + 1, :]

    def need(*groups):
        assert ready.issuperset(groups)

    def over(count, size, body):
        @pl.loop(0, count // size)
        def _(i):
            body(pl.ds(pl.multiple_of(i * size, size), size), i)

    def attend_all(query_ref, keys_at, values_at, kv_ref, bias_ref, mixed_ref):
        lane = lax.broadcasted_iota(jnp.int32, (8, wide), 1)
        for j in range(pairs):
            at = slice(j * wide, (j + 1) * wide)
            keys_in = slice(keys_at + j * wide, keys_at + (j + 1) * wide)
            values_in = slice(values_at + j * wide, values_at + (j + 1) * wide)

            def body(part, _):
                query = query_ref[part, at] * BF(HEAD_DIM ** (-0.5))
                outs = []
                for which in range(2):
                    mine = head_lanes(query.shape, which)
                    one = jnp.where(mine, query, jnp.zeros_like(query))
                    out, top = attend_tile(
                        one, kv_ref[:, keys_in], kv_ref[:, values_in], bias_ref[...]
                    )
                    outs.append(out)
                    top = jnp.broadcast_to(jnp.max(top, axis=0, keepdims=True), lane.shape)
                    best = jnp.where(lane == 2 * j + which, top, NEGATIVE)
                    crest[...] = jnp.maximum(crest[...], best)
                made = jnp.where(head_lanes(outs[0].shape, 0), outs[0], outs[1])
                mixed_ref[part, at] = made.astype(BF)

            over(total, step, body)
            yield

    def out_project(mixed_ref, weight, move, send, got, base, target):
        for zz in range(zs):
            cols = slice(zz * chunk, (zz + 1) * chunk)

            def body(part, i):
                left = mixed_ref[pl.ds(pl.multiple_of(rows + i * tile, tile), tile), :]
                send[part, cols] = nt(left, weight(zz)).astype(BF)

            over(rows, tile, body)
        move.start()
        yield
        for zz in range(zs):
            cols = slice(zz * chunk, (zz + 1) * chunk)

            def body(part, _):
                made = nt(mixed_ref[part, :], weight(zz))
                target[part, cols] = made + base(part, cols)

            over(rows, tile, body)
            yield
        move.arrived()

        def body(part, _):
            target[part, :] = target[part, :] + got[part, :].astype(F32)

        over(rows, tile, body)

    def compute():
        need(0)
        own_inputs.wait()
        mate_inputs.arrived()
        loads[0].wait()
        tail = w_in[..., columns : w_in.shape[-1]].reshape(width, w_in.shape[-1] - columns)
        vectors[...] = jnp.transpose(tail.astype(F32))
        saves[10].start()
        saves[14].start()
        crest[...] = jnp.full(crest.shape, NEGATIVE, F32)
        for side in range(2):

            def body(part, i):
                made = normalise(x_all[side, part, :].astype(F32), vec(0), vec(1))
                at = pl.multiple_of(side * rows + i * tile, tile)
                normed_self[pl.ds(at, tile), :] = made.astype(BF)

            over(rows, tile, body)
        saves[0].start()
        yield
        for start in range(0, columns, block):

            def body(part, _):
                weight = w_in[..., start : start + block].reshape(width, block)
                made = nn(normed_self[part, :], weight)
                for at in range(0, block, wide):
                    piece = made[:, at : at + wide]
                    if start + at < 2 * inner:
                        piece = turn(piece, cos_ref[part, :], sa_ref[part, :], sb_ref[part, :], 1.0)
                    taken[part, start + at : start + at + wide] = piece.astype(BF)

            over(total, step, body)
            yield
        saves[1].start()
        yield from attend_all(taken, inner, 2 * inner, taken, self_bias, mixed_self)
        saves[2].start()
        need(1)
        loads[1].wait()
        saves[11].start()
        saves[12].start()
        yield from out_project(
            mixed_self, lambda zz: w_a[zz, :, :, :, 0:inner].reshape(-1, inner), mate_self, part_send, part_got,
            lambda part, cols: x_all[0, part, cols].astype(F32), stream_cross,
        )
        saves[3].start()

        def second_norm(part, _):
            made = normalise(stream_cross[part, :], vec(2), vec(3))
            normed_cross[0, part, :] = made.astype(BF)

        over(rows, tile, second_norm)
        mate_normed.start()
        yield
        need(2)
        loads[2].wait()
        saves[13].start()
        depth = memory.shape[1]
        for side in range(2):
            for start in range(0, inner, block):
                part = slice(side * rows_kv, (side + 1) * rows_kv)
                weight = w_b[:, :, :, part, start : start + block].reshape(depth, block)
                at = side * inner + start
                taken_cross[:, at : at + block] = nn(memory[...], weight).astype(BF)
        saves[6].start()
        yield
        yield
        for side in range(2):
            if side == 1:
                mate_normed.arrived()
                saves[4].start()
            for start in range(0, inner, block):

                def body(part, i):
                    weight = w_a[..., inner + start : inner + start + block].reshape(width, block)
                    made = nn(normed_cross[side, part, :], weight).astype(BF)
                    at = pl.multiple_of(side * rows + i * tile, tile)
                    query_cross[pl.ds(at, tile), start : start + block] = made

                over(rows, tile, body)
                yield
        saves[5].start()
        yield from attend_all(query_cross, 0, inner, taken_cross, cross_bias, mixed_cross)
        saves[7].start()
        mate_self.sent()
        yield from out_project(
            mixed_cross, lambda zz: w_b[zz, :, :, :, inner : 2 * inner].reshape(-1, inner), mate_cross, part_send, part_got,
            lambda part, cols: stream_cross[part, cols], stream_feed,
        )
        saves[8].start()

        def third_norm(part, _):
            made = normalise(stream_feed[part, :], vec(4), vec(5))
            normed_feed[0, part, :] = made.astype(BF)

        over(rows, tile, third_norm)
        feed_moves[0].start()

    items = gathers + quarters
    names = ("begin", "far_first", "step", "far_step", "landed", "own_y_arrived")
    work = compute()
    for entry in PLAN:
        if entry < 0:
            next(work, None)
            continue
        kind, which, k, side = entry // 1000, entry // 100 % 10, entry // 10 % 10, entry % 10
        if kind == 6:
            cot_moves[1].start()
            continue
        if kind == 7:
            cot_moves[1].arrived()
            cot_moves[2].start()
            continue
        item = items[which]
        getattr(item, names[kind])(*((k, side) if kind in (2, 3) else ()))
        if kind == 4:
            ready.add(which)
            if which < 3:
                loads[which].start()
    for _ in work:
        pass
    peak_out[...] = crest[...]
    for i, item in enumerate(items):
        if i not in ready:
            item.landed()
    feed_moves[0].arrived()
    saves[9].start()
    cot_moves[0].arrived()
    cot_moves[2].arrived()
    own_cot.wait()
    for item in gathers + quarters:
        item.sent()
    for move in [mate_inputs, mate_normed, mate_cross] + cot_moves + feed_moves:
        move.sent()
    for save in saves:
        save.wait()


def forward(shards, quarters, inputs, cotangent, turns, self_bias, cross_bias, memory, zs):
    rows, width = inputs.shape
    seq_len, inner = 2 * rows, shards[1].shape[1]
    tokens = memory.shape[0]
    spread = []
    count = shards[1].shape[0]
    for columns in (3 * inner + shards[0].shape[1], 2 * inner, 2 * inner):
        spread.append(jax.ShapeDtypeStruct((zs, 2, 2, count, columns), BF))
    for shard in quarters:
        spread.append(
            jax.ShapeDtypeStruct((zs, 2, 2, shard.shape[0], shard.shape[1] // 2), shard.dtype)
        )
    results = [
        jax.ShapeDtypeStruct((seq_len, width), BF),
        jax.ShapeDtypeStruct((seq_len, 3 * inner), BF),
        jax.ShapeDtypeStruct((seq_len, inner), BF),
        jax.ShapeDtypeStruct((rows, width), F32),
        jax.ShapeDtypeStruct((2, rows, width), BF),
        jax.ShapeDtypeStruct((seq_len, inner), BF),
        jax.ShapeDtypeStruct((tokens, 2 * inner), BF),
        jax.ShapeDtypeStruct((seq_len, inner), BF),
        jax.ShapeDtypeStruct((rows, width), F32),
        jax.ShapeDtypeStruct((2, rows, width), BF),
    ]
    saved = [
        jax.ShapeDtypeStruct((zs, 2, 2, count, columns), BF)
        for columns in (3 * inner, inner, inner, inner)
    ]
    saved.append(jax.ShapeDtypeStruct((shards[0].shape[1], width), F32))
    cot_out = jax.ShapeDtypeStruct((4, rows, width), BF)
    peak = jax.ShapeDtypeStruct((8, 2 * HEAD_DIM), F32)
    moves = 3 * (3 + 8 * (zs - 1)) + 3 * (2 + 4 * (zs - 1)) + 8
    hbm = pl.BlockSpec(memory_space=pltpu.HBM)
    vmem = pl.BlockSpec(memory_space=pltpu.VMEM)
    held = [pltpu.VMEM(shape.shape, shape.dtype) for shape in spread[:3]]
    held += [pltpu.VMEM((2, rows, width), BF)]
    held += [pltpu.VMEM(shape.shape, shape.dtype) for shape in results]
    held += [pltpu.VMEM((rows, width), BF)] * 2
    held += [pltpu.VMEM((shards[0].shape[1], width), F32), pltpu.VMEM(peak.shape, F32)]
    flops = 2 * seq_len * inner * (7 * width + 4 * seq_len) // 1
    made = pl.pallas_call(
        functools.partial(forward_kernel, zs),
        out_shape=spread + results + saved + [cot_out, peak],
        in_specs=[hbm] * 14 + [vmem] * 6,
        out_specs=[hbm] * 22 + [vmem],
        scratch_shapes=[
            pltpu.SemaphoreType.DMA((moves,)),
            pltpu.SemaphoreType.DMA((moves,)),
            pltpu.SemaphoreType.DMA((9 + 2 + 3 + 3 + 15,)),
        ]
        + held,
        compiler_params=pltpu.CompilerParams(
            collective_id=1, has_side_effects=True, vmem_limit_bytes=62 * 2**20
        ),
        cost_estimate=pl.CostEstimate(flops=flops, bytes_accessed=10**8, transcendentals=10**7),
    )(*shards, *quarters, inputs, cotangent, *turns, self_bias, cross_bias, memory)
    return made[3:6], made[6:16], made[16:21], made[21], made[22]


def pair_rows(own):
    return jnp.concatenate([own, swap(own, "tensor")], axis=0)


def group_rows(own):
    both = jnp.stack([own, swap(own, "x")])
    other = swap(both, "tensor")
    return jnp.concatenate([both[0], other[0], both[1], other[1]], axis=0)


def spread_pair(left, right_t):
    rows = left.shape[0] // 2
    got = swap(nt(left[rows:], right_t), "tensor")
    return nt(left[:rows], right_t) + got


def spread_group(product):
    quarter = product.rows // 4
    far_send = product(3 * quarter, quarter)
    far = product(2 * quarter, quarter) + swap(far_send, "tensor")
    got_far = swap(far.astype(BF), "x")
    near = product(0, quarter) + swap(product(quarter, quarter), "tensor")
    return near + got_far.astype(F32)


class Product:
    def __init__(self, terms, transposed):
        self.terms = terms
        self.transposed = transposed
        self.rows = terms[0][0].shape[0]

    def __call__(self, first, count):
        total = None
        for left, right in self.terms:
            part = (nt if self.transposed else nn)(left[first : first + count], right)
            total = part if total is None else total + part
        return total


def per_device(
    inputs,
    cotangent,
    context,
    context_live,
    lengths,
    threshold,
    self_gain,
    self_bias,
    self_query,
    self_key,
    self_value,
    self_output,
    cross_gain,
    cross_bias,
    cross_query,
    cross_key,
    cross_value,
    cross_output,
    feed_gain,
    feed_bias,
    gate_weight,
    up_weight,
    down_weight,
):
    zs = lax.axis_size("z")
    x_at = lax.axis_index("x")
    t_at = lax.axis_index("tensor")
    width = inputs.shape[1]
    rows = inputs.shape[0]
    seq_len = 2 * rows
    inner = self_query.shape[1]
    heads_here = inner // HEAD_DIM
    ff = gate_weight.shape[1] // 2
    shard_rows = self_query.shape[0]

    quarters = [gate_weight, up_weight, down_weight.T]
    vector_list = [self_gain, self_bias, cross_gain, cross_bias, feed_gain, feed_bias]
    stream = inputs.astype(F32)
    local = jnp.arange(rows)
    places = jnp.concatenate([t_at * rows + local, (1 - t_at) * rows + local])
    turns = turn_tables(places.astype(F32))
    self_bias_row = jnp.where(places < lengths[0], 0.0, NEGATIVE).astype(F32)
    tokens = context.shape[1]
    token_rows = -(-tokens // 128) * 128
    cross_bias_row = jnp.pad(
        jnp.where(context_live[0] > 0, 0.0, NEGATIVE).astype(F32),
        (0, token_rows - tokens),
        constant_values=NEGATIVE,
    )
    memory = jnp.pad(context[0], ((0, token_rows - tokens), (0, 0)))
    pairs = inner // (2 * HEAD_DIM)

    if shard_rows % 32 == 0:
        vectors = jnp.pad(jnp.stack(vector_list, axis=1), ((0, 0), (0, 122)))
        spread, made, saved, cot_group, crest = forward(
            [
                vectors,
                self_query,
                self_key,
                self_value,
                self_output.T,
                cross_query,
                cross_key,
                cross_value,
                cross_output.T,
            ],
            quarters,
            inputs,
            cotangent,
            turns,
            self_bias_row[None],
            cross_bias_row[None],
            memory,
            zs,
        )
        in_weight, self_out_t, cross_in, cross_out_t, norms = saved
        (
            normed_self,
            taken,
            mixed_self,
            stream_cross,
            normed_cross,
            query_cross,
            taken_cross,
            mixed_cross,
            stream_feed,
            normed_feed,
        ) = made
        gate_full, up_full, down_t = spread
        normed_cross = normed_cross.reshape(seq_len, width)
        near_feed, cot_group = (v.reshape(-1, width) for v in (normed_feed, cot_group))
    else:
        vectors = jnp.stack(vector_list).astype(F32)
        vectors = jnp.pad(vectors, ((0, 2), (0, 128 - shard_rows)))
        (norms, in_weight, self_out_t, cross_in, memory_weight, cross_out_t, gate_full, up_full, down_t) = (
            gather_all(
                [
                    [vectors],
                    [self_query, self_key, self_value],
                    [self_output.T],
                    [cross_query],
                    [cross_key, cross_value],
                    [cross_output.T],
                ],
                quarters,
                zs,
            )
        )
        norms = norms.reshape(-1, 8, 128)[:, :6, :shard_rows].transpose(1, 0, 2).reshape(6, width)
        in_weight, memory_weight = in_weight.reshape(width, -1), memory_weight.reshape(-1, 2 * inner)
        self_out_t, cross_in, cross_out_t, gate_full, up_full, down_t = (
            w.reshape(width, -1)
            for w in (self_out_t, cross_in, cross_out_t, gate_full, up_full, down_t)
        )
        cot_group = group_rows(cotangent)
        all_inputs = pair_rows(inputs)
        normed, _, _ = norm_forward(all_inputs.astype(F32), norms[0], norms[1])
        normed_self = normed.astype(BF)
        taken = project(normed_self, in_weight, turns, 2 * inner)
        self_bias_rows = jnp.broadcast_to(self_bias_row, (pairs, seq_len))
        mixed_self, peak_self = attend(taken, taken, taken, self_bias_rows, (0, pairs, 2 * pairs))
        stream_cross = stream + spread_pair(mixed_self, self_out_t)
        normed, _, _ = norm_forward(stream_cross, norms[2], norms[3])
        normed_cross = pair_rows(normed.astype(BF))
        query_cross = nn(normed_cross, cross_in).astype(BF)
        taken_cross = nn(memory, memory_weight).astype(BF)
        cross_bias_rows = jnp.broadcast_to(cross_bias_row, (pairs, token_rows))
        mixed_cross, peak_cross = attend(
            query_cross, taken_cross, taken_cross, cross_bias_rows, (0, 0, pairs)
        )
        stream_feed = stream_cross + spread_pair(mixed_cross, cross_out_t)
        normed, _, _ = norm_forward(stream_feed, norms[4], norms[5])
        near_feed = pair_rows(normed.astype(BF))
        crest = jnp.pad(
            jnp.maximum(peak_self, peak_cross)[None], ((0, 7), (0, 128 - heads_here))
        )
    in_weight, self_out_t, cross_in, cross_out_t, gate_full, up_full, down_t = (
        w.reshape(width, -1)
        for w in (in_weight, self_out_t, cross_in, cross_out_t, gate_full, up_full, down_t)
    )
    unit_cross, inverse_cross = unit_rows_of(stream_cross)
    unit_feed, inverse_feed = unit_rows_of(stream_feed)
    far_own = swap(near_feed[:rows], "x")

    def feed_half(normed, cot_rows):
        gate_pre = nn(normed, gate_full)
        upward = nn(normed, up_full)
        sigmoid_gate = jax.nn.sigmoid(gate_pre)
        hidden = (gate_pre * sigmoid_gate * upward).astype(BF)
        grad_hidden = nn(cot_rows, down_t)
        grad_gate = grad_hidden * upward * sigmoid_gate * (1.0 + gate_pre * (1.0 - sigmoid_gate))
        grad_upward = grad_hidden * gate_pre * sigmoid_gate
        return hidden, grad_gate.astype(BF), grad_upward.astype(BF)

    def feed_back(grad_gate, grad_upward):
        return nt(grad_gate, gate_full) + nt(grad_upward, up_full)

    hidden_near, gate_near, up_near = feed_half(near_feed, cot_group[:seq_len])
    far_own, hidden_near, gate_near, up_near = lax.optimization_barrier(
        (far_own, hidden_near, gate_near, up_near)
    )
    far_feed = pair_rows(far_own)
    hidden_far, gate_far, up_far = feed_half(far_feed, cot_group[seq_len:])
    far_sum = feed_back(gate_far[:rows], up_far[:rows]) + swap(
        feed_back(gate_far[rows:], up_far[rows:]), "tensor"
    )
    far_sum = far_sum.astype(BF)
    got_far = swap(far_sum, "x")
    normed_feed = jnp.concatenate([near_feed, far_feed], axis=0)
    hidden = jnp.concatenate([hidden_near, hidden_far], axis=0)
    grad_gate = jnp.concatenate([gate_near, gate_far], axis=0)
    grad_upward = jnp.concatenate([up_near, up_far], axis=0)
    down_pair = PairSum(after(cot_group, far_sum), hidden, zs)
    gate_pair = PairSum(after(normed_feed, far_sum), grad_gate, zs)
    grad_normed = feed_back(gate_near[:rows], up_near[:rows]) + swap(
        feed_back(gate_near[rows:], up_near[rows:]), "tensor"
    )
    got_far = after(got_far, grad_normed, gate_pair.sent, down_pair.sent)
    grad_normed = grad_normed + got_far.astype(F32)
    stream_part, grad_feed_gain, grad_feed_bias = norm_backward(
        grad_normed, unit_feed, inverse_feed, norms[4]
    )
    grad_stream = cotangent.astype(F32) + stream_part
    grad_full = pair_rows(grad_stream.astype(BF))
    up_pair = PairSum(after(normed_feed, grad_full), grad_upward, zs)
    part_cross_output = tn(grad_full, mixed_cross).astype(BF)
    grad_mixed = nn(grad_full, cross_out_t).astype(BF)
    grad_query, grad_keys, grad_values = attend_back(
        query_cross, taken_cross, taken_cross, grad_mixed, cross_bias_row[:, None], (0, 0, pairs), None
    )
    down_pair.second(grad_query)
    grad_normed = spread_pair(grad_query, cross_in)
    part_cross_query = tn(normed_cross, grad_query).astype(BF)
    part_memory = tn(memory, jnp.concatenate([grad_keys, grad_values], axis=1))
    stream_part, grad_cross_gain, grad_cross_bias = norm_backward(
        grad_normed, unit_cross, inverse_cross, norms[2]
    )
    grad_stream = grad_stream + stream_part
    grad_full = pair_rows(grad_stream.astype(BF))
    gate_pair.second(grad_full)
    part_self_output = tn(grad_full, mixed_self)
    grad_mixed = nn(grad_full, self_out_t).astype(BF)
    grad_parts = attend_back(
        taken, taken, taken, grad_mixed, self_bias_row[:, None], (0, pairs, 2 * pairs), turns
    )
    grad_in = jnp.concatenate(grad_parts, axis=1)
    up_pair.second(grad_in)
    part_in = tn(normed_self, grad_in[:, : 2 * inner]).astype(BF)
    part_value = tn(normed_self, grad_parts[2]).astype(BF)
    def blocks(part):
        return part.astype(BF).reshape(zs, 2, 2, -1, part.shape[1])

    if shard_rows % 32 == 0:
        none = jnp.zeros_like(grad_feed_gain)
        other_sums = jnp.stack(
            [none, none, grad_cross_gain, grad_cross_bias, grad_feed_gain, grad_feed_bias, none, none]
        )
        vector_sums, sum_in, sum_value, sum_self_output, sum_cross_output, sum_cross_query, sum_memory, crest, grad_stream = (
            scatter_all(
                [
                    blocks(part_in),
                    blocks(part_value),
                    blocks(part_self_output),
                    blocks(part_cross_output),
                    blocks(part_cross_query),
                    blocks(part_memory),
                ],
                ["z", "x", "y", "y", "x", "y", "z"],
                crest,
                zs,
                (
                    grad_in,
                    in_weight.reshape(zs, 2, 2, shard_rows, -1),
                    inputs,
                    grad_stream,
                    norms[:1],
                    other_sums,
                ),
            )
        )
        vector_sums = vector_sums.T
    else:
        grad_normed = spread_pair(grad_in, in_weight)
        unit_self, inverse_self = unit_rows_of(stream)
        stream_part, grad_self_gain, grad_self_bias = norm_backward(
            grad_normed, unit_self, inverse_self, norms[0]
        )
        grad_stream = grad_stream + stream_part

        vector_sums = jnp.stack(
            [
                grad_self_gain,
                grad_self_bias,
                grad_cross_gain,
                grad_cross_bias,
                grad_feed_gain,
                grad_feed_bias,
            ]
        ).reshape(6, -1, shard_rows)
        vector_sums = vector_sums + swap(vector_sums, "tensor")
        vector_sums = jnp.pad(
            vector_sums.transpose(1, 0, 2), ((0, 0), (0, 2), (0, 128 - shard_rows))
        ).reshape(zs, 2, 2, 8, 128)

        vector_sums, sum_in, sum_value, sum_self_output, sum_cross_output, sum_cross_query, sum_memory, crest = scatter_all(
            [
                vector_sums,
                blocks(part_in),
                blocks(part_value),
                blocks(part_self_output),
                blocks(part_cross_output),
                blocks(part_cross_query),
                blocks(part_memory),
            ],
            ["z", "x", "y", "y", "x", "y", "z"],
            crest,
            zs,
        )
        vector_sums = vector_sums[:, :shard_rows]
    peaks = crest[0, :heads_here]
    factor = jnp.sqrt(threshold[0] / jnp.maximum(peaks, threshold[0]))
    columns = jnp.repeat(factor, HEAD_DIM)[None, :]
    result = stream_feed + spread_group(Product([(hidden, down_t)], True))
    result = result.astype(BF)
    down_keep, down_got = down_pair.third()
    gate_keep, gate_got = gate_pair.third()
    up_keep, up_got = up_pair.third()

    def side_by_side(kept, got):
        low = jnp.where(x_at == 0, kept, got).astype(F32)
        high = jnp.where(x_at == 0, got, kept).astype(F32)
        return jnp.concatenate([low, high], axis=1)

    down_sum = side_by_side(down_keep, down_got).T
    gate_sum = side_by_side(gate_keep, gate_got)
    up_sum = side_by_side(up_keep, up_got)
    return (
        result,
        grad_stream,
        vector_sums[0],
        vector_sums[1],
        sum_in[:, :inner],
        sum_in[:, inner:],
        sum_value,
        sum_self_output.T,
        vector_sums[2],
        vector_sums[3],
        sum_cross_query,
        sum_memory[:, :inner],
        sum_memory[:, inner:],
        sum_cross_output.T,
        vector_sums[4],
        vector_sums[5],
        gate_sum,
        up_sum,
        down_sum,
        peaks,
        self_query.astype(F32) * columns,
        self_key.astype(F32) * columns,
        cross_query.astype(F32) * columns,
        cross_key.astype(F32) * columns,
    )


def solution(mesh):
    count = mesh.shape["dp"]
    mesh = Mesh(
        mesh.devices.reshape(count // 4, 2, 2, mesh.shape["tensor"]), ("z", "y", "x", "tensor")
    )
    dp = ("z", "y", "x")
    both = P(dp + ("tensor",), None)
    split = P(dp)
    row_major = P(dp, "tensor")
    column_major = P("tensor", dp)
    in_specs = (
        both,
        both,
        P(dp, None, None),
        P(dp, None),
        split,
        P(),
        split,
        split,
        row_major,
        row_major,
        row_major,
        column_major,
        split,
        split,
        row_major,
        row_major,
        row_major,
        column_major,
        split,
        split,
        row_major,
        row_major,
        column_major,
    )
    out_specs = (
        both,
        both,
        split,
        split,
        row_major,
        row_major,
        row_major,
        column_major,
        split,
        split,
        row_major,
        row_major,
        row_major,
        column_major,
        split,
        split,
        row_major,
        row_major,
        column_major,
        P("tensor"),
        row_major,
        row_major,
        row_major,
        row_major,
    )
    return jax.shard_map(
        per_device, mesh=mesh, in_specs=in_specs, out_specs=out_specs, check_vma=False
    )
```

```python
import functools

import jax
import jax.numpy as jnp
from jax import lax
from jax.experimental import pallas as pl
from jax.experimental.pallas import tpu as pltpu
from jax.sharding import Mesh
from jax.sharding import PartitionSpec as P

HEAD_DIM = 64
ROT_DIM = 32
EPSILON = 1e-05
NEGATIVE = -1e30
BF = jnp.bfloat16
F32 = jnp.float32


def swap(value, axis):
    return lax.ppermute(value, axis, [(0, 1), (1, 0)])


def pick(value, index, dim):
    return lax.dynamic_index_in_dim(value, index, dim, keepdims=False)


class Lanes:
    def __init__(self, send_sems, recv_sems, local_sems, zs):
        self.send_sems, self.recv_sems, self.local_sems = send_sems, recv_sems, local_sems
        self.used = self.used_local = 0
        self.z = lax.axis_index("z")
        self.y = lax.axis_index("y")
        self.x = lax.axis_index("x")
        self.zs = zs

    def local(self):
        self.used_local += 1
        return self.local_sems.at[self.used_local - 1]

    def copy(self, source, target, device):
        return self.copies([source], target, device)[0]

    def copies(self, sources, target, device):
        slot = self.used
        self.used += 1
        return [
            pltpu.make_async_remote_copy(
                src_ref=source,
                dst_ref=target,
                send_sem=self.send_sems.at[slot],
                recv_sem=self.recv_sems.at[slot],
                device_id=device,
                device_id_type=pl.DeviceIdType.MESH,
            )
            for source in sources
        ]


def guarded(condition, action):
    if condition is None:
        action()
    else:
        pl.when(condition)(action)


class Move:
    def __init__(self, copy, sends, receives):
        self.copy_, self.sends, self.receives = copy, sends, receives

    def start(self):
        guarded(self.sends, self.copy_.start)

    def arrived(self):
        guarded(self.receives, self.copy_.wait_recv)

    def sent(self):
        guarded(self.sends, self.copy_.wait_send)


class Gather:
    def __init__(self, lanes, whole):
        zs, z, y, x = lanes.zs, lanes.z, lanes.y, lanes.x
        own = whole.at[z, y, x]

        def block(zz, yy):
            return whole.at[zz, yy, x]

        def along(source, target, axis, to, sends=None, receives=None):
            return Move(lanes.copy(source, target, {axis: to}), sends, receives)

        self.first = [
            along(own, block(z, y), "y", 1 - y),
            along(own, block(z, y), "x", 1 - x),
        ]
        self.far = [[along(block(z, 1 - y), block(z, 1 - y), "x", 1 - x)]]
        self.steps = []
        for k in range(zs - 1):
            right, left = jnp.maximum(z - k, 0), jnp.minimum(z + k, zs - 1)
            step = []
            for zz, to, sends, receives, got in (
                (right, z + 1, (z >= k) & (z < zs - 1), z >= k + 1, jnp.maximum(z - 1 - k, 0)),
                (left, z - 1, (z + k < zs) & (z > 0), z + k + 1 < zs, jnp.minimum(z + 1 + k, zs - 1)),
            ):
                source = own if k == 0 else block(zz, y)
                move = along(source, block(zz, y), "z", to, sends, receives)
                follow = [
                    along(block(got, y), block(got, y), "y", 1 - y, receives, receives),
                    along(block(got, y), block(got, y), "x", 1 - x, receives, receives),
                    along(block(got, 1 - y), block(got, 1 - y), "x", 1 - x, receives, receives),
                ]
                step.append((move, follow))
            self.steps.append(step)

    def begin(self):
        for move, _ in self.steps[0]:
            move.start()
        for move in self.first:
            move.start()

    def step(self, k, side):
        move, follow = self.steps[k][side]
        move.arrived()
        if k + 1 < len(self.steps):
            self.steps[k + 1][side][0].start()
        follow[0].start()
        follow[1].start()

    def far_first(self):
        self.first[0].arrived()
        self.far[0][0].start()

    def far_step(self, k, side):
        _, follow = self.steps[k][side]
        follow[0].arrived()
        follow[2].start()

    def landed(self):
        self.first[1].arrived()
        self.far[0][0].arrived()
        for step in self.steps:
            for _, follow in step:
                follow[1].arrived()
                follow[2].arrived()

    def sent(self):
        for move in self.first + self.far[0]:
            move.sent()
        for step in self.steps:
            for move, follow in step:
                move.sent()
                for other in follow:
                    other.sent()


class PairGather:
    def __init__(self, lanes, shard, whole, y_first):
        zs, z, y, x = lanes.zs, lanes.z, lanes.y, lanes.x
        ff = whole.shape[-1]
        kept = shard.at[:, pl.ds(pl.multiple_of(x * ff, ff), ff)]
        sent = shard.at[:, pl.ds(pl.multiple_of((1 - x) * ff, ff), ff)]
        self.y_first = y_first

        def along(piece, axis, to, sends=None, receives=None):
            return Move(lanes.copy(piece, piece, {axis: to}), sends, receives)

        self.swap = Move(lanes.copy(sent, whole.at[z, y, x], {"x": 1 - x}), None, None)
        self.local = pltpu.make_async_copy(kept, whole.at[z, y, x], lanes.local())
        self.own_y = along(whole.at[z, y], "y", 1 - y)
        self.steps = []
        for k in range(zs - 1):
            step = []
            for zz, to, sends, receives, got in (
                (jnp.maximum(z - k, 0), z + 1, (z >= k) & (z < zs - 1), z >= k + 1, jnp.maximum(z - 1 - k, 0)),
                (jnp.minimum(z + k, zs - 1), z - 1, (z + k < zs) & (z > 0), z + k + 1 < zs, jnp.minimum(z + 1 + k, zs - 1)),
            ):
                piece = whole.at[zz] if y_first else whole.at[zz, y]
                move = along(piece, "z", to, sends, receives)
                follow = [] if y_first else [along(whole.at[got, y], "y", 1 - y, receives, receives)]
                step.append((move, follow))
            self.steps.append(step)

    def begin(self):
        self.swap.start()
        self.local.start()

    def far_first(self):
        self.swap.arrived()
        self.local.wait()
        self.own_y.start()
        if not self.y_first:
            for move, _ in self.steps[0]:
                move.start()

    def own_y_arrived(self):
        self.own_y.arrived()
        if self.y_first:
            for move, _ in self.steps[0]:
                move.start()

    def step(self, k, side):
        move, follow = self.steps[k][side]
        move.arrived()
        if k + 1 < len(self.steps):
            self.steps[k + 1][side][0].start()
        for other in follow:
            other.start()

    def landed(self):
        if not self.y_first:
            self.own_y.arrived()
        for step in self.steps:
            for move, follow in step:
                for other in follow:
                    other.arrived()

    def sent(self):
        self.swap.sent()
        self.own_y.sent()
        for step in self.steps:
            for move, follow in step:
                move.sent()
                for other in follow:
                    other.sent()


def greet(zs, mates=False):
    z, y, x = lax.axis_index("z"), lax.axis_index("y"), lax.axis_index("x")
    barrier = pltpu.get_barrier_semaphore()

    def signal(device):
        pl.semaphore_signal(barrier, inc=1, device_id=device, device_id_type=pl.DeviceIdType.MESH)

    signal({"x": 1 - x})
    signal({"y": 1 - y})
    pl.when(z > 0)(lambda: signal({"z": z - 1}))
    pl.when(z < zs - 1)(lambda: signal({"z": z + 1}))
    if mates:
        signal({"tensor": 1 - lax.axis_index("tensor")})
    peers = (3 if mates else 2) + (z > 0).astype(jnp.int32) + (z < zs - 1).astype(jnp.int32)
    pl.semaphore_wait(barrier, peers)


def gather_kernel(zs, groups, pairs, *refs):
    shards = sum(groups)
    owns, pair_in = refs[:shards], refs[shards : shards + pairs]
    refs = refs[shards + pairs :]
    outs = refs[: len(groups) + pairs]
    lanes = Lanes(*refs[len(groups) + pairs :], zs)
    z, y, x = lanes.z, lanes.y, lanes.x
    pieces, at = [], 0
    for count, whole in zip(groups, outs):
        width = whole.shape[-1] // count
        for i in range(count):
            target = whole.at[z, y, x, :, pl.ds(i * width, width)]
            pieces.append(pltpu.make_async_copy(owns[at], target, lanes.local()))
            at += 1
    for piece in pieces:
        piece.start()
    greet(zs)
    gathers = [Gather(lanes, whole) for whole in outs[: len(groups)]]
    quarters = [
        PairGather(lanes, pair_in[i], outs[len(groups) + i], i == 0) for i in range(pairs)
    ]
    for quarter in quarters:
        quarter.begin()
    for piece in pieces:
        piece.wait()
    for gather in gathers:
        gather.begin()
    for quarter in quarters:
        quarter.far_first()
    for gather in gathers:
        gather.far_first()
    for k, side in [(k, side) for k in range(zs - 1) for side in range(2)]:
        for gather in gathers:
            gather.step(k, side)
        for quarter in quarters:
            if quarter.y_first:
                if k == 0 and side == 0:
                    quarter.own_y_arrived()
            else:
                quarter.step(k, side)
        for gather in gathers:
            gather.far_step(k, side)
        for quarter in quarters:
            if quarter.y_first:
                quarter.step(k, side)
    for item in gathers + quarters:
        item.landed()
        item.sent()


def gather_all(groups, quarters, zs):
    flat = [shard for group in groups for shard in group] + list(quarters)
    outs = []
    for group in groups:
        columns = sum(shard.shape[1] for shard in group)
        outs.append(
            jax.ShapeDtypeStruct((zs, 2, 2, group[0].shape[0], columns), group[0].dtype)
        )
    for shard in quarters:
        outs.append(
            jax.ShapeDtypeStruct((zs, 2, 2, shard.shape[0], shard.shape[1] // 2), shard.dtype)
        )
    count, pairs = len(groups), len(quarters)
    moves = count * (3 + 8 * (zs - 1)) + pairs * (2 + 4 * (zs - 1))
    hbm = pl.BlockSpec(memory_space=pltpu.HBM)
    return pl.pallas_call(
        functools.partial(gather_kernel, zs, tuple(len(group) for group in groups), pairs),
        out_shape=outs,
        in_specs=[hbm] * len(flat),
        out_specs=[hbm] * len(outs),
        scratch_shapes=[
            pltpu.SemaphoreType.DMA((moves,)),
            pltpu.SemaphoreType.DMA((moves,)),
            pltpu.SemaphoreType.DMA((len(flat),)),
        ],
        compiler_params=pltpu.CompilerParams(collective_id=1, has_side_effects=True),
    )(*flat)


def plus(*terms):
    total = terms[0].astype(F32)
    for term in terms[1:]:
        total = total + term.astype(F32)
    return total


def ends_first(zs):
    order = []
    for i in range(zs // 2):
        order += [zs - 1 - i, i]
    return order


class Line:
    def __init__(self, lanes, part, from_left, from_right):
        zs, z = lanes.zs, lanes.z
        self.zs, self.z, self.part = zs, z, part
        self.from_left, self.from_right = from_left, from_right
        self.right, self.left = {}, {}
        for d in ends_first(zs):
            after, before = jnp.minimum(z + 1, zs - 1), jnp.maximum(z - 1, 0)
            self.right[d] = lanes.copies(
                (part(d), from_left.at[d]), from_left.at[d], {"z": after}
            )
            self.left[d] = lanes.copies(
                (part(d), from_right.at[d]), from_right.at[d], {"z": before}
            )

    def pass_on(self, d):
        for moves, inbox, sends, edge in (
            (self.right[d], self.from_left, self.z < d, self.z == 0),
            (self.left[d], self.from_right, self.z > d, self.z == self.zs - 1),
        ):

            @pl.when(sends & edge)
            def _():
                moves[0].start()

            @pl.when(sends & jnp.logical_not(edge))
            def _():
                moves[1].wait_recv()
                inbox[d] = plus(self.part(d)[...], inbox[d]).astype(inbox.dtype)
                moves[1].start()

    def total(self, sink):
        for d in range(self.zs):

            @pl.when(self.z == d)
            def _():
                terms = [self.part(d)[...]]
                if d > 0:
                    self.right[d][0].wait_recv()
                    terms.append(self.from_left[d])
                if d < self.zs - 1:
                    self.left[d][0].wait_recv()
                    terms.append(self.from_right[d])
                sink[...] = plus(*terms).astype(sink.dtype)

    def finish(self):
        for d in ends_first(self.zs):
            pl.when(self.z < d)(self.right[d][0].wait_send)
            pl.when(self.z > d)(self.left[d][0].wait_send)


class Scatter:
    def __init__(self, lanes, part, held, out, first):
        zs, z, y, x = lanes.zs, lanes.z, lanes.y, lanes.x
        got, near, from_left, from_right = held
        second = "y" if first == "x" else "x"
        self.lanes, self.part, self.got, self.near, self.out = lanes, part, got, near, out
        f, s = (x, y) if first == "x" else (y, x)
        self.f, self.s = f, s

        def block(zz, a, b):
            return part.at[zz, b, a] if first == "x" else part.at[zz, a, b]

        self.block = block
        self.one, self.two = {}, {}
        for zz in ends_first(zs):
            for j, b in enumerate((1 - s, s)):
                self.one[zz, j] = Move(
                    lanes.copy(block(zz, 1 - f, b), got.at[zz, j], {first: 1 - f}), None, None
                )
        for zz in ends_first(zs):
            self.two[zz] = Move(
                lanes.copy(got.at[zz, 0], near.at[zz], {second: 1 - s}), None, None
            )
        self.line = Line(lanes, lambda d: got.at[d, 1], from_left, from_right)

    def begin(self, zz):
        for j in range(2):
            self.one[zz, j].start()

    def second(self, zz):
        self.one[zz, 0].arrived()
        mine, got = self.block(zz, self.f, 1 - self.s), self.got
        got[zz, 0] = plus(mine[...], got[zz, 0]).astype(got.dtype)
        self.two[zz].start()

    def third(self, zz):
        self.one[zz, 1].arrived()
        self.two[zz].arrived()
        mine = self.block(zz, self.f, self.s)
        got = self.got
        got[zz, 1] = plus(mine[...], got[zz, 1], self.near[zz]).astype(got.dtype)
        self.line.pass_on(zz)

    def finish(self):
        self.line.total(self.out)
        self.line.finish()
        for move in list(self.one.values()) + list(self.two.values()):
            move.sent()


class ScatterZ:
    def __init__(self, lanes, part, held, out):
        y, x = lanes.y, lanes.x
        from_left, from_right, held_z, near, last = held
        self.lanes, self.sum_z, self.near, self.last, self.out = lanes, held_z, near, last, out
        self.line = Line(lanes, lambda d: part.at[d], from_left, from_right)
        self.two = Move(lanes.copy(held_z.at[1 - y], near, {"y": 1 - y}), None, None)
        self.three = Move(lanes.copy(near.at[1 - x], last, {"x": 1 - x}), None, None)

    def pass_on(self, d):
        self.line.pass_on(d)

    def total(self):
        self.line.total(self.sum_z)
        self.two.start()

    def after(self):
        self.two.arrived()
        self.near[...] = plus(self.sum_z[self.lanes.y], self.near[...]).astype(self.near.dtype)
        self.three.start()

    def finish(self):
        self.three.arrived()
        self.out[...] = plus(self.near[self.lanes.x], self.last[...]).astype(self.out.dtype)
        self.line.finish()
        self.two.sent()
        self.three.sent()


class Crest:
    def __init__(self, lanes, own, held, out):
        zs, z, y, x = lanes.zs, lanes.z, lanes.y, lanes.x
        near_x, near_y, mine_x, mine_y, right, left, inbox_r, inbox_l = (
            held.at[i] for i in range(8)
        )
        self.zs, self.z, self.own, self.out = zs, z, own, out
        self.near_x, self.near_y, self.mine_x, self.mine_y = near_x, near_y, mine_x, mine_y
        self.ways = (
            (right, inbox_r, z > 0, z < zs - 1),
            (left, inbox_l, z < zs - 1, z > 0),
        )
        self.one = Move(lanes.copy(own, near_x, {"x": 1 - x}), None, None)
        self.two = Move(lanes.copy(mine_x, near_y, {"y": 1 - y}), None, None)
        self.moves = [
            Move(lanes.copy(right, inbox_r, {"z": jnp.minimum(z + 1, zs - 1)}), z < zs - 1, z > 0),
            Move(lanes.copy(left, inbox_l, {"z": jnp.maximum(z - 1, 0)}), z > 0, z < zs - 1),
        ]

    def second(self):
        self.one.arrived()
        self.mine_x[...] = jnp.maximum(self.own[...], self.near_x[...])
        self.two.start()

    def finish(self):
        self.two.arrived()
        self.mine_y[...] = jnp.maximum(self.mine_x[...], self.near_y[...])
        self.out[...] = self.mine_y[...]
        for move, (held, inbox, has_before, has_after) in zip(self.moves, self.ways):

            @pl.when(has_before)
            def _():
                move.copy_.wait_recv()
                self.out[...] = jnp.maximum(self.out[...], inbox[...])
                held[...] = jnp.maximum(self.mine_y[...], inbox[...])

            @pl.when(jnp.logical_not(has_before))
            def _():
                held[...] = self.mine_y[...]

            move.start()
        for move in [self.one, self.two] + self.moves:
            move.sent()


class LastNorm:
    def __init__(self, lanes, given, held, out, local_sems):
        grad_hbm, weight_hbm, self.inputs, self.stream, self.gain, self.others = given
        (
            self.grad, self.weight, self.send, self.got,
            self.rows8, self.got8, self.tall, self.blocks,
        ) = held
        self.out, self.zs = out, lanes.zs
        mate = {"tensor": 1 - lax.axis_index("tensor")}
        self.loads = [pltpu.make_async_copy(grad_hbm, self.grad, local_sems.at[0])] + [
            pltpu.make_async_copy(
                weight_hbm.at[zz], self.weight.at[zz % 2], local_sems.at[1 + zz % 2]
            )
            for zz in range(lanes.zs)
        ]
        self.mate_part = Move(lanes.copy(self.send, self.got, mate), None, None)
        self.mate_rows = Move(lanes.copy(self.rows8, self.got8, mate), None, None)

    def pieces(self):
        rows, width = self.out.shape
        tile = 128 if rows % 128 == 0 else rows
        chunk = width // self.zs

        def over(body):
            @pl.loop(0, rows // tile)
            def _(i):
                body(pl.multiple_of(i * tile, tile))

        def part_of(first, zz):
            weight = self.weight[zz % 2].reshape(chunk, self.weight.shape[-1])
            return nt(self.grad[pl.ds(first, tile), :], weight)

        self.loads[0].wait()
        for zz in range(self.zs):
            cols = slice(zz * chunk, (zz + 1) * chunk)
            self.loads[1 + zz].wait()

            def body(at):
                made = part_of(pl.multiple_of(rows + at, tile), zz)
                self.send[pl.ds(at, tile), cols] = made.astype(BF)
                self.out[pl.ds(at, tile), cols] = part_of(at, zz)

            over(body)
            if zz + 2 < self.zs:
                self.loads[3 + zz].start()
            yield
        self.mate_part.start()
        self.mate_part.arrived()
        self.rows8[...] = self.others[...]

        def body(at):
            part = pl.ds(at, tile)
            incoming = self.out[part, :] + self.got[part, :].astype(F32)
            stream = self.inputs[part, :].astype(F32)
            centred = stream - jnp.mean(stream, axis=-1, keepdims=True)
            inverse = lax.rsqrt(jnp.mean(centred * centred, axis=-1, keepdims=True) + EPSILON)
            unit = centred * inverse
            scaled = incoming * self.gain[...]
            slope = scaled - jnp.mean(scaled, axis=-1, keepdims=True)
            slope = slope - unit * jnp.mean(scaled * unit, axis=-1, keepdims=True)
            self.out[part, :] = self.stream[part, :] + inverse * slope
            self.rows8[0:1, :] += jnp.sum(incoming * unit, axis=0, keepdims=True)
            self.rows8[1:2, :] += jnp.sum(incoming, axis=0, keepdims=True)

        over(body)
        self.mate_rows.start()
        self.tall[...] = jnp.zeros_like(self.tall)
        yield
        self.mate_rows.arrived()
        self.tall[0:8, :] = self.rows8[...] + self.got8[...]
        turned = jnp.transpose(self.tall[...]).astype(BF)
        self.blocks[...] = turned.reshape(self.blocks.shape)
        yield

    def finish(self):
        self.mate_part.sent()
        self.mate_rows.sent()


def scatter_kernel(zs, orders, fused, *refs):
    refs = list(refs)

    def take(number):
        taken = refs[:number]
        del refs[:number]
        return taken

    count = len(orders)
    parts = take(count - 1 if fused else count)
    crest_in = take(1)[0]
    given = take(6) if fused else None
    outs = take(count)
    crest_out = take(1)[0]
    norm_out = take(1)[0] if fused else None
    send_sems, recv_sems, local_sems = take(3)
    lanes = Lanes(send_sems, recv_sems, None, zs)
    norm = None
    pieces = iter(())
    if fused:
        norm = LastNorm(lanes, given, take(8), norm_out, local_sems)
        for load in norm.loads[:3]:
            load.start()
        parts = [norm.blocks] + parts
        pieces = norm.pieces()
    greet(zs, fused)
    full, zfirst = [], []
    for i, order in enumerate(orders):
        held = take(5 if order == "z" else 4)
        if order == "z":
            zfirst.append(ScatterZ(lanes, parts[i], held, outs[i]))
        else:
            full.append(Scatter(lanes, parts[i], held, outs[i], order))
    late = [zfirst.pop(0)] if fused else []
    crest = Crest(lanes, crest_in, take(1)[0], crest_out)
    crest.one.start()
    order = ends_first(zs)
    for i in range(zs + 4):
        for item in full:
            if i < zs:
                item.begin(order[i])
        if i == 1:
            crest.second()
        if i < zs:
            for item in zfirst:
                item.pass_on(order[i])
        for _ in range((0, 2, 2, 1, 1)[i] if i < 5 else 0):
            next(pieces, None)
        for item in full:
            if 2 <= i < zs + 2:
                item.second(order[i - 2])
        if i == zs:
            for item in zfirst:
                item.total()
            for _ in pieces:
                pass
            for item in late:
                for d in order:
                    item.pass_on(d)
        for item in full:
            if 4 <= i:
                item.third(order[i - 4])
    for item in late:
        item.total()
    crest.finish()
    for item in zfirst + late:
        item.after()
    for item in full:
        item.finish()
    for item in zfirst + late:
        item.finish()
    if fused:
        norm.finish()


def scatter_all(parts, orders, crest, zs, given=None):
    scratch, moves = [], 4
    shapes_in = [(part.shape, part.dtype) for part in parts]
    extra_in, extra_out = [], []
    vmem = pl.BlockSpec(memory_space=pltpu.VMEM)
    specs = [vmem] * (len(parts) + 1)
    if given is not None:
        grad, weight, inputs = given[:3]
        rows, width = inputs.shape
        blocks = (zs, 2, 2, weight.shape[3], 128)
        shapes_in = [(blocks, BF)] + shapes_in
        extra_in = list(given)
        extra_out = [jax.ShapeDtypeStruct((rows, width), F32)]
        hbm = pl.BlockSpec(memory_space=pltpu.HBM)
        specs += [hbm, hbm] + [vmem] * 4
        moves += 2
        scratch += [
            pltpu.VMEM(grad.shape, grad.dtype),
            pltpu.VMEM((2,) + weight.shape[1:], weight.dtype),
            pltpu.VMEM((rows, width), BF),
            pltpu.VMEM((rows, width), BF),
            pltpu.VMEM((8, width), F32),
            pltpu.VMEM((8, width), F32),
            pltpu.VMEM((128, width), F32),
            pltpu.VMEM(blocks, BF),
        ]
    for (shape, dtype), order in zip(shapes_in, orders):
        block = shape[3:]
        if order == "z":
            shapes = [(zs, 2, 2) + block] * 2 + [(2, 2) + block, (2,) + block, block]
            moves += 2 * zs + 2
        else:
            shapes = [(zs, 2) + block] + [(zs,) + block] * 3
            moves += 5 * zs
        scratch += [pltpu.VMEM(shape, dtype) for shape in shapes]
    outs = [jax.ShapeDtypeStruct(shape[3:], F32) for shape, _ in shapes_in]
    outs += [jax.ShapeDtypeStruct(crest.shape, F32)] + extra_out
    return pl.pallas_call(
        functools.partial(scatter_kernel, zs, orders, given is not None),
        out_shape=outs,
        in_specs=specs,
        out_specs=[vmem] * len(outs),
        scratch_shapes=[
            pltpu.SemaphoreType.DMA((moves,)),
            pltpu.SemaphoreType.DMA((moves,)),
            pltpu.SemaphoreType.DMA((3,)),
        ]
        + scratch
        + [pltpu.VMEM((8,) + crest.shape, F32)],
        compiler_params=pltpu.CompilerParams(
            collective_id=2, has_side_effects=True, vmem_limit_bytes=62 * 2**20
        ),
    )(*parts, crest, *extra_in)


def nn(left, right):
    return lax.dot_general(left, right, (((1,), (0,)), ((), ())), preferred_element_type=F32)


def nt(left, right):
    return lax.dot_general(left, right, (((1,), (1,)), ((), ())), preferred_element_type=F32)


def tn(left, right):
    return lax.dot_general(left, right, (((0,), (0,)), ((), ())), preferred_element_type=F32)


def after(value, *others):
    return lax.optimization_barrier((value, others))[0]


class PairSum:
    def __init__(self, left, right, zs):
        held = tn(left, right).astype(BF)
        self.held = held.reshape(zs, 2, -1, held.shape[1])
        self.y = lax.axis_index("y")
        self.sent = pick(self.held, 1 - self.y, 1)
        self.got = swap(self.sent, "y")

    def second(self, *others):
        got = after(self.got, others)
        held = pick(self.held, self.y, 1).astype(F32) + got.astype(F32)
        held = lax.psum_scatter(held.astype(BF), "z", scatter_dimension=0, tiled=False)
        self.held = held.reshape(2, -1, held.shape[-1])

    def third(self):
        at = lax.axis_index("x")
        return pick(self.held, at, 0), swap(pick(self.held, 1 - at, 0), "x")


def norm_forward(stream, gain_vec, bias_vec):
    average = jnp.mean(stream, axis=-1, keepdims=True)
    centred = stream - average
    inverse = lax.rsqrt(jnp.mean(centred * centred, axis=-1, keepdims=True) + EPSILON)
    unit_rows = centred * inverse
    return (unit_rows * gain_vec + bias_vec, unit_rows, inverse)


def unit_rows_of(stream):
    _, unit_rows, inverse = norm_forward(stream, 1.0, 0.0)
    return unit_rows, inverse


def norm_backward(incoming, unit_rows, inverse, gain_vec):
    gain_grad = jnp.sum(incoming * unit_rows, axis=0)
    bias_grad = jnp.sum(incoming, axis=0)
    scaled = incoming * gain_vec
    stream_grad = inverse * (
        scaled
        - jnp.mean(scaled, axis=-1, keepdims=True)
        - unit_rows * jnp.mean(scaled * unit_rows, axis=-1, keepdims=True)
    )
    return (stream_grad, gain_grad, bias_grad)


def turn_tables(positions):
    rates = 10000.0 ** (-jnp.arange(0, ROT_DIM, 2).astype(F32) / ROT_DIM)
    angles = positions[:, None] * rates[None, :]
    cosine, sine = jnp.cos(angles), jnp.sin(angles)
    rest = jnp.ones((positions.shape[0], HEAD_DIM - ROT_DIM), F32)
    zero, none = jnp.zeros_like(rest), jnp.zeros_like(sine)
    return (
        jnp.concatenate([cosine, cosine, rest] * 2, axis=1),
        jnp.concatenate([-sine, none, zero] * 2, axis=1),
        jnp.concatenate([none, sine, zero] * 2, axis=1),
    )


def turn(field, cosine, sine_a, sine_b, direction):
    half = ROT_DIM // 2
    width = field.shape[-1]
    ahead = pltpu.roll(field, width - half, 1)
    behind = pltpu.roll(field, half, 1)
    return field * cosine + direction * (ahead * sine_a + behind * sine_b)


def head_lanes(shape, which):
    lanes = lax.broadcasted_iota(jnp.int32, shape, 1)
    return (lanes >= which * HEAD_DIM) & (lanes < (which + 1) * HEAD_DIM)


def attend_tile(query, keys, values, bias):
    scores = nt(query, keys) + bias
    top = jnp.max(scores, axis=-1, keepdims=True)
    weights = jnp.exp(scores - top)
    total = jnp.sum(weights, axis=-1, keepdims=True)
    return nn(weights.astype(BF), values) / total, top


def attend_kernel(q_ref, k_ref, v_ref, bias_ref, mixed_ref, peak_ref):
    rows = q_ref.shape[0]
    tile = rows // 3 if rows % 3 == 0 and (rows // 3) % 16 == 0 else rows
    keys, values, bias = k_ref[...], v_ref[...], bias_ref[...]
    peaks = [None, None]
    for start in range(0, rows, tile):
        query = q_ref[start : start + tile, :] * BF(HEAD_DIM ** (-0.5))
        outs = []
        for which in range(2):
            one = jnp.where(head_lanes(query.shape, which), query, jnp.zeros_like(query))
            out, top = attend_tile(one, keys, values, bias)
            outs.append(out)
            top = jnp.max(top, axis=0, keepdims=True)
            peaks[which] = top if peaks[which] is None else jnp.maximum(peaks[which], top)
        mixed = jnp.where(head_lanes(outs[0].shape, 0), outs[0], outs[1])
        mixed_ref[start : start + tile, :] = mixed.astype(BF)
    spot = head_lanes((8, 2 * HEAD_DIM), 0)
    peak_ref[0] = jnp.where(
        spot, jnp.broadcast_to(peaks[0], spot.shape), jnp.broadcast_to(peaks[1], spot.shape)
    )


def attend(query, keys, values, bias, offsets):
    rows, tokens = query.shape[0], keys.shape[0]
    pairs = bias.shape[0]
    wide = 2 * HEAD_DIM
    mixed, peak = pl.pallas_call(
        attend_kernel,
        grid=(pairs,),
        out_shape=[
            jax.ShapeDtypeStruct((rows, pairs * wide), BF),
            jax.ShapeDtypeStruct((pairs, 8, wide), F32),
        ],
        in_specs=[
            pl.BlockSpec((rows, wide), lambda j: (0, offsets[0] + j)),
            pl.BlockSpec((tokens, wide), lambda j: (0, offsets[1] + j)),
            pl.BlockSpec((tokens, wide), lambda j: (0, offsets[2] + j)),
            pl.BlockSpec((1, tokens), lambda j: (0, 0)),
        ],
        out_specs=[
            pl.BlockSpec((rows, wide), lambda j: (0, j)),
            pl.BlockSpec((1, 8, wide), lambda j: (j, 0, 0)),
        ],
        compiler_params=pltpu.CompilerParams(vmem_limit_bytes=48 * 2**20),
        cost_estimate=pl.CostEstimate(
            flops=8 * rows * tokens * pairs * wide,
            bytes_accessed=4 * (rows + tokens) * pairs * wide,
            transcendentals=2 * pairs * rows * tokens,
        ),
    )(query, keys, values, bias[:1])
    return mixed, peak[:, 0, ::HEAD_DIM].reshape(-1)


def attend_back_kernel(turned, q_ref, k_ref, v_ref, g_ref, bias_ref, *refs):
    if turned:
        cos_ref, sa_ref, sb_ref = refs[:3]
        refs = refs[3:]
    dq_ref, dk_ref, dv_ref, dk_acc, dv_acc = refs
    rows = q_ref.shape[0]
    tile = rows // 3 if rows % 3 == 0 and (rows // 3) % 128 == 0 else rows
    scale = BF(HEAD_DIM ** (-0.5))
    keys, values, bias = k_ref[...], v_ref[...], bias_ref[...]
    for start in range(0, rows, tile):
        part = slice(start, start + tile)
        query, grad = q_ref[part, :] * scale, g_ref[part, :]
        dq = None
        for which in range(2):
            mine = head_lanes(query.shape, which)
            one = jnp.where(mine, query, jnp.zeros_like(query))
            out = jnp.where(mine, grad, jnp.zeros_like(grad))
            scores = nt(keys, one) + bias
            weights = jnp.exp(scores - jnp.max(scores, axis=0, keepdims=True))
            weights = weights * (1.0 / jnp.sum(weights, axis=0, keepdims=True))
            slope = nt(values, out)
            slope = weights * (slope - jnp.sum(weights * slope, axis=0, keepdims=True))
            slope = slope.astype(BF)
            dv = nn(weights.astype(BF), out)
            dk = nn(slope, one)
            other = jnp.where(head_lanes(keys.shape, which), keys, jnp.zeros_like(keys))
            piece = tn(slope, other * scale)
            dq = piece if dq is None else dq + piece
            if start == 0 and which == 0:
                dv_acc[...] = dv
                dk_acc[...] = dk
            else:
                dv_acc[...] += dv
                dk_acc[...] += dk
        if turned:
            dq = turn(dq, cos_ref[part, :], sa_ref[part, :], sb_ref[part, :], -1.0)
        dq_ref[part, :] = dq.astype(BF)
    dk = dk_acc[...]
    if turned:
        dk = turn(dk, cos_ref[...], sa_ref[...], sb_ref[...], -1.0)
    dk_ref[...] = dk.astype(BF)
    dv_ref[...] = dv_acc[...].astype(BF)


def attend_back(query, keys, values, grad, bias_column, offsets, turns):
    rows, tokens = query.shape[0], keys.shape[0]
    wide = 2 * HEAD_DIM
    pairs = grad.shape[1] // wide
    ins = [query, keys, values, grad, bias_column]
    specs = [
        pl.BlockSpec((rows, wide), lambda j: (0, offsets[0] + j)),
        pl.BlockSpec((tokens, wide), lambda j: (0, offsets[1] + j)),
        pl.BlockSpec((tokens, wide), lambda j: (0, offsets[2] + j)),
        pl.BlockSpec((rows, wide), lambda j: (0, j)),
        pl.BlockSpec((tokens, 1), lambda j: (0, 0)),
    ]
    if turns is not None:
        ins += list(turns)
        specs += [pl.BlockSpec((rows, wide), lambda j: (0, 0))] * 3
    return pl.pallas_call(
        functools.partial(attend_back_kernel, turns is not None),
        grid=(pairs,),
        out_shape=[
            jax.ShapeDtypeStruct((rows, pairs * wide), BF),
            jax.ShapeDtypeStruct((tokens, pairs * wide), BF),
            jax.ShapeDtypeStruct((tokens, pairs * wide), BF),
        ],
        in_specs=specs,
        out_specs=[
            pl.BlockSpec((rows, wide), lambda j: (0, j)),
            pl.BlockSpec((tokens, wide), lambda j: (0, j)),
            pl.BlockSpec((tokens, wide), lambda j: (0, j)),
        ],
        scratch_shapes=[pltpu.VMEM((tokens, wide), F32), pltpu.VMEM((tokens, wide), F32)],
        compiler_params=pltpu.CompilerParams(vmem_limit_bytes=48 * 2**20),
        cost_estimate=pl.CostEstimate(
            flops=20 * rows * tokens * pairs * wide,
            bytes_accessed=8 * (rows + tokens) * pairs * wide,
            transcendentals=2 * pairs * rows * tokens,
        ),
    )(*ins)


def project_kernel(turned, x_ref, w_ref, cos_ref, sa_ref, sb_ref, out_ref):
    wide = 2 * HEAD_DIM
    made = nn(x_ref[...], w_ref[...])

    @pl.when(pl.program_id(0) < turned)
    def _():
        for start in range(0, made.shape[1], wide):
            piece = turn(made[:, start : start + wide], cos_ref[...], sa_ref[...], sb_ref[...], 1.0)
            out_ref[:, start : start + wide] = piece.astype(BF)

    @pl.when(pl.program_id(0) >= turned)
    def _():
        out_ref[...] = made.astype(BF)


def project(rows, weight, turns, turned_columns):
    count, depth = rows.shape
    columns = weight.shape[1]
    block = 2 * HEAD_DIM * (2 if turned_columns % (4 * HEAD_DIM) == 0 else 1)
    table = pl.BlockSpec((count, 2 * HEAD_DIM), lambda j: (0, 0))
    return pl.pallas_call(
        functools.partial(project_kernel, turned_columns // block),
        grid=(columns // block,),
        out_shape=jax.ShapeDtypeStruct((count, columns), BF),
        in_specs=[
            pl.BlockSpec((count, depth), lambda j: (0, 0)),
            pl.BlockSpec((depth, block), lambda j: (0, j)),
            table,
            table,
            table,
        ],
        out_specs=pl.BlockSpec((count, block), lambda j: (0, j)),
        compiler_params=pltpu.CompilerParams(vmem_limit_bytes=48 * 2**20),
        cost_estimate=pl.CostEstimate(
            flops=2 * count * depth * columns,
            bytes_accessed=2 * (count * depth + depth * columns + count * columns),
            transcendentals=0,
        ),
    )(rows, weight, *turns)


PLAN = (
    0, 100, 300, 400, 500, 200, 2000, 1100, 2020, 2010, 2001, 3010, 1000, 1300, 3000, 2011,
    2101, 3011, 1500, 3001, 2220, 2021, 3021, 2100, 2200, 2300, 2110, 2201, 3020, 2210, 1400,
    2111, 2121, 2221, 2120, 2211, 3101, 2301, 5500, 4000, -1, -1, 2400, 3201, 2310, 3110, -1,
    1200, 3111, 3120, -1, -1, -1, 2401, 2410, 2311, 3100, 3200, -1, -1, -1, 3121, -1, -1, -1,
    -1, 2411, 3221, -1, 2421, 2501, 3211, 2500, 2320, -1, -1, 3210, 3220, 4100, 2420, 6000, -1,
    -1, -1, -1, -1, -1, 2510, 2511, 4200, -1, -1, -1, -1, -1, -1, 2321, -1, -1, -1, -1, -1, -1,
    -1, -1, -1, -1, -1, -1, -1, -1, 2521, 7000, 2520,
)


def normalise(stream, gain_vec, bias_vec):
    average = jnp.mean(stream, axis=-1, keepdims=True)
    centred = stream - average
    inverse = lax.rsqrt(jnp.mean(centred * centred, axis=-1, keepdims=True) + EPSILON)
    return centred * inverse * gain_vec + bias_vec


def forward_kernel(zs, *refs):
    refs = list(refs)

    def take(count):
        taken_refs = refs[:count]
        del refs[:count]
        return taken_refs

    shards = take(9)
    quarters_in = take(3)
    inputs_hbm, cot_hbm, cos_ref, sa_ref, sb_ref, self_bias, cross_bias, memory = take(8)
    wholes = take(3)
    quarter_outs = take(3)
    outs = take(15)
    cot_out = take(1)[0]
    peak_out = take(1)[0]
    send_sems, recv_sems, local_sems = take(3)
    w_in, w_a, w_b = take(3)
    (
        x_all, normed_self, taken, mixed_self, stream_cross, normed_cross,
        query_cross, taken_cross, mixed_cross, stream_feed, normed_feed,
        part_send, part_got, vectors, crest,
    ) = take(15)
    lanes = Lanes(send_sems, recv_sems, local_sems, zs)
    z, y, x = lanes.z, lanes.y, lanes.x
    t = lax.axis_index("tensor")
    rows, width = inputs_hbm.shape
    wide = 2 * HEAD_DIM

    def local(source, target):
        return pltpu.make_async_copy(source, target, lanes.local())

    rows_here, inner = shards[1].shape
    rows_kv = shards[6].shape[0]

    def spot(whole, row, count, column, wide_):
        return whole.at[z, y, x, pl.ds(row, count), pl.ds(column, wide_)]

    places = [
        spot(wholes[0], 0, rows_here, 3 * inner, shards[0].shape[1]),
        spot(wholes[0], 0, rows_here, 0, inner),
        spot(wholes[0], 0, rows_here, inner, inner),
        spot(wholes[0], 0, rows_here, 2 * inner, inner),
        spot(wholes[1], 0, rows_here, 0, inner),
        spot(wholes[1], 0, rows_here, inner, inner),
        spot(wholes[2], 0, rows_kv, 0, inner),
        spot(wholes[2], rows_kv, rows_kv, 0, inner),
        spot(wholes[2], 0, rows_here, inner, inner),
    ]
    pieces = [local(shard, place) for shard, place in zip(shards, places)]
    own_inputs = local(inputs_hbm, x_all.at[0])
    own_cot = local(cot_hbm, cot_out.at[0])
    for piece in pieces + [own_inputs, own_cot]:
        piece.start()
    greet(zs, True)

    def mate(source, target):
        return Move(lanes.copy(source, target, {"tensor": 1 - t}), None, None)

    def across(source, target):
        return Move(lanes.copy(source, target, {"x": 1 - x}), None, None)

    mate_inputs = mate(inputs_hbm, x_all.at[1])
    cot_moves = [
        mate(cot_hbm, cot_out.at[1]),
        across(cot_hbm, cot_out.at[2]),
        mate(cot_out.at[2], cot_out.at[3]),
    ]
    feed_moves = [mate(normed_feed.at[0], normed_feed.at[1])]
    mate_self = mate(part_send, part_got)
    mate_normed = mate(normed_cross.at[0], normed_cross.at[1])
    mate_cross = mate(part_send, part_got)
    gathers = [Gather(lanes, whole) for whole in wholes]
    quarters = [
        PairGather(lanes, quarters_in[i], quarter_outs[i], i == 2) for i in range(3)
    ]
    loads = [
        local(whole, held)
        for whole, held in zip(wholes, (w_in, w_a, w_b))
    ]
    results = (
        normed_self, taken, mixed_self, stream_cross, normed_cross,
        query_cross, taken_cross, mixed_cross, stream_feed, normed_feed,
        w_in.at[:, :, :, :, pl.ds(0, 3 * inner)],
        w_a.at[:, :, :, :, pl.ds(0, inner)],
        w_a.at[:, :, :, :, pl.ds(inner, inner)],
        w_b.at[:, :, :, :, pl.ds(inner, inner)],
        vectors,
    )
    saves = [local(held, out) for held, out in zip(results, outs)]

    mate_inputs.start()
    cot_moves[0].start()
    for piece in pieces:
        piece.wait()
    columns = 3 * inner
    pairs = inner // wide
    block = 2 * wide
    tile = 128 if rows % 128 == 0 else rows
    chunk = width // zs
    total = 2 * rows
    step = total // 3 if total % 3 == 0 and (total // 3) % 16 == 0 else total
    ready = set()

    def vec(i):
        return vectors[i : i + 1, :]

    def need(*groups):
        assert ready.issuperset(groups)

    def over(count, size, body):
        @pl.loop(0, count // size)
        def _(i):
            body(pl.ds(pl.multiple_of(i * size, size), size), i)

    def attend_all(query_ref, keys_at, values_at, kv_ref, bias_ref, mixed_ref):
        lane = lax.broadcasted_iota(jnp.int32, (8, wide), 1)
        for j in range(pairs):
            at = slice(j * wide, (j + 1) * wide)
            keys_in = slice(keys_at + j * wide, keys_at + (j + 1) * wide)
            values_in = slice(values_at + j * wide, values_at + (j + 1) * wide)

            def body(part, _):
                query = query_ref[part, at] * BF(HEAD_DIM ** (-0.5))
                outs = []
                for which in range(2):
                    mine = head_lanes(query.shape, which)
                    one = jnp.where(mine, query, jnp.zeros_like(query))
                    out, top = attend_tile(
                        one, kv_ref[:, keys_in], kv_ref[:, values_in], bias_ref[...]
                    )
                    outs.append(out)
                    top = jnp.broadcast_to(jnp.max(top, axis=0, keepdims=True), lane.shape)
                    best = jnp.where(lane == 2 * j + which, top, NEGATIVE)
                    crest[...] = jnp.maximum(crest[...], best)
                made = jnp.where(head_lanes(outs[0].shape, 0), outs[0], outs[1])
                mixed_ref[part, at] = made.astype(BF)

            over(total, step, body)
            yield

    def out_project(mixed_ref, weight, move, send, got, base, target):
        for zz in range(zs):
            cols = slice(zz * chunk, (zz + 1) * chunk)

            def body(part, i):
                left = mixed_ref[pl.ds(pl.multiple_of(rows + i * tile, tile), tile), :]
                send[part, cols] = nt(left, weight(zz)).astype(BF)

            over(rows, tile, body)
        move.start()
        yield
        for zz in range(zs):
            cols = slice(zz * chunk, (zz + 1) * chunk)

            def body(part, _):
                made = nt(mixed_ref[part, :], weight(zz))
                target[part, cols] = made + base(part, cols)

            over(rows, tile, body)
            yield
        move.arrived()

        def body(part, _):
            target[part, :] = target[part, :] + got[part, :].astype(F32)

        over(rows, tile, body)

    def compute():
        need(0)
        own_inputs.wait()
        mate_inputs.arrived()
        loads[0].wait()
        tail = w_in[..., columns : w_in.shape[-1]].reshape(width, w_in.shape[-1] - columns)
        vectors[...] = jnp.transpose(tail.astype(F32))
        saves[10].start()
        saves[14].start()
        crest[...] = jnp.full(crest.shape, NEGATIVE, F32)
        for side in range(2):

            def body(part, i):
                made = normalise(x_all[side, part, :].astype(F32), vec(0), vec(1))
                at = pl.multiple_of(side * rows + i * tile, tile)
                normed_self[pl.ds(at, tile), :] = made.astype(BF)

            over(rows, tile, body)
        saves[0].start()
        yield
        for start in range(0, columns, block):

            def body(part, _):
                weight = w_in[..., start : start + block].reshape(width, block)
                made = nn(normed_self[part, :], weight)
                for at in range(0, block, wide):
                    piece = made[:, at : at + wide]
                    if start + at < 2 * inner:
                        piece = turn(piece, cos_ref[part, :], sa_ref[part, :], sb_ref[part, :], 1.0)
                    taken[part, start + at : start + at + wide] = piece.astype(BF)

            over(total, step, body)
            yield
        saves[1].start()
        yield from attend_all(taken, inner, 2 * inner, taken, self_bias, mixed_self)
        saves[2].start()
        need(1)
        loads[1].wait()
        saves[11].start()
        saves[12].start()
        yield from out_project(
            mixed_self, lambda zz: w_a[zz, :, :, :, 0:inner].reshape(-1, inner), mate_self, part_send, part_got,
            lambda part, cols: x_all[0, part, cols].astype(F32), stream_cross,
        )
        saves[3].start()

        def second_norm(part, _):
            made = normalise(stream_cross[part, :], vec(2), vec(3))
            normed_cross[0, part, :] = made.astype(BF)

        over(rows, tile, second_norm)
        mate_normed.start()
        yield
        need(2)
        loads[2].wait()
        saves[13].start()
        depth = memory.shape[1]
        for side in range(2):
            for start in range(0, inner, block):
                part = slice(side * rows_kv, (side + 1) * rows_kv)
                weight = w_b[:, :, :, part, start : start + block].reshape(depth, block)
                at = side * inner + start
                taken_cross[:, at : at + block] = nn(memory[...], weight).astype(BF)
        saves[6].start()
        yield
        yield
        for side in range(2):
            if side == 1:
                mate_normed.arrived()
                saves[4].start()
            for start in range(0, inner, block):

                def body(part, i):
                    weight = w_a[..., inner + start : inner + start + block].reshape(width, block)
                    made = nn(normed_cross[side, part, :], weight).astype(BF)
                    at = pl.multiple_of(side * rows + i * tile, tile)
                    query_cross[pl.ds(at, tile), start : start + block] = made

                over(rows, tile, body)
                yield
        saves[5].start()
        yield from attend_all(query_cross, 0, inner, taken_cross, cross_bias, mixed_cross)
        saves[7].start()
        mate_self.sent()
        yield from out_project(
            mixed_cross, lambda zz: w_b[zz, :, :, :, inner : 2 * inner].reshape(-1, inner), mate_cross, part_send, part_got,
            lambda part, cols: stream_cross[part, cols], stream_feed,
        )
        saves[8].start()

        def third_norm(part, _):
            made = normalise(stream_feed[part, :], vec(4), vec(5))
            normed_feed[0, part, :] = made.astype(BF)

        over(rows, tile, third_norm)
        feed_moves[0].start()

    items = gathers + quarters
    names = ("begin", "far_first", "step", "far_step", "landed", "own_y_arrived")
    work = compute()
    for entry in PLAN:
        if entry < 0:
            next(work, None)
            continue
        kind, which, k, side = entry // 1000, entry // 100 % 10, entry // 10 % 10, entry % 10
        if kind == 6:
            cot_moves[1].start()
            continue
        if kind == 7:
            cot_moves[1].arrived()
            cot_moves[2].start()
            continue
        item = items[which]
        getattr(item, names[kind])(*((k, side) if kind in (2, 3) else ()))
        if kind == 4:
            ready.add(which)
            if which < 3:
                loads[which].start()
    for _ in work:
        pass
    peak_out[...] = crest[...]
    for i, item in enumerate(items):
        if i not in ready:
            item.landed()
    feed_moves[0].arrived()
    saves[9].start()
    cot_moves[0].arrived()
    cot_moves[2].arrived()
    own_cot.wait()
    for item in gathers + quarters:
        item.sent()
    for move in [mate_inputs, mate_normed, mate_cross] + cot_moves + feed_moves:
        move.sent()
    for save in saves:
        save.wait()


def forward(shards, quarters, inputs, cotangent, turns, self_bias, cross_bias, memory, zs):
    rows, width = inputs.shape
    seq_len, inner = 2 * rows, shards[1].shape[1]
    tokens = memory.shape[0]
    spread = []
    count = shards[1].shape[0]
    for columns in (3 * inner + shards[0].shape[1], 2 * inner, 2 * inner):
        spread.append(jax.ShapeDtypeStruct((zs, 2, 2, count, columns), BF))
    for shard in quarters:
        spread.append(
            jax.ShapeDtypeStruct((zs, 2, 2, shard.shape[0], shard.shape[1] // 2), shard.dtype)
        )
    results = [
        jax.ShapeDtypeStruct((seq_len, width), BF),
        jax.ShapeDtypeStruct((seq_len, 3 * inner), BF),
        jax.ShapeDtypeStruct((seq_len, inner), BF),
        jax.ShapeDtypeStruct((rows, width), F32),
        jax.ShapeDtypeStruct((2, rows, width), BF),
        jax.ShapeDtypeStruct((seq_len, inner), BF),
        jax.ShapeDtypeStruct((tokens, 2 * inner), BF),
        jax.ShapeDtypeStruct((seq_len, inner), BF),
        jax.ShapeDtypeStruct((rows, width), F32),
        jax.ShapeDtypeStruct((2, rows, width), BF),
    ]
    saved = [
        jax.ShapeDtypeStruct((zs, 2, 2, count, columns), BF)
        for columns in (3 * inner, inner, inner, inner)
    ]
    saved.append(jax.ShapeDtypeStruct((shards[0].shape[1], width), F32))
    cot_out = jax.ShapeDtypeStruct((4, rows, width), BF)
    peak = jax.ShapeDtypeStruct((8, 2 * HEAD_DIM), F32)
    moves = 3 * (3 + 8 * (zs - 1)) + 3 * (2 + 4 * (zs - 1)) + 8
    hbm = pl.BlockSpec(memory_space=pltpu.HBM)
    vmem = pl.BlockSpec(memory_space=pltpu.VMEM)
    held = [pltpu.VMEM(shape.shape, shape.dtype) for shape in spread[:3]]
    held += [pltpu.VMEM((2, rows, width), BF)]
    held += [pltpu.VMEM(shape.shape, shape.dtype) for shape in results]
    held += [pltpu.VMEM((rows, width), BF)] * 2
    held += [pltpu.VMEM((shards[0].shape[1], width), F32), pltpu.VMEM(peak.shape, F32)]
    flops = 2 * seq_len * inner * (7 * width + 4 * seq_len) // 1
    made = pl.pallas_call(
        functools.partial(forward_kernel, zs),
        out_shape=spread + results + saved + [cot_out, peak],
        in_specs=[hbm] * 14 + [vmem] * 6,
        out_specs=[hbm] * 22 + [vmem],
        scratch_shapes=[
            pltpu.SemaphoreType.DMA((moves,)),
            pltpu.SemaphoreType.DMA((moves,)),
            pltpu.SemaphoreType.DMA((9 + 2 + 3 + 3 + 15,)),
        ]
        + held,
        compiler_params=pltpu.CompilerParams(
            collective_id=1, has_side_effects=True, vmem_limit_bytes=62 * 2**20
        ),
        cost_estimate=pl.CostEstimate(flops=flops, bytes_accessed=10**8, transcendentals=10**7),
    )(*shards, *quarters, inputs, cotangent, *turns, self_bias, cross_bias, memory)
    return made[3:6], made[6:16], made[16:21], made[21], made[22]


def pair_rows(own):
    return jnp.concatenate([own, swap(own, "tensor")], axis=0)


def group_rows(own):
    both = jnp.stack([own, swap(own, "x")])
    other = swap(both, "tensor")
    return jnp.concatenate([both[0], other[0], both[1], other[1]], axis=0)


def spread_pair(left, right_t):
    rows = left.shape[0] // 2
    got = swap(nt(left[rows:], right_t), "tensor")
    return nt(left[:rows], right_t) + got


def spread_group(product):
    quarter = product.rows // 4
    far_send = product(3 * quarter, quarter)
    far = product(2 * quarter, quarter) + swap(far_send, "tensor")
    got_far = swap(far.astype(BF), "x")
    near = product(0, quarter) + swap(product(quarter, quarter), "tensor")
    return near + got_far.astype(F32)


class Product:
    def __init__(self, terms, transposed):
        self.terms = terms
        self.transposed = transposed
        self.rows = terms[0][0].shape[0]

    def __call__(self, first, count):
        total = None
        for left, right in self.terms:
            part = (nt if self.transposed else nn)(left[first : first + count], right)
            total = part if total is None else total + part
        return total


def per_device(
    inputs,
    cotangent,
    context,
    context_live,
    lengths,
    threshold,
    self_gain,
    self_bias,
    self_query,
    self_key,
    self_value,
    self_output,
    cross_gain,
    cross_bias,
    cross_query,
    cross_key,
    cross_value,
    cross_output,
    feed_gain,
    feed_bias,
    gate_weight,
    up_weight,
    down_weight,
):
    zs = lax.axis_size("z")
    x_at = lax.axis_index("x")
    t_at = lax.axis_index("tensor")
    width = inputs.shape[1]
    rows = inputs.shape[0]
    seq_len = 2 * rows
    inner = self_query.shape[1]
    heads_here = inner // HEAD_DIM
    ff = gate_weight.shape[1] // 2
    shard_rows = self_query.shape[0]

    quarters = [gate_weight, up_weight, down_weight.T]
    vector_list = [self_gain, self_bias, cross_gain, cross_bias, feed_gain, feed_bias]
    stream = inputs.astype(F32)
    local = jnp.arange(rows)
    places = jnp.concatenate([t_at * rows + local, (1 - t_at) * rows + local])
    turns = turn_tables(places.astype(F32))
    self_bias_row = jnp.where(places < lengths[0], 0.0, NEGATIVE).astype(F32)
    tokens = context.shape[1]
    token_rows = -(-tokens // 128) * 128
    cross_bias_row = jnp.pad(
        jnp.where(context_live[0] > 0, 0.0, NEGATIVE).astype(F32),
        (0, token_rows - tokens),
        constant_values=NEGATIVE,
    )
    memory = jnp.pad(context[0], ((0, token_rows - tokens), (0, 0)))
    pairs = inner // (2 * HEAD_DIM)

    if shard_rows % 32 == 0:
        vectors = jnp.pad(jnp.stack(vector_list, axis=1), ((0, 0), (0, 122)))
        spread, made, saved, cot_group, crest = forward(
            [
                vectors,
                self_query,
                self_key,
                self_value,
                self_output.T,
                cross_query,
                cross_key,
                cross_value,
                cross_output.T,
            ],
            quarters,
            inputs,
            cotangent,
            turns,
            self_bias_row[None],
            cross_bias_row[None],
            memory,
            zs,
        )
        in_weight, self_out_t, cross_in, cross_out_t, norms = saved
        (
            normed_self,
            taken,
            mixed_self,
            stream_cross,
            normed_cross,
            query_cross,
            taken_cross,
            mixed_cross,
            stream_feed,
            normed_feed,
        ) = made
        gate_full, up_full, down_t = spread
        normed_cross = normed_cross.reshape(seq_len, width)
        near_feed, cot_group = (v.reshape(-1, width) for v in (normed_feed, cot_group))
    else:
        vectors = jnp.stack(vector_list).astype(F32)
        vectors = jnp.pad(vectors, ((0, 2), (0, 128 - shard_rows)))
        (norms, in_weight, self_out_t, cross_in, memory_weight, cross_out_t, gate_full, up_full, down_t) = (
            gather_all(
                [
                    [vectors],
                    [self_query, self_key, self_value],
                    [self_output.T],
                    [cross_query],
                    [cross_key, cross_value],
                    [cross_output.T],
                ],
                quarters,
                zs,
            )
        )
        norms = norms.reshape(-1, 8, 128)[:, :6, :shard_rows].transpose(1, 0, 2).reshape(6, width)
        in_weight, memory_weight = in_weight.reshape(width, -1), memory_weight.reshape(-1, 2 * inner)
        self_out_t, cross_in, cross_out_t, gate_full, up_full, down_t = (
            w.reshape(width, -1)
            for w in (self_out_t, cross_in, cross_out_t, gate_full, up_full, down_t)
        )
        cot_group = group_rows(cotangent)
        all_inputs = pair_rows(inputs)
        normed, _, _ = norm_forward(all_inputs.astype(F32), norms[0], norms[1])
        normed_self = normed.astype(BF)
        taken = project(normed_self, in_weight, turns, 2 * inner)
        self_bias_rows = jnp.broadcast_to(self_bias_row, (pairs, seq_len))
        mixed_self, peak_self = attend(taken, taken, taken, self_bias_rows, (0, pairs, 2 * pairs))
        stream_cross = stream + spread_pair(mixed_self, self_out_t)
        normed, _, _ = norm_forward(stream_cross, norms[2], norms[3])
        normed_cross = pair_rows(normed.astype(BF))
        query_cross = nn(normed_cross, cross_in).astype(BF)
        taken_cross = nn(memory, memory_weight).astype(BF)
        cross_bias_rows = jnp.broadcast_to(cross_bias_row, (pairs, token_rows))
        mixed_cross, peak_cross = attend(
            query_cross, taken_cross, taken_cross, cross_bias_rows, (0, 0, pairs)
        )
        stream_feed = stream_cross + spread_pair(mixed_cross, cross_out_t)
        normed, _, _ = norm_forward(stream_feed, norms[4], norms[5])
        near_feed = pair_rows(normed.astype(BF))
        crest = jnp.pad(
            jnp.maximum(peak_self, peak_cross)[None], ((0, 7), (0, 128 - heads_here))
        )
    in_weight, self_out_t, cross_in, cross_out_t, gate_full, up_full, down_t = (
        w.reshape(width, -1)
        for w in (in_weight, self_out_t, cross_in, cross_out_t, gate_full, up_full, down_t)
    )
    unit_cross, inverse_cross = unit_rows_of(stream_cross)
    unit_feed, inverse_feed = unit_rows_of(stream_feed)
    far_own = swap(near_feed[:rows], "x")

    def feed_half(normed, cot_rows):
        gate_pre = nn(normed, gate_full)
        upward = nn(normed, up_full)
        sigmoid_gate = jax.nn.sigmoid(gate_pre)
        hidden = (gate_pre * sigmoid_gate * upward).astype(BF)
        grad_hidden = nn(cot_rows, down_t)
        grad_gate = grad_hidden * upward * sigmoid_gate * (1.0 + gate_pre * (1.0 - sigmoid_gate))
        grad_upward = grad_hidden * gate_pre * sigmoid_gate
        return hidden, grad_gate.astype(BF), grad_upward.astype(BF)

    def feed_back(grad_gate, grad_upward):
        return nt(grad_gate, gate_full) + nt(grad_upward, up_full)

    hidden_near, gate_near, up_near = feed_half(near_feed, cot_group[:seq_len])
    far_own, hidden_near, gate_near, up_near = lax.optimization_barrier(
        (far_own, hidden_near, gate_near, up_near)
    )
    far_feed = pair_rows(far_own)
    hidden_far, gate_far, up_far = feed_half(far_feed, cot_group[seq_len:])
    far_sum = feed_back(gate_far[:rows], up_far[:rows]) + swap(
        feed_back(gate_far[rows:], up_far[rows:]), "tensor"
    )
    far_sum = far_sum.astype(BF)
    got_far = swap(far_sum, "x")
    normed_feed = jnp.concatenate([near_feed, far_feed], axis=0)
    hidden = jnp.concatenate([hidden_near, hidden_far], axis=0)
    grad_gate = jnp.concatenate([gate_near, gate_far], axis=0)
    grad_upward = jnp.concatenate([up_near, up_far], axis=0)
    down_pair = PairSum(after(cot_group, far_sum), hidden, zs)
    gate_pair = PairSum(after(normed_feed, far_sum), grad_gate, zs)
    grad_normed = feed_back(gate_near[:rows], up_near[:rows]) + swap(
        feed_back(gate_near[rows:], up_near[rows:]), "tensor"
    )
    got_far = after(got_far, grad_normed, gate_pair.sent, down_pair.sent)
    grad_normed = grad_normed + got_far.astype(F32)
    stream_part, grad_feed_gain, grad_feed_bias = norm_backward(
        grad_normed, unit_feed, inverse_feed, norms[4]
    )
    grad_stream = cotangent.astype(F32) + stream_part
    grad_full = pair_rows(grad_stream.astype(BF))
    up_pair = PairSum(after(normed_feed, grad_full), grad_upward, zs)
    part_cross_output = tn(grad_full, mixed_cross).astype(BF)
    grad_mixed = nn(grad_full, cross_out_t).astype(BF)
    grad_query, grad_keys, grad_values = attend_back(
        query_cross, taken_cross, taken_cross, grad_mixed, cross_bias_row[:, None], (0, 0, pairs), None
    )
    down_pair.second(grad_query)
    grad_normed = spread_pair(grad_query, cross_in)
    part_cross_query = tn(normed_cross, grad_query).astype(BF)
    part_memory = tn(memory, jnp.concatenate([grad_keys, grad_values], axis=1))
    stream_part, grad_cross_gain, grad_cross_bias = norm_backward(
        grad_normed, unit_cross, inverse_cross, norms[2]
    )
    grad_stream = grad_stream + stream_part
    grad_full = pair_rows(grad_stream.astype(BF))
    gate_pair.second(grad_full)
    part_self_output = tn(grad_full, mixed_self)
    grad_mixed = nn(grad_full, self_out_t).astype(BF)
    grad_parts = attend_back(
        taken, taken, taken, grad_mixed, self_bias_row[:, None], (0, pairs, 2 * pairs), turns
    )
    grad_in = jnp.concatenate(grad_parts, axis=1)
    up_pair.second(grad_in)
    part_in = tn(normed_self, grad_in[:, : 2 * inner]).astype(BF)
    part_value = tn(normed_self, grad_parts[2]).astype(BF)
    def blocks(part):
        return part.astype(BF).reshape(zs, 2, 2, -1, part.shape[1])

    if shard_rows % 32 == 0:
        none = jnp.zeros_like(grad_feed_gain)
        other_sums = jnp.stack(
            [none, none, grad_cross_gain, grad_cross_bias, grad_feed_gain, grad_feed_bias, none, none]
        )
        vector_sums, sum_in, sum_value, sum_self_output, sum_cross_output, sum_cross_query, sum_memory, crest, grad_stream = (
            scatter_all(
                [
                    blocks(part_in),
                    blocks(part_value),
                    blocks(part_self_output),
                    blocks(part_cross_output),
                    blocks(part_cross_query),
                    blocks(part_memory),
                ],
                ["z", "x", "y", "y", "x", "y", "z"],
                crest,
                zs,
                (
                    grad_in,
                    in_weight.reshape(zs, 2, 2, shard_rows, -1),
                    inputs,
                    grad_stream,
                    norms[:1],
                    other_sums,
                ),
            )
        )
        vector_sums = vector_sums.T
    else:
        grad_normed = spread_pair(grad_in, in_weight)
        unit_self, inverse_self = unit_rows_of(stream)
        stream_part, grad_self_gain, grad_self_bias = norm_backward(
            grad_normed, unit_self, inverse_self, norms[0]
        )
        grad_stream = grad_stream + stream_part

        vector_sums = jnp.stack(
            [
                grad_self_gain,
                grad_self_bias,
                grad_cross_gain,
                grad_cross_bias,
                grad_feed_gain,
                grad_feed_bias,
            ]
        ).reshape(6, -1, shard_rows)
        vector_sums = vector_sums + swap(vector_sums, "tensor")
        vector_sums = jnp.pad(
            vector_sums.transpose(1, 0, 2), ((0, 0), (0, 2), (0, 128 - shard_rows))
        ).reshape(zs, 2, 2, 8, 128)

        vector_sums, sum_in, sum_value, sum_self_output, sum_cross_output, sum_cross_query, sum_memory, crest = scatter_all(
            [
                vector_sums,
                blocks(part_in),
                blocks(part_value),
                blocks(part_self_output),
                blocks(part_cross_output),
                blocks(part_cross_query),
                blocks(part_memory),
            ],
            ["z", "x", "y", "y", "x", "y", "z"],
            crest,
            zs,
        )
        vector_sums = vector_sums[:, :shard_rows]
    peaks = crest[0, :heads_here]
    factor = jnp.sqrt(threshold[0] / jnp.maximum(peaks, threshold[0]))
    columns = jnp.repeat(factor, HEAD_DIM)[None, :]
    result = stream_feed + spread_group(Product([(hidden, down_t)], True))
    result = result.astype(BF)
    down_keep, down_got = down_pair.third()
    gate_keep, gate_got = gate_pair.third()
    up_keep, up_got = up_pair.third()

    def side_by_side(kept, got):
        low = jnp.where(x_at == 0, kept, got).astype(F32)
        high = jnp.where(x_at == 0, got, kept).astype(F32)
        return jnp.concatenate([low, high], axis=1)

    down_sum = side_by_side(down_keep, down_got).T
    gate_sum = side_by_side(gate_keep, gate_got)
    up_sum = side_by_side(up_keep, up_got)
    return (
        result,
        grad_stream,
        vector_sums[0],
        vector_sums[1],
        sum_in[:, :inner],
        sum_in[:, inner:],
        sum_value,
        sum_self_output.T,
        vector_sums[2],
        vector_sums[3],
        sum_cross_query,
        sum_memory[:, :inner],
        sum_memory[:, inner:],
        sum_cross_output.T,
        vector_sums[4],
        vector_sums[5],
        gate_sum,
        up_sum,
        down_sum,
        peaks,
        self_query.astype(F32) * columns,
        self_key.astype(F32) * columns,
        cross_query.astype(F32) * columns,
        cross_key.astype(F32) * columns,
    )


def solution(mesh):
    count = mesh.shape["dp"]
    mesh = Mesh(
        mesh.devices.reshape(count // 4, 2, 2, mesh.shape["tensor"]), ("z", "y", "x", "tensor")
    )
    dp = ("z", "y", "x")
    both = P(dp + ("tensor",), None)
    split = P(dp)
    row_major = P(dp, "tensor")
    column_major = P("tensor", dp)
    in_specs = (
        both,
        both,
        P(dp, None, None),
        P(dp, None),
        split,
        P(),
        split,
        split,
        row_major,
        row_major,
        row_major,
        column_major,
        split,
        split,
        row_major,
        row_major,
        row_major,
        column_major,
        split,
        split,
        row_major,
        row_major,
        column_major,
    )
    out_specs = (
        both,
        both,
        split,
        split,
        row_major,
        row_major,
        row_major,
        column_major,
        split,
        split,
        row_major,
        row_major,
        row_major,
        column_major,
        split,
        split,
        row_major,
        row_major,
        column_major,
        P("tensor"),
        row_major,
        row_major,
        row_major,
        row_major,
    )
    return jax.shard_map(
        per_device, mesh=mesh, in_specs=in_specs, out_specs=out_specs, check_vma=False
    )
```
